32 devices in a mesh: dp: 4 (over y, x), fsdp: 8 (over z, core).
Axes of the slice: x: 2, y: 2, z: 4, core: 2. Of those that a mesh axis runs over, the one named last changes fastest.
Arguments:
- inputs: float32 [64, 256, 512], P(('dp', 'fsdp')), may hold values from -6 to 6
- cotangent: float32 [64, 256, 512], P(('dp', 'fsdp')), may hold values from -6 to 6
- segments: int32 [64, 256], P(('dp', 'fsdp')), may hold values from 0 to 7, never falling along the last dimension, each value on 1 to 96 neighbouring positions
- valid_mask: int32 [64, 256], P(('dp', 'fsdp')), may hold values 0 or 1
- step_count: int32 [1], replicated, may hold values from 1 to 20
- feed_in: float32 [2, 512, 2048], P(None, ('dp', 'fsdp')), may hold values from -0.25 to 0.25
- feed_out: float32 [2, 2048, 512], P(None, ('dp', 'fsdp')), may hold values from -0.125 to 0.125
- square_proj: float32 [6, 512, 512], P(None, ('dp', 'fsdp')), may hold values from -0.53033009 to 0.53033009
- conv_proj: float32 [512, 1024], P(('dp', 'fsdp')), may hold values from -0.25 to 0.25
- small_params: float32 [40, 512], P(None, ('dp', 'fsdp')), may hold values from -0.6 to 1.4
- feed_in_first: float32 [2, 512, 2048], P(None, ('dp', 'fsdp')), may hold values from -0.00061035156 to 0.00061035156
- feed_in_second: float32 [2, 512, 2048], P(None, ('dp', 'fsdp')), may hold values from 7.9214996e-11 to 1.2674399e-09
- feed_out_first: float32 [2, 2048, 512], P(None, ('dp', 'fsdp')), may hold values from -0.00061035156 to 0.00061035156
- feed_out_second: float32 [2, 2048, 512], P(None, ('dp', 'fsdp')), may hold values from 7.9214996e-11 to 1.2674399e-09
- square_first: float32 [6, 512, 512], P(None, ('dp', 'fsdp')), may hold values from -0.00061035156 to 0.00061035156
- square_second: float32 [6, 512, 512], P(None, ('dp', 'fsdp')), may hold values from 7.9214996e-11 to 1.2674399e-09
- conv_first: float32 [512, 1024], P(('dp', 'fsdp')), may hold values from -0.00061035156 to 0.00061035156
- conv_second: float32 [512, 1024], P(('dp', 'fsdp')), may hold values from 7.9214996e-11 to 1.2674399e-09
- small_first: float32 [40, 512], P(None, ('dp', 'fsdp')), may hold values from -0.00061035156 to 0.00061035156
- small_second: float32 [40, 512], P(None, ('dp', 'fsdp')), may hold values from 7.9214996e-11 to 1.2674399e-09
Outputs:
- layer_output: float32 [64, 256, 512], P(('dp', 'fsdp'))
- input_gradient: float32 [64, 256, 512], P(('dp', 'fsdp'))
- gradient_norm: float32 [], replicated
- feed_in_first_next: float32 [2, 512, 2048], P(None, ('dp', 'fsdp'))
- feed_in_second_next: float32 [2, 512, 2048], P(None, ('dp', 'fsdp'))
- feed_in_next: float32 [2, 512, 2048], P(None, ('dp', 'fsdp'))
- feed_out_first_next: float32 [2, 2048, 512], P(None, ('dp', 'fsdp'))
- feed_out_second_next: float32 [2, 2048, 512], P(None, ('dp', 'fsdp'))
- feed_out_next: float32 [2, 2048, 512], P(None, ('dp', 'fsdp'))
- square_first_next: float32 [6, 512, 512], P(None, ('dp', 'fsdp'))
- square_second_next: float32 [6, 512, 512], P(None, ('dp', 'fsdp'))
- square_next: float32 [6, 512, 512], P(None, ('dp', 'fsdp'))
- conv_first_next: float32 [512, 1024], P(('dp', 'fsdp'))
- conv_second_next: float32 [512, 1024], P(('dp', 'fsdp'))
- conv_next: float32 [512, 1024], P(('dp', 'fsdp'))
- small_first_next: float32 [40, 512], P(None, ('dp', 'fsdp'))
- small_second_next: float32 [40, 512], P(None, ('dp', 'fsdp'))
- small_next: float32 [40, 512], P(None, ('dp', 'fsdp'))
The draws below stay inside these ranges and needn't reach their ends.
Inputs may be any that keep to these rules, and one draw needn't show every extreme that they name: `segments`: in each pack the utterance numbers never fall along the frames; each utterance has 1 to 96 frames, and one has exactly 96.
All inputs are finite; a program needn't handle non-finite values. No bound on the sum of `valid_mask` on one device may be relied on, other than what follows from the above.
Results may differ from the reference program's by a relative error of at most 0.0003.
Values sent between devices are 32-bit elements; how exact they have to be, the bound alone decides.
A program may use at most 256 MiB of HBM per device.

```python
import math
import jax
import jax.numpy as jnp
import numpy as np
from jax import lax

D = 512
H = 8
DH = 64
FF = 2048
K = 9
PACK_LEN = 256
UTT_MAX = 96
NVEC = 40
PACKS = 64
PARAMS = 6311936


def draw_square_proj(key, part):
    full_shape = (6, D, D)
    base_draw = jax.random.truncated_normal(key, -4.0, 4.0, full_shape, jnp.float32)
    slot_scale = jnp.array([1.0, 1.0, 1.0, 3.0, 1.0, 1.0], jnp.float32)
    return base_draw * slot_scale[:, None, None] * D ** (-0.5)


def draw_small_params(key, part):
    key_gain, key_bias, key_kernel = jax.random.split(key, 3)
    gain_draw = jax.random.uniform(key_gain, (NVEC, D), jnp.float32, 0.6, 1.4)
    biases = jax.random.uniform(key_bias, (NVEC, D), jnp.float32, -0.4, 0.4)
    kernel = jax.random.uniform(key_kernel, (NVEC, D), jnp.float32, -0.6, 0.6)
    row_index = jnp.arange(NVEC, dtype=jnp.int32)[:, None]
    is_gain = (row_index < 12) & (row_index % 2 == 0)
    is_kernel = row_index >= NVEC - K
    return jnp.where(is_gain, gain_draw, jnp.where(is_kernel, kernel, biases))


def touch_ends(drawn, own_key, low, high):
    spot = [jax.random.randint(jax.random.fold_in(own_key, axis), (), 0, length) for axis, length in enumerate(drawn.shape)]
    longest = drawn.shape.index(max(drawn.shape))
    neighbour = spot[:longest] + [(spot[longest] + 1) % drawn.shape[longest]] + spot[longest + 1:]
    return drawn.at[tuple(spot)].set(low).at[tuple(neighbour)].set(high)


def levels(rng, shape, pieces, least, largest):
    level, own = 1.0, jax.random.fold_in(rng, 6)
    for dim, parts in pieces:
        draws = jnp.exp(jax.random.uniform(jax.random.fold_in(own, dim), (parts,), jnp.float32, least / len(pieces), largest / len(pieces)))
        level = level * jnp.repeat(draws, shape[dim] // parts).reshape([-1 if axis == dim else 1 for axis in range(len(shape))])
    return level


def profile(count, total, bound, slope):
    loads = [(1 << 20) // math.isqrt(standing ** slope) + 1 for standing in range(2, count + 1)]
    surplus, holding = total - bound - (count - 1), [1] * (count - 1)
    while surplus > 0:
        candidates = [i for i in range(count - 1) if holding[i] < bound]
        mass, budget = sum([loads[i] for i in candidates]), surplus
        for i in candidates:
            extra = min(bound - holding[i], max(1, budget * loads[i] // mass), surplus)
            holding[i] = holding[i] + extra
            surplus = surplus - extra
    return np.array([bound] + holding)


def ragged_sizes(own_key, amount, total, most, skew):
    if amount == 2:
        one = jax.random.randint(own_key, (), max(1, total - most), min(most, total - 1) + 1)
        return jnp.stack([one, total - one])
    sizes = jnp.asarray(profile(amount, total, most, skew), jnp.int32)
    pairs = (amount - 1) // 2
    source_of, receiver = sizes[1:1 + 2 * pairs:2], sizes[2:2 + 2 * pairs:2]
    slack = jnp.minimum(source_of - 1, most - receiver)
    moved = jax.random.randint(jax.random.fold_in(own_key, 1), (pairs,), 0, 1 << 20) % (slack + 1)
    sizes = sizes.at[1:1 + 2 * pairs:2].set(source_of - moved).at[2:2 + 2 * pairs:2].set(receiver + moved)
    return sizes[jax.random.permutation(jax.random.fold_in(own_key, 2), amount)]


def normal_values(key, shape, deviation, bound, shards=(), held_as=jnp.bfloat16):
    drawn = jax.random.normal(key, shape, jnp.float32) * deviation
    if len(shards) > 0:
        drawn = levels(key, shape, shards, -0.22, 0.18) * drawn
    return jnp.clip(drawn, min=-bound, max=bound).astype(held_as)


def setup_inputs(seed: int = 0) -> dict:
    key_list = jax.random.split(jax.random.key(seed), 21)
    return {
        "inputs": normal_values(key_list[0], (PACKS, PACK_LEN, D), 1.0, 6.0, ((0, 32),), jnp.float32),
        "cotangent": normal_values(key_list[1], (PACKS, PACK_LEN, D), 1.0, 6.0, ((0, 32),), jnp.float32),
        "segments": jax.vmap(lambda own: jnp.searchsorted(jnp.cumsum(ragged_sizes(own, 8, PACK_LEN, UTT_MAX, 2)), jnp.arange(PACK_LEN), side="right"))(jax.random.split(key_list[2], PACKS)).reshape((PACKS, PACK_LEN)).astype(jnp.int32),
        "valid_mask": touch_ends((jax.random.randint(key_list[3], (PACKS, PACK_LEN), 0, 8) < 7).astype(jnp.int32), jax.random.fold_in(key_list[3], 1), 0, 1),
        "step_count": jax.random.randint(key_list[4], (1,), 1, 21).astype(jnp.int32),
        "feed_in": normal_values(key_list[5], (2, D, FF), D ** -0.5, 0.25, ((1, 32),), jnp.float32),
        "feed_out": normal_values(key_list[6], (2, FF, D), FF ** -0.5, 0.125, ((1, 32),), jnp.float32),
        "square_proj": draw_square_proj(jax.random.fold_in(key_list[20], 71), 0),
        "conv_proj": normal_values(key_list[8], (D, 2 * D), D ** -0.5, 0.25, ((0, 32),), jnp.float32),
        "small_params": draw_small_params(jax.random.fold_in(key_list[20], 71), 0),
        "feed_in_first": normal_values(key_list[10], (2, D, FF), (0.111 * PARAMS ** -0.5), 0.00061035156, ((1, 32),), jnp.float32),
        "feed_in_second": jnp.clip(jnp.exp(math.log(1.2674399307854856e-09) - 2.7725887 * jax.random.uniform(key_list[11], (2, D, FF), jnp.float32) ** levels(key_list[11], (2, D, FF), ((1, 32),), -0.2, 0.2)), 7.921499567409285e-11, 1.2674399307854856e-09),
        "feed_out_first": normal_values(key_list[12], (2, FF, D), (0.111 * PARAMS ** -0.5), 0.00061035156, ((1, 32),), jnp.float32),
        "feed_out_second": jnp.clip(jnp.exp(math.log(1.2674399307854856e-09) - 2.7725887 * jax.random.uniform(key_list[13], (2, FF, D), jnp.float32) ** levels(key_list[13], (2, FF, D), ((1, 32),), -0.2, 0.2)), 7.921499567409285e-11, 1.2674399307854856e-09),
        "square_first": normal_values(key_list[14], (6, D, D), (0.111 * PARAMS ** -0.5), 0.00061035156, ((1, 32),), jnp.float32),
        "square_second": jnp.clip(jnp.exp(math.log(1.2674399307854856e-09) - 2.7725887 * jax.random.uniform(key_list[15], (6, D, D), jnp.float32) ** levels(key_list[15], (6, D, D), ((1, 32),), -0.2, 0.2)), 7.921499567409285e-11, 1.2674399307854856e-09),
        "conv_first": normal_values(key_list[16], (D, 2 * D), (0.111 * PARAMS ** -0.5), 0.00061035156, ((0, 32),), jnp.float32),
        "conv_second": jnp.clip(jnp.exp(math.log(1.2674399307854856e-09) - 2.7725887 * jax.random.uniform(key_list[17], (D, 2 * D), jnp.float32) ** levels(key_list[17], (D, 2 * D), ((0, 32),), -0.2, 0.2)), 7.921499567409285e-11, 1.2674399307854856e-09),
        "small_first": normal_values(key_list[18], (NVEC, D), (0.111 * PARAMS ** -0.5), 0.00061035156, ((1, 32),), jnp.float32),
        "small_second": jnp.clip(jnp.exp(math.log(1.2674399307854856e-09) - 2.7725887 * jax.random.uniform(key_list[19], (NVEC, D), jnp.float32) ** levels(key_list[19], (NVEC, D), ((1, 32),), -0.2, 0.2)), 7.921499567409285e-11, 1.2674399307854856e-09),
    }


PRECISE = lax.Precision.HIGHEST
NORM_EPS = 1e-05
BETA_ONE = 0.9
BETA_TWO = 0.999
ADAM_EPS = 1e-08
CLIP_NORM = 1.0
MATRIX_RATE = 0.03
VECTOR_RATE = 0.4
MATRIX_DECAY = 0.01

def matmul(left, right):
    return jnp.dot(left, right, precision=PRECISE, preferred_element_type=jnp.float32)

def swish_unit(values):
    return values * jax.nn.sigmoid(values)

def layer_norm(values, gain_row, bias_row):
    centred = values - lax.optimization_barrier(jnp.mean(values, axis=-1, keepdims=True))
    variance = lax.optimization_barrier(jnp.mean(centred * centred, axis=-1, keepdims=True))
    return centred * lax.rsqrt(variance + NORM_EPS) * gain_row + bias_row

def feed_forward(normed, weight_in, weight_out, bias_in, bias_out):
    return matmul(swish_unit(matmul(normed, weight_in) + bias_in), weight_out) + bias_out

def sinusoid(offsets):
    half_width = D // 2
    frequency = jnp.exp(jnp.arange(half_width, dtype=jnp.int32).astype(jnp.float32) * (-2.0 * math.log(10000.0) / D))
    angles = offsets[:, None] * frequency[None, :]
    return jnp.concatenate([jnp.sin(angles), jnp.cos(angles)], axis=1)

def block_scores(arrays, block_item, length, block_rows):
    key_heads, value_heads, position_heads, segment, valid = arrays
    content_query, position_query, first_row = block_item
    content = jnp.einsum('ihc,jhc->hij', content_query, key_heads, precision=PRECISE)
    position_raw = jnp.einsum('ihc,shc->his', position_query, position_heads, precision=PRECISE)
    flattened = position_raw.reshape(H, block_rows * 2 * length)
    flattened = jnp.concatenate([flattened, jnp.zeros((H, length), jnp.float32)], axis=1)
    shifted = lax.dynamic_slice_in_dim(flattened, length - 1 - first_row, block_rows * (2 * length - 1), 1)
    relative = shifted.reshape(H, block_rows, 2 * length - 1)[:, :, :length]
    query_rows = first_row + jnp.arange(block_rows, dtype=jnp.int32)
    key_rows = jnp.arange(length, dtype=jnp.int32)
    query_segment = lax.dynamic_slice_in_dim(segment, first_row, block_rows, 0)
    same_segment = (query_segment[:, None] == segment[None, :]) & (valid[None, :] > 0)
    allowed = same_segment | (query_rows[:, None] == key_rows[None, :])
    scores = (content + relative) * (1.0 / math.sqrt(DH))
    scores = jnp.where(allowed[None, :, :], scores, -1e+30)
    row_peak = lax.optimization_barrier(jnp.max(scores, axis=-1, keepdims=True))
    weights = jnp.exp(scores - row_peak)
    weights = weights / lax.optimization_barrier(jnp.sum(weights, axis=-1, keepdims=True))
    context = jnp.einsum('hij,jhc->ihc', weights, value_heads, precision=PRECISE)
    return context.reshape(block_rows, D)

def attention(normed, segment, valid, square, small_rows):
    length = normed.shape[0]
    block_rows = min(512, length)
    block_count = length // block_rows
    queries = matmul(normed, square[0]) + small_rows[12]
    key_heads = matmul(normed, square[1]).reshape(length, H, DH)
    value_heads = (matmul(normed, square[2]) + small_rows[13]).reshape(length, H, DH)
    offsets = (length - 1 - jnp.arange(2 * length, dtype=jnp.int32)).astype(jnp.float32)
    position_heads = matmul(sinusoid(offsets), square[4]).reshape(2 * length, H, DH)
    content_query = (queries + small_rows[15]).reshape(block_count, block_rows, H, DH)
    position_query = (queries + small_rows[16]).reshape(block_count, block_rows, H, DH)
    first_rows = jnp.arange(block_count, dtype=jnp.int32) * block_rows
    arrays = (key_heads, value_heads, position_heads, segment, valid)
    checked = jax.checkpoint(lambda shared_arrays, block_item: block_scores(shared_arrays, block_item, length, block_rows))
    context = lax.map(lambda block_item: checked(arrays, block_item), (content_query, position_query, first_rows))
    return matmul(context.reshape(length, D), square[3]) + small_rows[14]

def convolution(normed, segment, valid, conv_proj, square, small_rows):
    length = normed.shape[0]
    doubled = matmul(normed, conv_proj) + jnp.concatenate([small_rows[19], small_rows[20]])
    gated = doubled[:, :D] * jax.nn.sigmoid(doubled[:, D:]) * valid.astype(jnp.float32)[:, None]
    half_kernel = (K - 1) // 2
    padded = jnp.pad(gated, ((half_kernel, half_kernel), (0, 0)))
    segment_pad = jnp.pad(segment, (half_kernel, half_kernel), constant_values=-1)
    kernel_first = 23 + 2 * (FF // D)
    mixed_rows = jnp.zeros_like(gated) + small_rows[21]
    for tap_index in range(K):
        matching = (segment_pad[tap_index:tap_index + length] == segment).astype(jnp.float32)[:, None]
        mixed_rows = mixed_rows + matching * padded[tap_index:tap_index + length] * small_rows[kernel_first + tap_index]
    normed_inner = layer_norm(mixed_rows, small_rows[6], small_rows[7])
    return matmul(swish_unit(normed_inner), square[5]) + small_rows[22]

def conformer(inputs_pack, segment, valid, params):
    feed_in, feed_out, square, conv_proj, small_rows = params
    bias_count = FF // D
    first_bias = small_rows[23:23 + bias_count].reshape(FF)
    second_bias = small_rows[23 + bias_count:23 + 2 * bias_count].reshape(FF)
    hidden = inputs_pack + 0.5 * feed_forward(layer_norm(inputs_pack, small_rows[0], small_rows[1]), feed_in[0], feed_out[0], first_bias, small_rows[17])
    hidden = hidden + attention(layer_norm(hidden, small_rows[2], small_rows[3]), segment, valid, square, small_rows)
    hidden = hidden + convolution(layer_norm(hidden, small_rows[4], small_rows[5]), segment, valid, conv_proj, square, small_rows)
    hidden = hidden + 0.5 * feed_forward(layer_norm(hidden, small_rows[8], small_rows[9]), feed_in[1], feed_out[1], second_bias, small_rows[18])
    return layer_norm(hidden, small_rows[10], small_rows[11])

def adamw_update(weight, first, second, gradient, clip_factor, step_float, step_rate, decay_rate):
    clipped = clip_factor * gradient
    first_next = BETA_ONE * first + (1.0 - BETA_ONE) * clipped
    second_next = BETA_TWO * second + (1.0 - BETA_TWO) * clipped * clipped
    first_hat = first_next / (1.0 - jnp.power(BETA_ONE, step_float))
    second_hat = second_next / (1.0 - jnp.power(BETA_TWO, step_float))
    weight_next = weight - step_rate * (first_hat / (jnp.sqrt(second_hat) + ADAM_EPS) + decay_rate * weight)
    return (first_next, second_next, weight_next)

def pack_function(params, packed_item):
    return conformer(packed_item[0], packed_item[1], packed_item[2], params)

def reference(inputs, cotangent, segments, valid_mask, step_count, feed_in, feed_out, square_proj, conv_proj, small_params, feed_in_first, feed_in_second, feed_out_first, feed_out_second, square_first, square_second, conv_first, conv_second, small_first, small_second):
    weights = (feed_in, feed_out, square_proj, conv_proj, small_params)
    checked_pack = jax.checkpoint(pack_function)

    def whole(inputs_all, params):
        return lax.map(lambda packed_item: checked_pack(params, packed_item), (inputs_all, segments, valid_mask))
    layer_output, pull_back = jax.vjp(whole, inputs, weights)
    input_gradient, gradients = pull_back(cotangent)
    squared = sum((jnp.sum(grad_part * grad_part) for grad_part in gradients))
    gradient_norm = jnp.sqrt(squared)
    clip_factor = jnp.minimum(1.0, CLIP_NORM / (gradient_norm + 1e-06))
    step_float = step_count[0].astype(jnp.float32)
    firsts = (feed_in_first, feed_out_first, square_first, conv_first, small_first)
    seconds = (feed_in_second, feed_out_second, square_second, conv_second, small_second)
    rates = (MATRIX_RATE, MATRIX_RATE, MATRIX_RATE, MATRIX_RATE, VECTOR_RATE)
    decays = (MATRIX_DECAY, MATRIX_DECAY, MATRIX_DECAY, MATRIX_DECAY, 0.0)
    results = [adamw_update(weights[number], firsts[number], seconds[number], gradients[number], clip_factor, step_float, rates[number], decays[number]) for number in range(5)]
    return (layer_output, input_gradient, gradient_norm, results[0][0], results[0][1], results[0][2], results[1][0], results[1][1], results[1][2], results[2][0], results[2][1], results[2][2], results[3][0], results[3][1], results[3][2], results[4][0], results[4][1], results[4][2])
```

```python
import functools
import math

import jax
import jax.numpy as jnp
import numpy as np
from jax import lax
from jax.experimental import pallas as pl
from jax.experimental.pallas import tpu as pltpu
from jax.sharding import PartitionSpec as P

D = 512
H = 8
DH = 64
FF = 2048
K = 9
NC = FF // D
TAP = 23 + 2 * NC
NORM_EPS = 1e-05
BETA_ONE = 0.9
BETA_TWO = 0.999
ADAM_EPS = 1e-08
CLIP_NORM = 1.0
MATRIX_RATE = 0.03
VECTOR_RATE = 0.4
MATRIX_DECAY = 0.01
VMEM_LIMIT = 60 * 2**20

f32 = jnp.float32
bf16 = jnp.bfloat16
NN = (((1,), (0,)), ((), ()))
NT = (((1,), (1,)), ((), ()))
TN = (((0,), (0,)), ((), ()))


def split(value):
    high = value.astype(bf16)
    return high, (value - high.astype(f32)).astype(bf16)


def dot(left, right, dims):
    return lax.dot_general(left, right, dims, preferred_element_type=f32)


def dot3(left, right, dims):
    return dot(left[0], right[0], dims) + (dot(left[0], right[1], dims) + dot(left[1], right[0], dims))


def normalize(values):
    centred = values - jnp.mean(values, axis=-1, keepdims=True)
    inverse = lax.rsqrt(jnp.mean(centred * centred, axis=-1, keepdims=True) + NORM_EPS)
    return centred * inverse, inverse


def normalize_back(scaled, xhat, inverse):
    return (scaled - jnp.mean(scaled, axis=-1, keepdims=True) - xhat * jnp.mean(scaled * xhat, axis=-1, keepdims=True)) * inverse


def column_sum(values):
    return jnp.sum(values, axis=0, keepdims=True)


def row(rows_ref, index):
    return rows_ref[pl.ds(index, 1), :]


def store_split(pair_ref, value):
    high, low = split(value)
    pair_ref[0] = high
    pair_ref[1] = low


def load_split(pair_ref, *index):
    if index:
        return pair_ref[(0,) + index], pair_ref[(1,) + index]
    return pair_ref[0], pair_ref[1]


def ffn_forward_chunk(normed, u_ref, win, wout, bias):
    u = dot3(normed, split(win), NN) + bias
    u_ref[...] = u
    return dot3(split(u * jax.nn.sigmoid(u)), split(wout), NN)


def ffn_backward_chunk(normed, u, df, win, wout):
    sig = jax.nn.sigmoid(u)
    dwout = dot3(split(u * sig), df, TN)
    du = dot3(df, split(wout), NT) * (sig * (1.0 + u * (1.0 - sig)))
    du_split = split(du)
    dwin = dot3(normed, du_split, TN)
    return dwin, dwout, column_sum(du), dot3(du_split, split(win), NT)


def ffn1_forward_kernel(x_ref, win_ref, wout_ref, s_ref, a1_ref, u_ref, normed):
    chunk = pl.program_id(0)

    @pl.when(chunk == 0)
    def _():
        xhat, _ = normalize(x_ref[...])
        store_split(normed, xhat * s_ref[0:1] + s_ref[1:2])
        a1_ref[...] = x_ref[...] + 0.5 * s_ref[17:18]

    out = ffn_forward_chunk(load_split(normed), u_ref, win_ref[...], wout_ref[...], row(s_ref, 23 + chunk))
    a1_ref[...] += 0.5 * out


def ffn1_forward(x, win, wout, s):
    frames = x.shape[0]
    whole = pl.BlockSpec((frames, D), lambda c: (0, 0))
    return pl.pallas_call(
        ffn1_forward_kernel,
        grid=(NC,),
        in_specs=[
            whole,
            pl.BlockSpec((D, D), lambda c: (0, c)),
            pl.BlockSpec((D, D), lambda c: (c, 0)),
            pl.BlockSpec(s.shape, lambda c: (0, 0)),
        ],
        out_specs=[whole, pl.BlockSpec((frames, D), lambda c: (0, c))],
        out_shape=[jax.ShapeDtypeStruct((frames, D), f32), jax.ShapeDtypeStruct((frames, FF), f32)],
        scratch_shapes=[pltpu.VMEM((2, frames, D), bf16)],
        compiler_params=pltpu.CompilerParams(vmem_limit_bytes=VMEM_LIMIT),
        name="ffn1_forward",
    )(x, win, wout, s)


def ffn1_backward_kernel(da_ref, x_ref, u_ref, win_ref, wout_ref, s_ref, dx_ref, dwin_ref, dwout_ref, ds_ref, normed, df):
    chunk = pl.program_id(0)

    @pl.when(chunk == 0)
    def _():
        xhat, _ = normalize(x_ref[...])
        store_split(normed, xhat * s_ref[0:1] + s_ref[1:2])
        half = 0.5 * da_ref[...]
        store_split(df, half)
        ds_ref[...] = jnp.zeros_like(ds_ref)
        ds_ref[2:3] = column_sum(half)
        dx_ref[...] = jnp.zeros_like(dx_ref)

    dwin, dwout, dbias, dnormed = ffn_backward_chunk(load_split(normed), u_ref[...], load_split(df), win_ref[...], wout_ref[...])
    dwin_ref[...] = dwin
    dwout_ref[...] = dwout
    ds_ref[pl.ds(4 + chunk, 1), :] = dbias
    dx_ref[...] += dnormed

    @pl.when(chunk == NC - 1)
    def _():
        xhat, inverse = normalize(x_ref[...])
        dn = dx_ref[...]
        ds_ref[0:1] = column_sum(dn * xhat)
        ds_ref[1:2] = column_sum(dn)
        dx_ref[...] = da_ref[...] + normalize_back(dn * s_ref[0:1], xhat, inverse)


def ffn1_backward(da, x, u, win, wout, s):
    frames = x.shape[0]
    whole = pl.BlockSpec((frames, D), lambda c: (0, 0))
    across = pl.BlockSpec((D, D), lambda c: (0, c))
    down = pl.BlockSpec((D, D), lambda c: (c, 0))
    return pl.pallas_call(
        ffn1_backward_kernel,
        grid=(NC,),
        in_specs=[whole, whole, pl.BlockSpec((frames, D), lambda c: (0, c)), across, down, pl.BlockSpec(s.shape, lambda c: (0, 0))],
        out_specs=[whole, across, down, pl.BlockSpec((8, D), lambda c: (0, 0))],
        out_shape=[
            jax.ShapeDtypeStruct((frames, D), f32),
            jax.ShapeDtypeStruct((D, FF), f32),
            jax.ShapeDtypeStruct((FF, D), f32),
            jax.ShapeDtypeStruct((8, D), f32),
        ],
        scratch_shapes=[pltpu.VMEM((2, frames, D), bf16), pltpu.VMEM((2, frames, D), bf16)],
        compiler_params=pltpu.CompilerParams(vmem_limit_bytes=VMEM_LIMIT),
        name="ffn1_backward",
    )(da, x, u, win, wout, s)


def ffn2_kernel(a3_ref, cot_ref, win_ref, wout_ref, s_ref, out_ref, da3_ref, dwin_ref, dwout_ref, ds_ref, normed, df, hidden, da4):
    step = pl.program_id(0)

    @pl.when(step == 0)
    def _():
        xhat, _ = normalize(a3_ref[...])
        store_split(normed, xhat * s_ref[8:9] + s_ref[9:10])
        da4[...] = a3_ref[...] + 0.5 * s_ref[18:19]

    @pl.when(step < NC)
    def _():
        out = ffn_forward_chunk(load_split(normed), hidden.at[step], win_ref[...], wout_ref[...], row(s_ref, 23 + NC + step))
        da4[...] += 0.5 * out

    @pl.when(step == NC - 1)
    def _():
        xhat, inverse = normalize(da4[...])
        out_ref[...] = xhat * s_ref[10:11] + s_ref[11:12]
        cot = cot_ref[...]
        ds_ref[...] = jnp.zeros_like(ds_ref)
        ds_ref[8:9] = column_sum(cot * xhat)
        ds_ref[9:10] = column_sum(cot)
        grad = normalize_back(cot * s_ref[10:11], xhat, inverse)
        da4[...] = grad
        half = 0.5 * grad
        store_split(df, half)
        ds_ref[2:3] = column_sum(half)
        da3_ref[...] = jnp.zeros_like(da3_ref)

    @pl.when(step >= NC)
    def _():
        dwin, dwout, dbias, dnormed = ffn_backward_chunk(load_split(normed), hidden[step - NC], load_split(df), win_ref[...], wout_ref[...])
        dwin_ref[...] = dwin
        dwout_ref[...] = dwout
        ds_ref[pl.ds(4 + step - NC, 1), :] = dbias
        da3_ref[...] += dnormed

    @pl.when(step == 2 * NC - 1)
    def _():
        xhat, inverse = normalize(a3_ref[...])
        dn = da3_ref[...]
        ds_ref[0:1] = column_sum(dn * xhat)
        ds_ref[1:2] = column_sum(dn)
        da3_ref[...] = da4[...] + normalize_back(dn * s_ref[8:9], xhat, inverse)


def ffn2(a3, cot, win, wout, s):
    frames = a3.shape[0]
    whole = pl.BlockSpec((frames, D), lambda c: (0, 0))
    return pl.pallas_call(
        ffn2_kernel,
        grid=(2 * NC,),
        in_specs=[
            whole,
            whole,
            pl.BlockSpec((D, D), lambda c: (0, lax.rem(c, NC))),
            pl.BlockSpec((D, D), lambda c: (lax.rem(c, NC), 0)),
            pl.BlockSpec(s.shape, lambda c: (0, 0)),
        ],
        out_specs=[
            whole,
            whole,
            pl.BlockSpec((D, D), lambda c: (0, jnp.maximum(c - NC, 0))),
            pl.BlockSpec((D, D), lambda c: (jnp.maximum(c - NC, 0), 0)),
            pl.BlockSpec((16, D), lambda c: (0, 0)),
        ],
        out_shape=[
            jax.ShapeDtypeStruct((frames, D), f32),
            jax.ShapeDtypeStruct((frames, D), f32),
            jax.ShapeDtypeStruct((D, FF), f32),
            jax.ShapeDtypeStruct((FF, D), f32),
            jax.ShapeDtypeStruct((16, D), f32),
        ],
        scratch_shapes=[
            pltpu.VMEM((2, frames, D), bf16),
            pltpu.VMEM((2, frames, D), bf16),
            pltpu.VMEM((NC, frames, D), f32),
            pltpu.VMEM((frames, D), f32),
        ],
        compiler_params=pltpu.CompilerParams(vmem_limit_bytes=VMEM_LIMIT),
        name="ffn2",
    )(a3, cot, win, wout, s)


def sinusoid_table(length):
    offsets = length // 2 - np.arange(length, dtype=np.float64)
    frequency = 10000.0 ** (-2.0 * np.arange(D // 2, dtype=np.float64) / D)
    angles = offsets[:, None] * frequency[None, :]
    table = np.concatenate([np.sin(angles), np.cos(angles)], axis=1).astype(np.float32)
    return np.stack([table, table[::-1]])


def shift_rows(scores):
    return pltpu.roll(scores, scores.shape[1] // 2, 1, stride=1, stride_axis=0)


def pair_masks():
    lane = lax.broadcasted_iota(jnp.int32, (1, 2 * DH), 1)
    first = (lane < DH).astype(f32)
    return first, 1.0 - first


def attention_forward_kernel(length, a1_ref, w_ref, pe_ref, s_ref, segcol_ref, keyrow_ref, a2_ref, qkv_ref, rel_ref, probs_ref, ctx_ref, bias):
    packs = a1_ref.shape[0] // length
    xhat, _ = normalize(a1_ref[...])
    normed = split(xhat * s_ref[2:3] + s_ref[3:4])
    qkv_ref[0] = dot3(normed, split(w_ref[0]), NN) + s_ref[12:13]
    qkv_ref[1] = dot3(normed, split(w_ref[1]), NN)
    qkv_ref[2] = dot3(normed, split(w_ref[2]), NN) + s_ref[13:14]
    rel_ref[...] = dot3(split(pe_ref[0]), split(w_ref[4]), NN)
    query = lax.broadcasted_iota(jnp.int32, (length, length), 0)
    key = lax.broadcasted_iota(jnp.int32, (length, length), 1)
    for pack in range(packs):
        same = segcol_ref[pl.ds(pack * length, length), 0:1] == keyrow_ref[pack : pack + 1, 0:length]
        bias[pack] = jnp.where(same | (query == key), 0.0, -1e30)
    first, second = pair_masks()

    def heads(item, carry):
        pack, pair = item // (H // 2), item % (H // 2)
        frames = pl.ds(pl.multiple_of(pack * length, length), length)
        lanes = pl.ds(pl.multiple_of(pair * 2 * DH, 2 * DH), 2 * DH)
        q = qkv_ref[0, frames, lanes]
        content = q + s_ref[15:16, lanes]
        position = q + s_ref[16:17, lanes]
        k = split(qkv_ref[1, frames, lanes])
        v = split(qkv_ref[2, frames, lanes])
        rel = split(rel_ref[:, lanes])
        total = jnp.zeros_like(q)
        for index, mask in enumerate((first, second)):
            scores = dot3(split(content * mask), k, NT) + shift_rows(dot3(split(position * mask), rel, NT))
            scores = scores * (1.0 / math.sqrt(DH)) + bias[pack]
            weights = jnp.exp(scores - jnp.max(scores, axis=-1, keepdims=True))
            weights = weights / jnp.sum(weights, axis=-1, keepdims=True)
            probs_ref[item * 2 + index] = weights
            total = total + dot3(split(weights), v, NN) * mask
        ctx_ref[frames, lanes] = total
        return carry

    lax.fori_loop(0, packs * (H // 2), heads, 0)
    a2_ref[...] = a1_ref[...] + dot3(split(ctx_ref[...]), split(w_ref[3]), NN) + s_ref[14:15]


def attention_forward(length, a1, square, pe, s, segcol, keyrow):
    frames = a1.shape[0]
    packs = frames // length
    vmem = pl.BlockSpec(memory_space=pltpu.VMEM)
    return pl.pallas_call(
        functools.partial(attention_forward_kernel, length),
        in_specs=[vmem] * 6,
        out_specs=[vmem] * 5,
        out_shape=[
            jax.ShapeDtypeStruct((frames, D), f32),
            jax.ShapeDtypeStruct((3, frames, D), f32),
            jax.ShapeDtypeStruct((length, D), f32),
            jax.ShapeDtypeStruct((packs * H, length, length), f32),
            jax.ShapeDtypeStruct((frames, D), f32),
        ],
        scratch_shapes=[pltpu.VMEM((packs, length, length), f32)],
        compiler_params=pltpu.CompilerParams(vmem_limit_bytes=VMEM_LIMIT),
        name="attention_forward",
    )(a1, square, pe, s, segcol, keyrow)


def attention_backward_kernel(
    length, da2_ref, a1_ref, qkv_ref, rel_ref, probs_ref, ctx_ref, w_ref, pe_ref, s_ref, da1_ref, dw_ref, ds_ref, dctx, dqkv, drel, relback, du, dv
):
    packs = a1_ref.shape[0] // length
    row_index = lax.broadcasted_iota(jnp.int32, (length, length), 0)
    lane_index = lax.broadcasted_iota(jnp.int32, (length, length), 1)
    flip = (row_index + lane_index == length - 1).astype(bf16)
    da2 = da2_ref[...]
    da2_split = split(da2)
    ds_ref[...] = jnp.zeros_like(ds_ref)
    ds_ref[2:3] = column_sum(da2)
    dw_ref[3] = dot3(split(ctx_ref[...]), da2_split, TN)
    dctx[...] = dot3(da2_split, split(w_ref[3]), NT)
    rel_split = split(rel_ref[...])
    relback[...] = dot(flip, rel_split[0], NN) + dot(flip, rel_split[1], NN)
    drel[...] = jnp.zeros_like(drel)
    du[...] = jnp.zeros_like(du)
    dv[...] = jnp.zeros_like(dv)
    first, second = pair_masks()

    def heads(item, carry):
        pack, pair = item // (H // 2), item % (H // 2)
        frames = pl.ds(pl.multiple_of(pack * length, length), length)
        lanes = pl.ds(pl.multiple_of(pair * 2 * DH, 2 * DH), 2 * DH)
        q = qkv_ref[0, frames, lanes]
        content = q + s_ref[15:16, lanes]
        position = q + s_ref[16:17, lanes]
        k = qkv_ref[1, frames, lanes]
        v = split(qkv_ref[2, frames, lanes])
        rel = relback[:, lanes]
        dc = dctx[frames, lanes]
        dcontent = jnp.zeros_like(q)
        dposition = jnp.zeros_like(q)
        dkey = jnp.zeros_like(q)
        dvalue = jnp.zeros_like(q)
        drelation = jnp.zeros_like(rel)
        for index, mask in enumerate((first, second)):
            weights = probs_ref[item * 2 + index]
            dc_split = split(dc * mask)
            dvalue = dvalue + dot3(split(weights), dc_split, TN)
            dweights = dot3(dc_split, v, NT)
            dscores = weights * (dweights - jnp.sum(weights * dweights, axis=-1, keepdims=True)) * (1.0 / math.sqrt(DH))
            ds_split = split(dscores)
            dcontent = dcontent + dot3(ds_split, split(k * mask), NN)
            dkey = dkey + dot3(ds_split, split(content * mask), TN)
            shifted = split(shift_rows(dot(ds_split[0], flip, NN) + dot(ds_split[1], flip, NN)))
            dposition = dposition + dot3(shifted, split(rel * mask), NN)
            drelation = drelation + dot3(shifted, split(position * mask), TN)
        dqkv[0, frames, lanes] = dcontent + dposition
        dqkv[1, frames, lanes] = dkey
        dqkv[2, frames, lanes] = dvalue
        drel[:, lanes] += drelation
        du[0:1, lanes] += column_sum(dcontent)
        dv[0:1, lanes] += column_sum(dposition)
        return carry

    lax.fori_loop(0, packs * (H // 2), heads, 0)
    ds_ref[3:4] = du[0:1]
    ds_ref[4:5] = dv[0:1]
    ds_ref[5:6] = column_sum(dqkv[0])
    ds_ref[6:7] = column_sum(dqkv[2])
    xhat, inverse = normalize(a1_ref[...])
    normed = split(xhat * s_ref[2:3] + s_ref[3:4])
    dnormed = jnp.zeros_like(xhat)
    for index in range(3):
        grad = split(dqkv[index])
        dw_ref[index] = dot3(normed, grad, TN)
        dnormed = dnormed + dot3(grad, split(w_ref[index]), NT)
    dw_ref[4] = dot3(split(pe_ref[1]), split(drel[...]), TN)
    ds_ref[0:1] = column_sum(dnormed * xhat)
    ds_ref[1:2] = column_sum(dnormed)
    da1_ref[...] = da2_ref[...] + normalize_back(dnormed * s_ref[2:3], xhat, inverse)


def attention_backward(length, da2, a1, qkv, rel, probs, ctx, square, pe, s):
    frames = a1.shape[0]
    vmem = pl.BlockSpec(memory_space=pltpu.VMEM)
    return pl.pallas_call(
        functools.partial(attention_backward_kernel, length),
        in_specs=[vmem] * 9,
        out_specs=[vmem] * 3,
        out_shape=[
            jax.ShapeDtypeStruct((frames, D), f32),
            jax.ShapeDtypeStruct((5, D, D), f32),
            jax.ShapeDtypeStruct((8, D), f32),
        ],
        scratch_shapes=[
            pltpu.VMEM((frames, D), f32),
            pltpu.VMEM((3, frames, D), f32),
            pltpu.VMEM((length, D), f32),
            pltpu.VMEM((length, D), f32),
            pltpu.VMEM((8, D), f32),
            pltpu.VMEM((8, D), f32),
        ],
        compiler_params=pltpu.CompilerParams(vmem_limit_bytes=VMEM_LIMIT),
        name="attention_backward",
    )(da2, a1, qkv, rel, probs, ctx, square, pe, s)


EDGE = 8
HALF = (K - 1) // 2
STRIP = 64


def convolution_forward_kernel(a2_ref, proj_ref, w_ref, s_ref, match_ref, a3_ref, u_ref, mixed_ref, padded):
    frames = a2_ref.shape[0]
    xhat, _ = normalize(a2_ref[...])
    normed = split(xhat * s_ref[4:5] + s_ref[5:6])
    u_ref[:, :D] = dot3(normed, split(proj_ref[:, :D]), NN) + s_ref[19:20]
    u_ref[:, D:] = dot3(normed, split(proj_ref[:, D:]), NN) + s_ref[20:21]
    padded[0:EDGE] = jnp.zeros((EDGE, D), f32)
    padded[EDGE + frames :] = jnp.zeros((EDGE, D), f32)
    padded[EDGE : EDGE + frames] = u_ref[:, :D] * jax.nn.sigmoid(u_ref[:, D:]) * match_ref[:, K : K + 1]
    for base in range(0, frames, STRIP):
        total = jnp.zeros((STRIP, D), f32) + s_ref[21:22]
        for tap in range(K):
            source = padded[base + EDGE + tap - HALF : base + EDGE + tap - HALF + STRIP]
            total = total + match_ref[base : base + STRIP, tap : tap + 1] * source * s_ref[TAP + tap : TAP + tap + 1]
        mixed_ref[base : base + STRIP] = total
    inner, _ = normalize(mixed_ref[...])
    inner = inner * s_ref[6:7] + s_ref[7:8]
    a3_ref[...] = a2_ref[...] + dot3(split(inner * jax.nn.sigmoid(inner)), split(w_ref[...]), NN) + s_ref[22:23]


def convolution_forward(a2, proj, weight, s, match):
    frames = a2.shape[0]
    vmem = pl.BlockSpec(memory_space=pltpu.VMEM)
    return pl.pallas_call(
        convolution_forward_kernel,
        in_specs=[vmem] * 5,
        out_specs=[vmem] * 3,
        out_shape=[
            jax.ShapeDtypeStruct((frames, D), f32),
            jax.ShapeDtypeStruct((frames, 2 * D), f32),
            jax.ShapeDtypeStruct((frames, D), f32),
        ],
        scratch_shapes=[pltpu.VMEM((frames + 2 * EDGE, D), f32)],
        compiler_params=pltpu.CompilerParams(vmem_limit_bytes=VMEM_LIMIT),
        name="convolution_forward",
    )(a2, proj, weight, s, match)


def convolution_backward_kernel(
    da3_ref, a2_ref, u_ref, mixed_ref, proj_ref, w_ref, s_ref, match_ref, da2_ref, dproj_ref, dw_ref, ds_ref, padded, dpadded, dgated
):
    frames = a2_ref.shape[0]
    da3 = da3_ref[...]
    da3_split = split(da3)
    ds_ref[...] = jnp.zeros_like(ds_ref)
    ds_ref[2:3] = column_sum(da3)
    hat, inverse = normalize(mixed_ref[...])
    inner = hat * s_ref[6:7] + s_ref[7:8]
    sig = jax.nn.sigmoid(inner)
    dw_ref[...] = dot3(split(inner * sig), da3_split, TN)
    dinner = dot3(da3_split, split(w_ref[...]), NT) * (sig * (1.0 + inner * (1.0 - sig)))
    ds_ref[3:4] = column_sum(dinner * hat)
    ds_ref[4:5] = column_sum(dinner)
    dmixed = normalize_back(dinner * s_ref[6:7], hat, inverse)
    ds_ref[5:6] = column_sum(dmixed)
    zeros = jnp.zeros((EDGE, D), f32)
    padded[0:EDGE] = zeros
    padded[EDGE + frames :] = zeros
    padded[EDGE : EDGE + frames] = u_ref[:, :D] * jax.nn.sigmoid(u_ref[:, D:]) * match_ref[:, K : K + 1]
    dpadded[0:EDGE] = zeros
    dpadded[EDGE + frames :] = zeros
    dpadded[EDGE : EDGE + frames] = dmixed
    for base in range(0, frames, STRIP):
        total = jnp.zeros((STRIP, D), f32)
        center = dpadded[base + EDGE : base + EDGE + STRIP]
        for tap in range(K):
            rows = slice(base + EDGE + tap - HALF, base + EDGE + tap - HALF + STRIP)
            match = match_ref[base : base + STRIP, tap : tap + 1]
            total = total + match * dpadded[rows] * s_ref[TAP + K - 1 - tap : TAP + K - tap]
            ds_ref[8 + tap : 9 + tap] += column_sum(center * (match * padded[rows]))
        dgated[base : base + STRIP] = total * match_ref[base : base + STRIP, K : K + 1]
    gate = jax.nn.sigmoid(u_ref[:, D:])
    dfirst = dgated[...] * gate
    dsecond = dfirst * u_ref[:, :D] * (1.0 - gate)
    ds_ref[6:7] = column_sum(dfirst)
    ds_ref[7:8] = column_sum(dsecond)
    xhat, inverse = normalize(a2_ref[...])
    normed = split(xhat * s_ref[4:5] + s_ref[5:6])
    dfirst = split(dfirst)
    dsecond = split(dsecond)
    dproj_ref[:, :D] = dot3(normed, dfirst, TN)
    dproj_ref[:, D:] = dot3(normed, dsecond, TN)
    dnormed = dot3(dfirst, split(proj_ref[:, :D]), NT) + dot3(dsecond, split(proj_ref[:, D:]), NT)
    ds_ref[0:1] = column_sum(dnormed * xhat)
    ds_ref[1:2] = column_sum(dnormed)
    da2_ref[...] = da3_ref[...] + normalize_back(dnormed * s_ref[4:5], xhat, inverse)


def convolution_backward(da3, a2, u, mixed, proj, weight, s, match):
    frames = a2.shape[0]
    vmem = pl.BlockSpec(memory_space=pltpu.VMEM)
    return pl.pallas_call(
        convolution_backward_kernel,
        in_specs=[vmem] * 8,
        out_specs=[vmem] * 4,
        out_shape=[
            jax.ShapeDtypeStruct((frames, D), f32),
            jax.ShapeDtypeStruct((D, 2 * D), f32),
            jax.ShapeDtypeStruct((D, D), f32),
            jax.ShapeDtypeStruct((24, D), f32),
        ],
        scratch_shapes=[
            pltpu.VMEM((frames + 2 * EDGE, D), f32),
            pltpu.VMEM((frames + 2 * EDGE, D), f32),
            pltpu.VMEM((frames, D), f32),
        ],
        compiler_params=pltpu.CompilerParams(vmem_limit_bytes=VMEM_LIMIT),
        name="convolution_backward",
    )(da3, a2, u, mixed, proj, weight, s, match)


def frame_tables(segments, valid_mask):
    packs, length = segments.shape
    position = jnp.arange(length, dtype=jnp.int32)
    columns = []
    for tap in range(K):
        moved = jnp.roll(segments, HALF - tap, axis=1)
        inside = (position + tap - HALF >= 0) & (position + tap - HALF < length)
        columns.append(((moved == segments) & inside[None, :]).astype(f32))
    columns.append(valid_mask.astype(f32))
    match = jnp.stack(columns, axis=-1).reshape(packs * length, K + 1)
    match = jnp.pad(match, ((0, 0), (0, 128 - K - 1)))
    segcol = jnp.broadcast_to(segments.reshape(packs * length, 1), (packs * length, 128))
    keyrow = jnp.pad(jnp.where(valid_mask > 0, segments, -1), ((0, -packs % 8), (0, 0)))
    return match, segcol, keyrow


def small_rows(parts):
    first, attend, conv, second = parts
    return jnp.concatenate(
        [
            first[0:2],
            attend[0:2],
            conv[0:2],
            conv[3:5],
            second[0:2],
            second[8:10],
            attend[5:7],
            attend[2:5],
            first[2:3],
            second[2:3],
            conv[6:8],
            conv[5:6],
            conv[2:3],
            first[4:8],
            second[4:8],
            conv[8 : 8 + K],
        ],
        axis=0,
    )


def layer(inputs, cotangent, segments, valid_mask, weights):
    feed_in, feed_out, square, proj, s = weights
    packs, length, _ = inputs.shape
    frames = packs * length
    x = inputs.reshape(frames, D)
    cot = cotangent.reshape(frames, D)
    match, segcol, keyrow = frame_tables(segments, valid_mask)
    pe = jnp.asarray(sinusoid_table(length))
    a1, u1 = ffn1_forward(x, feed_in[0], feed_out[0], s)
    a2, qkv, rel, probs, ctx = attention_forward(length, a1, square, pe, s, segcol, keyrow)
    a3, u, mixed = convolution_forward(a2, proj, square[5], s, match)
    out, da3, dwin2, dwout2, ds2 = ffn2(a3, cot, feed_in[1], feed_out[1], s)
    da2, dproj, dw5, dsc = convolution_backward(da3, a2, u, mixed, proj, square[5], s, match)
    da1, dw, dsa = attention_backward(length, da2, a1, qkv, rel, probs, ctx, square, pe, s)
    dx, dwin1, dwout1, ds1 = ffn1_backward(da1, x, u1, feed_in[0], feed_out[0], s)
    grads = (dwin1, dwin2), (dwout1, dwout2), (dw, dw5), dproj, small_rows((ds1, dsa, dsc, ds2))
    return out.reshape(inputs.shape), dx.reshape(inputs.shape), grads

MESH_ID = pl.DeviceIdType.MESH


def chip_grid(devices):
    side = 1
    while side * side * 2 * side * 2 < devices:
        side *= 2
    return side, side, 2 * side


class Place:
    def __init__(self, sizes):
        self.fsdp = sizes[1]
        self.y_size, self.x_size, self.z_size = chip_grid(sizes[0] * sizes[1])
        index = lax.axis_index("dp") * sizes[1] + lax.axis_index("fsdp")
        self.index = index
        self.core = lax.rem(index, 2)
        self.z = lax.rem(index // 2, self.z_size)
        self.x = lax.rem(index // (2 * self.z_size), 2)
        self.y = index // (4 * self.z_size)

    def device(self, y=None, x=None, z=None, core=None):
        y = self.y if y is None else y
        x = self.x if x is None else x
        z = self.z if z is None else z
        core = self.core if core is None else core
        index = ((y * 2 + x) * self.z_size + z) * 2 + core
        return index // self.fsdp, lax.rem(index, self.fsdp)

    def neighbour(self, axis):
        if axis == "core":
            return self.device(core=1 - self.core)
        if axis == "x":
            return self.device(x=1 - self.x)
        if axis == "y":
            return self.device(y=1 - self.y)
        return self.device(z=self.z + (1 if axis == "right" else -1))

    def greet(self):
        barrier = pltpu.get_barrier_semaphore()
        for axis in ("core", "x", "y"):
            pl.semaphore_signal(barrier, inc=1, device_id=self.neighbour(axis), device_id_type=MESH_ID)

        @pl.when(self.z > 0)
        def _():
            pl.semaphore_signal(barrier, inc=1, device_id=self.neighbour("left"), device_id_type=MESH_ID)

        @pl.when(self.z < self.z_size - 1)
        def _():
            pl.semaphore_signal(barrier, inc=1, device_id=self.neighbour("right"), device_id_type=MESH_ID)

        peers = 3 + (self.z > 0).astype(jnp.int32) + (self.z < self.z_size - 1).astype(jnp.int32)
        pl.semaphore_wait(barrier, peers)


EVERY = slice(None)


class Piece:
    def __init__(self, lead, first_row, rows, zfirst, near):
        self.lead, self.rows, self.zfirst, self.near = lead, pl.ds(first_row, rows), zfirst, near
        self.far = "y" if near == "x" else "x"

    def own(self, shard):
        return shard.at[self.rows] if self.lead is None else shard.at[self.lead, self.rows]

    def blocks(self, full, place, near, far, z, core):
        y, x = (near, far) if self.near == "y" else (far, near)
        index = (y, x, z, core, self.rows)
        return full.at[index] if self.lead is None else full.at[(self.lead,) + index]

    def here(self, place):
        return (place.x, place.y) if self.near == "x" else (place.y, place.x)


G_RIGHT, G_LEFT, G_NEAR, G_FAR, G_CORE = range(5)


class Gather:
    def __init__(self, place, piece, shard, full, send, recv, local):
        self.place, self.piece, self.shard, self.full = place, piece, shard, full
        self.send, self.recv, self.local = send, recv, local

    def view(self, near, far, z, core=None):
        return self.piece.blocks(self.full, self.place, near, far, z, self.place.core if core is None else core)

    def copy(self, kind, z, ref, axis, source=None):
        return pltpu.make_async_remote_copy(
            src_ref=ref if source is None else source,
            dst_ref=ref,
            send_sem=self.send.at[kind, z],
            recv_sem=self.recv.at[G_RIGHT if kind == G_LEFT else kind, z],
            device_id=self.place.neighbour(axis),
            device_id_type=MESH_ID,
        )

    def z_view(self, z):
        near, far = self.piece.here(self.place)
        return self.view(near if self.piece.zfirst else EVERY, far, z)

    def near_view(self, near, z):
        return self.view(near, self.piece.here(self.place)[1], z)

    def far_view(self, far, z):
        return self.view(EVERY, far, z)

    def core_view(self, core, z):
        return self.view(EVERY, EVERY, z, core)

    def own_copy(self):
        near, far = self.piece.here(self.place)
        return pltpu.make_async_copy(self.piece.own(self.shard), self.view(near, far, self.place.z), self.local)

    def begin(self):
        near, _ = self.piece.here(self.place)
        self.own_copy().start()
        own = self.piece.own(self.shard)
        if not self.piece.zfirst:
            self.copy(G_NEAR, self.place.z, self.near_view(near, self.place.z), self.piece.near, own).start()

    def z_send(self, z, source=None, right=True, left=True):
        place = self.place
        if right:

            @pl.when(place.z < place.z_size - 1)
            def _():
                self.copy(G_RIGHT, z, self.z_view(z), "right", source).start()

        if left:

            @pl.when(place.z > 0)
            def _():
                self.copy(G_LEFT, z, self.z_view(z), "left", source).start()

    def onward(self, z, source=None):
        near, far = self.piece.here(self.place)
        if self.piece.zfirst:
            self.copy(G_NEAR, z, self.near_view(near, z), self.piece.near, source).start()
        else:
            self.copy(G_FAR, z, self.far_view(far, z), self.piece.far).start()

    def at_distance(self, distance, step):
        place = self.place
        if distance == 0:
            step(place.z, None)
            return

        @pl.when(place.z >= distance)
        def _():
            step(place.z - distance, True)

        @pl.when(place.z + distance < place.z_size)
        def _():
            step(place.z + distance, False)

    def z_step(self, distance):
        near, _ = self.piece.here(self.place)

        def step(z, from_left):
            if from_left is None:
                if self.piece.zfirst:
                    own = self.piece.own(self.shard)
                    self.z_send(z, own)
                    self.onward(z, own)
                else:
                    self.copy(G_NEAR, z, self.near_view(1 - near, z), self.piece.near).wait_recv()
                    self.own_copy().wait()
                    self.z_send(z)
                    self.onward(z)
                return
            self.copy(G_RIGHT, z, self.z_view(z), "left").wait_recv()
            self.z_send(z, None, from_left, not from_left)
            self.onward(z)

        self.at_distance(distance, step)

    def near_step(self, distance):
        near, far = self.piece.here(self.place)

        def step(z, from_left):
            if from_left is None:
                self.own_copy().wait()
            self.copy(G_NEAR, z, self.near_view(1 - near, z), self.piece.near).wait_recv()
            self.copy(G_FAR, z, self.far_view(far, z), self.piece.far).start()

        if self.piece.zfirst:
            self.at_distance(distance, step)

    def far_step(self, distance):
        _, far = self.piece.here(self.place)

        def step(z, from_left):
            self.copy(G_FAR, z, self.far_view(1 - far, z), self.piece.far).wait_recv()
            self.copy(G_CORE, z, self.core_view(self.place.core, z), "core").start()

        self.at_distance(distance, step)

    def finish(self):
        place = self.place
        near, far = self.piece.here(place)
        for z in range(place.z_size):
            self.copy(G_CORE, z, self.core_view(1 - place.core, z), "core").wait_recv()
            self.copy(G_CORE, z, self.core_view(place.core, z), "core").wait_send()
            self.copy(G_FAR, z, self.far_view(far, z), self.piece.far).wait_send()
            if self.piece.zfirst:
                self.copy(G_NEAR, z, self.near_view(near, z), self.piece.near).wait_send()

            @pl.when((place.z < place.z_size - 1) & (z <= place.z))
            def _():
                self.copy(G_RIGHT, z, self.z_view(z), "right").wait_send()

            @pl.when((place.z > 0) & (z >= place.z))
            def _():
                self.copy(G_LEFT, z, self.z_view(z), "left").wait_send()

        if not self.piece.zfirst:
            self.copy(G_NEAR, place.z, self.near_view(near, place.z), self.piece.near).wait_send()


def gather_ticks(gathers, z_size):
    ticks = [[] for _ in range(z_size + 4)]
    for gather in gathers:
        ticks[0].append(gather.begin)
        shift = 0 if gather.piece.zfirst else 1
        for distance in range(z_size):
            ticks[distance + shift].append(functools.partial(gather.z_step, distance))
            ticks[distance + 1].append(functools.partial(gather.near_step, distance))
            ticks[distance + 2].append(functools.partial(gather.far_step, distance))
    ticks[-1] += [gather.finish for gather in gathers]
    return ticks


def halves(rows, zfirst, lead=None):
    return [Piece(lead, 0, rows // 2, zfirst, "x"), Piece(lead, rows // 2, rows // 2, zfirst, "y")]


def whole_shape(shard, sizes):
    y, x, z = chip_grid(sizes[0] * sizes[1])
    return shard.shape[:-2] + (y, x, z, 2) + shard.shape[-2:]


def gather_kernel(sizes, plans, offsets, *refs):
    arrays = sum(len(plan) for plan in plans)
    pieces = sum(len(p) for plan in plans for p in plan)
    shards, fulls = refs[:arrays], refs[arrays : 2 * arrays]
    send, recv, local = refs[2 * arrays :]
    place = Place(sizes)
    place.greet()
    schedule = {}
    array = count = 0
    for plan, offset in zip(plans, offsets):
        gathers = []
        for group in plan:
            for piece in group:
                gathers.append(Gather(place, piece, shards[array], fulls[array], send.at[count], recv.at[count], local.at[count]))
                count += 1
            array += 1
        for tick, steps in enumerate(gather_ticks(gathers, place.z_size)):
            schedule.setdefault(tick + offset, []).extend(steps)
    for tick in sorted(schedule):
        for step in schedule[tick]:
            step()


def gather(shards, plans, offsets, sizes, number, name):
    pieces = sum(len(p) for plan in plans for p in plan)
    z_size = chip_grid(sizes[0] * sizes[1])[2]
    return pl.pallas_call(
        functools.partial(gather_kernel, sizes, plans, offsets),
        in_specs=[pl.BlockSpec(memory_space=pltpu.VMEM)] * len(shards),
        out_specs=[pl.BlockSpec(memory_space=pl.ANY)] * len(shards),
        out_shape=[jax.ShapeDtypeStruct(whole_shape(shard, sizes), f32) for shard in shards],
        scratch_shapes=[
            pltpu.SemaphoreType.DMA((pieces, 5, z_size)),
            pltpu.SemaphoreType.DMA((pieces, 5, z_size)),
            pltpu.SemaphoreType.DMA((pieces,)),
        ],
        compiler_params=pltpu.CompilerParams(collective_id=number, has_side_effects=True, vmem_limit_bytes=VMEM_LIMIT),
        name=name,
    )(*shards)
S_CORE, S_FAR, S_NEAR, S_FROM_LEFT, S_FROM_RIGHT = range(5)


class Scatter:
    def __init__(self, place, piece, full, out, total, cores, fars, nears, lines, send, recv, local):
        self.place, self.piece, self.full, self.out = place, piece, full, out
        self.total, self.cores, self.fars, self.nears, self.lines = total, cores, fars, nears, lines
        self.send, self.recv, self.local = send, recv, local
        self.near, self.far = piece.here(place)

    def part(self, ref, near, far, z):
        y, x = (near, far) if self.piece.near == "y" else (far, near)
        index = (y, x, z)
        return ref.at[index] if self.piece.lead is None else ref.at[(EVERY,) + index]

    def staged(self, ref, *index):
        return ref.at[index] if self.piece.lead is None else ref.at[(EVERY,) + index]

    def add(self, target, source):
        target[...] = target[...] + source[...]

    def copy(self, kind, z, source, target, axis):
        return pltpu.make_async_remote_copy(
            src_ref=source,
            dst_ref=target,
            send_sem=self.send.at[kind, z],
            recv_sem=self.recv.at[kind, z],
            device_id=self.place.neighbour(axis),
            device_id_type=MESH_ID,
        )

    def core_copy(self, z):
        given = self.piece.blocks(self.full, self.place, EVERY, EVERY, z, 1 - self.place.core)
        return self.copy(S_CORE, z, given, self.part(self.cores, EVERY, EVERY, z), "core")

    def own_copy(self, z):
        kept = self.piece.blocks(self.full, self.place, EVERY, EVERY, z, self.place.core)
        return pltpu.make_async_copy(kept, self.part(self.total, EVERY, EVERY, z), self.local.at[z])

    def far_copy(self, z):
        return self.copy(S_FAR, z, self.part(self.total, EVERY, 1 - self.far, z), self.staged(self.fars, EVERY, z), self.piece.far)

    def near_copy(self, z):
        target = self.staged(self.nears, z if self.piece.zfirst else 0)
        return self.copy(S_NEAR, z, self.part(self.total, 1 - self.near, self.far, z), target, self.piece.near)

    def line_view(self, z):
        return self.part(self.total, self.near if self.piece.zfirst else EVERY, self.far, z)

    def line_staged(self, side, z):
        if self.piece.zfirst:
            return self.staged(self.lines, side, z)
        return self.staged(self.lines, side, EVERY, z)

    def line_copy(self, z, to_right):
        kind, side = (S_FROM_LEFT, 0) if to_right else (S_FROM_RIGHT, 1)
        return self.copy(kind, z, self.line_view(z), self.line_staged(side, z), "right" if to_right else "left")

    def begin(self):
        for distance in reversed(range(self.place.z_size)):
            for sign in (-1, 1) if distance else (1,):
                z = self.place.z + sign * distance

                @pl.when((z >= 0) & (z < self.place.z_size))
                def _():
                    self.core_copy(z).start()
                    self.own_copy(z).start()

    def core_step(self, z):
        self.core_copy(z).wait_recv()
        self.own_copy(z).wait()
        self.add(self.part(self.total, EVERY, EVERY, z), self.part(self.cores, EVERY, EVERY, z))

    def core_send(self, z):
        self.far_copy(z).start()

    def far_step(self, z):
        self.far_copy(z).wait_recv()
        self.add(self.part(self.total, EVERY, self.far, z), self.staged(self.fars, EVERY, z))

    def far_send(self, z):
        self.near_copy(z).start()

    def near_step(self, z):
        self.near_copy(z).wait_recv()
        self.add(self.part(self.total, self.near, self.far, z), self.staged(self.nears, z))

    def line_step(self, z):
        here = self.place.z

        @pl.when((z >= here) & (here > 0))
        def _():
            self.line_copy(z, True).wait_recv()
            self.add(self.line_view(z), self.line_staged(0, z))

        @pl.when((z <= here) & (here < self.place.z_size - 1))
        def _():
            self.line_copy(z, False).wait_recv()
            self.add(self.line_view(z), self.line_staged(1, z))

    def line_send(self, z):
        here = self.place.z

        @pl.when(z > here)
        def _():
            self.line_copy(z, True).start()

        @pl.when(z < here)
        def _():
            self.line_copy(z, False).start()

    def last_send(self):
        if not self.piece.zfirst:
            self.near_copy(self.place.z).start()

    def finish(self):
        z = self.place.z
        value = self.part(self.total, self.near, self.far, z)[...]
        if not self.piece.zfirst:
            self.near_copy(z).wait_recv()
            value = value + self.staged(self.nears, 0)[...]
        self.piece.own(self.out)[...] = value

    def drain(self):
        place = self.place
        for z in range(place.z_size):
            self.core_copy(z).wait_send()
            self.far_copy(z).wait_send()
            if self.piece.zfirst:
                self.near_copy(z).wait_send()

            @pl.when(z > place.z)
            def _():
                self.line_copy(z, True).wait_send()

            @pl.when(z < place.z)
            def _():
                self.line_copy(z, False).wait_send()

        if not self.piece.zfirst:
            self.near_copy(place.z).wait_send()


def scatter_stages(scatter):
    stages = [(scatter.core_step, scatter.core_send)]
    if scatter.piece.zfirst:
        return stages + [(scatter.far_step, scatter.far_send), (scatter.near_step, None), (scatter.line_step, scatter.line_send)]
    return stages + [(scatter.far_step, None), (scatter.line_step, scatter.line_send)]


def run_scatters(place, scatters, offsets, lag):
    blocks = 2 * place.z_size - 1
    for scatter in scatters:
        scatter.begin()
    staged = []
    for scatter, offset in zip(scatters, offsets):
        behind = offset
        for index, (work, send) in enumerate(scatter_stages(scatter)):
            staged.append((behind, work, send))
            behind += 0 if send is None else lag
    staged.sort(key=lambda stage: -stage[0])
    steps = max(stage[0] for stage in staged) + blocks

    def body(step, carry):
        for action in (1, 2):
            for stage in staged:
                if stage[action] is None:
                    continue
                item = step - stage[0]
                distance = place.z_size - 1 - item // 2
                z = place.z + jnp.where(lax.rem(item, 2) == 0, -distance, distance)

                @pl.when((item >= 0) & (item < blocks) & (z >= 0) & (z < place.z_size))
                def _():
                    stage[action](z)

        return carry

    lax.fori_loop(0, steps, body, 0)
    for scatter in scatters:
        scatter.last_send()
    for scatter in scatters:
        scatter.finish()
    for scatter in scatters:
        scatter.drain()


def scatter_scratch(piece, columns, place_sizes, lead):
    y, x, z = chip_grid(place_sizes[0] * place_sizes[1])
    rows = piece.rows.size
    head = () if piece.lead is None else (lead,)
    return [
        pltpu.VMEM(head + (y, x, z, rows, columns), f32),
        pltpu.VMEM(head + (y, x, z, rows, columns), f32),
        pltpu.VMEM(head + (2, z, rows, columns), f32),
        pltpu.VMEM(head + ((z,) if piece.zfirst else (1,)) + (rows, columns), f32),
        pltpu.VMEM(head + ((2, z) if piece.zfirst else (2, 2, z)) + (rows, columns), f32),
    ]


def scatter_kernel(sizes, plans, starts, lag, total_norm, *refs):
    arrays = sum(len(plan) for plan in plans)
    pieces = sum(len(p) for plan in plans for p in plan)
    fulls, refs = refs[:arrays], refs[arrays:]
    outs, refs = refs[:arrays], refs[arrays:]
    if total_norm:
        norms, refs = refs[0], refs[1:]
    scratch, refs = refs[: 5 * pieces], refs[5 * pieces :]
    send, recv, local = refs[:3]
    place = Place(sizes)
    if total_norm:
        greet_all(place, sizes)
    else:
        place.greet()
    scatters, offsets = [], []
    array = count = 0
    for plan, start in zip(plans, starts):
        for group in plan:
            for piece in group:
                scatters.append(
                    Scatter(place, piece, fulls[array], outs[array], *scratch[5 * count : 5 * count + 5], send.at[count], recv.at[count], local.at[count])
                )
                offsets.append(start)
                count += 1
            array += 1
    run_scatters(place, scatters, offsets, lag)
    if total_norm:
        share_norm(place, sizes, outs, norms, *refs[3:])


def greet_all(place, sizes):
    devices = sizes[0] * sizes[1]
    barrier = pltpu.get_barrier_semaphore()

    def signal(offset, carry):
        other = lax.rem(place.index + offset, devices)
        pl.semaphore_signal(barrier, inc=1, device_id=(other // sizes[1], lax.rem(other, sizes[1])), device_id_type=MESH_ID)
        return carry

    lax.fori_loop(1, devices, signal, 0)
    pl.semaphore_wait(barrier, devices - 1)


def square_tile(values):
    squares = values * values
    tile = jnp.zeros((8, 128), f32)
    for r in range(0, values.shape[0], 8):
        for c in range(0, values.shape[1], 128):
            tile = tile + squares[r : r + 8, c : c + 128]
    return tile


def share_norm(place, sizes, outs, norms, own, send, recv):
    devices = sizes[0] * sizes[1]
    tile = jnp.zeros((8, 128), f32)
    for out in outs:
        for lead in range(out.shape[0]) if len(out.shape) == 3 else (None,):
            tile = tile + square_tile(out[...] if lead is None else out[lead])
    own[...] = tile
    norms[place.index] = tile

    def copy(offset, to):
        other = lax.rem(place.index + offset, devices)
        slot = place.index if to else other
        return pltpu.make_async_remote_copy(
            src_ref=own,
            dst_ref=norms.at[slot],
            send_sem=send.at[other],
            recv_sem=recv.at[slot],
            device_id=(other // sizes[1], lax.rem(other, sizes[1])),
            device_id_type=MESH_ID,
        )

    lax.fori_loop(1, devices, lambda offset, carry: (copy(offset, True).start(), carry)[1], 0)
    lax.fori_loop(1, devices, lambda offset, carry: (copy(offset, False).wait_recv(), carry)[1], 0)
    lax.fori_loop(1, devices, lambda offset, carry: (copy(offset, True).wait_send(), carry)[1], 0)


def shard_shape(full):
    return full.shape[:-6] + full.shape[-2:]


def scatter(fulls, plans, starts, lag, sizes, number, name, total_norm):
    devices = sizes[0] * sizes[1]
    pieces = sum(len(p) for plan in plans for p in plan)
    z_size = chip_grid(devices)[2]
    scratch = []
    array = 0
    for plan in plans:
        for group in plan:
            for piece in group:
                lead = None if piece.lead is None else piece.lead.size
                scratch += scatter_scratch(piece, fulls[array].shape[-1], sizes, lead)
            array += 1
    vmem = pl.BlockSpec(memory_space=pltpu.VMEM)
    shapes = [jax.ShapeDtypeStruct(shard_shape(full), f32) for full in fulls]
    sems = [
        pltpu.SemaphoreType.DMA((pieces, 5, z_size)),
        pltpu.SemaphoreType.DMA((pieces, 5, z_size)),
        pltpu.SemaphoreType.DMA((pieces, z_size)),
    ]
    if total_norm:
        shapes.append(jax.ShapeDtypeStruct((devices, 8, 128), f32))
        sems += [pltpu.VMEM((8, 128), f32), pltpu.SemaphoreType.DMA((devices,)), pltpu.SemaphoreType.DMA((devices,))]
    return pl.pallas_call(
        functools.partial(scatter_kernel, sizes, plans, starts, lag, total_norm),
        in_specs=[pl.BlockSpec(memory_space=pl.ANY)] * len(fulls),
        out_specs=[vmem] * len(shapes),
        out_shape=shapes,
        scratch_shapes=scratch + sems,
        compiler_params=pltpu.CompilerParams(collective_id=number, has_side_effects=True, vmem_limit_bytes=VMEM_LIMIT),
        name=name,
    )(*fulls)


def adamw_kernel(step_ref, norms_ref, *refs):
    (g_in1, g_in2, g_out1, g_out2, g_sq, g_conv, g_small), refs = refs[:7], refs[7:]
    weights, firsts, seconds, outs = refs[0:5], refs[5:10], refs[10:15], refs[16:]
    norm = jnp.sqrt(jnp.sum(norms_ref[...], axis=(0, 1, 2), keepdims=True)[0])
    refs[15][...] = norm
    clip = jnp.minimum(1.0, CLIP_NORM / (norm + 1e-06))

    def geometric(_, carry):
        one, one_power, two, two_power = carry
        return one + one_power, one_power * BETA_ONE, two + two_power, two_power * BETA_TWO

    zero, unit = jnp.float32(0.0), jnp.float32(1.0)
    one, _, two, _ = lax.fori_loop(0, step_ref[0], geometric, (zero, unit, zero, unit))
    first_scale = jnp.full((1, 1), (1.0 - BETA_ONE) * one, f32)
    second_scale = jnp.full((1, 1), (1.0 - BETA_TWO) * two, f32)
    first_scale = 1.0 / first_scale
    second_scale = 1.0 / second_scale

    def update(number, index, gradient, rate, decay):
        weight, first, second = weights[number][index], firsts[number][index], seconds[number][index]
        clipped = clip * gradient
        first_next = BETA_ONE * first + (1.0 - BETA_ONE) * clipped
        second_next = BETA_TWO * second + (1.0 - BETA_TWO) * clipped * clipped
        step = (first_next * first_scale) / (jnp.sqrt(second_next * second_scale) + ADAM_EPS)
        if decay:
            step = step + decay * weight
        outs[3 * number][index] = first_next
        outs[3 * number + 1][index] = second_next
        outs[3 * number + 2][index] = weight - rate * step

    for half, (g_in, g_out) in enumerate(((g_in1, g_out1), (g_in2, g_out2))):
        update(0, half, g_in[...], MATRIX_RATE, MATRIX_DECAY)
        update(1, half, g_out[...], MATRIX_RATE, MATRIX_DECAY)
    for index in range(6):
        update(2, index, g_sq[index], MATRIX_RATE, MATRIX_DECAY)
    update(3, EVERY, g_conv[...], MATRIX_RATE, MATRIX_DECAY)
    update(4, EVERY, g_small[...], VECTOR_RATE, 0.0)


def adamw(step, norms, grads, weights, firsts, seconds):
    vmem = pl.BlockSpec(memory_space=pltpu.VMEM)
    shapes = [jax.ShapeDtypeStruct((1, 1), f32)]
    for weight in weights:
        shapes += [jax.ShapeDtypeStruct(weight.shape, f32)] * 3
    return pl.pallas_call(
        adamw_kernel,
        in_specs=[pl.BlockSpec(memory_space=pltpu.SMEM)] + [vmem] * 23,
        out_specs=[vmem] * 16,
        out_shape=shapes,
        compiler_params=pltpu.CompilerParams(vmem_limit_bytes=VMEM_LIMIT),
        name="adamw",
    )(step, norms, *grads, *weights, *firsts, *seconds)


AXES = ("dp", "fsdp")
SMALL_LANES = 128


def plans():
    feed = [halves(16, False), halves(64, True)]
    small = [Piece(None, 0, 16, False, "x")]
    square = [
        Piece(pl.ds(0, 4), 0, 8, False, "x"),
        Piece(pl.ds(0, 4), 8, 8, False, "y"),
        Piece(pl.ds(4, 2), 0, 8, True, "x"),
        Piece(pl.ds(4, 2), 8, 8, True, "y"),
    ]
    return [small] + feed, [square, halves(16, True)], feed


def gather_weights(sizes, feed_in, feed_out, square, proj, small):
    first, middle, last = plans()
    small = jnp.pad(small.T, ((0, 0), (0, SMALL_LANES - small.shape[0])))
    shards = [small, feed_in[0], feed_out[0], square, proj, feed_in[1], feed_out[1]]
    s, in1, out1, sq, conv, in2, out2 = gather(shards, [first, middle, last], (0, 1, 2), sizes, 0, "gather_weights")
    return (
        (in1.reshape(D, FF), in2.reshape(D, FF)),
        (out1.reshape(FF, D), out2.reshape(FF, D)),
        sq.reshape(6, D, D),
        conv.reshape(D, 2 * D),
        s.reshape(D, SMALL_LANES).T,
    )


def scatter_gradients(sizes, grads):
    (in1, in2), (out1, out2), (dw, dw5), dproj, ds = grads
    grid = chip_grid(sizes[0] * sizes[1]) + (2,)
    first, middle, last = plans()
    ds = jnp.pad(ds, ((0, SMALL_LANES - ds.shape[0]), (0, 0))).T

    def split_rows(full):
        rows = full.shape[-2] // (sizes[0] * sizes[1])
        return full.reshape(full.shape[:-2] + grid + (rows, full.shape[-1]))

    fulls = [split_rows(v) for v in (in2, out2, jnp.concatenate([dw, dw5[None]]), dproj, ds, in1, out1)]
    g_in2, g_out2, g_sq, g_conv, g_s, g_in1, g_out1, norms = scatter(
        fulls, [last, middle, first], (0, 4, 8), 2, sizes, 1, "scatter_gradients", True
    )
    return (g_in1, g_in2, g_out1, g_out2, g_sq, g_conv, g_s), norms


def gather_plain(feed_in, feed_out, square, proj, small):
    feed_in = lax.all_gather(feed_in, AXES, axis=1, tiled=True)
    feed_out = lax.all_gather(feed_out, AXES, axis=1, tiled=True)
    square = lax.all_gather(square, AXES, axis=1, tiled=True)
    proj = lax.all_gather(proj, AXES, axis=0, tiled=True)
    small = lax.all_gather(small, AXES, axis=1, tiled=True)
    return feed_in, feed_out, square, proj, small


def scatter_plain(grads):
    (in1, in2), (out1, out2), (dw, dw5), dproj, ds = grads
    parts = [lax.psum_scatter(v, AXES, scatter_dimension=0, tiled=True) for v in (in1, in2, out1, out2)]
    parts.append(lax.psum_scatter(jnp.concatenate([dw, dw5[None]]), AXES, scatter_dimension=1, tiled=True))
    parts.append(lax.psum_scatter(dproj, AXES, scatter_dimension=0, tiled=True))
    parts.append(lax.psum_scatter(ds, AXES, scatter_dimension=1, tiled=True))
    total = lax.psum(sum(jnp.sum(part * part) for part in parts), AXES)
    return tuple(parts), jnp.zeros((1, 8, 128), f32).at[0, 0, 0].set(total)


def local(sizes, inputs, cotangent, segments, valid_mask, step_count, *state):
    weights, moments = state[:5], state[5:]
    firsts, seconds = moments[0::2], moments[1::2]
    devices = sizes[0] * sizes[1]
    kernels = D // devices % 16 == 0 and chip_grid(devices)[:2] == (2, 2)
    full = gather_weights(sizes, *weights) if kernels else gather_plain(*weights)
    out, dx, grads = layer(inputs, cotangent, segments, valid_mask, full)
    if kernels:
        grads, norms = scatter_gradients(sizes, grads)
        grads = grads[:6] + (grads[6].T[: weights[4].shape[0]],)
    else:
        grads, norms = scatter_plain(grads)
    norm, *updated = adamw(step_count, norms, grads, weights, firsts, seconds)
    return (out, dx, norm.reshape(()), *updated)


def solution(mesh):
    sizes = (mesh.shape["dp"], mesh.shape["fsdp"])
    batch = P(AXES, None, None)
    rows = P(AXES, None)
    middle = P(None, AXES, None)
    columns = P(None, AXES)
    weights = (middle, middle, middle, rows, columns)
    moments = tuple(spec for spec in weights for _ in range(2))
    return jax.shard_map(
        functools.partial(local, sizes),
        mesh=mesh,
        in_specs=(batch, batch, rows, rows, P()) + weights + moments,
        out_specs=(batch, batch, P()) + tuple(spec for spec in weights for _ in range(3)),
        check_vma=False,
    )
```

```python
import functools
import math

import jax
import jax.numpy as jnp
import numpy as np
from jax import lax
from jax.experimental import pallas as pl
from jax.experimental.pallas import tpu as pltpu
from jax.sharding import PartitionSpec as P

D = 512
H = 8
DH = 64
FF = 2048
K = 9
NC = FF // D
TAP = 23 + 2 * NC
NORM_EPS = 1e-05
BETA_ONE = 0.9
BETA_TWO = 0.999
ADAM_EPS = 1e-08
CLIP_NORM = 1.0
MATRIX_RATE = 0.03
VECTOR_RATE = 0.4
MATRIX_DECAY = 0.01
VMEM_LIMIT = 60 * 2**20

f32 = jnp.float32
bf16 = jnp.bfloat16
NN = (((1,), (0,)), ((), ()))
NT = (((1,), (1,)), ((), ()))
TN = (((0,), (0,)), ((), ()))


def split(value):
    high = value.astype(bf16)
    return high, (value - high.astype(f32)).astype(bf16)


def dot(left, right, dims):
    return lax.dot_general(left, right, dims, preferred_element_type=f32)


def dot3(left, right, dims):
    return dot(left[0], right[0], dims) + (dot(left[0], right[1], dims) + dot(left[1], right[0], dims))


def normalize(values):
    centred = values - jnp.mean(values, axis=-1, keepdims=True)
    inverse = lax.rsqrt(jnp.mean(centred * centred, axis=-1, keepdims=True) + NORM_EPS)
    return centred * inverse, inverse


def normalize_back(scaled, xhat, inverse):
    return (scaled - jnp.mean(scaled, axis=-1, keepdims=True) - xhat * jnp.mean(scaled * xhat, axis=-1, keepdims=True)) * inverse


def column_sum(values):
    return jnp.sum(values, axis=0, keepdims=True)


def row(rows_ref, index):
    return rows_ref[pl.ds(index, 1), :]


def store_split(pair_ref, value):
    high, low = split(value)
    pair_ref[0] = high
    pair_ref[1] = low


def load_split(pair_ref, *index):
    if index:
        return pair_ref[(0,) + index], pair_ref[(1,) + index]
    return pair_ref[0], pair_ref[1]


def ffn_forward_chunk(normed, u_ref, win, wout, bias):
    u = dot3(normed, split(win), NN) + bias
    u_ref[...] = u
    return dot3(split(u * jax.nn.sigmoid(u)), split(wout), NN)


def ffn_backward_chunk(normed, u, df, win, wout):
    sig = jax.nn.sigmoid(u)
    dwout = dot3(split(u * sig), df, TN)
    du = dot3(df, split(wout), NT) * (sig * (1.0 + u * (1.0 - sig)))
    du_split = split(du)
    dwin = dot3(normed, du_split, TN)
    return dwin, dwout, column_sum(du), dot3(du_split, split(win), NT)


def ffn1_forward_kernel(x_ref, win_ref, wout_ref, s_ref, a1_ref, u_ref, normed):
    chunk = pl.program_id(0)

    @pl.when(chunk == 0)
    def _():
        xhat, _ = normalize(x_ref[...])
        store_split(normed, xhat * s_ref[0:1] + s_ref[1:2])
        a1_ref[...] = x_ref[...] + 0.5 * s_ref[17:18]

    out = ffn_forward_chunk(load_split(normed), u_ref, win_ref[...], wout_ref[...], row(s_ref, 23 + chunk))
    a1_ref[...] += 0.5 * out


def ffn1_forward(x, win, wout, s):
    frames = x.shape[0]
    whole = pl.BlockSpec((frames, D), lambda c: (0, 0))
    return pl.pallas_call(
        ffn1_forward_kernel,
        grid=(NC,),
        in_specs=[
            whole,
            pl.BlockSpec((D, D), lambda c: (0, c)),
            pl.BlockSpec((D, D), lambda c: (c, 0)),
            pl.BlockSpec(s.shape, lambda c: (0, 0)),
        ],
        out_specs=[whole, pl.BlockSpec((frames, D), lambda c: (0, c))],
        out_shape=[jax.ShapeDtypeStruct((frames, D), f32), jax.ShapeDtypeStruct((frames, FF), f32)],
        scratch_shapes=[pltpu.VMEM((2, frames, D), bf16)],
        compiler_params=pltpu.CompilerParams(vmem_limit_bytes=VMEM_LIMIT),
        name="ffn1_forward",
    )(x, win, wout, s)


def ffn1_backward_kernel(da_ref, x_ref, u_ref, win_ref, wout_ref, s_ref, dx_ref, dwin_ref, dwout_ref, ds_ref, normed, df):
    chunk = pl.program_id(0)

    @pl.when(chunk == 0)
    def _():
        xhat, _ = normalize(x_ref[...])
        store_split(normed, xhat * s_ref[0:1] + s_ref[1:2])
        half = 0.5 * da_ref[...]
        store_split(df, half)
        ds_ref[...] = jnp.zeros_like(ds_ref)
        ds_ref[2:3] = column_sum(half)
        dx_ref[...] = jnp.zeros_like(dx_ref)

    dwin, dwout, dbias, dnormed = ffn_backward_chunk(load_split(normed), u_ref[...], load_split(df), win_ref[...], wout_ref[...])
    dwin_ref[...] = dwin
    dwout_ref[...] = dwout
    ds_ref[pl.ds(4 + chunk, 1), :] = dbias
    dx_ref[...] += dnormed

    @pl.when(chunk == NC - 1)
    def _():
        xhat, inverse = normalize(x_ref[...])
        dn = dx_ref[...]
        ds_ref[0:1] = column_sum(dn * xhat)
        ds_ref[1:2] = column_sum(dn)
        dx_ref[...] = da_ref[...] + normalize_back(dn * s_ref[0:1], xhat, inverse)


def ffn1_backward(da, x, u, win, wout, s):
    frames = x.shape[0]
    whole = pl.BlockSpec((frames, D), lambda c: (0, 0))
    across = pl.BlockSpec((D, D), lambda c: (0, c))
    down = pl.BlockSpec((D, D), lambda c: (c, 0))
    return pl.pallas_call(
        ffn1_backward_kernel,
        grid=(NC,),
        in_specs=[whole, whole, pl.BlockSpec((frames, D), lambda c: (0, c)), across, down, pl.BlockSpec(s.shape, lambda c: (0, 0))],
        out_specs=[whole, across, down, pl.BlockSpec((8, D), lambda c: (0, 0))],
        out_shape=[
            jax.ShapeDtypeStruct((frames, D), f32),
            jax.ShapeDtypeStruct((D, FF), f32),
            jax.ShapeDtypeStruct((FF, D), f32),
            jax.ShapeDtypeStruct((8, D), f32),
        ],
        scratch_shapes=[pltpu.VMEM((2, frames, D), bf16), pltpu.VMEM((2, frames, D), bf16)],
        compiler_params=pltpu.CompilerParams(vmem_limit_bytes=VMEM_LIMIT),
        name="ffn1_backward",
    )(da, x, u, win, wout, s)


def ffn2_kernel(a3_ref, cot_ref, win_ref, wout_ref, s_ref, out_ref, da3_ref, dwin_ref, dwout_ref, ds_ref, normed, df, hidden, da4):
    step = pl.program_id(0)

    @pl.when(step == 0)
    def _():
        xhat, _ = normalize(a3_ref[...])
        store_split(normed, xhat * s_ref[8:9] + s_ref[9:10])
        da4[...] = a3_ref[...] + 0.5 * s_ref[18:19]

    @pl.when(step < NC)
    def _():
        out = ffn_forward_chunk(load_split(normed), hidden.at[step], win_ref[...], wout_ref[...], row(s_ref, 23 + NC + step))
        da4[...] += 0.5 * out

    @pl.when(step == NC - 1)
    def _():
        xhat, inverse = normalize(da4[...])
        out_ref[...] = xhat * s_ref[10:11] + s_ref[11:12]
        cot = cot_ref[...]
        ds_ref[...] = jnp.zeros_like(ds_ref)
        ds_ref[8:9] = column_sum(cot * xhat)
        ds_ref[9:10] = column_sum(cot)
        grad = normalize_back(cot * s_ref[10:11], xhat, inverse)
        da4[...] = grad
        half = 0.5 * grad
        store_split(df, half)
        ds_ref[2:3] = column_sum(half)
        da3_ref[...] = jnp.zeros_like(da3_ref)

    @pl.when(step >= NC)
    def _():
        dwin, dwout, dbias, dnormed = ffn_backward_chunk(load_split(normed), hidden[step - NC], load_split(df), win_ref[...], wout_ref[...])
        dwin_ref[...] = dwin
        dwout_ref[...] = dwout
        ds_ref[pl.ds(4 + step - NC, 1), :] = dbias
        da3_ref[...] += dnormed

    @pl.when(step == 2 * NC - 1)
    def _():
        xhat, inverse = normalize(a3_ref[...])
        dn = da3_ref[...]
        ds_ref[0:1] = column_sum(dn * xhat)
        ds_ref[1:2] = column_sum(dn)
        da3_ref[...] = da4[...] + normalize_back(dn * s_ref[8:9], xhat, inverse)


def ffn2(a3, cot, win, wout, s):
    frames = a3.shape[0]
    whole = pl.BlockSpec((frames, D), lambda c: (0, 0))
    return pl.pallas_call(
        ffn2_kernel,
        grid=(2 * NC,),
        in_specs=[
            whole,
            whole,
            pl.BlockSpec((D, D), lambda c: (0, lax.rem(c, NC))),
            pl.BlockSpec((D, D), lambda c: (lax.rem(c, NC), 0)),
            pl.BlockSpec(s.shape, lambda c: (0, 0)),
        ],
        out_specs=[
            whole,
            whole,
            pl.BlockSpec((D, D), lambda c: (0, jnp.maximum(c - NC, 0))),
            pl.BlockSpec((D, D), lambda c: (jnp.maximum(c - NC, 0), 0)),
            pl.BlockSpec((16, D), lambda c: (0, 0)),
        ],
        out_shape=[
            jax.ShapeDtypeStruct((frames, D), f32),
            jax.ShapeDtypeStruct((frames, D), f32),
            jax.ShapeDtypeStruct((D, FF), f32),
            jax.ShapeDtypeStruct((FF, D), f32),
            jax.ShapeDtypeStruct((16, D), f32),
        ],
        scratch_shapes=[
            pltpu.VMEM((2, frames, D), bf16),
            pltpu.VMEM((2, frames, D), bf16),
            pltpu.VMEM((NC, frames, D), f32),
            pltpu.VMEM((frames, D), f32),
        ],
        compiler_params=pltpu.CompilerParams(vmem_limit_bytes=VMEM_LIMIT),
        name="ffn2",
    )(a3, cot, win, wout, s)


def sinusoid_table(length):
    offsets = length // 2 - np.arange(length, dtype=np.float64)
    frequency = 10000.0 ** (-2.0 * np.arange(D // 2, dtype=np.float64) / D)
    angles = offsets[:, None] * frequency[None, :]
    table = np.concatenate([np.sin(angles), np.cos(angles)], axis=1).astype(np.float32)
    return np.stack([table, table[::-1]])


def shift_rows(scores):
    return pltpu.roll(scores, scores.shape[1] // 2, 1, stride=1, stride_axis=0)


def pair_masks():
    lane = lax.broadcasted_iota(jnp.int32, (1, 2 * DH), 1)
    first = (lane < DH).astype(f32)
    return first, 1.0 - first


def attention_forward_kernel(length, a1_ref, w_ref, pe_ref, s_ref, segcol_ref, keyrow_ref, a2_ref, qkv_ref, rel_ref, probs_ref, ctx_ref, bias):
    packs = a1_ref.shape[0] // length
    xhat, _ = normalize(a1_ref[...])
    normed = split(xhat * s_ref[2:3] + s_ref[3:4])
    qkv_ref[0] = dot3(normed, split(w_ref[0]), NN) + s_ref[12:13]
    qkv_ref[1] = dot3(normed, split(w_ref[1]), NN)
    qkv_ref[2] = dot3(normed, split(w_ref[2]), NN) + s_ref[13:14]
    rel_ref[...] = dot3(split(pe_ref[0]), split(w_ref[4]), NN)
    query = lax.broadcasted_iota(jnp.int32, (length, length), 0)
    key = lax.broadcasted_iota(jnp.int32, (length, length), 1)
    for pack in range(packs):
        same = segcol_ref[pl.ds(pack * length, length), 0:1] == keyrow_ref[pack : pack + 1, 0:length]
        bias[pack] = jnp.where(same | (query == key), 0.0, -1e30)
    first, second = pair_masks()

    def heads(item, carry):
        pack, pair = item // (H // 2), item % (H // 2)
        frames = pl.ds(pl.multiple_of(pack * length, length), length)
        lanes = pl.ds(pl.multiple_of(pair * 2 * DH, 2 * DH), 2 * DH)
        q = qkv_ref[0, frames, lanes]
        content = q + s_ref[15:16, lanes]
        position = q + s_ref[16:17, lanes]
        k = split(qkv_ref[1, frames, lanes])
        v = split(qkv_ref[2, frames, lanes])
        rel = split(rel_ref[:, lanes])
        total = jnp.zeros_like(q)
        for index, mask in enumerate((first, second)):
            scores = dot3(split(content * mask), k, NT) + shift_rows(dot3(split(position * mask), rel, NT))
            scores = scores * (1.0 / math.sqrt(DH)) + bias[pack]
            weights = jnp.exp(scores - jnp.max(scores, axis=-1, keepdims=True))
            weights = weights / jnp.sum(weights, axis=-1, keepdims=True)
            probs_ref[item * 2 + index] = weights
            total = total + dot3(split(weights), v, NN) * mask
        ctx_ref[frames, lanes] = total
        return carry

    lax.fori_loop(0, packs * (H // 2), heads, 0)
    a2_ref[...] = a1_ref[...] + dot3(split(ctx_ref[...]), split(w_ref[3]), NN) + s_ref[14:15]


def attention_forward(length, a1, square, pe, s, segcol, keyrow):
    frames = a1.shape[0]
    packs = frames // length
    vmem = pl.BlockSpec(memory_space=pltpu.VMEM)
    return pl.pallas_call(
        functools.partial(attention_forward_kernel, length),
        in_specs=[vmem] * 6,
        out_specs=[vmem] * 5,
        out_shape=[
            jax.ShapeDtypeStruct((frames, D), f32),
            jax.ShapeDtypeStruct((3, frames, D), f32),
            jax.ShapeDtypeStruct((length, D), f32),
            jax.ShapeDtypeStruct((packs * H, length, length), f32),
            jax.ShapeDtypeStruct((frames, D), f32),
        ],
        scratch_shapes=[pltpu.VMEM((packs, length, length), f32)],
        compiler_params=pltpu.CompilerParams(vmem_limit_bytes=VMEM_LIMIT),
        name="attention_forward",
    )(a1, square, pe, s, segcol, keyrow)


def attention_backward_kernel(
    length, da2_ref, a1_ref, qkv_ref, rel_ref, probs_ref, ctx_ref, w_ref, pe_ref, s_ref, da1_ref, dw_ref, ds_ref, dctx, dqkv, drel, relback, du, dv
):
    packs = a1_ref.shape[0] // length
    row_index = lax.broadcasted_iota(jnp.int32, (length, length), 0)
    lane_index = lax.broadcasted_iota(jnp.int32, (length, length), 1)
    flip = (row_index + lane_index == length - 1).astype(bf16)
    da2 = da2_ref[...]
    da2_split = split(da2)
    ds_ref[...] = jnp.zeros_like(ds_ref)
    ds_ref[2:3] = column_sum(da2)
    dw_ref[3] = dot3(split(ctx_ref[...]), da2_split, TN)
    dctx[...] = dot3(da2_split, split(w_ref[3]), NT)
    rel_split = split(rel_ref[...])
    relback[...] = dot(flip, rel_split[0], NN) + dot(flip, rel_split[1], NN)
    drel[...] = jnp.zeros_like(drel)
    du[...] = jnp.zeros_like(du)
    dv[...] = jnp.zeros_like(dv)
    first, second = pair_masks()

    def heads(item, carry):
        pack, pair = item // (H // 2), item % (H // 2)
        frames = pl.ds(pl.multiple_of(pack * length, length), length)
        lanes = pl.ds(pl.multiple_of(pair * 2 * DH, 2 * DH), 2 * DH)
        q = qkv_ref[0, frames, lanes]
        content = q + s_ref[15:16, lanes]
        position = q + s_ref[16:17, lanes]
        k = qkv_ref[1, frames, lanes]
        v = split(qkv_ref[2, frames, lanes])
        rel = relback[:, lanes]
        dc = dctx[frames, lanes]
        dcontent = jnp.zeros_like(q)
        dposition = jnp.zeros_like(q)
        dkey = jnp.zeros_like(q)
        dvalue = jnp.zeros_like(q)
        drelation = jnp.zeros_like(rel)
        for index, mask in enumerate((first, second)):
            weights = probs_ref[item * 2 + index]
            dc_split = split(dc * mask)
            dvalue = dvalue + dot3(split(weights), dc_split, TN)
            dweights = dot3(dc_split, v, NT)
            dscores = weights * (dweights - jnp.sum(weights * dweights, axis=-1, keepdims=True)) * (1.0 / math.sqrt(DH))
            ds_split = split(dscores)
            dcontent = dcontent + dot3(ds_split, split(k * mask), NN)
            dkey = dkey + dot3(ds_split, split(content * mask), TN)
            shifted = split(shift_rows(dot(ds_split[0], flip, NN) + dot(ds_split[1], flip, NN)))
            dposition = dposition + dot3(shifted, split(rel * mask), NN)
            drelation = drelation + dot3(shifted, split(position * mask), TN)
        dqkv[0, frames, lanes] = dcontent + dposition
        dqkv[1, frames, lanes] = dkey
        dqkv[2, frames, lanes] = dvalue
        drel[:, lanes] += drelation
        du[0:1, lanes] += column_sum(dcontent)
        dv[0:1, lanes] += column_sum(dposition)
        return carry

    lax.fori_loop(0, packs * (H // 2), heads, 0)
    ds_ref[3:4] = du[0:1]
    ds_ref[4:5] = dv[0:1]
    ds_ref[5:6] = column_sum(dqkv[0])
    ds_ref[6:7] = column_sum(dqkv[2])
    xhat, inverse = normalize(a1_ref[...])
    normed = split(xhat * s_ref[2:3] + s_ref[3:4])
    dnormed = jnp.zeros_like(xhat)
    for index in range(3):
        grad = split(dqkv[index])
        dw_ref[index] = dot3(normed, grad, TN)
        dnormed = dnormed + dot3(grad, split(w_ref[index]), NT)
    dw_ref[4] = dot3(split(pe_ref[1]), split(drel[...]), TN)
    ds_ref[0:1] = column_sum(dnormed * xhat)
    ds_ref[1:2] = column_sum(dnormed)
    da1_ref[...] = da2_ref[...] + normalize_back(dnormed * s_ref[2:3], xhat, inverse)


def attention_backward(length, da2, a1, qkv, rel, probs, ctx, square, pe, s):
    frames = a1.shape[0]
    vmem = pl.BlockSpec(memory_space=pltpu.VMEM)
    return pl.pallas_call(
        functools.partial(attention_backward_kernel, length),
        in_specs=[vmem] * 9,
        out_specs=[vmem] * 3,
        out_shape=[
            jax.ShapeDtypeStruct((frames, D), f32),
            jax.ShapeDtypeStruct((5, D, D), f32),
            jax.ShapeDtypeStruct((8, D), f32),
        ],
        scratch_shapes=[
            pltpu.VMEM((frames, D), f32),
            pltpu.VMEM((3, frames, D), f32),
            pltpu.VMEM((length, D), f32),
            pltpu.VMEM((length, D), f32),
            pltpu.VMEM((8, D), f32),
            pltpu.VMEM((8, D), f32),
        ],
        compiler_params=pltpu.CompilerParams(vmem_limit_bytes=VMEM_LIMIT),
        name="attention_backward",
    )(da2, a1, qkv, rel, probs, ctx, square, pe, s)


EDGE = 8
HALF = (K - 1) // 2
STRIP = 64


def convolution_forward_kernel(a2_ref, proj_ref, w_ref, s_ref, match_ref, a3_ref, u_ref, mixed_ref, padded):
    frames = a2_ref.shape[0]
    xhat, _ = normalize(a2_ref[...])
    normed = split(xhat * s_ref[4:5] + s_ref[5:6])
    u_ref[:, :D] = dot3(normed, split(proj_ref[:, :D]), NN) + s_ref[19:20]
    u_ref[:, D:] = dot3(normed, split(proj_ref[:, D:]), NN) + s_ref[20:21]
    padded[0:EDGE] = jnp.zeros((EDGE, D), f32)
    padded[EDGE + frames :] = jnp.zeros((EDGE, D), f32)
    padded[EDGE : EDGE + frames] = u_ref[:, :D] * jax.nn.sigmoid(u_ref[:, D:]) * match_ref[:, K : K + 1]
    for base in range(0, frames, STRIP):
        total = jnp.zeros((STRIP, D), f32) + s_ref[21:22]
        for tap in range(K):
            source = padded[base + EDGE + tap - HALF : base + EDGE + tap - HALF + STRIP]
            total = total + match_ref[base : base + STRIP, tap : tap + 1] * source * s_ref[TAP + tap : TAP + tap + 1]
        mixed_ref[base : base + STRIP] = total
    inner, _ = normalize(mixed_ref[...])
    inner = inner * s_ref[6:7] + s_ref[7:8]
    a3_ref[...] = a2_ref[...] + dot3(split(inner * jax.nn.sigmoid(inner)), split(w_ref[...]), NN) + s_ref[22:23]


def convolution_forward(a2, proj, weight, s, match):
    frames = a2.shape[0]
    vmem = pl.BlockSpec(memory_space=pltpu.VMEM)
    return pl.pallas_call(
        convolution_forward_kernel,
        in_specs=[vmem] * 5,
        out_specs=[vmem] * 3,
        out_shape=[
            jax.ShapeDtypeStruct((frames, D), f32),
            jax.ShapeDtypeStruct((frames, 2 * D), f32),
            jax.ShapeDtypeStruct((frames, D), f32),
        ],
        scratch_shapes=[pltpu.VMEM((frames + 2 * EDGE, D), f32)],
        compiler_params=pltpu.CompilerParams(vmem_limit_bytes=VMEM_LIMIT),
        name="convolution_forward",
    )(a2, proj, weight, s, match)


def convolution_backward_kernel(
    da3_ref, a2_ref, u_ref, mixed_ref, proj_ref, w_ref, s_ref, match_ref, da2_ref, dproj_ref, dw_ref, ds_ref, padded, dpadded, dgated
):
    frames = a2_ref.shape[0]
    da3 = da3_ref[...]
    da3_split = split(da3)
    ds_ref[...] = jnp.zeros_like(ds_ref)
    ds_ref[2:3] = column_sum(da3)
    hat, inverse = normalize(mixed_ref[...])
    inner = hat * s_ref[6:7] + s_ref[7:8]
    sig = jax.nn.sigmoid(inner)
    dw_ref[...] = dot3(split(inner * sig), da3_split, TN)
    dinner = dot3(da3_split, split(w_ref[...]), NT) * (sig * (1.0 + inner * (1.0 - sig)))
    ds_ref[3:4] = column_sum(dinner * hat)
    ds_ref[4:5] = column_sum(dinner)
    dmixed = normalize_back(dinner * s_ref[6:7], hat, inverse)
    ds_ref[5:6] = column_sum(dmixed)
    zeros = jnp.zeros((EDGE, D), f32)
    padded[0:EDGE] = zeros
    padded[EDGE + frames :] = zeros
    padded[EDGE : EDGE + frames] = u_ref[:, :D] * jax.nn.sigmoid(u_ref[:, D:]) * match_ref[:, K : K + 1]
    dpadded[0:EDGE] = zeros
    dpadded[EDGE + frames :] = zeros
    dpadded[EDGE : EDGE + frames] = dmixed
    for base in range(0, frames, STRIP):
        total = jnp.zeros((STRIP, D), f32)
        center = dpadded[base + EDGE : base + EDGE + STRIP]
        for tap in range(K):
            rows = slice(base + EDGE + tap - HALF, base + EDGE + tap - HALF + STRIP)
            match = match_ref[base : base + STRIP, tap : tap + 1]
            total = total + match * dpadded[rows] * s_ref[TAP + K - 1 - tap : TAP + K - tap]
            ds_ref[8 + tap : 9 + tap] += column_sum(center * (match * padded[rows]))
        dgated[base : base + STRIP] = total * match_ref[base : base + STRIP, K : K + 1]
    gate = jax.nn.sigmoid(u_ref[:, D:])
    dfirst = dgated[...] * gate
    dsecond = dfirst * u_ref[:, :D] * (1.0 - gate)
    ds_ref[6:7] = column_sum(dfirst)
    ds_ref[7:8] = column_sum(dsecond)
    xhat, inverse = normalize(a2_ref[...])
    normed = split(xhat * s_ref[4:5] + s_ref[5:6])
    dfirst = split(dfirst)
    dsecond = split(dsecond)
    dproj_ref[:, :D] = dot3(normed, dfirst, TN)
    dproj_ref[:, D:] = dot3(normed, dsecond, TN)
    dnormed = dot3(dfirst, split(proj_ref[:, :D]), NT) + dot3(dsecond, split(proj_ref[:, D:]), NT)
    ds_ref[0:1] = column_sum(dnormed * xhat)
    ds_ref[1:2] = column_sum(dnormed)
    da2_ref[...] = da3_ref[...] + normalize_back(dnormed * s_ref[4:5], xhat, inverse)


def convolution_backward(da3, a2, u, mixed, proj, weight, s, match):
    frames = a2.shape[0]
    vmem = pl.BlockSpec(memory_space=pltpu.VMEM)
    return pl.pallas_call(
        convolution_backward_kernel,
        in_specs=[vmem] * 8,
        out_specs=[vmem] * 4,
        out_shape=[
            jax.ShapeDtypeStruct((frames, D), f32),
            jax.ShapeDtypeStruct((D, 2 * D), f32),
            jax.ShapeDtypeStruct((D, D), f32),
            jax.ShapeDtypeStruct((24, D), f32),
        ],
        scratch_shapes=[
            pltpu.VMEM((frames + 2 * EDGE, D), f32),
            pltpu.VMEM((frames + 2 * EDGE, D), f32),
            pltpu.VMEM((frames, D), f32),
        ],
        compiler_params=pltpu.CompilerParams(vmem_limit_bytes=VMEM_LIMIT),
        name="convolution_backward",
    )(da3, a2, u, mixed, proj, weight, s, match)


def frame_tables(segments, valid_mask):
    packs, length = segments.shape
    position = jnp.arange(length, dtype=jnp.int32)
    columns = []
    for tap in range(K):
        moved = jnp.roll(segments, HALF - tap, axis=1)
        inside = (position + tap - HALF >= 0) & (position + tap - HALF < length)
        columns.append(((moved == segments) & inside[None, :]).astype(f32))
    columns.append(valid_mask.astype(f32))
    match = jnp.stack(columns, axis=-1).reshape(packs * length, K + 1)
    match = jnp.pad(match, ((0, 0), (0, 128 - K - 1)))
    segcol = jnp.broadcast_to(segments.reshape(packs * length, 1), (packs * length, 128))
    keyrow = jnp.pad(jnp.where(valid_mask > 0, segments, -1), ((0, -packs % 8), (0, 0)))
    return match, segcol, keyrow


def small_rows(parts):
    first, attend, conv, second = parts
    return jnp.concatenate(
        [
            first[0:2],
            attend[0:2],
            conv[0:2],
            conv[3:5],
            second[0:2],
            second[8:10],
            attend[5:7],
            attend[2:5],
            first[2:3],
            second[2:3],
            conv[6:8],
            conv[5:6],
            conv[2:3],
            first[4:8],
            second[4:8],
            conv[8 : 8 + K],
        ],
        axis=0,
    )


def layer(inputs, cotangent, segments, valid_mask, weights):
    feed_in, feed_out, square, proj, s = weights
    packs, length, _ = inputs.shape
    frames = packs * length
    x = inputs.reshape(frames, D)
    cot = cotangent.reshape(frames, D)
    match, segcol, keyrow = frame_tables(segments, valid_mask)
    pe = jnp.asarray(sinusoid_table(length))
    a1, u1 = ffn1_forward(x, feed_in[0], feed_out[0], s)
    a2, qkv, rel, probs, ctx = attention_forward(length, a1, square, pe, s, segcol, keyrow)
    a3, u, mixed = convolution_forward(a2, proj, square[5], s, match)
    out, da3, dwin2, dwout2, ds2 = ffn2(a3, cot, feed_in[1], feed_out[1], s)
    da2, dproj, dw5, dsc = convolution_backward(da3, a2, u, mixed, proj, square[5], s, match)
    da1, dw, dsa = attention_backward(length, da2, a1, qkv, rel, probs, ctx, square, pe, s)
    dx, dwin1, dwout1, ds1 = ffn1_backward(da1, x, u1, feed_in[0], feed_out[0], s)
    grads = (dwin1, dwin2), (dwout1, dwout2), (dw, dw5), dproj, small_rows((ds1, dsa, dsc, ds2))
    return out.reshape(inputs.shape), dx.reshape(inputs.shape), grads

MESH_ID = pl.DeviceIdType.MESH


def chip_grid(devices):
    side = 1
    while side * side * 2 * side * 2 < devices:
        side *= 2
    return side, side, 2 * side


class Place:
    def __init__(self, sizes):
        self.fsdp = sizes[1]
        self.y_size, self.x_size, self.z_size = chip_grid(sizes[0] * sizes[1])
        index = lax.axis_index("dp") * sizes[1] + lax.axis_index("fsdp")
        self.index = index
        self.core = lax.rem(index, 2)
        self.z = lax.rem(index // 2, self.z_size)
        self.x = lax.rem(index // (2 * self.z_size), 2)
        self.y = index // (4 * self.z_size)

    def device(self, y=None, x=None, z=None, core=None):
        y = self.y if y is None else y
        x = self.x if x is None else x
        z = self.z if z is None else z
        core = self.core if core is None else core
        index = ((y * 2 + x) * self.z_size + z) * 2 + core
        return index // self.fsdp, lax.rem(index, self.fsdp)

    def neighbour(self, axis):
        if axis == "core":
            return self.device(core=1 - self.core)
        if axis == "x":
            return self.device(x=1 - self.x)
        if axis == "y":
            return self.device(y=1 - self.y)
        return self.device(z=self.z + (1 if axis == "right" else -1))

    def greet(self):
        barrier = pltpu.get_barrier_semaphore()
        for axis in ("core", "x", "y"):
            pl.semaphore_signal(barrier, inc=1, device_id=self.neighbour(axis), device_id_type=MESH_ID)

        @pl.when(self.z > 0)
        def _():
            pl.semaphore_signal(barrier, inc=1, device_id=self.neighbour("left"), device_id_type=MESH_ID)

        @pl.when(self.z < self.z_size - 1)
        def _():
            pl.semaphore_signal(barrier, inc=1, device_id=self.neighbour("right"), device_id_type=MESH_ID)

        peers = 3 + (self.z > 0).astype(jnp.int32) + (self.z < self.z_size - 1).astype(jnp.int32)
        pl.semaphore_wait(barrier, peers)


EVERY = slice(None)


class Piece:
    def __init__(self, lead, first_row, rows, zfirst, near):
        self.lead, self.rows, self.zfirst, self.near = lead, pl.ds(first_row, rows), zfirst, near
        self.far = "y" if near == "x" else "x"

    def own(self, shard):
        return shard.at[self.rows] if self.lead is None else shard.at[self.lead, self.rows]

    def blocks(self, full, place, near, far, z, core):
        y, x = (near, far) if self.near == "y" else (far, near)
        index = (y, x, z, core, self.rows)
        return full.at[index] if self.lead is None else full.at[(self.lead,) + index]

    def here(self, place):
        return (place.x, place.y) if self.near == "x" else (place.y, place.x)


G_RIGHT, G_LEFT, G_NEAR, G_FAR, G_CORE = range(5)


class Gather:
    def __init__(self, place, piece, shard, full, send, recv, local):
        self.place, self.piece, self.shard, self.full = place, piece, shard, full
        self.send, self.recv, self.local = send, recv, local

    def view(self, near, far, z, core=None):
        return self.piece.blocks(self.full, self.place, near, far, z, self.place.core if core is None else core)

    def copy(self, kind, z, ref, axis, source=None):
        return pltpu.make_async_remote_copy(
            src_ref=ref if source is None else source,
            dst_ref=ref,
            send_sem=self.send.at[kind, z],
            recv_sem=self.recv.at[G_RIGHT if kind == G_LEFT else kind, z],
            device_id=self.place.neighbour(axis),
            device_id_type=MESH_ID,
        )

    def z_view(self, z):
        near, far = self.piece.here(self.place)
        return self.view(near if self.piece.zfirst else EVERY, far, z)

    def near_view(self, near, z):
        return self.view(near, self.piece.here(self.place)[1], z)

    def far_view(self, far, z):
        return self.view(EVERY, far, z)

    def core_view(self, core, z):
        return self.view(EVERY, EVERY, z, core)

    def own_copy(self):
        near, far = self.piece.here(self.place)
        return pltpu.make_async_copy(self.piece.own(self.shard), self.view(near, far, self.place.z), self.local)

    def begin(self):
        self.own_copy().start()
        if not self.piece.zfirst:
            near, _ = self.piece.here(self.place)
            self.copy(G_NEAR, self.place.z, self.near_view(near, self.place.z), self.piece.near, self.piece.own(self.shard)).start()

    def z_step(self, z, own, from_left):
        place = self.place
        near, far = self.piece.here(place)

        @pl.when(own)
        def _():
            self.own_copy().wait()
            if not self.piece.zfirst:
                self.copy(G_NEAR, z, self.near_view(1 - near, z), self.piece.near).wait_recv()

        @pl.when(jnp.logical_not(own))
        def _():
            self.copy(G_RIGHT, z, self.z_view(z), "left").wait_recv()

        @pl.when((own | from_left) & (place.z < place.z_size - 1))
        def _():
            self.copy(G_RIGHT, z, self.z_view(z), "right").start()

        @pl.when((own | jnp.logical_not(from_left)) & (place.z > 0))
        def _():
            self.copy(G_LEFT, z, self.z_view(z), "left").start()

        if self.piece.zfirst:
            self.copy(G_NEAR, z, self.near_view(near, z), self.piece.near).start()
        else:
            self.copy(G_FAR, z, self.far_view(far, z), self.piece.far).start()

    def near_step(self, z, own, from_left):
        near, far = self.piece.here(self.place)
        self.copy(G_NEAR, z, self.near_view(1 - near, z), self.piece.near).wait_recv()
        self.copy(G_FAR, z, self.far_view(far, z), self.piece.far).start()

    def far_step(self, z, own, from_left):
        _, far = self.piece.here(self.place)
        self.copy(G_FAR, z, self.far_view(1 - far, z), self.piece.far).wait_recv()
        self.copy(G_CORE, z, self.core_view(self.place.core, z), "core").start()

    def stages(self):
        if self.piece.zfirst:
            return [(0, self.z_step), (1, self.near_step), (2, self.far_step)]
        return [(1, self.z_step), (2, self.far_step)]

    def arrive(self):
        for z in range(self.place.z_size):
            self.copy(G_CORE, z, self.core_view(1 - self.place.core, z), "core").wait_recv()

    def drain(self):
        place = self.place
        near, far = self.piece.here(place)
        for z in range(place.z_size):
            self.copy(G_CORE, z, self.core_view(place.core, z), "core").wait_send()
            self.copy(G_FAR, z, self.far_view(far, z), self.piece.far).wait_send()
            if self.piece.zfirst:
                self.copy(G_NEAR, z, self.near_view(near, z), self.piece.near).wait_send()

            @pl.when((place.z < place.z_size - 1) & (z <= place.z))
            def _():
                self.copy(G_RIGHT, z, self.z_view(z), "right").wait_send()

            @pl.when((place.z > 0) & (z >= place.z))
            def _():
                self.copy(G_LEFT, z, self.z_view(z), "left").wait_send()

        if not self.piece.zfirst:
            self.copy(G_NEAR, place.z, self.near_view(near, place.z), self.piece.near).wait_send()


class GatherProgram:
    PARTS = 3

    def __init__(self, place, groups, offsets):
        self.place, self.groups, self.offsets = place, groups, offsets
        self.cursor = 0
        self.length = self.PARTS * (max(offsets) + place.z_size + 2)

    def begin(self):
        for group in self.groups:
            for piece in group:
                piece.begin()

    def part(self, number):
        step, part = number // self.PARTS, lax.rem(number, self.PARTS)
        place = self.place
        for group, offset in zip(self.groups, self.offsets):
            stages = {}
            for piece in group:
                for index, (behind, work) in enumerate(piece.stages()):
                    stages.setdefault((index if piece.piece.zfirst else 2 * index, behind), []).append(work)
            for (index, behind), works in stages.items():
                distance = step - offset - behind
                for from_left in (True, False):
                    z = place.z - distance if from_left else place.z + distance
                    least = 0 if from_left else 1

                    @pl.when((part == index) & (distance >= least) & (distance < place.z_size) & (z >= 0) & (z < place.z_size))
                    def _():
                        for work in works:
                            work(z, distance == 0, jnp.bool_(from_left))

    def run(self, count):
        last = min(self.length, self.cursor + count)
        if last > self.cursor:
            lax.fori_loop(self.cursor, last, lambda number, carry: (self.part(number), carry)[1], 0)
        self.cursor = last

    def run_in(self, index, each):
        def body(number, carry):
            @pl.when(number < self.length)
            def _():
                self.part(number)

            return carry

        lax.fori_loop(self.cursor + index * each, self.cursor + (index + 1) * each, body, 0)

    def skip(self, count):
        self.cursor = min(self.length, self.cursor + count)

    def run_until(self, group):
        self.run(self.PARTS * (self.offsets[group] + self.place.z_size + 2) - self.cursor)
        for piece in self.groups[group]:
            piece.arrive()

    def drain(self):
        self.run(self.length)
        for group in self.groups:
            for piece in group:
                piece.drain()


def halves(rows, zfirst, lead=None):
    return [Piece(lead, 0, rows // 2, zfirst, "x"), Piece(lead, rows // 2, rows // 2, zfirst, "y")]


def whole_shape(shard, sizes):
    y, x, z = chip_grid(sizes[0] * sizes[1])
    return shard.shape[:-2] + (y, x, z, 2) + shard.shape[-2:]


SMALL_LANES = 128


def plans():
    def feed(half):
        return [
            [Piece(pl.ds(half, 1), 0, 8, False, "x"), Piece(pl.ds(half, 1), 8, 8, False, "y")],
            [Piece(pl.ds(half, 1), 0, 32, True, "x"), Piece(pl.ds(half, 1), 32, 32, True, "y")],
        ]

    small = [Piece(None, 0, 16, False, "x")]
    square = [
        Piece(pl.ds(0, 4), 0, 8, False, "x"),
        Piece(pl.ds(0, 4), 8, 8, False, "y"),
        Piece(pl.ds(4, 2), 0, 8, True, "x"),
        Piece(pl.ds(4, 2), 8, 8, True, "y"),
    ]
    return [small] + feed(0), [square, halves(16, True)], feed(1)


def match_table(segments, valid):
    length = segments.shape[1]
    rows = lax.broadcasted_iota(jnp.int32, (128, length), 0)
    position = lax.broadcasted_iota(jnp.int32, (1, length), 1)
    table = jnp.where(rows == K, valid, jnp.where(rows == K + 1, segments, 0.0))
    for tap in range(K):
        moved = segments if tap == HALF else pltpu.roll(segments, (HALF - tap) % length, 1)
        inside = (position + tap - HALF >= 0) & (position + tap - HALF < length)
        table = jnp.where(rows == tap, jnp.where((moved == segments) & inside, 1.0, 0.0), table)
    return table.T


def forward_kernel(sizes, length, offsets, *refs):
    x_ref, seg_ref, valid_ref, pe_ref, small_ref, in_shard, out_shard, sq_shard, conv_shard = refs[:9]
    (a1_out, u1_out, qkv_out, rel_out, probs_out, ctx_out, a2_out, u_out, mixed_out, a3_out, s_out, match_out) = refs[9:21]
    in_full, out_full, sq_full, conv_full, small_full = refs[21:26]
    (a1, u1, qkv, rel, probs, ctx, a2, u, mixed, a3, s_ref, match, normed, padded, bias, small_own, small_whole, win, wout, square, conv) = refs[26:47]
    send, recv, local, loads, stores = refs[47:]
    frames = x_ref.shape[0]
    packs = frames // length

    place = Place(sizes)
    place.greet()
    small_own[...] = jnp.zeros_like(small_own)
    small_own[:, : small_ref.shape[1]] = small_ref[...]
    first, middle, last = plans()
    sources = [
        [(small_own, small_full), (in_shard, in_full), (out_shard, out_full)],
        [(sq_shard, sq_full), (conv_shard, conv_full)],
        [(in_shard, in_full), (out_shard, out_full)],
    ]
    groups, count = [], 0
    for plan, pairs in zip((first, middle, last), sources):
        group = []
        for pieces, (shard, full) in zip(plan, pairs):
            for piece in pieces:
                group.append(Gather(place, piece, shard, full, send.at[count], recv.at[count], local.at[count]))
                count += 1
        groups.append(group)
    program = GatherProgram(place, groups, offsets)
    program.begin()

    spilled = []

    def spill(source, target):
        copy = pltpu.make_async_copy(source, target, stores.at[len(spilled)])
        copy.start()
        spilled.append(copy)

    program.run(3)
    for pack in range(packs):
        rows = slice(pack * length, (pack + 1) * length)
        match[rows] = match_table(seg_ref[pack : pack + 1].astype(f32), valid_ref[pack : pack + 1].astype(f32))
    spill(match, match_out)
    query = lax.broadcasted_iota(jnp.int32, (length, length), 0)
    key = lax.broadcasted_iota(jnp.int32, (length, length), 1)
    for pack in range(packs):
        keyrow = jnp.where(valid_ref[pack : pack + 1] > 0, seg_ref[pack : pack + 1], -1).astype(f32)
        same = match[pack * length : (pack + 1) * length, K + 1 : K + 2] == keyrow
        bias[pack] = jnp.where(same | (query == key), 0.0, -1e30)

    program.run_until(0)
    load_small = pltpu.make_async_copy(small_full, small_whole, loads.at[0])
    load_in = pltpu.make_async_copy(in_full.at[0], win, loads.at[1])
    load_out = pltpu.make_async_copy(out_full.at[0], wout, loads.at[2])
    for load in (load_small, load_in, load_out):
        load.start()
    program.run(1)
    load_small.wait()
    s_ref[...] = small_whole[...].reshape(D, SMALL_LANES).T
    spill(s_ref, s_out)
    xhat, _ = normalize(x_ref[...])
    store_split(normed, xhat * s_ref[0:1] + s_ref[1:2])
    a1[...] = x_ref[...] + 0.5 * s_ref[17:18]
    load_in.wait()
    load_out.wait()
    width = FF // 8

    def chunk(index, carry):
        lanes = pl.ds(pl.multiple_of(index * width, width), width)
        bias_row = s_ref[pl.ds(23 + index // 2, 1), pl.ds(pl.multiple_of(lax.rem(index, 2) * width, width), width)]
        weight = win[:, :, :, :, :, lanes].reshape(D, width)
        value = dot3(load_split(normed), split(weight), NN) + bias_row
        u1[:, lanes] = value
        weight = wout[index // 4, lax.rem(index // 2, 2), pl.ds(lax.rem(index, 2) * 2, 2)].reshape(width, D)
        a1[...] += 0.5 * dot3(split(value * jax.nn.sigmoid(value)), split(weight), NN)
        program.run_in(index, 1)
        return carry

    lax.fori_loop(0, 8, chunk, 0)
    program.skip(8)
    spill(u1, u1_out)
    spill(a1, a1_out)
    xhat, _ = normalize(a1[...])
    store_split(normed, xhat * s_ref[2:3] + s_ref[3:4])

    program.run_until(1)
    load_square = pltpu.make_async_copy(sq_full, square, loads.at[3])
    load_conv = pltpu.make_async_copy(conv_full, conv, loads.at[4])
    load_square.start()
    load_conv.start()
    program.run(1)
    load_square.wait()
    load_conv.wait()

    def weight_split(index):
        return split(square[index].reshape(D, D))

    qkv[0] = dot3(load_split(normed), weight_split(0), NN) + s_ref[12:13]
    program.run(1)
    qkv[1] = dot3(load_split(normed), weight_split(1), NN)
    program.run(1)
    qkv[2] = dot3(load_split(normed), weight_split(2), NN) + s_ref[13:14]
    rel[...] = dot3(split(pe_ref[...]), weight_split(4), NN)
    program.run(1)
    spill(qkv, qkv_out)
    spill(rel, rel_out)
    attend(length, packs, qkv, rel, s_ref, bias, probs, ctx, lambda item: program.run_in(item, 1))
    program.skip(packs * (H // 2))
    spill(probs, probs_out)
    spill(ctx, ctx_out)
    a2[...] = a1[...] + dot3(split(ctx[...]), weight_split(3), NN) + s_ref[14:15]
    spill(a2, a2_out)
    program.run(1)

    xhat, _ = normalize(a2[...])
    store_split(normed, xhat * s_ref[4:5] + s_ref[5:6])
    for half in range(2):
        lanes = slice(half * D, (half + 1) * D)
        u[:, lanes] = dot3(load_split(normed), split(conv[:, :, :, :, :, lanes].reshape(D, D)), NN) + s_ref[19 + half : 20 + half]
        program.run(1)
    spill(u, u_out)
    mix(u, match, s_ref, padded, mixed)
    spill(mixed, mixed_out)
    program.run(1)
    inner, _ = normalize(mixed[...])
    inner = inner * s_ref[6:7] + s_ref[7:8]
    a3[...] = a2[...] + dot3(split(inner * jax.nn.sigmoid(inner)), weight_split(5), NN) + s_ref[22:23]
    spill(a3, a3_out)

    program.run_until(2)
    program.drain()
    for copy in spilled:
        copy.wait()


def attend(length, packs, qkv_ref, rel_ref, s_ref, bias, probs_ref, ctx_ref, between):
    first, second = pair_masks()

    def heads(item, carry):
        pack, pair = item // (H // 2), lax.rem(item, H // 2)
        frames = pl.ds(pl.multiple_of(pack * length, length), length)
        lanes = pl.ds(pl.multiple_of(pair * 2 * DH, 2 * DH), 2 * DH)
        q = qkv_ref[0, frames, lanes]
        content = q + s_ref[15:16, lanes]
        position = q + s_ref[16:17, lanes]
        k = split(qkv_ref[1, frames, lanes])
        v = split(qkv_ref[2, frames, lanes])
        rel = split(rel_ref[:, lanes])
        total = jnp.zeros_like(q)
        for index, mask in enumerate((first, second)):
            scores = dot3(split(content * mask), k, NT) + shift_rows(dot3(split(position * mask), rel, NT))
            scores = scores * (1.0 / math.sqrt(DH)) + bias[pack]
            weights = jnp.exp(scores - jnp.max(scores, axis=-1, keepdims=True))
            weights = weights / jnp.sum(weights, axis=-1, keepdims=True)
            probs_ref[item * 2 + index] = weights
            total = total + dot3(split(weights), v, NN) * mask
        ctx_ref[frames, lanes] = total
        between(item)
        return carry

    lax.fori_loop(0, packs * (H // 2), heads, 0)


def mix(u_ref, match_ref, s_ref, padded, mixed_ref):
    frames = mixed_ref.shape[0]
    padded[0:EDGE] = jnp.zeros((EDGE, D), f32)
    padded[EDGE + frames :] = jnp.zeros((EDGE, D), f32)
    padded[EDGE : EDGE + frames] = u_ref[:, :D] * jax.nn.sigmoid(u_ref[:, D:]) * match_ref[:, K : K + 1]
    for base in range(0, frames, STRIP):
        total = jnp.zeros((STRIP, D), f32) + s_ref[21:22]
        for tap in range(K):
            source = padded[base + EDGE + tap - HALF : base + EDGE + tap - HALF + STRIP]
            total = total + match_ref[base : base + STRIP, tap : tap + 1] * source * s_ref[TAP + tap : TAP + tap + 1]
        mixed_ref[base : base + STRIP] = total


def forward(sizes, x, segments, valid_mask, weights):
    feed_in, feed_out, square, proj, small = weights
    frames = x.shape[0]
    packs, length = segments.shape
    devices = sizes[0] * sizes[1]
    grid = chip_grid(devices) + (2,)
    z_size = grid[2]
    pe = jnp.asarray(sinusoid_table(length)[0])
    small_rows_here = small.shape[1]
    vmem = pl.BlockSpec(memory_space=pltpu.VMEM)
    kept = [
        (frames, D),
        (frames, FF),
        (3, frames, D),
        (length, D),
        (packs * H, length, length),
        (frames, D),
        (frames, D),
        (frames, 2 * D),
        (frames, D),
        (frames, D),
        (SMALL_LANES, D),
        (frames, 128),
    ]
    full = [
        (2,) + grid + feed_in.shape[1:],
        (2,) + grid + feed_out.shape[1:],
        (6,) + grid + square.shape[1:],
        grid + proj.shape,
        grid + (small_rows_here, SMALL_LANES),
    ]
    pieces = sum(len(p) for plan in plans() for p in plan)
    outs = pl.pallas_call(
        functools.partial(forward_kernel, sizes, length, GATHER_OFFSETS),
        in_specs=[vmem] * 9,
        out_specs=[pl.BlockSpec(memory_space=pl.ANY)] * (len(kept) + len(full)),
        out_shape=[jax.ShapeDtypeStruct(shape, f32) for shape in kept + full],
        scratch_shapes=[pltpu.VMEM(shape, f32) for shape in kept]
        + [
            pltpu.VMEM((2, frames, D), bf16),
            pltpu.VMEM((frames + 2 * EDGE, D), f32),
            pltpu.VMEM((packs, length, length), f32),
            pltpu.VMEM((small_rows_here, SMALL_LANES), f32),
            pltpu.VMEM(full[4], f32),
            pltpu.VMEM(full[0][1:], f32),
            pltpu.VMEM(full[1][1:], f32),
            pltpu.VMEM(full[2], f32),
            pltpu.VMEM(full[3], f32),
            pltpu.SemaphoreType.DMA((pieces, 5, z_size)),
            pltpu.SemaphoreType.DMA((pieces, 5, z_size)),
            pltpu.SemaphoreType.DMA((pieces,)),
            pltpu.SemaphoreType.DMA((5,)),
            pltpu.SemaphoreType.DMA((len(kept),)),
        ],
        compiler_params=pltpu.CompilerParams(collective_id=0, has_side_effects=True, vmem_limit_bytes=VMEM_LIMIT),
        name="forward",
    )(x, segments, valid_mask, pe, small.T, feed_in, feed_out, square, proj)
    return outs[: len(kept)], outs[len(kept) :]


GATHER_OFFSETS = (0, 3, 6)
S_CORE, S_FAR, S_NEAR, S_FROM_LEFT, S_FROM_RIGHT = range(5)


class Scatter:
    def __init__(self, place, piece, full, out, total, cores, fars, nears, lines, send, recv, local):
        self.place, self.piece, self.full, self.out = place, piece, full, out
        self.total, self.cores, self.fars, self.nears, self.lines = total, cores, fars, nears, lines
        self.send, self.recv, self.local = send, recv, local
        self.near, self.far = piece.here(place)

    def part(self, ref, near, far, z):
        y, x = (near, far) if self.piece.near == "y" else (far, near)
        index = (y, x, z)
        return ref.at[index] if self.piece.lead is None else ref.at[(EVERY,) + index]

    def staged(self, ref, *index):
        return ref.at[index] if self.piece.lead is None else ref.at[(EVERY,) + index]

    def add(self, target, source):
        target[...] = target[...] + source[...]

    def copy(self, kind, z, source, target, axis):
        return pltpu.make_async_remote_copy(
            src_ref=source,
            dst_ref=target,
            send_sem=self.send.at[kind, z],
            recv_sem=self.recv.at[kind, z],
            device_id=self.place.neighbour(axis),
            device_id_type=MESH_ID,
        )

    def core_copy(self, z):
        given = self.piece.blocks(self.full, self.place, EVERY, EVERY, z, 1 - self.place.core)
        return self.copy(S_CORE, z, given, self.part(self.cores, EVERY, EVERY, z), "core")

    def own_copy(self, z):
        kept = self.piece.blocks(self.full, self.place, EVERY, EVERY, z, self.place.core)
        return pltpu.make_async_copy(kept, self.part(self.total, EVERY, EVERY, z), self.local.at[z])

    def far_copy(self, z):
        return self.copy(S_FAR, z, self.part(self.total, EVERY, 1 - self.far, z), self.staged(self.fars, EVERY, z), self.piece.far)

    def near_copy(self, z):
        target = self.staged(self.nears, z if self.piece.zfirst else 0)
        return self.copy(S_NEAR, z, self.part(self.total, 1 - self.near, self.far, z), target, self.piece.near)

    def line_view(self, z):
        return self.part(self.total, self.near if self.piece.zfirst else EVERY, self.far, z)

    def line_staged(self, side, z):
        if self.piece.zfirst:
            return self.staged(self.lines, side, z)
        return self.staged(self.lines, side, EVERY, z)

    def line_copy(self, z, to_right):
        kind, side = (S_FROM_LEFT, 0) if to_right else (S_FROM_RIGHT, 1)
        return self.copy(kind, z, self.line_view(z), self.line_staged(side, z), "right" if to_right else "left")

    def begin(self):
        for distance in reversed(range(self.place.z_size)):
            for sign in (-1, 1) if distance else (1,):
                z = self.place.z + sign * distance

                @pl.when((z >= 0) & (z < self.place.z_size))
                def _():
                    self.core_copy(z).start()
                    self.own_copy(z).start()

    def core_step(self, z):
        self.core_copy(z).wait_recv()
        self.own_copy(z).wait()
        self.add(self.part(self.total, EVERY, EVERY, z), self.part(self.cores, EVERY, EVERY, z))

    def core_send(self, z):
        self.far_copy(z).start()

    def far_step(self, z):
        self.far_copy(z).wait_recv()
        self.add(self.part(self.total, EVERY, self.far, z), self.staged(self.fars, EVERY, z))

    def far_send(self, z):
        self.near_copy(z).start()

    def near_step(self, z):
        self.near_copy(z).wait_recv()
        self.add(self.part(self.total, self.near, self.far, z), self.staged(self.nears, z))

    def line_step(self, z):
        here = self.place.z

        @pl.when((z >= here) & (here > 0))
        def _():
            self.line_copy(z, True).wait_recv()
            self.add(self.line_view(z), self.line_staged(0, z))

        @pl.when((z <= here) & (here < self.place.z_size - 1))
        def _():
            self.line_copy(z, False).wait_recv()
            self.add(self.line_view(z), self.line_staged(1, z))

    def line_send(self, z):
        here = self.place.z

        @pl.when(z > here)
        def _():
            self.line_copy(z, True).start()

        @pl.when(z < here)
        def _():
            self.line_copy(z, False).start()

    def last_send(self):
        if not self.piece.zfirst:
            self.near_copy(self.place.z).start()

    def finish(self):
        z = self.place.z
        value = self.part(self.total, self.near, self.far, z)[...]
        if not self.piece.zfirst:
            self.near_copy(z).wait_recv()
            value = value + self.staged(self.nears, 0)[...]
        self.piece.own(self.out)[...] = value

    def drain(self):
        place = self.place
        for z in range(place.z_size):
            self.core_copy(z).wait_send()
            self.far_copy(z).wait_send()
            if self.piece.zfirst:
                self.near_copy(z).wait_send()

            @pl.when(z > place.z)
            def _():
                self.line_copy(z, True).wait_send()

            @pl.when(z < place.z)
            def _():
                self.line_copy(z, False).wait_send()

        if not self.piece.zfirst:
            self.near_copy(place.z).wait_send()


def scatter_stages(scatter):
    stages = [(scatter.core_step, scatter.core_send)]
    if scatter.piece.zfirst:
        return stages + [(scatter.far_step, scatter.far_send), (scatter.near_step, None), (scatter.line_step, scatter.line_send)]
    return stages + [(scatter.far_step, None), (scatter.line_step, scatter.line_send)]


def run_scatters(place, scatters, offsets, lag):
    blocks = 2 * place.z_size - 1
    for scatter in scatters:
        scatter.begin()
    staged = []
    for scatter, offset in zip(scatters, offsets):
        behind = offset
        for index, (work, send) in enumerate(scatter_stages(scatter)):
            staged.append((behind, work, send))
            behind += 0 if send is None else lag
    staged.sort(key=lambda stage: -stage[0])
    steps = max(stage[0] for stage in staged) + blocks

    def body(step, carry):
        for action in (1, 2):
            for stage in staged:
                if stage[action] is None:
                    continue
                item = step - stage[0]
                distance = place.z_size - 1 - item // 2
                z = place.z + jnp.where(lax.rem(item, 2) == 0, -distance, distance)

                @pl.when((item >= 0) & (item < blocks) & (z >= 0) & (z < place.z_size))
                def _():
                    stage[action](z)

        return carry

    lax.fori_loop(0, steps, body, 0)
    for scatter in scatters:
        scatter.last_send()
    for scatter in scatters:
        scatter.finish()
    for scatter in scatters:
        scatter.drain()


def scatter_scratch(piece, columns, place_sizes, lead):
    y, x, z = chip_grid(place_sizes[0] * place_sizes[1])
    rows = piece.rows.size
    head = () if piece.lead is None else (lead,)
    return [
        pltpu.VMEM(head + (y, x, z, rows, columns), f32),
        pltpu.VMEM(head + (y, x, z, rows, columns), f32),
        pltpu.VMEM(head + (2, z, rows, columns), f32),
        pltpu.VMEM(head + ((z,) if piece.zfirst else (1,)) + (rows, columns), f32),
        pltpu.VMEM(head + ((2, z) if piece.zfirst else (2, 2, z)) + (rows, columns), f32),
    ]


def scatter_kernel(sizes, plans, starts, lag, total_norm, *refs):
    arrays = sum(len(plan) for plan in plans)
    pieces = sum(len(p) for plan in plans for p in plan)
    fulls, refs = refs[:arrays], refs[arrays:]
    outs, refs = refs[:arrays], refs[arrays:]
    if total_norm:
        norms, refs = refs[0], refs[1:]
    scratch, refs = refs[: 5 * pieces], refs[5 * pieces :]
    send, recv, local = refs[:3]
    place = Place(sizes)
    if total_norm:
        greet_all(place, sizes)
    else:
        place.greet()
    scatters, offsets = [], []
    array = count = 0
    for plan, start in zip(plans, starts):
        for group in plan:
            for piece in group:
                scatters.append(
                    Scatter(place, piece, fulls[array], outs[array], *scratch[5 * count : 5 * count + 5], send.at[count], recv.at[count], local.at[count])
                )
                offsets.append(start)
                count += 1
            array += 1
    run_scatters(place, scatters, offsets, lag)
    if total_norm:
        share_norm(place, sizes, outs, norms, *refs[3:])


def greet_all(place, sizes):
    devices = sizes[0] * sizes[1]
    barrier = pltpu.get_barrier_semaphore()

    def signal(offset, carry):
        other = lax.rem(place.index + offset, devices)
        pl.semaphore_signal(barrier, inc=1, device_id=(other // sizes[1], lax.rem(other, sizes[1])), device_id_type=MESH_ID)
        return carry

    lax.fori_loop(1, devices, signal, 0)
    pl.semaphore_wait(barrier, devices - 1)


def square_tile(values):
    squares = values * values
    tile = jnp.zeros((8, 128), f32)
    for r in range(0, values.shape[0], 8):
        for c in range(0, values.shape[1], 128):
            tile = tile + squares[r : r + 8, c : c + 128]
    return tile


def share_norm(place, sizes, outs, norms, own, send, recv):
    devices = sizes[0] * sizes[1]
    tile = jnp.zeros((8, 128), f32)
    for out in outs:
        for lead in range(out.shape[0]) if len(out.shape) == 3 else (None,):
            tile = tile + square_tile(out[...] if lead is None else out[lead])
    own[...] = tile
    norms[place.index] = tile

    def copy(offset, to):
        other = lax.rem(place.index + offset, devices)
        slot = place.index if to else other
        return pltpu.make_async_remote_copy(
            src_ref=own,
            dst_ref=norms.at[slot],
            send_sem=send.at[other],
            recv_sem=recv.at[slot],
            device_id=(other // sizes[1], lax.rem(other, sizes[1])),
            device_id_type=MESH_ID,
        )

    lax.fori_loop(1, devices, lambda offset, carry: (copy(offset, True).start(), carry)[1], 0)
    lax.fori_loop(1, devices, lambda offset, carry: (copy(offset, False).wait_recv(), carry)[1], 0)
    lax.fori_loop(1, devices, lambda offset, carry: (copy(offset, True).wait_send(), carry)[1], 0)


def shard_shape(full):
    return full.shape[:-6] + full.shape[-2:]


def scatter(fulls, plans, starts, lag, sizes, number, name, total_norm):
    devices = sizes[0] * sizes[1]
    pieces = sum(len(p) for plan in plans for p in plan)
    z_size = chip_grid(devices)[2]
    scratch = []
    array = 0
    for plan in plans:
        for group in plan:
            for piece in group:
                lead = None if piece.lead is None else piece.lead.size
                scratch += scatter_scratch(piece, fulls[array].shape[-1], sizes, lead)
            array += 1
    vmem = pl.BlockSpec(memory_space=pltpu.VMEM)
    shapes = [jax.ShapeDtypeStruct(shard_shape(full), f32) for full in fulls]
    sems = [
        pltpu.SemaphoreType.DMA((pieces, 5, z_size)),
        pltpu.SemaphoreType.DMA((pieces, 5, z_size)),
        pltpu.SemaphoreType.DMA((pieces, z_size)),
    ]
    if total_norm:
        shapes.append(jax.ShapeDtypeStruct((devices, 8, 128), f32))
        sems += [pltpu.VMEM((8, 128), f32), pltpu.SemaphoreType.DMA((devices,)), pltpu.SemaphoreType.DMA((devices,))]
    return pl.pallas_call(
        functools.partial(scatter_kernel, sizes, plans, starts, lag, total_norm),
        in_specs=[pl.BlockSpec(memory_space=pl.ANY)] * len(fulls),
        out_specs=[vmem] * len(shapes),
        out_shape=shapes,
        scratch_shapes=scratch + sems,
        compiler_params=pltpu.CompilerParams(collective_id=number, has_side_effects=True, vmem_limit_bytes=VMEM_LIMIT),
        name=name,
    )(*fulls)


def adamw_kernel(step_ref, norms_ref, *refs):
    (g_in1, g_in2, g_out1, g_out2, g_sq, g_conv, g_small), refs = refs[:7], refs[7:]
    weights, firsts, seconds, outs = refs[0:5], refs[5:10], refs[10:15], refs[16:]
    norm = jnp.sqrt(jnp.sum(norms_ref[...], axis=(0, 1, 2), keepdims=True)[0])
    refs[15][...] = norm
    clip = jnp.minimum(1.0, CLIP_NORM / (norm + 1e-06))

    def geometric(_, carry):
        one, one_power, two, two_power = carry
        return one + one_power, one_power * BETA_ONE, two + two_power, two_power * BETA_TWO

    zero, unit = jnp.float32(0.0), jnp.float32(1.0)
    one, _, two, _ = lax.fori_loop(0, step_ref[0], geometric, (zero, unit, zero, unit))
    first_scale = jnp.full((1, 1), (1.0 - BETA_ONE) * one, f32)
    second_scale = jnp.full((1, 1), (1.0 - BETA_TWO) * two, f32)
    first_scale = 1.0 / first_scale
    second_scale = 1.0 / second_scale

    def update(number, index, gradient, rate, decay):
        weight, first, second = weights[number][index], firsts[number][index], seconds[number][index]
        clipped = clip * gradient
        first_next = BETA_ONE * first + (1.0 - BETA_ONE) * clipped
        second_next = BETA_TWO * second + (1.0 - BETA_TWO) * clipped * clipped
        step = (first_next * first_scale) / (jnp.sqrt(second_next * second_scale) + ADAM_EPS)
        if decay:
            step = step + decay * weight
        outs[3 * number][index] = first_next
        outs[3 * number + 1][index] = second_next
        outs[3 * number + 2][index] = weight - rate * step

    for half, (g_in, g_out) in enumerate(((g_in1, g_out1), (g_in2, g_out2))):
        update(0, half, g_in[...], MATRIX_RATE, MATRIX_DECAY)
        update(1, half, g_out[...], MATRIX_RATE, MATRIX_DECAY)
    for index in range(6):
        update(2, index, g_sq[index], MATRIX_RATE, MATRIX_DECAY)
    update(3, EVERY, g_conv[...], MATRIX_RATE, MATRIX_DECAY)
    update(4, EVERY, g_small[...], VECTOR_RATE, 0.0)


def adamw(step, norms, grads, weights, firsts, seconds):
    vmem = pl.BlockSpec(memory_space=pltpu.VMEM)
    shapes = [jax.ShapeDtypeStruct((1, 1), f32)]
    for weight in weights:
        shapes += [jax.ShapeDtypeStruct(weight.shape, f32)] * 3
    return pl.pallas_call(
        adamw_kernel,
        in_specs=[pl.BlockSpec(memory_space=pltpu.SMEM)] + [vmem] * 23,
        out_specs=[vmem] * 16,
        out_shape=shapes,
        compiler_params=pltpu.CompilerParams(vmem_limit_bytes=VMEM_LIMIT),
        name="adamw",
    )(step, norms, *grads, *weights, *firsts, *seconds)


AXES = ("dp", "fsdp")


def scatter_gradients(sizes, grads):
    (in1, in2), (out1, out2), (dw, dw5), dproj, ds = grads
    grid = chip_grid(sizes[0] * sizes[1]) + (2,)
    feed = [halves(16, False), halves(64, True)]
    first, middle, last = [[Piece(None, 0, 16, False, "x")]] + feed, plans()[1], feed
    ds = jnp.pad(ds, ((0, SMALL_LANES - ds.shape[0]), (0, 0))).T

    def split_rows(full):
        rows = full.shape[-2] // (sizes[0] * sizes[1])
        return full.reshape(full.shape[:-2] + grid + (rows, full.shape[-1]))

    fulls = [split_rows(v) for v in (in2, out2, jnp.concatenate([dw, dw5[None]]), dproj, ds, in1, out1)]
    g_in2, g_out2, g_sq, g_conv, g_s, g_in1, g_out1, norms = scatter(
        fulls, [last, middle, first], (0, 4, 8), 2, sizes, 1, "scatter_gradients", True
    )
    return (g_in1, g_in2, g_out1, g_out2, g_sq, g_conv, g_s), norms


def gather_plain(feed_in, feed_out, square, proj, small):
    feed_in = lax.all_gather(feed_in, AXES, axis=1, tiled=True)
    feed_out = lax.all_gather(feed_out, AXES, axis=1, tiled=True)
    square = lax.all_gather(square, AXES, axis=1, tiled=True)
    proj = lax.all_gather(proj, AXES, axis=0, tiled=True)
    small = lax.all_gather(small, AXES, axis=1, tiled=True)
    return feed_in, feed_out, square, proj, small


def scatter_plain(grads):
    (in1, in2), (out1, out2), (dw, dw5), dproj, ds = grads
    parts = [lax.psum_scatter(v, AXES, scatter_dimension=0, tiled=True) for v in (in1, in2, out1, out2)]
    parts.append(lax.psum_scatter(jnp.concatenate([dw, dw5[None]]), AXES, scatter_dimension=1, tiled=True))
    parts.append(lax.psum_scatter(dproj, AXES, scatter_dimension=0, tiled=True))
    parts.append(lax.psum_scatter(ds, AXES, scatter_dimension=1, tiled=True))
    total = lax.psum(sum(jnp.sum(part * part) for part in parts), AXES)
    return tuple(parts), jnp.zeros((1, 8, 128), f32).at[0, 0, 0].set(total)


def overlapped_layer(sizes, inputs, cotangent, segments, valid_mask, weights):
    packs, length, _ = inputs.shape
    frames = packs * length
    x = inputs.reshape(frames, D)
    saved, full = forward(sizes, x, segments, valid_mask, weights)
    a1, u1, qkv, rel, probs, ctx, a2, u, mixed, a3, s, match = saved
    feed_in, feed_out, square, proj = (
        full[0].reshape(2, D, FF),
        full[1].reshape(2, FF, D),
        full[2].reshape(6, D, D),
        full[3].reshape(D, 2 * D),
    )
    pe = jnp.asarray(sinusoid_table(length))
    out, da3, dwin2, dwout2, ds2 = ffn2(a3, cotangent.reshape(frames, D), feed_in[1], feed_out[1], s)
    da2, dproj, dw5, dsc = convolution_backward(da3, a2, u, mixed, proj, square[5], s, match)
    da1, dw, dsa = attention_backward(length, da2, a1, qkv, rel, probs, ctx, square, pe, s)
    dx, dwin1, dwout1, ds1 = ffn1_backward(da1, x, u1, feed_in[0], feed_out[0], s)
    grads = (dwin1, dwin2), (dwout1, dwout2), (dw, dw5), dproj, small_rows((ds1, dsa, dsc, ds2))
    return out.reshape(inputs.shape), dx.reshape(inputs.shape), grads


def local(sizes, inputs, cotangent, segments, valid_mask, step_count, *state):
    weights, moments = state[:5], state[5:]
    firsts, seconds = moments[0::2], moments[1::2]
    devices = sizes[0] * sizes[1]
    kernels = D // devices % 16 == 0 and chip_grid(devices)[:2] == (2, 2)
    if kernels:
        out, dx, grads = overlapped_layer(sizes, inputs, cotangent, segments, valid_mask, weights)
    else:
        out, dx, grads = layer(inputs, cotangent, segments, valid_mask, gather_plain(*weights))
    if kernels:
        grads, norms = scatter_gradients(sizes, grads)
        grads = grads[:6] + (grads[6].T[: weights[4].shape[0]],)
    else:
        grads, norms = scatter_plain(grads)
    norm, *updated = adamw(step_count, norms, grads, weights, firsts, seconds)
    return (out, dx, norm.reshape(()), *updated)


def solution(mesh):
    sizes = (mesh.shape["dp"], mesh.shape["fsdp"])
    batch = P(AXES, None, None)
    rows = P(AXES, None)
    middle = P(None, AXES, None)
    columns = P(None, AXES)
    weights = (middle, middle, middle, rows, columns)
    moments = tuple(spec for spec in weights for _ in range(2))
    return jax.shard_map(
        functools.partial(local, sizes),
        mesh=mesh,
        in_specs=(batch, batch, rows, rows, P()) + weights + moments,
        out_specs=(batch, batch, P()) + tuple(spec for spec in weights for _ in range(3)),
        check_vma=False,
    )
```

```python
import functools
import math

import jax
import jax.numpy as jnp
import numpy as np
from jax import lax
from jax.experimental import pallas as pl
from jax.experimental.pallas import tpu as pltpu
from jax.sharding import PartitionSpec as P

D = 512
H = 8
DH = 64
FF = 2048
K = 9
NC = FF // D
TAP = 23 + 2 * NC
NORM_EPS = 1e-05
BETA_ONE = 0.9
BETA_TWO = 0.999
ADAM_EPS = 1e-08
CLIP_NORM = 1.0
MATRIX_RATE = 0.03
VECTOR_RATE = 0.4
MATRIX_DECAY = 0.01
VMEM_LIMIT = 60 * 2**20
VMEM_TOP = 67043328

f32 = jnp.float32
bf16 = jnp.bfloat16
NN = (((1,), (0,)), ((), ()))
NT = (((1,), (1,)), ((), ()))
TN = (((0,), (0,)), ((), ()))


def split(value):
    high = value.astype(bf16)
    return high, (value - high.astype(f32)).astype(bf16)


def dot(left, right, dims):
    return lax.dot_general(left, right, dims, preferred_element_type=f32)


def dot3(left, right, dims):
    return dot(left[0], right[0], dims) + (dot(left[0], right[1], dims) + dot(left[1], right[0], dims))


def normalize(values):
    centred = values - jnp.mean(values, axis=-1, keepdims=True)
    inverse = lax.rsqrt(jnp.mean(centred * centred, axis=-1, keepdims=True) + NORM_EPS)
    return centred * inverse, inverse


def normalize_back(scaled, xhat, inverse):
    return (scaled - jnp.mean(scaled, axis=-1, keepdims=True) - xhat * jnp.mean(scaled * xhat, axis=-1, keepdims=True)) * inverse


def column_sum(values):
    return jnp.sum(values, axis=0, keepdims=True)


def row(rows_ref, index):
    return rows_ref[pl.ds(index, 1), :]


def store_split(pair_ref, value):
    high, low = split(value)
    pair_ref[0] = high
    pair_ref[1] = low


def load_split(pair_ref, *index):
    if index:
        return pair_ref[(0,) + index], pair_ref[(1,) + index]
    return pair_ref[0], pair_ref[1]


def ffn_forward_chunk(normed, u_ref, win, wout, bias):
    u = dot3(normed, split(win), NN) + bias
    u_ref[...] = u
    return dot3(split(u * jax.nn.sigmoid(u)), split(wout), NN)


def ffn_backward_chunk(normed, u, df, win, wout):
    sig = jax.nn.sigmoid(u)
    dwout = dot3(split(u * sig), df, TN)
    du = dot3(df, split(wout), NT) * (sig * (1.0 + u * (1.0 - sig)))
    du_split = split(du)
    dwin = dot3(normed, du_split, TN)
    return dwin, dwout, column_sum(du), dot3(du_split, split(win), NT)


def ffn1_forward_kernel(x_ref, win_ref, wout_ref, s_ref, a1_ref, u_ref, normed):
    chunk = pl.program_id(0)

    @pl.when(chunk == 0)
    def _():
        xhat, _ = normalize(x_ref[...])
        store_split(normed, xhat * s_ref[0:1] + s_ref[1:2])
        a1_ref[...] = x_ref[...] + 0.5 * s_ref[17:18]

    out = ffn_forward_chunk(load_split(normed), u_ref, win_ref[...], wout_ref[...], row(s_ref, 23 + chunk))
    a1_ref[...] += 0.5 * out


def ffn1_forward(x, win, wout, s):
    frames = x.shape[0]
    whole = pl.BlockSpec((frames, D), lambda c: (0, 0))
    return pl.pallas_call(
        ffn1_forward_kernel,
        grid=(NC,),
        in_specs=[
            whole,
            pl.BlockSpec((D, D), lambda c: (0, c)),
            pl.BlockSpec((D, D), lambda c: (c, 0)),
            pl.BlockSpec(s.shape, lambda c: (0, 0)),
        ],
        out_specs=[whole, pl.BlockSpec((frames, D), lambda c: (0, c))],
        out_shape=[jax.ShapeDtypeStruct((frames, D), f32), jax.ShapeDtypeStruct((frames, FF), f32)],
        scratch_shapes=[pltpu.VMEM((2, frames, D), bf16)],
        compiler_params=pltpu.CompilerParams(vmem_limit_bytes=VMEM_LIMIT),
        name="ffn1_forward",
    )(x, win, wout, s)


def ffn1_backward_kernel(da_ref, x_ref, u_ref, win_ref, wout_ref, s_ref, dx_ref, dwin_ref, dwout_ref, ds_ref, normed, df):
    chunk = pl.program_id(0)

    @pl.when(chunk == 0)
    def _():
        xhat, _ = normalize(x_ref[...])
        store_split(normed, xhat * s_ref[0:1] + s_ref[1:2])
        half = 0.5 * da_ref[...]
        store_split(df, half)
        ds_ref[...] = jnp.zeros_like(ds_ref)
        ds_ref[2:3] = column_sum(half)
        dx_ref[...] = jnp.zeros_like(dx_ref)

    dwin, dwout, dbias, dnormed = ffn_backward_chunk(load_split(normed), u_ref[...], load_split(df), win_ref[...], wout_ref[...])
    dwin_ref[...] = dwin
    dwout_ref[...] = dwout
    ds_ref[pl.ds(4 + chunk, 1), :] = dbias
    dx_ref[...] += dnormed

    @pl.when(chunk == NC - 1)
    def _():
        xhat, inverse = normalize(x_ref[...])
        dn = dx_ref[...]
        ds_ref[0:1] = column_sum(dn * xhat)
        ds_ref[1:2] = column_sum(dn)
        dx_ref[...] = da_ref[...] + normalize_back(dn * s_ref[0:1], xhat, inverse)


def ffn1_backward(da, x, u, win, wout, s):
    frames = x.shape[0]
    whole = pl.BlockSpec((frames, D), lambda c: (0, 0))
    across = pl.BlockSpec((D, D), lambda c: (0, c))
    down = pl.BlockSpec((D, D), lambda c: (c, 0))
    return pl.pallas_call(
        ffn1_backward_kernel,
        grid=(NC,),
        in_specs=[whole, whole, pl.BlockSpec((frames, D), lambda c: (0, c)), across, down, pl.BlockSpec(s.shape, lambda c: (0, 0))],
        out_specs=[whole, across, down, pl.BlockSpec((8, D), lambda c: (0, 0))],
        out_shape=[
            jax.ShapeDtypeStruct((frames, D), f32),
            jax.ShapeDtypeStruct((D, FF), f32),
            jax.ShapeDtypeStruct((FF, D), f32),
            jax.ShapeDtypeStruct((8, D), f32),
        ],
        scratch_shapes=[pltpu.VMEM((2, frames, D), bf16), pltpu.VMEM((2, frames, D), bf16)],
        compiler_params=pltpu.CompilerParams(vmem_limit_bytes=VMEM_LIMIT),
        name="ffn1_backward",
    )(da, x, u, win, wout, s)


def ffn2_kernel(a3_ref, cot_ref, win_ref, wout_ref, s_ref, out_ref, da3_ref, dwin_ref, dwout_ref, ds_ref, normed, df, hidden, da4):
    step = pl.program_id(0)

    @pl.when(step == 0)
    def _():
        xhat, _ = normalize(a3_ref[...])
        store_split(normed, xhat * s_ref[8:9] + s_ref[9:10])
        da4[...] = a3_ref[...] + 0.5 * s_ref[18:19]

    @pl.when(step < NC)
    def _():
        out = ffn_forward_chunk(load_split(normed), hidden.at[step], win_ref[...], wout_ref[...], row(s_ref, 23 + NC + step))
        da4[...] += 0.5 * out

    @pl.when(step == NC - 1)
    def _():
        xhat, inverse = normalize(da4[...])
        out_ref[...] = xhat * s_ref[10:11] + s_ref[11:12]
        cot = cot_ref[...]
        ds_ref[...] = jnp.zeros_like(ds_ref)
        ds_ref[8:9] = column_sum(cot * xhat)
        ds_ref[9:10] = column_sum(cot)
        grad = normalize_back(cot * s_ref[10:11], xhat, inverse)
        da4[...] = grad
        half = 0.5 * grad
        store_split(df, half)
        ds_ref[2:3] = column_sum(half)
        da3_ref[...] = jnp.zeros_like(da3_ref)

    @pl.when(step >= NC)
    def _():
        dwin, dwout, dbias, dnormed = ffn_backward_chunk(load_split(normed), hidden[step - NC], load_split(df), win_ref[...], wout_ref[...])
        dwin_ref[...] = dwin
        dwout_ref[...] = dwout
        ds_ref[pl.ds(4 + step - NC, 1), :] = dbias
        da3_ref[...] += dnormed

    @pl.when(step == 2 * NC - 1)
    def _():
        xhat, inverse = normalize(a3_ref[...])
        dn = da3_ref[...]
        ds_ref[0:1] = column_sum(dn * xhat)
        ds_ref[1:2] = column_sum(dn)
        da3_ref[...] = da4[...] + normalize_back(dn * s_ref[8:9], xhat, inverse)


def ffn2(a3, cot, win, wout, s):
    frames = a3.shape[0]
    whole = pl.BlockSpec((frames, D), lambda c: (0, 0))
    return pl.pallas_call(
        ffn2_kernel,
        grid=(2 * NC,),
        in_specs=[
            whole,
            whole,
            pl.BlockSpec((D, D), lambda c: (0, lax.rem(c, NC))),
            pl.BlockSpec((D, D), lambda c: (lax.rem(c, NC), 0)),
            pl.BlockSpec(s.shape, lambda c: (0, 0)),
        ],
        out_specs=[
            whole,
            whole,
            pl.BlockSpec((D, D), lambda c: (0, jnp.maximum(c - NC, 0))),
            pl.BlockSpec((D, D), lambda c: (jnp.maximum(c - NC, 0), 0)),
            pl.BlockSpec((16, D), lambda c: (0, 0)),
        ],
        out_shape=[
            jax.ShapeDtypeStruct((frames, D), f32),
            jax.ShapeDtypeStruct((frames, D), f32),
            jax.ShapeDtypeStruct((D, FF), f32),
            jax.ShapeDtypeStruct((FF, D), f32),
            jax.ShapeDtypeStruct((16, D), f32),
        ],
        scratch_shapes=[
            pltpu.VMEM((2, frames, D), bf16),
            pltpu.VMEM((2, frames, D), bf16),
            pltpu.VMEM((NC, frames, D), f32),
            pltpu.VMEM((frames, D), f32),
        ],
        compiler_params=pltpu.CompilerParams(vmem_limit_bytes=VMEM_LIMIT),
        name="ffn2",
    )(a3, cot, win, wout, s)


def sinusoid_table(length):
    offsets = length // 2 - np.arange(length, dtype=np.float64)
    frequency = 10000.0 ** (-2.0 * np.arange(D // 2, dtype=np.float64) / D)
    angles = offsets[:, None] * frequency[None, :]
    table = np.concatenate([np.sin(angles), np.cos(angles)], axis=1).astype(np.float32)
    return np.stack([table, table[::-1]])


def shift_rows(scores):
    return pltpu.roll(scores, scores.shape[1] // 2, 1, stride=1, stride_axis=0)


def pair_masks():
    lane = lax.broadcasted_iota(jnp.int32, (1, 2 * DH), 1)
    first = (lane < DH).astype(f32)
    return first, 1.0 - first


def attention_forward_kernel(length, a1_ref, w_ref, pe_ref, s_ref, segcol_ref, keyrow_ref, a2_ref, qkv_ref, rel_ref, probs_ref, ctx_ref, bias):
    packs = a1_ref.shape[0] // length
    xhat, _ = normalize(a1_ref[...])
    normed = split(xhat * s_ref[2:3] + s_ref[3:4])
    qkv_ref[0] = dot3(normed, split(w_ref[0]), NN) + s_ref[12:13]
    qkv_ref[1] = dot3(normed, split(w_ref[1]), NN)
    qkv_ref[2] = dot3(normed, split(w_ref[2]), NN) + s_ref[13:14]
    rel_ref[...] = dot3(split(pe_ref[0]), split(w_ref[4]), NN)
    query = lax.broadcasted_iota(jnp.int32, (length, length), 0)
    key = lax.broadcasted_iota(jnp.int32, (length, length), 1)
    for pack in range(packs):
        same = segcol_ref[pl.ds(pack * length, length), 0:1] == keyrow_ref[pack : pack + 1, 0:length]
        bias[pack] = jnp.where(same | (query == key), 0.0, -1e30)
    first, second = pair_masks()

    def heads(item, carry):
        pack, pair = item // (H // 2), item % (H // 2)
        frames = pl.ds(pl.multiple_of(pack * length, length), length)
        lanes = pl.ds(pl.multiple_of(pair * 2 * DH, 2 * DH), 2 * DH)
        q = qkv_ref[0, frames, lanes]
        content = q + s_ref[15:16, lanes]
        position = q + s_ref[16:17, lanes]
        k = split(qkv_ref[1, frames, lanes])
        v = split(qkv_ref[2, frames, lanes])
        rel = split(rel_ref[:, lanes])
        total = jnp.zeros_like(q)
        for index, mask in enumerate((first, second)):
            scores = dot3(split(content * mask), k, NT) + shift_rows(dot3(split(position * mask), rel, NT))
            scores = scores * (1.0 / math.sqrt(DH)) + bias[pack]
            weights = jnp.exp(scores - jnp.max(scores, axis=-1, keepdims=True))
            weights = weights / jnp.sum(weights, axis=-1, keepdims=True)
            probs_ref[item * 2 + index] = weights
            total = total + dot3(split(weights), v, NN) * mask
        ctx_ref[frames, lanes] = total
        return carry

    lax.fori_loop(0, packs * (H // 2), heads, 0)
    a2_ref[...] = a1_ref[...] + dot3(split(ctx_ref[...]), split(w_ref[3]), NN) + s_ref[14:15]


def attention_forward(length, a1, square, pe, s, segcol, keyrow):
    frames = a1.shape[0]
    packs = frames // length
    vmem = pl.BlockSpec(memory_space=pltpu.VMEM)
    return pl.pallas_call(
        functools.partial(attention_forward_kernel, length),
        in_specs=[vmem] * 6,
        out_specs=[vmem] * 5,
        out_shape=[
            jax.ShapeDtypeStruct((frames, D), f32),
            jax.ShapeDtypeStruct((3, frames, D), f32),
            jax.ShapeDtypeStruct((length, D), f32),
            jax.ShapeDtypeStruct((packs * H, length, length), f32),
            jax.ShapeDtypeStruct((frames, D), f32),
        ],
        scratch_shapes=[pltpu.VMEM((packs, length, length), f32)],
        compiler_params=pltpu.CompilerParams(vmem_limit_bytes=VMEM_LIMIT),
        name="attention_forward",
    )(a1, square, pe, s, segcol, keyrow)


def attention_backward_kernel(
    length, da2_ref, a1_ref, qkv_ref, rel_ref, probs_ref, ctx_ref, w_ref, pe_ref, s_ref, da1_ref, dw_ref, ds_ref, dctx, dqkv, drel, relback, du, dv
):
    packs = a1_ref.shape[0] // length
    row_index = lax.broadcasted_iota(jnp.int32, (length, length), 0)
    lane_index = lax.broadcasted_iota(jnp.int32, (length, length), 1)
    flip = (row_index + lane_index == length - 1).astype(bf16)
    da2 = da2_ref[...]
    da2_split = split(da2)
    ds_ref[...] = jnp.zeros_like(ds_ref)
    ds_ref[2:3] = column_sum(da2)
    dw_ref[3] = dot3(split(ctx_ref[...]), da2_split, TN)
    dctx[...] = dot3(da2_split, split(w_ref[3]), NT)
    rel_split = split(rel_ref[...])
    relback[...] = dot(flip, rel_split[0], NN) + dot(flip, rel_split[1], NN)
    drel[...] = jnp.zeros_like(drel)
    du[...] = jnp.zeros_like(du)
    dv[...] = jnp.zeros_like(dv)
    first, second = pair_masks()

    def heads(item, carry):
        pack, pair = item // (H // 2), item % (H // 2)
        frames = pl.ds(pl.multiple_of(pack * length, length), length)
        lanes = pl.ds(pl.multiple_of(pair * 2 * DH, 2 * DH), 2 * DH)
        q = qkv_ref[0, frames, lanes]
        content = q + s_ref[15:16, lanes]
        position = q + s_ref[16:17, lanes]
        k = qkv_ref[1, frames, lanes]
        v = split(qkv_ref[2, frames, lanes])
        rel = relback[:, lanes]
        dc = dctx[frames, lanes]
        dcontent = jnp.zeros_like(q)
        dposition = jnp.zeros_like(q)
        dkey = jnp.zeros_like(q)
        dvalue = jnp.zeros_like(q)
        drelation = jnp.zeros_like(rel)
        for index, mask in enumerate((first, second)):
            weights = probs_ref[item * 2 + index]
            dc_split = split(dc * mask)
            dvalue = dvalue + dot3(split(weights), dc_split, TN)
            dweights = dot3(dc_split, v, NT)
            dscores = weights * (dweights - jnp.sum(weights * dweights, axis=-1, keepdims=True)) * (1.0 / math.sqrt(DH))
            ds_split = split(dscores)
            dcontent = dcontent + dot3(ds_split, split(k * mask), NN)
            dkey = dkey + dot3(ds_split, split(content * mask), TN)
            shifted = split(shift_rows(dot(ds_split[0], flip, NN) + dot(ds_split[1], flip, NN)))
            dposition = dposition + dot3(shifted, split(rel * mask), NN)
            drelation = drelation + dot3(shifted, split(position * mask), TN)
        dqkv[0, frames, lanes] = dcontent + dposition
        dqkv[1, frames, lanes] = dkey
        dqkv[2, frames, lanes] = dvalue
        drel[:, lanes] += drelation
        du[0:1, lanes] += column_sum(dcontent)
        dv[0:1, lanes] += column_sum(dposition)
        return carry

    lax.fori_loop(0, packs * (H // 2), heads, 0)
    ds_ref[3:4] = du[0:1]
    ds_ref[4:5] = dv[0:1]
    ds_ref[5:6] = column_sum(dqkv[0])
    ds_ref[6:7] = column_sum(dqkv[2])
    xhat, inverse = normalize(a1_ref[...])
    normed = split(xhat * s_ref[2:3] + s_ref[3:4])
    dnormed = jnp.zeros_like(xhat)
    for index in range(3):
        grad = split(dqkv[index])
        dw_ref[index] = dot3(normed, grad, TN)
        dnormed = dnormed + dot3(grad, split(w_ref[index]), NT)
    dw_ref[4] = dot3(split(pe_ref[1]), split(drel[...]), TN)
    ds_ref[0:1] = column_sum(dnormed * xhat)
    ds_ref[1:2] = column_sum(dnormed)
    da1_ref[...] = da2_ref[...] + normalize_back(dnormed * s_ref[2:3], xhat, inverse)


def attention_backward(length, da2, a1, qkv, rel, probs, ctx, square, pe, s):
    frames = a1.shape[0]
    vmem = pl.BlockSpec(memory_space=pltpu.VMEM)
    return pl.pallas_call(
        functools.partial(attention_backward_kernel, length),
        in_specs=[vmem] * 9,
        out_specs=[vmem] * 3,
        out_shape=[
            jax.ShapeDtypeStruct((frames, D), f32),
            jax.ShapeDtypeStruct((5, D, D), f32),
            jax.ShapeDtypeStruct((8, D), f32),
        ],
        scratch_shapes=[
            pltpu.VMEM((frames, D), f32),
            pltpu.VMEM((3, frames, D), f32),
            pltpu.VMEM((length, D), f32),
            pltpu.VMEM((length, D), f32),
            pltpu.VMEM((8, D), f32),
            pltpu.VMEM((8, D), f32),
        ],
        compiler_params=pltpu.CompilerParams(vmem_limit_bytes=VMEM_LIMIT),
        name="attention_backward",
    )(da2, a1, qkv, rel, probs, ctx, square, pe, s)


EDGE = 8
HALF = (K - 1) // 2
STRIP = 64


def convolution_forward_kernel(a2_ref, proj_ref, w_ref, s_ref, match_ref, a3_ref, u_ref, mixed_ref, padded):
    frames = a2_ref.shape[0]
    xhat, _ = normalize(a2_ref[...])
    normed = split(xhat * s_ref[4:5] + s_ref[5:6])
    u_ref[:, :D] = dot3(normed, split(proj_ref[:, :D]), NN) + s_ref[19:20]
    u_ref[:, D:] = dot3(normed, split(proj_ref[:, D:]), NN) + s_ref[20:21]
    padded[0:EDGE] = jnp.zeros((EDGE, D), f32)
    padded[EDGE + frames :] = jnp.zeros((EDGE, D), f32)
    padded[EDGE : EDGE + frames] = u_ref[:, :D] * jax.nn.sigmoid(u_ref[:, D:]) * match_ref[:, K : K + 1]
    for base in range(0, frames, STRIP):
        total = jnp.zeros((STRIP, D), f32) + s_ref[21:22]
        for tap in range(K):
            source = padded[base + EDGE + tap - HALF : base + EDGE + tap - HALF + STRIP]
            total = total + match_ref[base : base + STRIP, tap : tap + 1] * source * s_ref[TAP + tap : TAP + tap + 1]
        mixed_ref[base : base + STRIP] = total
    inner, _ = normalize(mixed_ref[...])
    inner = inner * s_ref[6:7] + s_ref[7:8]
    a3_ref[...] = a2_ref[...] + dot3(split(inner * jax.nn.sigmoid(inner)), split(w_ref[...]), NN) + s_ref[22:23]


def convolution_forward(a2, proj, weight, s, match):
    frames = a2.shape[0]
    vmem = pl.BlockSpec(memory_space=pltpu.VMEM)
    return pl.pallas_call(
        convolution_forward_kernel,
        in_specs=[vmem] * 5,
        out_specs=[vmem] * 3,
        out_shape=[
            jax.ShapeDtypeStruct((frames, D), f32),
            jax.ShapeDtypeStruct((frames, 2 * D), f32),
            jax.ShapeDtypeStruct((frames, D), f32),
        ],
        scratch_shapes=[pltpu.VMEM((frames + 2 * EDGE, D), f32)],
        compiler_params=pltpu.CompilerParams(vmem_limit_bytes=VMEM_LIMIT),
        name="convolution_forward",
    )(a2, proj, weight, s, match)


def convolution_backward_kernel(
    da3_ref, a2_ref, u_ref, mixed_ref, proj_ref, w_ref, s_ref, match_ref, da2_ref, dproj_ref, dw_ref, ds_ref, padded, dpadded, dgated
):
    frames = a2_ref.shape[0]
    da3 = da3_ref[...]
    da3_split = split(da3)
    ds_ref[...] = jnp.zeros_like(ds_ref)
    ds_ref[2:3] = column_sum(da3)
    hat, inverse = normalize(mixed_ref[...])
    inner = hat * s_ref[6:7] + s_ref[7:8]
    sig = jax.nn.sigmoid(inner)
    dw_ref[...] = dot3(split(inner * sig), da3_split, TN)
    dinner = dot3(da3_split, split(w_ref[...]), NT) * (sig * (1.0 + inner * (1.0 - sig)))
    ds_ref[3:4] = column_sum(dinner * hat)
    ds_ref[4:5] = column_sum(dinner)
    dmixed = normalize_back(dinner * s_ref[6:7], hat, inverse)
    ds_ref[5:6] = column_sum(dmixed)
    zeros = jnp.zeros((EDGE, D), f32)
    padded[0:EDGE] = zeros
    padded[EDGE + frames :] = zeros
    padded[EDGE : EDGE + frames] = u_ref[:, :D] * jax.nn.sigmoid(u_ref[:, D:]) * match_ref[:, K : K + 1]
    dpadded[0:EDGE] = zeros
    dpadded[EDGE + frames :] = zeros
    dpadded[EDGE : EDGE + frames] = dmixed
    for base in range(0, frames, STRIP):
        total = jnp.zeros((STRIP, D), f32)
        center = dpadded[base + EDGE : base + EDGE + STRIP]
        for tap in range(K):
            rows = slice(base + EDGE + tap - HALF, base + EDGE + tap - HALF + STRIP)
            match = match_ref[base : base + STRIP, tap : tap + 1]
            total = total + match * dpadded[rows] * s_ref[TAP + K - 1 - tap : TAP + K - tap]
            ds_ref[8 + tap : 9 + tap] += column_sum(center * (match * padded[rows]))
        dgated[base : base + STRIP] = total * match_ref[base : base + STRIP, K : K + 1]
    gate = jax.nn.sigmoid(u_ref[:, D:])
    dfirst = dgated[...] * gate
    dsecond = dfirst * u_ref[:, :D] * (1.0 - gate)
    ds_ref[6:7] = column_sum(dfirst)
    ds_ref[7:8] = column_sum(dsecond)
    xhat, inverse = normalize(a2_ref[...])
    normed = split(xhat * s_ref[4:5] + s_ref[5:6])
    dfirst = split(dfirst)
    dsecond = split(dsecond)
    dproj_ref[:, :D] = dot3(normed, dfirst, TN)
    dproj_ref[:, D:] = dot3(normed, dsecond, TN)
    dnormed = dot3(dfirst, split(proj_ref[:, :D]), NT) + dot3(dsecond, split(proj_ref[:, D:]), NT)
    ds_ref[0:1] = column_sum(dnormed * xhat)
    ds_ref[1:2] = column_sum(dnormed)
    da2_ref[...] = da3_ref[...] + normalize_back(dnormed * s_ref[4:5], xhat, inverse)


def convolution_backward(da3, a2, u, mixed, proj, weight, s, match):
    frames = a2.shape[0]
    vmem = pl.BlockSpec(memory_space=pltpu.VMEM)
    return pl.pallas_call(
        convolution_backward_kernel,
        in_specs=[vmem] * 8,
        out_specs=[vmem] * 4,
        out_shape=[
            jax.ShapeDtypeStruct((frames, D), f32),
            jax.ShapeDtypeStruct((D, 2 * D), f32),
            jax.ShapeDtypeStruct((D, D), f32),
            jax.ShapeDtypeStruct((24, D), f32),
        ],
        scratch_shapes=[
            pltpu.VMEM((frames + 2 * EDGE, D), f32),
            pltpu.VMEM((frames + 2 * EDGE, D), f32),
            pltpu.VMEM((frames, D), f32),
        ],
        compiler_params=pltpu.CompilerParams(vmem_limit_bytes=VMEM_LIMIT),
        name="convolution_backward",
    )(da3, a2, u, mixed, proj, weight, s, match)


def frame_tables(segments, valid_mask):
    packs, length = segments.shape
    position = jnp.arange(length, dtype=jnp.int32)
    columns = []
    for tap in range(K):
        moved = jnp.roll(segments, HALF - tap, axis=1)
        inside = (position + tap - HALF >= 0) & (position + tap - HALF < length)
        columns.append(((moved == segments) & inside[None, :]).astype(f32))
    columns.append(valid_mask.astype(f32))
    match = jnp.stack(columns, axis=-1).reshape(packs * length, K + 1)
    match = jnp.pad(match, ((0, 0), (0, 128 - K - 1)))
    segcol = jnp.broadcast_to(segments.reshape(packs * length, 1), (packs * length, 128))
    keyrow = jnp.pad(jnp.where(valid_mask > 0, segments, -1), ((0, -packs % 8), (0, 0)))
    return match, segcol, keyrow


def small_rows(parts):
    first, attend, conv, second = parts
    return jnp.concatenate(
        [
            first[0:2],
            attend[0:2],
            conv[0:2],
            conv[3:5],
            second[0:2],
            second[8:10],
            attend[5:7],
            attend[2:5],
            first[2:3],
            second[2:3],
            conv[6:8],
            conv[5:6],
            conv[2:3],
            first[4:8],
            second[4:8],
            conv[8 : 8 + K],
        ],
        axis=0,
    )


def layer(inputs, cotangent, segments, valid_mask, weights):
    feed_in, feed_out, square, proj, s = weights
    packs, length, _ = inputs.shape
    frames = packs * length
    x = inputs.reshape(frames, D)
    cot = cotangent.reshape(frames, D)
    match, segcol, keyrow = frame_tables(segments, valid_mask)
    pe = jnp.asarray(sinusoid_table(length))
    a1, u1 = ffn1_forward(x, feed_in[0], feed_out[0], s)
    a2, qkv, rel, probs, ctx = attention_forward(length, a1, square, pe, s, segcol, keyrow)
    a3, u, mixed = convolution_forward(a2, proj, square[5], s, match)
    out, da3, dwin2, dwout2, ds2 = ffn2(a3, cot, feed_in[1], feed_out[1], s)
    da2, dproj, dw5, dsc = convolution_backward(da3, a2, u, mixed, proj, square[5], s, match)
    da1, dw, dsa = attention_backward(length, da2, a1, qkv, rel, probs, ctx, square, pe, s)
    dx, dwin1, dwout1, ds1 = ffn1_backward(da1, x, u1, feed_in[0], feed_out[0], s)
    grads = (dwin1, dwin2), (dwout1, dwout2), (dw, dw5), dproj, small_rows((ds1, dsa, dsc, ds2))
    return out.reshape(inputs.shape), dx.reshape(inputs.shape), grads

MESH_ID = pl.DeviceIdType.MESH


def chip_grid(devices):
    side = 1
    while side * side * 2 * side * 2 < devices:
        side *= 2
    return side, side, 2 * side


class Place:
    def __init__(self, sizes):
        self.fsdp = sizes[1]
        self.y_size, self.x_size, self.z_size = chip_grid(sizes[0] * sizes[1])
        index = lax.axis_index("dp") * sizes[1] + lax.axis_index("fsdp")
        self.index = index
        self.core = lax.rem(index, 2)
        self.z = lax.rem(index // 2, self.z_size)
        self.x = lax.rem(index // (2 * self.z_size), 2)
        self.y = index // (4 * self.z_size)

    def device(self, y=None, x=None, z=None, core=None):
        y = self.y if y is None else y
        x = self.x if x is None else x
        z = self.z if z is None else z
        core = self.core if core is None else core
        index = ((y * 2 + x) * self.z_size + z) * 2 + core
        return index // self.fsdp, lax.rem(index, self.fsdp)

    def neighbour(self, axis):
        if axis == "core":
            return self.device(core=1 - self.core)
        if axis == "x":
            return self.device(x=1 - self.x)
        if axis == "y":
            return self.device(y=1 - self.y)
        return self.device(z=self.z + (1 if axis == "right" else -1))

    def greet(self):
        barrier = pltpu.get_barrier_semaphore()
        for axis in ("core", "x", "y"):
            pl.semaphore_signal(barrier, inc=1, device_id=self.neighbour(axis), device_id_type=MESH_ID)

        @pl.when(self.z > 0)
        def _():
            pl.semaphore_signal(barrier, inc=1, device_id=self.neighbour("left"), device_id_type=MESH_ID)

        @pl.when(self.z < self.z_size - 1)
        def _():
            pl.semaphore_signal(barrier, inc=1, device_id=self.neighbour("right"), device_id_type=MESH_ID)

        peers = 3 + (self.z > 0).astype(jnp.int32) + (self.z < self.z_size - 1).astype(jnp.int32)
        pl.semaphore_wait(barrier, peers)


EVERY = slice(None)


class Piece:
    def __init__(self, lead, first_row, rows, zfirst, near):
        self.lead, self.rows, self.zfirst, self.near = lead, pl.ds(first_row, rows), zfirst, near
        self.far = "y" if near == "x" else "x"

    def own(self, shard):
        return shard.at[self.rows] if self.lead is None else shard.at[self.lead, self.rows]

    def blocks(self, full, place, near, far, z, core):
        y, x = (near, far) if self.near == "y" else (far, near)
        index = (y, x, z, core, self.rows)
        return full.at[index] if self.lead is None else full.at[(self.lead,) + index]

    def here(self, place):
        return (place.x, place.y) if self.near == "x" else (place.y, place.x)


G_RIGHT, G_LEFT, G_NEAR, G_FAR, G_CORE = range(5)


class Gather:
    def __init__(self, place, piece, shard, full, send, recv, local):
        self.place, self.piece, self.shard, self.full = place, piece, shard, full
        self.send, self.recv, self.local = send, recv, local

    def view(self, near, far, z, core=None):
        return self.piece.blocks(self.full, self.place, near, far, z, self.place.core if core is None else core)

    def copy(self, kind, z, ref, axis, source=None):
        return pltpu.make_async_remote_copy(
            src_ref=ref if source is None else source,
            dst_ref=ref,
            send_sem=self.send.at[kind, z],
            recv_sem=self.recv.at[G_RIGHT if kind == G_LEFT else kind, z],
            device_id=self.place.neighbour(axis),
            device_id_type=MESH_ID,
        )

    def z_view(self, z):
        near, far = self.piece.here(self.place)
        return self.view(near if self.piece.zfirst else EVERY, far, z)

    def near_view(self, near, z):
        return self.view(near, self.piece.here(self.place)[1], z)

    def far_view(self, far, z):
        return self.view(EVERY, far, z)

    def core_view(self, core, z):
        return self.view(EVERY, EVERY, z, core)

    def own_copy(self):
        near, far = self.piece.here(self.place)
        return pltpu.make_async_copy(self.piece.own(self.shard), self.view(near, far, self.place.z), self.local)

    def begin(self):
        self.own_copy().start()
        if not self.piece.zfirst:
            near, _ = self.piece.here(self.place)
            self.copy(G_NEAR, self.place.z, self.near_view(near, self.place.z), self.piece.near, self.piece.own(self.shard)).start()

    def z_step(self, z, own, from_left):
        place = self.place
        near, far = self.piece.here(place)

        @pl.when(own)
        def _():
            self.own_copy().wait()
            if not self.piece.zfirst:
                self.copy(G_NEAR, z, self.near_view(1 - near, z), self.piece.near).wait_recv()

        @pl.when(jnp.logical_not(own))
        def _():
            self.copy(G_RIGHT, z, self.z_view(z), "left").wait_recv()

        @pl.when((own | from_left) & (place.z < place.z_size - 1))
        def _():
            self.copy(G_RIGHT, z, self.z_view(z), "right").start()

        @pl.when((own | jnp.logical_not(from_left)) & (place.z > 0))
        def _():
            self.copy(G_LEFT, z, self.z_view(z), "left").start()

        if self.piece.zfirst:
            self.copy(G_NEAR, z, self.near_view(near, z), self.piece.near).start()
        else:
            self.copy(G_FAR, z, self.far_view(far, z), self.piece.far).start()

    def near_step(self, z, own, from_left):
        near, far = self.piece.here(self.place)
        self.copy(G_NEAR, z, self.near_view(1 - near, z), self.piece.near).wait_recv()
        self.copy(G_FAR, z, self.far_view(far, z), self.piece.far).start()

    def far_step(self, z, own, from_left):
        _, far = self.piece.here(self.place)
        self.copy(G_FAR, z, self.far_view(1 - far, z), self.piece.far).wait_recv()
        self.copy(G_CORE, z, self.core_view(self.place.core, z), "core").start()

    def stages(self):
        if self.piece.zfirst:
            return [(0, self.z_step), (1, self.near_step), (2, self.far_step)]
        return [(1, self.z_step), (2, self.far_step)]

    def arrive(self):
        for z in range(self.place.z_size):
            self.copy(G_CORE, z, self.core_view(1 - self.place.core, z), "core").wait_recv()

    def drain(self):
        place = self.place
        near, far = self.piece.here(place)
        for z in range(place.z_size):
            self.copy(G_CORE, z, self.core_view(place.core, z), "core").wait_send()
            self.copy(G_FAR, z, self.far_view(far, z), self.piece.far).wait_send()
            if self.piece.zfirst:
                self.copy(G_NEAR, z, self.near_view(near, z), self.piece.near).wait_send()

            @pl.when((place.z < place.z_size - 1) & (z <= place.z))
            def _():
                self.copy(G_RIGHT, z, self.z_view(z), "right").wait_send()

            @pl.when((place.z > 0) & (z >= place.z))
            def _():
                self.copy(G_LEFT, z, self.z_view(z), "left").wait_send()

        if not self.piece.zfirst:
            self.copy(G_NEAR, place.z, self.near_view(near, place.z), self.piece.near).wait_send()


class GatherProgram:
    PARTS = 3

    def __init__(self, place, groups, offsets):
        self.place, self.groups, self.offsets = place, groups, offsets
        self.cursor = 0
        self.length = self.PARTS * (max(offsets) + place.z_size + 2)

    def begin(self):
        for group in self.groups:
            for piece in group:
                piece.begin()

    def part(self, number):
        step, part = number // self.PARTS, lax.rem(number, self.PARTS)
        place = self.place
        for group, offset in zip(self.groups, self.offsets):
            stages = {}
            for piece in group:
                for index, (behind, work) in enumerate(piece.stages()):
                    stages.setdefault((index if piece.piece.zfirst else 2 * index, behind), []).append(work)
            for (index, behind), works in stages.items():
                distance = step - offset - behind
                for from_left in (True, False):
                    z = place.z - distance if from_left else place.z + distance
                    least = 0 if from_left else 1

                    @pl.when((part == index) & (distance >= least) & (distance < place.z_size) & (z >= 0) & (z < place.z_size))
                    def _():
                        for work in works:
                            work(z, distance == 0, jnp.bool_(from_left))

    def run(self, count):
        last = min(self.length, self.cursor + count)
        if last > self.cursor:
            lax.fori_loop(self.cursor, last, lambda number, carry: (self.part(number), carry)[1], 0)
        self.cursor = last

    def run_in(self, index, each):
        def body(number, carry):
            @pl.when(number < self.length)
            def _():
                self.part(number)

            return carry

        lax.fori_loop(self.cursor + index * each, self.cursor + (index + 1) * each, body, 0)

    def skip(self, count):
        self.cursor = min(self.length, self.cursor + count)

    def run_until(self, group):
        self.run(self.PARTS * (self.offsets[group] + self.place.z_size + 2) - self.cursor)
        for piece in self.groups[group]:
            piece.arrive()

    def drain(self):
        self.run(self.length)
        for group in self.groups:
            for piece in group:
                piece.drain()


def halves(rows, zfirst, lead=None):
    return [Piece(lead, 0, rows // 2, zfirst, "x"), Piece(lead, rows // 2, rows // 2, zfirst, "y")]


def whole_shape(shard, sizes):
    y, x, z = chip_grid(sizes[0] * sizes[1])
    return shard.shape[:-2] + (y, x, z, 2) + shard.shape[-2:]


SMALL_LANES = 128


def plans():
    def feed(half):
        return [
            [Piece(pl.ds(half, 1), 0, 8, False, "x"), Piece(pl.ds(half, 1), 8, 8, False, "y")],
            [Piece(pl.ds(half, 1), 0, 32, True, "x"), Piece(pl.ds(half, 1), 32, 32, True, "y")],
        ]

    small = [Piece(None, 0, 16, False, "x")]
    square = [
        Piece(pl.ds(0, 4), 0, 8, False, "x"),
        Piece(pl.ds(0, 4), 8, 8, False, "y"),
        Piece(pl.ds(4, 2), 0, 8, True, "x"),
        Piece(pl.ds(4, 2), 8, 8, True, "y"),
    ]
    return [small] + feed(0), [square, halves(16, True)], feed(1)


def match_table(segments, valid):
    length = segments.shape[1]
    rows = lax.broadcasted_iota(jnp.int32, (128, length), 0)
    position = lax.broadcasted_iota(jnp.int32, (1, length), 1)
    table = jnp.where(rows == K, valid, jnp.where(rows == K + 1, segments, 0.0))
    for tap in range(K):
        moved = segments if tap == HALF else pltpu.roll(segments, (HALF - tap) % length, 1)
        inside = (position + tap - HALF >= 0) & (position + tap - HALF < length)
        table = jnp.where(rows == tap, jnp.where((moved == segments) & inside, 1.0, 0.0), table)
    return table.T


def forward_kernel(sizes, length, offsets, *refs):
    x_ref, seg_ref, valid_ref, pe_ref, small_ref, in_shard, out_shard, sq_shard, conv_shard = refs[:9]
    (a1_out, u1_out, qkv_out, rel_out, probs_out, ctx_out, a2_out, u_out, mixed_out, a3_out, s_out, match_out) = refs[9:21]
    in_full, out_full, sq_full, conv_full, small_full = refs[21:26]
    (a1, u1, qkv, rel, probs, ctx, a2, u, mixed, a3, s_ref, match, normed, padded, bias, small_own, small_whole, win, wout, square, conv) = refs[26:47]
    send, recv, local, loads, stores = refs[47:]
    frames = x_ref.shape[0]
    packs = frames // length

    place = Place(sizes)
    place.greet()
    small_own[...] = jnp.zeros_like(small_own)
    small_own[:, : small_ref.shape[1]] = small_ref[...]
    first, middle, last = plans()
    sources = [
        [(small_own, small_full), (in_shard, in_full), (out_shard, out_full)],
        [(sq_shard, sq_full), (conv_shard, conv_full)],
        [(in_shard, in_full), (out_shard, out_full)],
    ]
    groups, count = [], 0
    for plan, pairs in zip((first, middle, last), sources):
        group = []
        for pieces, (shard, full) in zip(plan, pairs):
            for piece in pieces:
                group.append(Gather(place, piece, shard, full, send.at[count], recv.at[count], local.at[count]))
                count += 1
        groups.append(group)
    program = GatherProgram(place, groups, offsets)
    program.begin()

    spilled = []

    def spill(source, target):
        copy = pltpu.make_async_copy(source, target, stores.at[len(spilled)])
        copy.start()
        spilled.append(copy)

    program.run(3)
    for pack in range(packs):
        rows = slice(pack * length, (pack + 1) * length)
        match[rows] = match_table(seg_ref[pack : pack + 1].astype(f32), valid_ref[pack : pack + 1].astype(f32))
    spill(match, match_out)
    query = lax.broadcasted_iota(jnp.int32, (length, length), 0)
    key = lax.broadcasted_iota(jnp.int32, (length, length), 1)
    for pack in range(packs):
        keyrow = jnp.where(valid_ref[pack : pack + 1] > 0, seg_ref[pack : pack + 1], -1).astype(f32)
        same = match[pack * length : (pack + 1) * length, K + 1 : K + 2] == keyrow
        bias[pack] = jnp.where(same | (query == key), 0.0, -1e30)

    program.run_until(0)
    load_small = pltpu.make_async_copy(small_full, small_whole, loads.at[0])
    load_in = pltpu.make_async_copy(in_full.at[0], win, loads.at[1])
    load_out = pltpu.make_async_copy(out_full.at[0], wout, loads.at[2])
    for load in (load_small, load_in, load_out):
        load.start()
    program.run(1)
    load_small.wait()
    s_ref[...] = small_whole[...].reshape(D, SMALL_LANES).T
    spill(s_ref, s_out)
    xhat, _ = normalize(x_ref[...])
    store_split(normed, xhat * s_ref[0:1] + s_ref[1:2])
    a1[...] = x_ref[...] + 0.5 * s_ref[17:18]
    load_in.wait()
    load_out.wait()
    width = FF // 8

    def chunk(index, carry):
        lanes = pl.ds(pl.multiple_of(index * width, width), width)
        bias_row = s_ref[pl.ds(23 + index // 2, 1), pl.ds(pl.multiple_of(lax.rem(index, 2) * width, width), width)]
        weight = win[:, :, :, :, :, lanes].reshape(D, width)
        value = dot3(load_split(normed), split(weight), NN) + bias_row
        u1[:, lanes] = value
        weight = wout[index // 4, lax.rem(index // 2, 2), pl.ds(lax.rem(index, 2) * 2, 2)].reshape(width, D)
        a1[...] += 0.5 * dot3(split(value * jax.nn.sigmoid(value)), split(weight), NN)
        program.run_in(index, 1)
        return carry

    lax.fori_loop(0, 8, chunk, 0)
    program.skip(8)
    spill(u1, u1_out)
    spill(a1, a1_out)
    xhat, _ = normalize(a1[...])
    store_split(normed, xhat * s_ref[2:3] + s_ref[3:4])

    program.run_until(1)
    load_square = pltpu.make_async_copy(sq_full, square, loads.at[3])
    load_conv = pltpu.make_async_copy(conv_full, conv, loads.at[4])
    load_square.start()
    load_conv.start()
    program.run(1)
    load_square.wait()
    load_conv.wait()

    def weight_split(index):
        return split(square[index].reshape(D, D))

    qkv[0] = dot3(load_split(normed), weight_split(0), NN) + s_ref[12:13]
    program.run(1)
    qkv[1] = dot3(load_split(normed), weight_split(1), NN)
    program.run(1)
    qkv[2] = dot3(load_split(normed), weight_split(2), NN) + s_ref[13:14]
    rel[...] = dot3(split(pe_ref[...]), weight_split(4), NN)
    program.run(1)
    spill(qkv, qkv_out)
    spill(rel, rel_out)
    attend(length, packs, qkv, rel, s_ref, bias, probs, ctx, lambda item: program.run_in(item, 1))
    program.skip(packs * (H // 2))
    spill(probs, probs_out)
    spill(ctx, ctx_out)
    a2[...] = a1[...] + dot3(split(ctx[...]), weight_split(3), NN) + s_ref[14:15]
    spill(a2, a2_out)
    program.run(1)

    xhat, _ = normalize(a2[...])
    store_split(normed, xhat * s_ref[4:5] + s_ref[5:6])
    for half in range(2):
        lanes = slice(half * D, (half + 1) * D)
        u[:, lanes] = dot3(load_split(normed), split(conv[:, :, :, :, :, lanes].reshape(D, D)), NN) + s_ref[19 + half : 20 + half]
        program.run(1)
    spill(u, u_out)
    mix(u, match, s_ref, padded, mixed)
    spill(mixed, mixed_out)
    program.run(1)
    inner, _ = normalize(mixed[...])
    inner = inner * s_ref[6:7] + s_ref[7:8]
    a3[...] = a2[...] + dot3(split(inner * jax.nn.sigmoid(inner)), weight_split(5), NN) + s_ref[22:23]
    spill(a3, a3_out)

    program.run_until(2)
    program.drain()
    for copy in spilled:
        copy.wait()


def head_lanes(pair, index, length):
    return pl.ds(pl.multiple_of((pair * 2 + index) * length, length), length)


def attend(length, packs, qkv_ref, rel_ref, s_ref, bias, probs_ref, ctx_ref, between):
    first, second = pair_masks()

    def heads(item, carry):
        pack, pair = item // (H // 2), lax.rem(item, H // 2)
        frames = pl.ds(pl.multiple_of(pack * length, length), length)
        lanes = pl.ds(pl.multiple_of(pair * 2 * DH, 2 * DH), 2 * DH)
        q = qkv_ref[0, frames, lanes]
        content = q + s_ref[15:16, lanes]
        position = q + s_ref[16:17, lanes]
        k = split(qkv_ref[1, frames, lanes])
        v = split(qkv_ref[2, frames, lanes])
        rel = split(rel_ref[:, lanes])
        total = jnp.zeros_like(q)
        for index, mask in enumerate((first, second)):
            scores = dot3(split(content * mask), k, NT) + shift_rows(dot3(split(position * mask), rel, NT))
            scores = scores * (1.0 / math.sqrt(DH)) + bias[pack]
            weights = jnp.exp(scores - jnp.max(scores, axis=-1, keepdims=True))
            weights = weights / jnp.sum(weights, axis=-1, keepdims=True)
            probs_ref[frames, head_lanes(pair, index, length)] = weights
            total = total + dot3(split(weights), v, NN) * mask
        ctx_ref[frames, lanes] = total
        between(item)
        return carry

    lax.fori_loop(0, packs * (H // 2), heads, 0)


def mix(u_ref, match_ref, s_ref, padded, mixed_ref):
    frames = mixed_ref.shape[0]
    padded[0:EDGE] = jnp.zeros((EDGE, D), f32)
    padded[EDGE + frames :] = jnp.zeros((EDGE, D), f32)
    padded[EDGE : EDGE + frames] = u_ref[:, :D] * jax.nn.sigmoid(u_ref[:, D:]) * match_ref[:, K : K + 1]
    for base in range(0, frames, STRIP):
        total = jnp.zeros((STRIP, D), f32) + s_ref[21:22]
        for tap in range(K):
            source = padded[base + EDGE + tap - HALF : base + EDGE + tap - HALF + STRIP]
            total = total + match_ref[base : base + STRIP, tap : tap + 1] * source * s_ref[TAP + tap : TAP + tap + 1]
        mixed_ref[base : base + STRIP] = total


def forward(sizes, x, segments, valid_mask, weights):
    feed_in, feed_out, square, proj, small = weights
    frames = x.shape[0]
    packs, length = segments.shape
    devices = sizes[0] * sizes[1]
    grid = chip_grid(devices) + (2,)
    z_size = grid[2]
    pe = jnp.asarray(sinusoid_table(length)[0])
    small_rows_here = small.shape[1]
    vmem = pl.BlockSpec(memory_space=pltpu.VMEM)
    kept = [
        (frames, D),
        (frames, FF),
        (3, frames, D),
        (length, D),
        (frames, H * length),
        (frames, D),
        (frames, D),
        (frames, 2 * D),
        (frames, D),
        (frames, D),
        (SMALL_LANES, D),
        (frames, 128),
    ]
    full = [
        (2,) + grid + feed_in.shape[1:],
        (2,) + grid + feed_out.shape[1:],
        (6,) + grid + square.shape[1:],
        grid + proj.shape,
        grid + (small_rows_here, SMALL_LANES),
    ]
    pieces = sum(len(p) for plan in plans() for p in plan)
    outs = pl.pallas_call(
        functools.partial(forward_kernel, sizes, length, GATHER_OFFSETS),
        in_specs=[vmem] * 9,
        out_specs=[pl.BlockSpec(memory_space=pl.ANY)] * (len(kept) + len(full)),
        out_shape=[jax.ShapeDtypeStruct(shape, f32) for shape in kept + full],
        scratch_shapes=[pltpu.VMEM(shape, f32) for shape in kept]
        + [
            pltpu.VMEM((2, frames, D), bf16),
            pltpu.VMEM((frames + 2 * EDGE, D), f32),
            pltpu.VMEM((packs, length, length), f32),
            pltpu.VMEM((small_rows_here, SMALL_LANES), f32),
            pltpu.VMEM(full[4], f32),
            pltpu.VMEM(full[0][1:], f32),
            pltpu.VMEM(full[1][1:], f32),
            pltpu.VMEM(full[2], f32),
            pltpu.VMEM(full[3], f32),
            pltpu.SemaphoreType.DMA((pieces, 5, z_size)),
            pltpu.SemaphoreType.DMA((pieces, 5, z_size)),
            pltpu.SemaphoreType.DMA((pieces,)),
            pltpu.SemaphoreType.DMA((5,)),
            pltpu.SemaphoreType.DMA((len(kept),)),
        ],
        compiler_params=pltpu.CompilerParams(collective_id=0, has_side_effects=True, vmem_limit_bytes=VMEM_LIMIT),
        name="forward",
    )(x, segments, valid_mask, pe, small.T, feed_in, feed_out, square, proj)
    return outs[: len(kept)], outs[len(kept) :]


GATHER_OFFSETS = (0, 3, 6)
S_CORE, S_FAR, S_NEAR, S_FROM_LEFT, S_FROM_RIGHT = range(5)


class Scatter:
    def __init__(self, place, piece, full, out, total, cores, fars, nears, lines, send, recv, local):
        self.place, self.piece, self.full, self.out = place, piece, full, out
        self.total, self.cores, self.fars, self.nears, self.lines = total, cores, fars, nears, lines
        self.send, self.recv, self.local = send, recv, local
        self.near, self.far = piece.here(place)

    def part(self, ref, near, far, z):
        y, x = (near, far) if self.piece.near == "y" else (far, near)
        index = (y, x, z)
        return ref.at[index] if self.piece.lead is None else ref.at[(EVERY,) + index]

    def staged(self, ref, *index):
        return ref.at[index] if self.piece.lead is None else ref.at[(EVERY,) + index]

    def add(self, target, source):
        target[...] = target[...] + source[...]

    def copy(self, kind, z, source, target, axis):
        return pltpu.make_async_remote_copy(
            src_ref=source,
            dst_ref=target,
            send_sem=self.send.at[kind, z],
            recv_sem=self.recv.at[kind, z],
            device_id=self.place.neighbour(axis),
            device_id_type=MESH_ID,
        )

    def core_copy(self, z):
        given = self.piece.blocks(self.full, self.place, EVERY, EVERY, z, 1 - self.place.core)
        return self.copy(S_CORE, z, given, self.part(self.cores, EVERY, EVERY, z), "core")

    def own_copy(self, z):
        kept = self.piece.blocks(self.full, self.place, EVERY, EVERY, z, self.place.core)
        return pltpu.make_async_copy(kept, self.part(self.total, EVERY, EVERY, z), self.local.at[z])

    def far_copy(self, z):
        return self.copy(S_FAR, z, self.part(self.total, EVERY, 1 - self.far, z), self.staged(self.fars, EVERY, z), self.piece.far)

    def near_copy(self, z):
        target = self.staged(self.nears, z if self.piece.zfirst else 0)
        return self.copy(S_NEAR, z, self.part(self.total, 1 - self.near, self.far, z), target, self.piece.near)

    def line_view(self, z):
        return self.part(self.total, self.near if self.piece.zfirst else EVERY, self.far, z)

    def line_staged(self, side, z):
        if self.piece.zfirst:
            return self.staged(self.lines, side, z)
        return self.staged(self.lines, side, EVERY, z)

    def line_copy(self, z, to_right):
        kind, side = (S_FROM_LEFT, 0) if to_right else (S_FROM_RIGHT, 1)
        return self.copy(kind, z, self.line_view(z), self.line_staged(side, z), "right" if to_right else "left")

    def begin(self):
        for distance in reversed(range(self.place.z_size)):
            for sign in (-1, 1) if distance else (1,):
                z = self.place.z + sign * distance

                @pl.when((z >= 0) & (z < self.place.z_size))
                def _():
                    self.core_copy(z).start()
                    self.own_copy(z).start()

    def core_step(self, z):
        self.core_copy(z).wait_recv()
        self.own_copy(z).wait()
        self.add(self.part(self.total, EVERY, EVERY, z), self.part(self.cores, EVERY, EVERY, z))

    def core_send(self, z):
        self.far_copy(z).start()

    def far_step(self, z):
        self.far_copy(z).wait_recv()
        self.add(self.part(self.total, EVERY, self.far, z), self.staged(self.fars, EVERY, z))

    def far_send(self, z):
        self.near_copy(z).start()

    def near_step(self, z):
        self.near_copy(z).wait_recv()
        self.add(self.part(self.total, self.near, self.far, z), self.staged(self.nears, z))

    def line_step(self, z):
        here = self.place.z

        @pl.when((z >= here) & (here > 0))
        def _():
            self.line_copy(z, True).wait_recv()
            self.add(self.line_view(z), self.line_staged(0, z))

        @pl.when((z <= here) & (here < self.place.z_size - 1))
        def _():
            self.line_copy(z, False).wait_recv()
            self.add(self.line_view(z), self.line_staged(1, z))

    def line_send(self, z):
        here = self.place.z

        @pl.when(z > here)
        def _():
            self.line_copy(z, True).start()

        @pl.when(z < here)
        def _():
            self.line_copy(z, False).start()

    def last_send(self):
        if not self.piece.zfirst:
            self.near_copy(self.place.z).start()

    def finish(self):
        z = self.place.z
        value = self.part(self.total, self.near, self.far, z)[...]
        if not self.piece.zfirst:
            self.near_copy(z).wait_recv()
            value = value + self.staged(self.nears, 0)[...]
        self.piece.own(self.out)[...] = value

    def drain(self):
        place = self.place
        for z in range(place.z_size):
            self.core_copy(z).wait_send()
            self.far_copy(z).wait_send()
            if self.piece.zfirst:
                self.near_copy(z).wait_send()

            @pl.when(z > place.z)
            def _():
                self.line_copy(z, True).wait_send()

            @pl.when(z < place.z)
            def _():
                self.line_copy(z, False).wait_send()

        if not self.piece.zfirst:
            self.near_copy(place.z).wait_send()


def scatter_stages(scatter):
    stages = [(scatter.core_step, scatter.core_send)]
    if scatter.piece.zfirst:
        return stages + [(scatter.far_step, scatter.far_send), (scatter.near_step, None), (scatter.line_step, scatter.line_send)]
    return stages + [(scatter.far_step, None), (scatter.line_step, scatter.line_send)]


class ScatterProgram:
    def __init__(self, place, scatters, lag):
        self.place, self.scatters = place, scatters
        self.blocks = 2 * place.z_size - 1
        self.staged = []
        for scatter in scatters:
            behind = 0
            for work, send in scatter_stages(scatter):
                self.staged.append((behind, work, send))
                behind += 0 if send is None else lag
        self.staged.sort(key=lambda stage: -stage[0])
        self.length = max(stage[0] for stage in self.staged) + self.blocks
        self.cursor = 0

    def begin(self):
        for scatter in self.scatters:
            scatter.begin()

    def part(self, step):
        place = self.place
        for behind in sorted({stage[0] for stage in self.staged}, reverse=True):
            item = step - behind
            distance = place.z_size - 1 - item // 2
            z = place.z + jnp.where(lax.rem(item, 2) == 0, -distance, distance)

            @pl.when((item >= 0) & (item < self.blocks) & (z >= 0) & (z < place.z_size))
            def _():
                for action in (1, 2):
                    for stage in self.staged:
                        if stage[0] == behind and stage[action] is not None:
                            stage[action](z)

    def run(self, count):
        last = min(self.length, self.cursor + count)
        if last > self.cursor:
            lax.fori_loop(self.cursor, last, lambda number, carry: (self.part(number), carry)[1], 0)
        self.cursor = last

    def run_in(self, index, each=1):
        for extra in range(each):
            self.part(self.cursor + index * each + extra)

    def skip(self, count):
        self.cursor = min(self.length, self.cursor + count)

    def last_send(self):
        self.run(self.length)
        for scatter in self.scatters:
            scatter.last_send()

    def finish(self):
        for scatter in self.scatters:
            scatter.finish()
        for scatter in self.scatters:
            scatter.drain()


def scatter_scratch(piece, columns, place_sizes, lead):
    y, x, z = chip_grid(place_sizes[0] * place_sizes[1])
    rows = piece.rows.size
    head = () if piece.lead is None else (lead,)
    return [
        pltpu.VMEM(head + (y, x, z, rows, columns), f32),
        pltpu.VMEM(head + (y, x, z, rows, columns), f32),
        pltpu.VMEM(head + (2, z, rows, columns), f32),
        pltpu.VMEM(head + ((z,) if piece.zfirst else (1,)) + (rows, columns), f32),
        pltpu.VMEM(head + ((2, z) if piece.zfirst else (2, 2, z)) + (rows, columns), f32),
    ]


def greet_all(place, sizes):
    devices = sizes[0] * sizes[1]
    barrier = pltpu.get_barrier_semaphore()

    def signal(offset, carry):
        other = lax.rem(place.index + offset, devices)
        pl.semaphore_signal(barrier, inc=1, device_id=(other // sizes[1], lax.rem(other, sizes[1])), device_id_type=MESH_ID)
        return carry

    lax.fori_loop(1, devices, signal, 0)
    pl.semaphore_wait(barrier, devices - 1)


def square_tile(values):
    squares = values * values
    tile = jnp.zeros((8, 128), f32)
    for r in range(0, values.shape[0], 8):
        for c in range(0, values.shape[1], 128):
            tile = tile + squares[r : r + 8, c : c + 128]
    return tile


def share_norm(place, sizes, outs, norms, own, send, recv):
    devices = sizes[0] * sizes[1]
    tile = jnp.zeros((8, 128), f32)
    for out in outs:
        for lead in range(out.shape[0]) if len(out.shape) == 3 else (None,):
            tile = tile + square_tile(out[...] if lead is None else out[lead])
    own[...] = tile
    norms[place.index] = tile

    def copy(offset, to):
        other = lax.rem(place.index + offset, devices)
        slot = place.index if to else other
        return pltpu.make_async_remote_copy(
            src_ref=own,
            dst_ref=norms.at[slot],
            send_sem=send.at[other],
            recv_sem=recv.at[slot],
            device_id=(other // sizes[1], lax.rem(other, sizes[1])),
            device_id_type=MESH_ID,
        )

    lax.fori_loop(1, devices, lambda offset, carry: (copy(offset, True).start(), carry)[1], 0)
    lax.fori_loop(1, devices, lambda offset, carry: (copy(offset, False).wait_recv(), carry)[1], 0)
    lax.fori_loop(1, devices, lambda offset, carry: (copy(offset, True).wait_send(), carry)[1], 0)


LAG = 2
WIDTH = FF // 8


def lanes_of(index, width=WIDTH):
    return pl.ds(pl.multiple_of(index * width, width), width)


def hidden_bias(s_ref, first_row, index):
    return s_ref.at[pl.ds(first_row + index // 2, 1), lanes_of(lax.rem(index, 2))]


def in_chunk(ref, index):
    return ref.at[:, :, :, :, :, lanes_of(index)]


def out_chunk(ref, index):
    return ref.at[index // 4, lax.rem(index // 2, 2), pl.ds(lax.rem(index, 2) * 2, 2)]


class Copies:
    def __init__(self, semaphores):
        self.semaphores, self.started = semaphores, []

    def start(self, source, target):
        copy = pltpu.make_async_copy(source, target, self.semaphores.at[len(self.started)])
        copy.start()
        self.started.append(copy)
        return copy


class Outbox:
    def __init__(self, slots, semaphores):
        self.slots, self.semaphores = slots, semaphores

    def put(self, index, value, target, columns=None):
        slot = lax.rem(index, 2)
        source = self.slots.at[slot] if columns is None else self.slots.at[slot, :, :, :, :, :, :columns]
        copy = pltpu.make_async_copy(source, target, self.semaphores.at[slot])

        @pl.when(index >= 2)
        def _():
            copy.wait()

        source[...] = value
        copy.start()

    def close(self, count, target, columns=None):
        for index in range(max(0, count - 2), count):
            slot = index % 2
            source = self.slots.at[slot] if columns is None else self.slots.at[slot, :, :, :, :, :, :columns]
            pltpu.make_async_copy(source, target, self.semaphores.at[slot]).wait()


def make_scatters(place, pieces, full, out, scratch, sems, start):
    send, recv, local = sems
    made = []
    for index, piece in enumerate(pieces):
        count = start + index
        made.append(Scatter(place, piece, full, out, *scratch[5 * count : 5 * count + 5], send.at[count], recv.at[count], local.at[count]))
    return made


def pieces_scratch(listed, sizes):
    scratch = []
    for pieces, columns in listed:
        for piece in pieces:
            scratch += scatter_scratch(piece, columns, sizes, None if piece.lead is None else piece.lead.size)
    return scratch


def feed_out_pass(index, hidden, df, box, out_full):
    u = hidden[:, lanes_of(index)]
    value = dot3(split(u * jax.nn.sigmoid(u)), load_split(df), TN)
    box.put(index, value.reshape(2, 2, 64, D), out_chunk(out_full, index))


def feed_in_pass(index, hidden, df, normed, win, wout, total, ds_ref, first_row, box, grid, in_full):
    u = hidden[:, lanes_of(index)]
    sig = jax.nn.sigmoid(u)
    weight = split(out_chunk(wout, index)[...].reshape(WIDTH, D))
    du = dot3(load_split(df), weight, NT) * (sig * (1.0 + u * (1.0 - sig)))
    hidden_bias(ds_ref, first_row, index)[...] = column_sum(du)
    du = split(du)
    weight = split(in_chunk(win, index)[...].reshape(D, WIDTH))
    total[...] += dot3(du, weight, NT)
    value = dot3(load_split(normed), du, TN)
    box.put(index, value.reshape(grid + (D // math.prod(grid), WIDTH)), in_chunk(in_full, index), WIDTH)


def first_backward_kernel(sizes, length, *refs):
    (cot_in, a3_in, a2_in, a1_in, qkv_in, rel_in, probs_in, ctx_in, u_in, mixed_in, s_in, match_in, pe_in, in_all, out_all, sq_all, conv_all) = refs[:17]
    out_out, da1_out, ds_out, sq_full, in_full, out_full, conv_full, sq5_full, g_in, g_out, g_conv, g_sq5 = refs[17:29]
    (da3, a2, mixed, ctx, a1, u, conv, square, qkv, rel, hidden, s_ref, match, pe, ds_ref, normed, df, box_in, box_out) = refs[29:48]
    scratch = refs[48 : 48 + 5 * 8]
    send, recv, local, loads, stores, box_sems = refs[48 + 5 * 8 :]
    frames = da3.shape[0]
    packs = frames // length
    grid = chip_grid(sizes[0] * sizes[1]) + (2,)
    place = Place(sizes)
    loading, storing = Copies(loads), Copies(stores)
    sems = (send, recv, local)
    halves_in, halves_out = halves(16, False), halves(64, True)
    out_program = ScatterProgram(place, make_scatters(place, halves_out, out_full, g_out, scratch, sems, 0), LAG)
    in_program = ScatterProgram(place, make_scatters(place, halves_in, in_full, g_in, scratch, sems, 2), LAG)
    conv_program = ScatterProgram(
        place,
        make_scatters(place, halves(16, True), conv_full, g_conv, scratch, sems, 4)
        + make_scatters(place, halves(16, False), sq5_full, g_sq5, scratch, sems, 6),
        LAG,
    )
    in_outbox = Outbox(box_in, box_sems.at[0])
    out_outbox = Outbox(box_out, box_sems.at[1])

    def second_module(a3, cot, da4, result, win, wout):
        waits = [
            loading.start(source, target)
            for source, target in ((s_in, s_ref), (a3_in, a3), (in_all.at[1], win), (out_all.at[1], wout), (cot_in, cot))
        ]
        place.greet()
        waits[0].wait()
        waits[1].wait()
        later = [
            loading.start(source, target)
            for source, target in (
                (match_in, match),
                (mixed_in, mixed),
                (sq_all, square),
                (u_in, u),
                (conv_all, conv),
                (a2_in, a2),
                (qkv_in, qkv),
                (ctx_in, ctx),
                (a1_in, a1),
                (rel_in, rel),
                (pe_in, pe),
            )
        ]
        ds_ref[...] = jnp.zeros_like(ds_ref)
        xhat, _ = normalize(a3[...])
        store_split(normed, xhat * s_ref[8:9] + s_ref[9:10])
        da4[...] = a3[...] + 0.5 * s_ref[18:19]
        waits[2].wait()
        waits[3].wait()

        def forward_chunk(index, carry):
            weight = in_chunk(win, index)[...].reshape(D, WIDTH)
            value = dot3(load_split(normed), split(weight), NN) + hidden_bias(s_ref, 23 + NC, index)[...]
            hidden[:, lanes_of(index)] = value
            weight = out_chunk(wout, index)[...].reshape(WIDTH, D)
            da4[...] += 0.5 * dot3(split(value * jax.nn.sigmoid(value)), split(weight), NN)
            return carry

        lax.fori_loop(0, 8, forward_chunk, 0)
        waits[4].wait()
        xhat, inverse = normalize(da4[...])
        result[...] = xhat * s_ref[10:11] + s_ref[11:12]
        storing.start(result, out_out)
        grad = cot[...]
        ds_ref[10:11] = column_sum(grad * xhat)
        ds_ref[11:12] = column_sum(grad)
        grad = normalize_back(grad * s_ref[10:11], xhat, inverse)
        da4[...] = grad
        half = 0.5 * grad
        store_split(df, half)
        ds_ref[18:19] = column_sum(half)
        da3[...] = jnp.zeros_like(da3)

        def out_pass(index, carry):
            feed_out_pass(index, hidden, df, out_outbox, out_full)
            return carry

        lax.fori_loop(0, 8, out_pass, 0)
        out_outbox.close(8, out_chunk(out_full, 0))
        out_program.begin()

        def in_pass(index, carry):
            out_program.run_in(index)
            feed_in_pass(index, hidden, df, normed, win, wout, da3, ds_ref, 23 + NC, in_outbox, grid, in_full)
            return carry

        lax.fori_loop(0, 8, in_pass, 0)
        out_program.skip(8)
        in_outbox.close(8, in_chunk(in_full, 0), WIDTH)
        in_program.begin()
        xhat, inverse = normalize(a3[...])
        dn = da3[...]
        ds_ref[8:9] = column_sum(dn * xhat)
        ds_ref[9:10] = column_sum(dn)
        da3[...] = da4[...] + normalize_back(dn * s_ref[8:9], xhat, inverse)
        for copy in later:
            copy.wait()
        storing.started[0].wait()

    piece = pltpu.VMEM((frames, D), f32)
    pl.run_scoped(
        second_module,
        piece,
        piece,
        piece,
        piece,
        pltpu.VMEM(grid + (D // math.prod(grid), FF), f32),
        pltpu.VMEM(grid + (FF // math.prod(grid), D), f32),
    )
    probs = hidden.at[:, : probs_in.shape[1]]
    load_probs = loading.start(probs_in, probs)
    out_program.run(1)

    def convolution(padded, dpadded, dgated):
        da3_split = split(da3[...])
        ds_ref[22:23] = column_sum(da3[...])
        hat, inverse = normalize(mixed[...])
        inner = hat * s_ref[6:7] + s_ref[7:8]
        sig = jax.nn.sigmoid(inner)
        in_outbox.slots[0] = dot3(split(inner * sig), da3_split, TN).reshape(box_in.shape[1:])
        store_square = storing.start(in_outbox.slots.at[0], sq5_full)
        dinner = dot3(da3_split, split(square[5].reshape(D, D)), NT) * (sig * (1.0 + inner * (1.0 - sig)))
        ds_ref[6:7] = column_sum(dinner * hat)
        ds_ref[7:8] = column_sum(dinner)
        dmixed = normalize_back(dinner * s_ref[6:7], hat, inverse)
        ds_ref[21:22] = column_sum(dmixed)
        out_program.last_send()
        in_program.run(1)
        zeros = jnp.zeros((EDGE, D), f32)
        padded[0:EDGE] = zeros
        padded[EDGE + frames :] = zeros
        padded[EDGE : EDGE + frames] = u[:, :D] * jax.nn.sigmoid(u[:, D:]) * match[:, K : K + 1]
        dpadded[0:EDGE] = zeros
        dpadded[EDGE + frames :] = zeros
        dpadded[EDGE : EDGE + frames] = dmixed
        in_program.run(1)
        for base in range(0, frames, STRIP):
            total = jnp.zeros((STRIP, D), f32)
            center = dpadded[base + EDGE : base + EDGE + STRIP]
            for tap in range(K):
                rows = slice(base + EDGE + tap - HALF, base + EDGE + tap - HALF + STRIP)
                same = match[base : base + STRIP, tap : tap + 1]
                total = total + same * dpadded[rows] * s_ref[TAP + K - 1 - tap : TAP + K - tap]
                ds_ref[TAP + tap : TAP + tap + 1] += column_sum(center * (same * padded[rows]))
            dgated[base : base + STRIP] = total * match[base : base + STRIP, K : K + 1]
        in_program.run(1)
        out_program.finish()
        gate = jax.nn.sigmoid(u[:, D:])
        dfirst = dgated[...] * gate
        dsecond = dfirst * u[:, :D] * (1.0 - gate)
        ds_ref[19:20] = column_sum(dfirst)
        ds_ref[20:21] = column_sum(dsecond)
        dfirst, dsecond = split(dfirst), split(dsecond)
        xhat, inverse = normalize(a2[...])
        store_split(normed, xhat * s_ref[4:5] + s_ref[5:6])
        store_square.wait()
        stored = []
        for half, grad in enumerate((dfirst, dsecond)):
            lanes = slice(half * D, (half + 1) * D)
            in_outbox.slots[half] = dot3(load_split(normed), grad, TN).reshape(box_in.shape[1:])
            stored.append(storing.start(in_outbox.slots.at[half], conv_full.at[:, :, :, :, :, lanes]))
            in_program.run(1)
        dn = dot3(dfirst, split(conv[:, :, :, :, :, :D].reshape(D, D)), NT) + dot3(dsecond, split(conv[:, :, :, :, :, D:].reshape(D, D)), NT)
        ds_ref[4:5] = column_sum(dn * xhat)
        ds_ref[5:6] = column_sum(dn)
        da3[...] = da3[...] + normalize_back(dn * s_ref[4:5], xhat, inverse)
        for copy in stored:
            copy.wait()
        conv_program.begin()
        in_program.run(1)

    padded = pltpu.VMEM((frames + 2 * EDGE, D), f32)
    pl.run_scoped(convolution, padded, padded, piece)

    def attention(dqkv, dctx, relback, drel, row_sums):
        da2_split = split(da3[...])
        ds_ref[14:15] = column_sum(da3[...])
        in_outbox.slots[0] = dot3(split(ctx[...]), da2_split, TN).reshape(box_in.shape[1:])
        stored = [storing.start(in_outbox.slots.at[0], sq_full.at[3])]
        dctx[...] = dot3(da2_split, split(square[3].reshape(D, D)), NT)
        in_program.run(1)
        row_index = lax.broadcasted_iota(jnp.int32, (length, length), 0)
        lane_index = lax.broadcasted_iota(jnp.int32, (length, length), 1)
        flip = (row_index + lane_index == length - 1).astype(bf16)
        rel_split = split(rel[...])
        relback[...] = dot(flip, rel_split[0], NN) + dot(flip, rel_split[1], NN)
        drel[...] = jnp.zeros_like(drel)
        row_sums[...] = jnp.zeros_like(row_sums)
        load_probs.wait()

        def between(item):
            in_program.run_in(item)
            conv_program.run_in(item)

        attend_back(length, packs, qkv, relback, probs, dctx, s_ref, flip, dqkv, drel, row_sums, between)
        in_program.skip(packs * (H // 2))
        conv_program.skip(packs * (H // 2))
        in_program.last_send()
        conv_program.run(1)
        ds_ref[15:17] = row_sums[0:2]
        ds_ref[12:13] = column_sum(dqkv[0])
        ds_ref[13:14] = column_sum(dqkv[2])
        xhat, inverse = normalize(a1[...])
        store_split(normed, xhat * s_ref[2:3] + s_ref[3:4])
        dn = jnp.zeros_like(xhat)
        for index in range(3):
            grad = split(dqkv[index])
            slot = (index + 1) % 2
            if index >= 1:
                stored[index - 1].wait()
            in_outbox.slots[slot] = dot3(load_split(normed), grad, TN).reshape(box_in.shape[1:])
            stored.append(storing.start(in_outbox.slots.at[slot], sq_full.at[index]))
            dn = dn + dot3(grad, split(square[index].reshape(D, D)), NT)
            conv_program.run(1)
        stored[2].wait()
        in_outbox.slots[0] = dot3(split(pe[...]), split(drel[...]), TN).reshape(box_in.shape[1:])
        stored.append(storing.start(in_outbox.slots.at[0], sq_full.at[4]))
        conv_program.last_send()
        in_program.finish()
        ds_ref[2:3] = column_sum(dn * xhat)
        ds_ref[3:4] = column_sum(dn)
        dctx[...] = da3[...] + normalize_back(dn * s_ref[2:3], xhat, inverse)
        stored.append(storing.start(dctx, da1_out))
        stored.append(storing.start(ds_ref, ds_out))
        for copy in stored[3:]:
            copy.wait()

    pl.run_scoped(
        attention,
        pltpu.VMEM((3, frames, D), f32),
        piece,
        pltpu.VMEM((length, D), f32),
        pltpu.VMEM((length, D), f32),
        pltpu.VMEM((8, D), f32),
    )
    conv_program.finish()


def attend_back(length, packs, qkv_ref, relback_ref, probs_ref, dctx_ref, s_ref, flip, dqkv_ref, drel_ref, sums_ref, between):
    first, second = pair_masks()

    def heads(item, carry):
        between(item)
        pack, pair = item // (H // 2), lax.rem(item, H // 2)
        frames = pl.ds(pl.multiple_of(pack * length, length), length)
        lanes = pl.ds(pl.multiple_of(pair * 2 * DH, 2 * DH), 2 * DH)
        q = qkv_ref[0, frames, lanes]
        content = q + s_ref[15:16, lanes]
        position = q + s_ref[16:17, lanes]
        k = qkv_ref[1, frames, lanes]
        v = split(qkv_ref[2, frames, lanes])
        rel = relback_ref[:, lanes]
        dc = dctx_ref[frames, lanes]
        dcontent = jnp.zeros_like(q)
        dposition = jnp.zeros_like(q)
        dkey = jnp.zeros_like(q)
        dvalue = jnp.zeros_like(q)
        drelation = jnp.zeros_like(rel)
        for index, mask in enumerate((first, second)):
            weights = probs_ref[frames, head_lanes(pair, index, length)]
            dc_split = split(dc * mask)
            dvalue = dvalue + dot3(split(weights), dc_split, TN)
            dweights = dot3(dc_split, v, NT)
            dscores = weights * (dweights - jnp.sum(weights * dweights, axis=-1, keepdims=True)) * (1.0 / math.sqrt(DH))
            ds_split = split(dscores)
            dcontent = dcontent + dot3(ds_split, split(k * mask), NN)
            dkey = dkey + dot3(ds_split, split(content * mask), TN)
            shifted = split(shift_rows(dot(ds_split[0], flip, NN) + dot(ds_split[1], flip, NN)))
            dposition = dposition + dot3(shifted, split(rel * mask), NN)
            drelation = drelation + dot3(shifted, split(position * mask), TN)
        dqkv_ref[0, frames, lanes] = dcontent + dposition
        dqkv_ref[1, frames, lanes] = dkey
        dqkv_ref[2, frames, lanes] = dvalue
        drel_ref[:, lanes] += drelation
        sums_ref[0:1, lanes] += column_sum(dcontent)
        sums_ref[1:2, lanes] += column_sum(dposition)
        return carry

    lax.fori_loop(0, packs * (H // 2), heads, 0)


def first_backward(sizes, length, cot, saved, full):
    a1, u1, qkv, rel, probs, ctx, a2, u, mixed, a3, s, match = saved
    in_all, out_all, sq_all, conv_all, _ = full
    frames = cot.shape[0]
    packs = frames // length
    grid = chip_grid(sizes[0] * sizes[1]) + (2,)
    z_size = grid[2]
    devices = math.prod(grid)
    pe = jnp.asarray(sinusoid_table(length)[1])
    rows = D // devices
    hbm, vmem = pl.BlockSpec(memory_space=pl.ANY), pl.BlockSpec(memory_space=pltpu.VMEM)
    piece = (frames, D)
    shapes = [
        piece,
        piece,
        (SMALL_LANES, D),
        (5,) + grid + (rows, D),
        grid + (rows, FF),
        grid + (FF // devices, D),
        grid + (rows, 2 * D),
        grid + (rows, D),
        (rows, FF),
        (FF // devices, D),
        (rows, 2 * D),
        (rows, D),
    ]
    listed = [(halves(64, True), D), (halves(16, False), FF), (halves(16, True), 2 * D), (halves(16, False), D)]
    return pl.pallas_call(
        functools.partial(first_backward_kernel, sizes, length),
        in_specs=[hbm] * 17,
        out_specs=[hbm] * 8 + [vmem] * 4,
        out_shape=[jax.ShapeDtypeStruct(shape, f32) for shape in shapes],
        scratch_shapes=[pltpu.VMEM(piece, f32)] * 5
        + [
            pltpu.VMEM((frames, 2 * D), f32),
            pltpu.VMEM(grid + (rows, 2 * D), f32),
            pltpu.VMEM((6,) + grid + (rows, D), f32),
            pltpu.VMEM((3, frames, D), f32),
            pltpu.VMEM((length, D), f32),
            pltpu.VMEM((frames, max(FF, H * length)), f32),
            pltpu.VMEM((SMALL_LANES, D), f32),
            pltpu.VMEM((frames, 128), f32),
            pltpu.VMEM((length, D), f32),
            pltpu.VMEM((SMALL_LANES, D), f32),
            pltpu.VMEM((2, frames, D), bf16),
            pltpu.VMEM((2, frames, D), bf16),
            pltpu.VMEM((2,) + grid + (rows, D), f32),
            pltpu.VMEM((2, 2, 2, FF // devices, D), f32),
        ]
        + pieces_scratch(listed, sizes)
        + [
            pltpu.SemaphoreType.DMA((8, 5, z_size)),
            pltpu.SemaphoreType.DMA((8, 5, z_size)),
            pltpu.SemaphoreType.DMA((8, z_size)),
            pltpu.SemaphoreType.DMA((17,)),
            pltpu.SemaphoreType.DMA((11,)),
            pltpu.SemaphoreType.DMA((2, 2)),
        ],
        compiler_params=pltpu.CompilerParams(collective_id=1, has_side_effects=True, vmem_limit_bytes=VMEM_TOP),
        name="first_backward",
    )(cot, a3, a2, a1, qkv, rel, probs, ctx, u, mixed, s, match, pe, in_all, out_all, sq_all, conv_all)


def second_backward_kernel(sizes, *refs):
    da1_in, x_in, u1_in, s_in, ds_in, in_all, out_all, sq_full, g_in2, g_out2, g_conv, g_sq5 = refs[:12]
    dx_out, in_full, out_full, g_in1, g_out1, g_sq, g_small, norms = refs[12:20]
    (da1, x, dx, hidden, s_ref, ds_ref, normed, df, win, wout, small_full, box_in, box_out) = refs[20:33]
    scratch = refs[33 : 33 + 5 * 8]
    send, recv, local, loads, stores, box_sems, norm_own, norm_send, norm_recv = refs[33 + 5 * 8 :]
    grid = chip_grid(sizes[0] * sizes[1]) + (2,)
    place = Place(sizes)
    loading, storing = Copies(loads), Copies(stores)
    sems = (send, recv, local)
    square = [Piece(pl.ds(0, 4), 0, 8, False, "x"), Piece(pl.ds(0, 4), 8, 8, False, "y"), Piece(pl.ds(4, 1), 0, 16, True, "x")]
    sq_program = ScatterProgram(place, make_scatters(place, square, sq_full, g_sq, scratch, sems, 0), LAG)
    out_program = ScatterProgram(place, make_scatters(place, halves(64, True), out_full, g_out1, scratch, sems, 3), LAG)
    in_program = ScatterProgram(
        place,
        make_scatters(place, halves(16, False), in_full, g_in1, scratch, sems, 5)
        + make_scatters(place, [Piece(None, 0, 16, False, "x")], small_full, g_small, scratch, sems, 7),
        LAG,
    )
    in_outbox = Outbox(box_in, box_sems.at[0])
    out_outbox = Outbox(box_out, box_sems.at[1])
    waits = [
        loading.start(source, target)
        for source, target in (
            (s_in, s_ref),
            (x_in, x),
            (da1_in, da1),
            (ds_in, ds_ref),
            (u1_in, hidden),
            (in_all.at[0], win),
            (out_all.at[0], wout),
        )
    ]
    greet_all(place, sizes)
    sq_program.begin()
    for copy in waits[:4]:
        copy.wait()
    xhat, _ = normalize(x[...])
    store_split(normed, xhat * s_ref[0:1] + s_ref[1:2])
    half = 0.5 * da1[...]
    store_split(df, half)
    ds_ref[17:18] = column_sum(half)
    dx[...] = jnp.zeros_like(dx)
    for copy in waits[4:]:
        copy.wait()

    def out_pass(index, carry):
        feed_out_pass(index, hidden, df, out_outbox, out_full)

        @pl.when(lax.rem(index, 4) == 3)
        def _():
            sq_program.run_in(index // 4)

        return carry

    lax.fori_loop(0, 8, out_pass, 0)
    sq_program.skip(2)
    out_outbox.close(8, out_chunk(out_full, 0))
    out_program.begin()

    def in_pass(index, carry):
        feed_in_pass(index, hidden, df, normed, win, wout, dx, ds_ref, 23, in_outbox, grid, in_full)
        sq_program.run_in(index)
        out_program.run_in(index)
        return carry

    lax.fori_loop(0, 8, in_pass, 0)
    sq_program.skip(8)
    out_program.skip(8)
    in_outbox.close(8, in_chunk(in_full, 0), WIDTH)
    xhat, inverse = normalize(x[...])
    dn = dx[...]
    ds_ref[0:1] = column_sum(dn * xhat)
    ds_ref[1:2] = column_sum(dn)
    small_full[...] = ds_ref[...].T.reshape(small_full.shape)
    dx[...] = da1[...] + normalize_back(dn * s_ref[0:1], xhat, inverse)
    store_dx = storing.start(dx, dx_out)
    in_program.begin()
    sq_program.last_send()
    out_program.run(1)
    in_program.run(1)
    out_program.last_send()
    in_program.run(2)
    sq_program.finish()
    in_program.run(3)
    out_program.finish()
    in_program.last_send()
    in_program.finish()
    share_norm(place, sizes, (g_in1, g_in2, g_out1, g_out2, g_sq, g_sq5, g_conv, g_small), norms, norm_own, norm_send, norm_recv)
    store_dx.wait()


def second_backward(sizes, da1, x, u1, s, ds, full, sq_full, reduced):
    in_all, out_all = full[0], full[1]
    frames = x.shape[0]
    grid = chip_grid(sizes[0] * sizes[1]) + (2,)
    z_size = grid[2]
    devices = math.prod(grid)
    rows = D // devices
    hbm, vmem = pl.BlockSpec(memory_space=pl.ANY), pl.BlockSpec(memory_space=pltpu.VMEM)
    piece = (frames, D)
    shapes = [
        piece,
        grid + (rows, FF),
        grid + (FF // devices, D),
        (rows, FF),
        (FF // devices, D),
        (5, rows, D),
        (rows, SMALL_LANES),
        (devices, 8, 128),
    ]
    square = [Piece(pl.ds(0, 4), 0, 8, False, "x"), Piece(pl.ds(0, 4), 8, 8, False, "y"), Piece(pl.ds(4, 1), 0, 16, True, "x")]
    listed = [(square, D), (halves(64, True), D), (halves(16, False), FF), ([Piece(None, 0, 16, False, "x")], SMALL_LANES)]
    return pl.pallas_call(
        functools.partial(second_backward_kernel, sizes),
        in_specs=[hbm] * 8 + [vmem] * 4,
        out_specs=[hbm] * 3 + [vmem] * 5,
        out_shape=[jax.ShapeDtypeStruct(shape, f32) for shape in shapes],
        scratch_shapes=[pltpu.VMEM(piece, f32)] * 3
        + [
            pltpu.VMEM((frames, FF), f32),
            pltpu.VMEM((SMALL_LANES, D), f32),
            pltpu.VMEM((SMALL_LANES, D), f32),
            pltpu.VMEM((2, frames, D), bf16),
            pltpu.VMEM((2, frames, D), bf16),
            pltpu.VMEM(grid + (rows, FF), f32),
            pltpu.VMEM(grid + (FF // devices, D), f32),
            pltpu.VMEM(grid + (rows, SMALL_LANES), f32),
            pltpu.VMEM((2,) + grid + (rows, WIDTH), f32),
            pltpu.VMEM((2, 2, 2, FF // devices, D), f32),
        ]
        + pieces_scratch(listed, sizes)
        + [
            pltpu.SemaphoreType.DMA((8, 5, z_size)),
            pltpu.SemaphoreType.DMA((8, 5, z_size)),
            pltpu.SemaphoreType.DMA((8, z_size)),
            pltpu.SemaphoreType.DMA((7,)),
            pltpu.SemaphoreType.DMA((1,)),
            pltpu.SemaphoreType.DMA((2, 2)),
            pltpu.VMEM((8, 128), f32),
            pltpu.SemaphoreType.DMA((devices,)),
            pltpu.SemaphoreType.DMA((devices,)),
        ],
        compiler_params=pltpu.CompilerParams(collective_id=2, has_side_effects=True, vmem_limit_bytes=VMEM_TOP),
        name="second_backward",
    )(da1, x, u1, s, ds, in_all, out_all, sq_full, *reduced)


def adamw_kernel(step_ref, norms_ref, *refs):
    (g_in1, g_in2, g_out1, g_out2, g_sq, g_sq5, g_conv, g_small), refs = refs[:8], refs[8:]
    weights, firsts, seconds, outs = refs[0:5], refs[5:10], refs[10:15], refs[16:]
    norm = jnp.sqrt(jnp.sum(norms_ref[...], axis=(0, 1, 2), keepdims=True)[0])
    refs[15][...] = norm
    clip = jnp.minimum(1.0, CLIP_NORM / (norm + 1e-06))

    def geometric(_, carry):
        one, one_power, two, two_power = carry
        return one + one_power, one_power * BETA_ONE, two + two_power, two_power * BETA_TWO

    zero, unit = jnp.float32(0.0), jnp.float32(1.0)
    one, _, two, _ = lax.fori_loop(0, step_ref[0], geometric, (zero, unit, zero, unit))
    first_scale = jnp.full((1, 1), (1.0 - BETA_ONE) * one, f32)
    second_scale = jnp.full((1, 1), (1.0 - BETA_TWO) * two, f32)
    first_scale = 1.0 / first_scale
    second_scale = 1.0 / second_scale

    def update(number, index, gradient, rate, decay):
        weight, first, second = weights[number][index], firsts[number][index], seconds[number][index]
        clipped = clip * gradient
        first_next = BETA_ONE * first + (1.0 - BETA_ONE) * clipped
        second_next = BETA_TWO * second + (1.0 - BETA_TWO) * clipped * clipped
        step = (first_next * first_scale) / (jnp.sqrt(second_next * second_scale) + ADAM_EPS)
        if decay:
            step = step + decay * weight
        outs[3 * number][index] = first_next
        outs[3 * number + 1][index] = second_next
        outs[3 * number + 2][index] = weight - rate * step

    for half, (g_in, g_out) in enumerate(((g_in1, g_out1), (g_in2, g_out2))):
        update(0, half, g_in[...], MATRIX_RATE, MATRIX_DECAY)
        update(1, half, g_out[...], MATRIX_RATE, MATRIX_DECAY)
    for index in range(6):
        update(2, index, g_sq[index] if index < 5 else g_sq5[...], MATRIX_RATE, MATRIX_DECAY)
    update(3, EVERY, g_conv[...], MATRIX_RATE, MATRIX_DECAY)
    update(4, EVERY, g_small[:, : weights[4].shape[1]], VECTOR_RATE, 0.0)


def adamw(step, norms, grads, weights, firsts, seconds):
    vmem = pl.BlockSpec(memory_space=pltpu.VMEM)
    shapes = [jax.ShapeDtypeStruct((1, 1), f32)]
    for weight in weights:
        shapes += [jax.ShapeDtypeStruct(weight.shape, f32)] * 3
    return pl.pallas_call(
        adamw_kernel,
        in_specs=[pl.BlockSpec(memory_space=pltpu.SMEM)] + [vmem] * 24,
        out_specs=[vmem] * 16,
        out_shape=shapes,
        compiler_params=pltpu.CompilerParams(vmem_limit_bytes=VMEM_LIMIT),
        name="adamw",
    )(step, norms, *grads, *weights, *firsts, *seconds)


AXES = ("dp", "fsdp")


def gather_plain(feed_in, feed_out, square, proj, small):
    feed_in = lax.all_gather(feed_in, AXES, axis=1, tiled=True)
    feed_out = lax.all_gather(feed_out, AXES, axis=1, tiled=True)
    square = lax.all_gather(square, AXES, axis=1, tiled=True)
    proj = lax.all_gather(proj, AXES, axis=0, tiled=True)
    small = lax.all_gather(small, AXES, axis=1, tiled=True)
    return feed_in, feed_out, square, proj, small


def scatter_plain(grads):
    (in1, in2), (out1, out2), (dw, dw5), dproj, ds = grads
    parts = [lax.psum_scatter(v, AXES, scatter_dimension=0, tiled=True) for v in (in1, in2, out1, out2)]
    parts.append(lax.psum_scatter(dw, AXES, scatter_dimension=1, tiled=True))
    parts.append(lax.psum_scatter(dw5, AXES, scatter_dimension=0, tiled=True))
    parts.append(lax.psum_scatter(dproj, AXES, scatter_dimension=0, tiled=True))
    parts.append(lax.psum_scatter(ds.T, AXES, scatter_dimension=0, tiled=True))
    total = lax.psum(sum(jnp.sum(part * part) for part in parts), AXES)
    return tuple(parts), jnp.zeros((1, 8, 128), f32).at[0, 0, 0].set(total)


def overlapped_layer(sizes, inputs, cotangent, segments, valid_mask, weights):
    packs, length, _ = inputs.shape
    frames = packs * length
    x = inputs.reshape(frames, D)
    saved, full = forward(sizes, x, segments, valid_mask, weights)
    out, da1, ds, sq_full, _, _, _, _, g_in2, g_out2, g_conv, g_sq5 = first_backward(sizes, length, cotangent.reshape(frames, D), saved, full)
    dx, _, _, g_in1, g_out1, g_sq, g_small, norms = second_backward(
        sizes, da1, x, saved[1], saved[10], ds, full, sq_full, (g_in2, g_out2, g_conv, g_sq5)
    )
    grads = (g_in1, g_in2, g_out1, g_out2, g_sq, g_sq5, g_conv, g_small)
    return out.reshape(inputs.shape), dx.reshape(inputs.shape), grads, norms


def local(sizes, inputs, cotangent, segments, valid_mask, step_count, *state):
    weights, moments = state[:5], state[5:]
    devices = sizes[0] * sizes[1]
    if D // devices % 16 == 0 and chip_grid(devices)[:2] == (2, 2):
        out, dx, grads, norms = overlapped_layer(sizes, inputs, cotangent, segments, valid_mask, weights)
    else:
        out, dx, grads = layer(inputs, cotangent, segments, valid_mask, gather_plain(*weights))
        grads, norms = scatter_plain(grads)

    def turned(values):
        return tuple(values[:-1]) + (values[-1].T,)

    norm, *updated = adamw(step_count, norms, grads, turned(weights), turned(moments[0::2]), turned(moments[1::2]))
    return (out, dx, norm.reshape(()), *updated[:-3], *(value.T for value in updated[-3:]))


def solution(mesh):
    sizes = (mesh.shape["dp"], mesh.shape["fsdp"])
    batch = P(AXES, None, None)
    rows = P(AXES, None)
    middle = P(None, AXES, None)
    columns = P(None, AXES)
    weights = (middle, middle, middle, rows, columns)
    moments = tuple(spec for spec in weights for _ in range(2))
    return jax.shard_map(
        functools.partial(local, sizes),
        mesh=mesh,
        in_specs=(batch, batch, rows, rows, P()) + weights + moments,
        out_specs=(batch, batch, P()) + tuple(spec for spec in weights for _ in range(3)),
        check_vma=False,
    )
```

```python
import functools
import math

import jax
import jax.numpy as jnp
import numpy as np
from jax import lax
from jax.experimental import pallas as pl
from jax.experimental.pallas import tpu as pltpu
from jax.sharding import PartitionSpec as P

D = 512
H = 8
DH = 64
FF = 2048
K = 9
NC = FF // D
TAP = 23 + 2 * NC
NORM_EPS = 1e-05
BETA_ONE = 0.9
BETA_TWO = 0.999
ADAM_EPS = 1e-08
CLIP_NORM = 1.0
MATRIX_RATE = 0.03
VECTOR_RATE = 0.4
MATRIX_DECAY = 0.01
VMEM_LIMIT = 60 * 2**20
VMEM_TOP = 67043328

f32 = jnp.float32
bf16 = jnp.bfloat16
NN = (((1,), (0,)), ((), ()))
NT = (((1,), (1,)), ((), ()))
TN = (((0,), (0,)), ((), ()))


def split(value):
    high = value.astype(bf16)
    return high, (value - high.astype(f32)).astype(bf16)


def dot(left, right, dims):
    return lax.dot_general(left, right, dims, preferred_element_type=f32)


def dot3(left, right, dims):
    return dot(left[0], right[0], dims) + (dot(left[0], right[1], dims) + dot(left[1], right[0], dims))


def normalize(values):
    centred = values - jnp.mean(values, axis=-1, keepdims=True)
    inverse = lax.rsqrt(jnp.mean(centred * centred, axis=-1, keepdims=True) + NORM_EPS)
    return centred * inverse, inverse


def normalize_back(scaled, xhat, inverse):
    return (scaled - jnp.mean(scaled, axis=-1, keepdims=True) - xhat * jnp.mean(scaled * xhat, axis=-1, keepdims=True)) * inverse


def column_sum(values):
    return jnp.sum(values, axis=0, keepdims=True)


def row(rows_ref, index):
    return rows_ref[pl.ds(index, 1), :]


def store_split(pair_ref, value):
    high, low = split(value)
    pair_ref[0] = high
    pair_ref[1] = low


def load_split(pair_ref, *index):
    if index:
        return pair_ref[(0,) + index], pair_ref[(1,) + index]
    return pair_ref[0], pair_ref[1]


def ffn_forward_chunk(normed, u_ref, win, wout, bias):
    u = dot3(normed, split(win), NN) + bias
    u_ref[...] = u
    return dot3(split(u * jax.nn.sigmoid(u)), split(wout), NN)


def ffn_backward_chunk(normed, u, df, win, wout):
    sig = jax.nn.sigmoid(u)
    dwout = dot3(split(u * sig), df, TN)
    du = dot3(df, split(wout), NT) * (sig * (1.0 + u * (1.0 - sig)))
    du_split = split(du)
    dwin = dot3(normed, du_split, TN)
    return dwin, dwout, column_sum(du), dot3(du_split, split(win), NT)


def ffn1_forward_kernel(x_ref, win_ref, wout_ref, s_ref, a1_ref, u_ref, normed):
    chunk = pl.program_id(0)

    @pl.when(chunk == 0)
    def _():
        xhat, _ = normalize(x_ref[...])
        store_split(normed, xhat * s_ref[0:1] + s_ref[1:2])
        a1_ref[...] = x_ref[...] + 0.5 * s_ref[17:18]

    out = ffn_forward_chunk(load_split(normed), u_ref, win_ref[...], wout_ref[...], row(s_ref, 23 + chunk))
    a1_ref[...] += 0.5 * out


def ffn1_forward(x, win, wout, s):
    frames = x.shape[0]
    whole = pl.BlockSpec((frames, D), lambda c: (0, 0))
    return pl.pallas_call(
        ffn1_forward_kernel,
        grid=(NC,),
        in_specs=[
            whole,
            pl.BlockSpec((D, D), lambda c: (0, c)),
            pl.BlockSpec((D, D), lambda c: (c, 0)),
            pl.BlockSpec(s.shape, lambda c: (0, 0)),
        ],
        out_specs=[whole, pl.BlockSpec((frames, D), lambda c: (0, c))],
        out_shape=[jax.ShapeDtypeStruct((frames, D), f32), jax.ShapeDtypeStruct((frames, FF), f32)],
        scratch_shapes=[pltpu.VMEM((2, frames, D), bf16)],
        compiler_params=pltpu.CompilerParams(vmem_limit_bytes=VMEM_LIMIT),
        name="ffn1_forward",
    )(x, win, wout, s)


def ffn1_backward_kernel(da_ref, x_ref, u_ref, win_ref, wout_ref, s_ref, dx_ref, dwin_ref, dwout_ref, ds_ref, normed, df):
    chunk = pl.program_id(0)

    @pl.when(chunk == 0)
    def _():
        xhat, _ = normalize(x_ref[...])
        store_split(normed, xhat * s_ref[0:1] + s_ref[1:2])
        half = 0.5 * da_ref[...]
        store_split(df, half)
        ds_ref[...] = jnp.zeros_like(ds_ref)
        ds_ref[2:3] = column_sum(half)
        dx_ref[...] = jnp.zeros_like(dx_ref)

    dwin, dwout, dbias, dnormed = ffn_backward_chunk(load_split(normed), u_ref[...], load_split(df), win_ref[...], wout_ref[...])
    dwin_ref[...] = dwin
    dwout_ref[...] = dwout
    ds_ref[pl.ds(4 + chunk, 1), :] = dbias
    dx_ref[...] += dnormed

    @pl.when(chunk == NC - 1)
    def _():
        xhat, inverse = normalize(x_ref[...])
        dn = dx_ref[...]
        ds_ref[0:1] = column_sum(dn * xhat)
        ds_ref[1:2] = column_sum(dn)
        dx_ref[...] = da_ref[...] + normalize_back(dn * s_ref[0:1], xhat, inverse)


def ffn1_backward(da, x, u, win, wout, s):
    frames = x.shape[0]
    whole = pl.BlockSpec((frames, D), lambda c: (0, 0))
    across = pl.BlockSpec((D, D), lambda c: (0, c))
    down = pl.BlockSpec((D, D), lambda c: (c, 0))
    return pl.pallas_call(
        ffn1_backward_kernel,
        grid=(NC,),
        in_specs=[whole, whole, pl.BlockSpec((frames, D), lambda c: (0, c)), across, down, pl.BlockSpec(s.shape, lambda c: (0, 0))],
        out_specs=[whole, across, down, pl.BlockSpec((8, D), lambda c: (0, 0))],
        out_shape=[
            jax.ShapeDtypeStruct((frames, D), f32),
            jax.ShapeDtypeStruct((D, FF), f32),
            jax.ShapeDtypeStruct((FF, D), f32),
            jax.ShapeDtypeStruct((8, D), f32),
        ],
        scratch_shapes=[pltpu.VMEM((2, frames, D), bf16), pltpu.VMEM((2, frames, D), bf16)],
        compiler_params=pltpu.CompilerParams(vmem_limit_bytes=VMEM_LIMIT),
        name="ffn1_backward",
    )(da, x, u, win, wout, s)


def ffn2_kernel(a3_ref, cot_ref, win_ref, wout_ref, s_ref, out_ref, da3_ref, dwin_ref, dwout_ref, ds_ref, normed, df, hidden, da4):
    step = pl.program_id(0)

    @pl.when(step == 0)
    def _():
        xhat, _ = normalize(a3_ref[...])
        store_split(normed, xhat * s_ref[8:9] + s_ref[9:10])
        da4[...] = a3_ref[...] + 0.5 * s_ref[18:19]

    @pl.when(step < NC)
    def _():
        out = ffn_forward_chunk(load_split(normed), hidden.at[step], win_ref[...], wout_ref[...], row(s_ref, 23 + NC + step))
        da4[...] += 0.5 * out

    @pl.when(step == NC - 1)
    def _():
        xhat, inverse = normalize(da4[...])
        out_ref[...] = xhat * s_ref[10:11] + s_ref[11:12]
        cot = cot_ref[...]
        ds_ref[...] = jnp.zeros_like(ds_ref)
        ds_ref[8:9] = column_sum(cot * xhat)
        ds_ref[9:10] = column_sum(cot)
        grad = normalize_back(cot * s_ref[10:11], xhat, inverse)
        da4[...] = grad
        half = 0.5 * grad
        store_split(df, half)
        ds_ref[2:3] = column_sum(half)
        da3_ref[...] = jnp.zeros_like(da3_ref)

    @pl.when(step >= NC)
    def _():
        dwin, dwout, dbias, dnormed = ffn_backward_chunk(load_split(normed), hidden[step - NC], load_split(df), win_ref[...], wout_ref[...])
        dwin_ref[...] = dwin
        dwout_ref[...] = dwout
        ds_ref[pl.ds(4 + step - NC, 1), :] = dbias
        da3_ref[...] += dnormed

    @pl.when(step == 2 * NC - 1)
    def _():
        xhat, inverse = normalize(a3_ref[...])
        dn = da3_ref[...]
        ds_ref[0:1] = column_sum(dn * xhat)
        ds_ref[1:2] = column_sum(dn)
        da3_ref[...] = da4[...] + normalize_back(dn * s_ref[8:9], xhat, inverse)


def ffn2(a3, cot, win, wout, s):
    frames = a3.shape[0]
    whole = pl.BlockSpec((frames, D), lambda c: (0, 0))
    return pl.pallas_call(
        ffn2_kernel,
        grid=(2 * NC,),
        in_specs=[
            whole,
            whole,
            pl.BlockSpec((D, D), lambda c: (0, lax.rem(c, NC))),
            pl.BlockSpec((D, D), lambda c: (lax.rem(c, NC), 0)),
            pl.BlockSpec(s.shape, lambda c: (0, 0)),
        ],
        out_specs=[
            whole,
            whole,
            pl.BlockSpec((D, D), lambda c: (0, jnp.maximum(c - NC, 0))),
            pl.BlockSpec((D, D), lambda c: (jnp.maximum(c - NC, 0), 0)),
            pl.BlockSpec((16, D), lambda c: (0, 0)),
        ],
        out_shape=[
            jax.ShapeDtypeStruct((frames, D), f32),
            jax.ShapeDtypeStruct((frames, D), f32),
            jax.ShapeDtypeStruct((D, FF), f32),
            jax.ShapeDtypeStruct((FF, D), f32),
            jax.ShapeDtypeStruct((16, D), f32),
        ],
        scratch_shapes=[
            pltpu.VMEM((2, frames, D), bf16),
            pltpu.VMEM((2, frames, D), bf16),
            pltpu.VMEM((NC, frames, D), f32),
            pltpu.VMEM((frames, D), f32),
        ],
        compiler_params=pltpu.CompilerParams(vmem_limit_bytes=VMEM_LIMIT),
        name="ffn2",
    )(a3, cot, win, wout, s)


def sinusoid_table(length):
    offsets = length // 2 - np.arange(length, dtype=np.float64)
    frequency = 10000.0 ** (-2.0 * np.arange(D // 2, dtype=np.float64) / D)
    angles = offsets[:, None] * frequency[None, :]
    table = np.concatenate([np.sin(angles), np.cos(angles)], axis=1).astype(np.float32)
    return np.stack([table, table[::-1]])


def shift_rows(scores):
    return pltpu.roll(scores, scores.shape[1] // 2, 1, stride=1, stride_axis=0)


def pair_masks():
    lane = lax.broadcasted_iota(jnp.int32, (1, 2 * DH), 1)
    first = (lane < DH).astype(f32)
    return first, 1.0 - first


def attention_forward_kernel(length, a1_ref, w_ref, pe_ref, s_ref, segcol_ref, keyrow_ref, a2_ref, qkv_ref, rel_ref, probs_ref, ctx_ref, bias):
    packs = a1_ref.shape[0] // length
    xhat, _ = normalize(a1_ref[...])
    normed = split(xhat * s_ref[2:3] + s_ref[3:4])
    qkv_ref[0] = dot3(normed, split(w_ref[0]), NN) + s_ref[12:13]
    qkv_ref[1] = dot3(normed, split(w_ref[1]), NN)
    qkv_ref[2] = dot3(normed, split(w_ref[2]), NN) + s_ref[13:14]
    rel_ref[...] = dot3(split(pe_ref[0]), split(w_ref[4]), NN)
    query = lax.broadcasted_iota(jnp.int32, (length, length), 0)
    key = lax.broadcasted_iota(jnp.int32, (length, length), 1)
    for pack in range(packs):
        same = segcol_ref[pl.ds(pack * length, length), 0:1] == keyrow_ref[pack : pack + 1, 0:length]
        bias[pack] = jnp.where(same | (query == key), 0.0, -1e30)
    first, second = pair_masks()

    def heads(item, carry):
        pack, pair = item // (H // 2), item % (H // 2)
        frames = pl.ds(pl.multiple_of(pack * length, length), length)
        lanes = pl.ds(pl.multiple_of(pair * 2 * DH, 2 * DH), 2 * DH)
        q = qkv_ref[0, frames, lanes]
        content = q + s_ref[15:16, lanes]
        position = q + s_ref[16:17, lanes]
        k = split(qkv_ref[1, frames, lanes])
        v = split(qkv_ref[2, frames, lanes])
        rel = split(rel_ref[:, lanes])
        total = jnp.zeros_like(q)
        for index, mask in enumerate((first, second)):
            scores = dot3(split(content * mask), k, NT) + shift_rows(dot3(split(position * mask), rel, NT))
            scores = scores * (1.0 / math.sqrt(DH)) + bias[pack]
            weights = jnp.exp(scores - jnp.max(scores, axis=-1, keepdims=True))
            weights = weights / jnp.sum(weights, axis=-1, keepdims=True)
            probs_ref[item * 2 + index] = weights
            total = total + dot3(split(weights), v, NN) * mask
        ctx_ref[frames, lanes] = total
        return carry

    lax.fori_loop(0, packs * (H // 2), heads, 0)
    a2_ref[...] = a1_ref[...] + dot3(split(ctx_ref[...]), split(w_ref[3]), NN) + s_ref[14:15]


def attention_forward(length, a1, square, pe, s, segcol, keyrow):
    frames = a1.shape[0]
    packs = frames // length
    vmem = pl.BlockSpec(memory_space=pltpu.VMEM)
    return pl.pallas_call(
        functools.partial(attention_forward_kernel, length),
        in_specs=[vmem] * 6,
        out_specs=[vmem] * 5,
        out_shape=[
            jax.ShapeDtypeStruct((frames, D), f32),
            jax.ShapeDtypeStruct((3, frames, D), f32),
            jax.ShapeDtypeStruct((length, D), f32),
            jax.ShapeDtypeStruct((packs * H, length, length), f32),
            jax.ShapeDtypeStruct((frames, D), f32),
        ],
        scratch_shapes=[pltpu.VMEM((packs, length, length), f32)],
        compiler_params=pltpu.CompilerParams(vmem_limit_bytes=VMEM_LIMIT),
        name="attention_forward",
    )(a1, square, pe, s, segcol, keyrow)


def attention_backward_kernel(
    length, da2_ref, a1_ref, qkv_ref, rel_ref, probs_ref, ctx_ref, w_ref, pe_ref, s_ref, da1_ref, dw_ref, ds_ref, dctx, dqkv, drel, relback, du, dv
):
    packs = a1_ref.shape[0] // length
    row_index = lax.broadcasted_iota(jnp.int32, (length, length), 0)
    lane_index = lax.broadcasted_iota(jnp.int32, (length, length), 1)
    flip = (row_index + lane_index == length - 1).astype(bf16)
    da2 = da2_ref[...]
    da2_split = split(da2)
    ds_ref[...] = jnp.zeros_like(ds_ref)
    ds_ref[2:3] = column_sum(da2)
    dw_ref[3] = dot3(split(ctx_ref[...]), da2_split, TN)
    dctx[...] = dot3(da2_split, split(w_ref[3]), NT)
    rel_split = split(rel_ref[...])
    relback[...] = dot(flip, rel_split[0], NN) + dot(flip, rel_split[1], NN)
    drel[...] = jnp.zeros_like(drel)
    du[...] = jnp.zeros_like(du)
    dv[...] = jnp.zeros_like(dv)
    first, second = pair_masks()

    def heads(item, carry):
        pack, pair = item // (H // 2), item % (H // 2)
        frames = pl.ds(pl.multiple_of(pack * length, length), length)
        lanes = pl.ds(pl.multiple_of(pair * 2 * DH, 2 * DH), 2 * DH)
        q = qkv_ref[0, frames, lanes]
        content = q + s_ref[15:16, lanes]
        position = q + s_ref[16:17, lanes]
        k = qkv_ref[1, frames, lanes]
        v = split(qkv_ref[2, frames, lanes])
        rel = relback[:, lanes]
        dc = dctx[frames, lanes]
        dcontent = jnp.zeros_like(q)
        dposition = jnp.zeros_like(q)
        dkey = jnp.zeros_like(q)
        dvalue = jnp.zeros_like(q)
        drelation = jnp.zeros_like(rel)
        for index, mask in enumerate((first, second)):
            weights = probs_ref[item * 2 + index]
            dc_split = split(dc * mask)
            dvalue = dvalue + dot3(split(weights), dc_split, TN)
            dweights = dot3(dc_split, v, NT)
            dscores = weights * (dweights - jnp.sum(weights * dweights, axis=-1, keepdims=True)) * (1.0 / math.sqrt(DH))
            ds_split = split(dscores)
            dcontent = dcontent + dot3(ds_split, split(k * mask), NN)
            dkey = dkey + dot3(ds_split, split(content * mask), TN)
            shifted = split(shift_rows(dot(ds_split[0], flip, NN) + dot(ds_split[1], flip, NN)))
            dposition = dposition + dot3(shifted, split(rel * mask), NN)
            drelation = drelation + dot3(shifted, split(position * mask), TN)
        dqkv[0, frames, lanes] = dcontent + dposition
        dqkv[1, frames, lanes] = dkey
        dqkv[2, frames, lanes] = dvalue
        drel[:, lanes] += drelation
        du[0:1, lanes] += column_sum(dcontent)
        dv[0:1, lanes] += column_sum(dposition)
        return carry

    lax.fori_loop(0, packs * (H // 2), heads, 0)
    ds_ref[3:4] = du[0:1]
    ds_ref[4:5] = dv[0:1]
    ds_ref[5:6] = column_sum(dqkv[0])
    ds_ref[6:7] = column_sum(dqkv[2])
    xhat, inverse = normalize(a1_ref[...])
    normed = split(xhat * s_ref[2:3] + s_ref[3:4])
    dnormed = jnp.zeros_like(xhat)
    for index in range(3):
        grad = split(dqkv[index])
        dw_ref[index] = dot3(normed, grad, TN)
        dnormed = dnormed + dot3(grad, split(w_ref[index]), NT)
    dw_ref[4] = dot3(split(pe_ref[1]), split(drel[...]), TN)
    ds_ref[0:1] = column_sum(dnormed * xhat)
    ds_ref[1:2] = column_sum(dnormed)
    da1_ref[...] = da2_ref[...] + normalize_back(dnormed * s_ref[2:3], xhat, inverse)


def attention_backward(length, da2, a1, qkv, rel, probs, ctx, square, pe, s):
    frames = a1.shape[0]
    vmem = pl.BlockSpec(memory_space=pltpu.VMEM)
    return pl.pallas_call(
        functools.partial(attention_backward_kernel, length),
        in_specs=[vmem] * 9,
        out_specs=[vmem] * 3,
        out_shape=[
            jax.ShapeDtypeStruct((frames, D), f32),
            jax.ShapeDtypeStruct((5, D, D), f32),
            jax.ShapeDtypeStruct((8, D), f32),
        ],
        scratch_shapes=[
            pltpu.VMEM((frames, D), f32),
            pltpu.VMEM((3, frames, D), f32),
            pltpu.VMEM((length, D), f32),
            pltpu.VMEM((length, D), f32),
            pltpu.VMEM((8, D), f32),
            pltpu.VMEM((8, D), f32),
        ],
        compiler_params=pltpu.CompilerParams(vmem_limit_bytes=VMEM_LIMIT),
        name="attention_backward",
    )(da2, a1, qkv, rel, probs, ctx, square, pe, s)


EDGE = 8
HALF = (K - 1) // 2
STRIP = 64


def convolution_forward_kernel(a2_ref, proj_ref, w_ref, s_ref, match_ref, a3_ref, u_ref, mixed_ref, padded):
    frames = a2_ref.shape[0]
    xhat, _ = normalize(a2_ref[...])
    normed = split(xhat * s_ref[4:5] + s_ref[5:6])
    u_ref[:, :D] = dot3(normed, split(proj_ref[:, :D]), NN) + s_ref[19:20]
    u_ref[:, D:] = dot3(normed, split(proj_ref[:, D:]), NN) + s_ref[20:21]
    padded[0:EDGE] = jnp.zeros((EDGE, D), f32)
    padded[EDGE + frames :] = jnp.zeros((EDGE, D), f32)
    padded[EDGE : EDGE + frames] = u_ref[:, :D] * jax.nn.sigmoid(u_ref[:, D:]) * match_ref[:, K : K + 1]
    for base in range(0, frames, STRIP):
        total = jnp.zeros((STRIP, D), f32) + s_ref[21:22]
        for tap in range(K):
            source = padded[base + EDGE + tap - HALF : base + EDGE + tap - HALF + STRIP]
            total = total + match_ref[base : base + STRIP, tap : tap + 1] * source * s_ref[TAP + tap : TAP + tap + 1]
        mixed_ref[base : base + STRIP] = total
    inner, _ = normalize(mixed_ref[...])
    inner = inner * s_ref[6:7] + s_ref[7:8]
    a3_ref[...] = a2_ref[...] + dot3(split(inner * jax.nn.sigmoid(inner)), split(w_ref[...]), NN) + s_ref[22:23]


def convolution_forward(a2, proj, weight, s, match):
    frames = a2.shape[0]
    vmem = pl.BlockSpec(memory_space=pltpu.VMEM)
    return pl.pallas_call(
        convolution_forward_kernel,
        in_specs=[vmem] * 5,
        out_specs=[vmem] * 3,
        out_shape=[
            jax.ShapeDtypeStruct((frames, D), f32),
            jax.ShapeDtypeStruct((frames, 2 * D), f32),
            jax.ShapeDtypeStruct((frames, D), f32),
        ],
        scratch_shapes=[pltpu.VMEM((frames + 2 * EDGE, D), f32)],
        compiler_params=pltpu.CompilerParams(vmem_limit_bytes=VMEM_LIMIT),
        name="convolution_forward",
    )(a2, proj, weight, s, match)


def convolution_backward_kernel(
    da3_ref, a2_ref, u_ref, mixed_ref, proj_ref, w_ref, s_ref, match_ref, da2_ref, dproj_ref, dw_ref, ds_ref, padded, dpadded, dgated
):
    frames = a2_ref.shape[0]
    da3 = da3_ref[...]
    da3_split = split(da3)
    ds_ref[...] = jnp.zeros_like(ds_ref)
    ds_ref[2:3] = column_sum(da3)
    hat, inverse = normalize(mixed_ref[...])
    inner = hat * s_ref[6:7] + s_ref[7:8]
    sig = jax.nn.sigmoid(inner)
    dw_ref[...] = dot3(split(inner * sig), da3_split, TN)
    dinner = dot3(da3_split, split(w_ref[...]), NT) * (sig * (1.0 + inner * (1.0 - sig)))
    ds_ref[3:4] = column_sum(dinner * hat)
    ds_ref[4:5] = column_sum(dinner)
    dmixed = normalize_back(dinner * s_ref[6:7], hat, inverse)
    ds_ref[5:6] = column_sum(dmixed)
    zeros = jnp.zeros((EDGE, D), f32)
    padded[0:EDGE] = zeros
    padded[EDGE + frames :] = zeros
    padded[EDGE : EDGE + frames] = u_ref[:, :D] * jax.nn.sigmoid(u_ref[:, D:]) * match_ref[:, K : K + 1]
    dpadded[0:EDGE] = zeros
    dpadded[EDGE + frames :] = zeros
    dpadded[EDGE : EDGE + frames] = dmixed
    for base in range(0, frames, STRIP):
        total = jnp.zeros((STRIP, D), f32)
        center = dpadded[base + EDGE : base + EDGE + STRIP]
        for tap in range(K):
            rows = slice(base + EDGE + tap - HALF, base + EDGE + tap - HALF + STRIP)
            match = match_ref[base : base + STRIP, tap : tap + 1]
            total = total + match * dpadded[rows] * s_ref[TAP + K - 1 - tap : TAP + K - tap]
            ds_ref[8 + tap : 9 + tap] += column_sum(center * (match * padded[rows]))
        dgated[base : base + STRIP] = total * match_ref[base : base + STRIP, K : K + 1]
    gate = jax.nn.sigmoid(u_ref[:, D:])
    dfirst = dgated[...] * gate
    dsecond = dfirst * u_ref[:, :D] * (1.0 - gate)
    ds_ref[6:7] = column_sum(dfirst)
    ds_ref[7:8] = column_sum(dsecond)
    xhat, inverse = normalize(a2_ref[...])
    normed = split(xhat * s_ref[4:5] + s_ref[5:6])
    dfirst = split(dfirst)
    dsecond = split(dsecond)
    dproj_ref[:, :D] = dot3(normed, dfirst, TN)
    dproj_ref[:, D:] = dot3(normed, dsecond, TN)
    dnormed = dot3(dfirst, split(proj_ref[:, :D]), NT) + dot3(dsecond, split(proj_ref[:, D:]), NT)
    ds_ref[0:1] = column_sum(dnormed * xhat)
    ds_ref[1:2] = column_sum(dnormed)
    da2_ref[...] = da3_ref[...] + normalize_back(dnormed * s_ref[4:5], xhat, inverse)


def convolution_backward(da3, a2, u, mixed, proj, weight, s, match):
    frames = a2.shape[0]
    vmem = pl.BlockSpec(memory_space=pltpu.VMEM)
    return pl.pallas_call(
        convolution_backward_kernel,
        in_specs=[vmem] * 8,
        out_specs=[vmem] * 4,
        out_shape=[
            jax.ShapeDtypeStruct((frames, D), f32),
            jax.ShapeDtypeStruct((D, 2 * D), f32),
            jax.ShapeDtypeStruct((D, D), f32),
            jax.ShapeDtypeStruct((24, D), f32),
        ],
        scratch_shapes=[
            pltpu.VMEM((frames + 2 * EDGE, D), f32),
            pltpu.VMEM((frames + 2 * EDGE, D), f32),
            pltpu.VMEM((frames, D), f32),
        ],
        compiler_params=pltpu.CompilerParams(vmem_limit_bytes=VMEM_LIMIT),
        name="convolution_backward",
    )(da3, a2, u, mixed, proj, weight, s, match)


def frame_tables(segments, valid_mask):
    packs, length = segments.shape
    position = jnp.arange(length, dtype=jnp.int32)
    columns = []
    for tap in range(K):
        moved = jnp.roll(segments, HALF - tap, axis=1)
        inside = (position + tap - HALF >= 0) & (position + tap - HALF < length)
        columns.append(((moved == segments) & inside[None, :]).astype(f32))
    columns.append(valid_mask.astype(f32))
    match = jnp.stack(columns, axis=-1).reshape(packs * length, K + 1)
    match = jnp.pad(match, ((0, 0), (0, 128 - K - 1)))
    segcol = jnp.broadcast_to(segments.reshape(packs * length, 1), (packs * length, 128))
    keyrow = jnp.pad(jnp.where(valid_mask > 0, segments, -1), ((0, -packs % 8), (0, 0)))
    return match, segcol, keyrow


def small_rows(parts):
    first, attend, conv, second = parts
    return jnp.concatenate(
        [
            first[0:2],
            attend[0:2],
            conv[0:2],
            conv[3:5],
            second[0:2],
            second[8:10],
            attend[5:7],
            attend[2:5],
            first[2:3],
            second[2:3],
            conv[6:8],
            conv[5:6],
            conv[2:3],
            first[4:8],
            second[4:8],
            conv[8 : 8 + K],
        ],
        axis=0,
    )


def layer(inputs, cotangent, segments, valid_mask, weights):
    feed_in, feed_out, square, proj, s = weights
    packs, length, _ = inputs.shape
    frames = packs * length
    x = inputs.reshape(frames, D)
    cot = cotangent.reshape(frames, D)
    match, segcol, keyrow = frame_tables(segments, valid_mask)
    pe = jnp.asarray(sinusoid_table(length))
    a1, u1 = ffn1_forward(x, feed_in[0], feed_out[0], s)
    a2, qkv, rel, probs, ctx = attention_forward(length, a1, square, pe, s, segcol, keyrow)
    a3, u, mixed = convolution_forward(a2, proj, square[5], s, match)
    out, da3, dwin2, dwout2, ds2 = ffn2(a3, cot, feed_in[1], feed_out[1], s)
    da2, dproj, dw5, dsc = convolution_backward(da3, a2, u, mixed, proj, square[5], s, match)
    da1, dw, dsa = attention_backward(length, da2, a1, qkv, rel, probs, ctx, square, pe, s)
    dx, dwin1, dwout1, ds1 = ffn1_backward(da1, x, u1, feed_in[0], feed_out[0], s)
    grads = (dwin1, dwin2), (dwout1, dwout2), (dw, dw5), dproj, small_rows((ds1, dsa, dsc, ds2))
    return out.reshape(inputs.shape), dx.reshape(inputs.shape), grads

MESH_ID = pl.DeviceIdType.MESH


def chip_grid(devices):
    side = 1
    while side * side * 2 * side * 2 < devices:
        side *= 2
    return side, side, 2 * side


class Place:
    def __init__(self, sizes):
        self.fsdp = sizes[1]
        self.y_size, self.x_size, self.z_size = chip_grid(sizes[0] * sizes[1])
        index = lax.axis_index("dp") * sizes[1] + lax.axis_index("fsdp")
        self.index = index
        self.core = lax.rem(index, 2)
        self.z = lax.rem(index // 2, self.z_size)
        self.x = lax.rem(index // (2 * self.z_size), 2)
        self.y = index // (4 * self.z_size)

    def device(self, y=None, x=None, z=None, core=None):
        y = self.y if y is None else y
        x = self.x if x is None else x
        z = self.z if z is None else z
        core = self.core if core is None else core
        index = ((y * 2 + x) * self.z_size + z) * 2 + core
        return index // self.fsdp, lax.rem(index, self.fsdp)

    def neighbour(self, axis):
        if axis == "core":
            return self.device(core=1 - self.core)
        if axis == "x":
            return self.device(x=1 - self.x)
        if axis == "y":
            return self.device(y=1 - self.y)
        return self.device(z=self.z + (1 if axis == "right" else -1))

    def greet(self):
        barrier = pltpu.get_barrier_semaphore()
        for axis in ("core", "x", "y"):
            pl.semaphore_signal(barrier, inc=1, device_id=self.neighbour(axis), device_id_type=MESH_ID)

        @pl.when(self.z > 0)
        def _():
            pl.semaphore_signal(barrier, inc=1, device_id=self.neighbour("left"), device_id_type=MESH_ID)

        @pl.when(self.z < self.z_size - 1)
        def _():
            pl.semaphore_signal(barrier, inc=1, device_id=self.neighbour("right"), device_id_type=MESH_ID)

        pl.semaphore_wait(barrier, self.peers())

    def peers(self):
        return 3 + (self.z > 0).astype(jnp.int32) + (self.z < self.z_size - 1).astype(jnp.int32)


EVERY = slice(None)


class Piece:
    def __init__(self, lead, first_row, rows, zfirst, near):
        self.lead, self.rows, self.zfirst, self.near = lead, pl.ds(first_row, rows), zfirst, near
        self.far = "y" if near == "x" else "x"

    def own(self, shard):
        return shard.at[self.rows] if self.lead is None else shard.at[self.lead, self.rows]

    def blocks(self, full, place, near, far, z, core):
        y, x = (near, far) if self.near == "y" else (far, near)
        index = (y, x, z, core, self.rows)
        return full.at[index] if self.lead is None else full.at[(self.lead,) + index]

    def here(self, place):
        return (place.x, place.y) if self.near == "x" else (place.y, place.x)


G_RIGHT, G_LEFT, G_NEAR, G_FAR, G_CORE = range(5)


class Gather:
    def __init__(self, place, piece, shard, full, send, recv, local):
        self.place, self.piece, self.shard, self.full = place, piece, shard, full
        self.send, self.recv, self.local = send, recv, local

    def view(self, near, far, z, core=None):
        return self.piece.blocks(self.full, self.place, near, far, z, self.place.core if core is None else core)

    def copy(self, kind, z, ref, axis, source=None):
        return pltpu.make_async_remote_copy(
            src_ref=ref if source is None else source,
            dst_ref=ref,
            send_sem=self.send.at[kind, z],
            recv_sem=self.recv.at[G_RIGHT if kind == G_LEFT else kind, z],
            device_id=self.place.neighbour(axis),
            device_id_type=MESH_ID,
        )

    def z_view(self, z):
        near, far = self.piece.here(self.place)
        return self.view(near if self.piece.zfirst else EVERY, far, z)

    def near_view(self, near, z):
        return self.view(near, self.piece.here(self.place)[1], z)

    def far_view(self, far, z):
        return self.view(EVERY, far, z)

    def core_view(self, core, z):
        return self.view(EVERY, EVERY, z, core)

    def own_copy(self):
        near, far = self.piece.here(self.place)
        return pltpu.make_async_copy(self.piece.own(self.shard), self.view(near, far, self.place.z), self.local)

    def begin(self):
        self.own_copy().start()
        if not self.piece.zfirst:
            near, _ = self.piece.here(self.place)
            self.copy(G_NEAR, self.place.z, self.near_view(near, self.place.z), self.piece.near, self.piece.own(self.shard)).start()

    def z_step(self, z, own, from_left):
        place = self.place
        near, far = self.piece.here(place)

        @pl.when(own)
        def _():
            self.own_copy().wait()
            if not self.piece.zfirst:
                self.copy(G_NEAR, z, self.near_view(1 - near, z), self.piece.near).wait_recv()

        @pl.when(jnp.logical_not(own))
        def _():
            self.copy(G_RIGHT, z, self.z_view(z), "left").wait_recv()

        @pl.when((own | from_left) & (place.z < place.z_size - 1))
        def _():
            self.copy(G_RIGHT, z, self.z_view(z), "right").start()

        @pl.when((own | jnp.logical_not(from_left)) & (place.z > 0))
        def _():
            self.copy(G_LEFT, z, self.z_view(z), "left").start()

        if self.piece.zfirst:
            self.copy(G_NEAR, z, self.near_view(near, z), self.piece.near).start()
        else:
            self.copy(G_FAR, z, self.far_view(far, z), self.piece.far).start()

    def near_step(self, z, own, from_left):
        near, far = self.piece.here(self.place)
        self.copy(G_NEAR, z, self.near_view(1 - near, z), self.piece.near).wait_recv()
        self.copy(G_FAR, z, self.far_view(far, z), self.piece.far).start()

    def far_step(self, z, own, from_left):
        _, far = self.piece.here(self.place)
        self.copy(G_FAR, z, self.far_view(1 - far, z), self.piece.far).wait_recv()
        self.copy(G_CORE, z, self.core_view(self.place.core, z), "core").start()

    def stages(self):
        if self.piece.zfirst:
            return [(0, self.z_step), (1, self.near_step), (2, self.far_step)]
        return [(1, self.z_step), (2, self.far_step)]

    def arrive(self):
        for z in range(self.place.z_size):
            self.copy(G_CORE, z, self.core_view(1 - self.place.core, z), "core").wait_recv()

    def drain(self):
        place = self.place
        near, far = self.piece.here(place)
        for z in range(place.z_size):
            self.copy(G_CORE, z, self.core_view(place.core, z), "core").wait_send()
            self.copy(G_FAR, z, self.far_view(far, z), self.piece.far).wait_send()
            if self.piece.zfirst:
                self.copy(G_NEAR, z, self.near_view(near, z), self.piece.near).wait_send()

            @pl.when((place.z < place.z_size - 1) & (z <= place.z))
            def _():
                self.copy(G_RIGHT, z, self.z_view(z), "right").wait_send()

            @pl.when((place.z > 0) & (z >= place.z))
            def _():
                self.copy(G_LEFT, z, self.z_view(z), "left").wait_send()

        if not self.piece.zfirst:
            self.copy(G_NEAR, place.z, self.near_view(near, place.z), self.piece.near).wait_send()


class GatherProgram:
    PARTS = 3

    def __init__(self, place, groups, offsets):
        self.place, self.groups, self.offsets = place, groups, offsets
        self.cursor = 0
        self.length = self.PARTS * (max(offsets) + place.z_size + 2)

    def begin(self):
        for group in self.groups:
            for piece in group:
                piece.begin()

    def part(self, number):
        step, part = number // self.PARTS, lax.rem(number, self.PARTS)
        place = self.place
        for group, offset in zip(self.groups, self.offsets):
            stages = {}
            for piece in group:
                for index, (behind, work) in enumerate(piece.stages()):
                    stages.setdefault((index if piece.piece.zfirst else 2 * index, behind), []).append(work)
            for (index, behind), works in stages.items():
                distance = step - offset - behind
                for from_left in (True, False):
                    z = place.z - distance if from_left else place.z + distance
                    least = 0 if from_left else 1

                    @pl.when((part == index) & (distance >= least) & (distance < place.z_size) & (z >= 0) & (z < place.z_size))
                    def _():
                        for work in works:
                            work(z, distance == 0, jnp.bool_(from_left))

    def run(self, count):
        last = min(self.length, self.cursor + count)
        if last > self.cursor:
            lax.fori_loop(self.cursor, last, lambda number, carry: (self.part(number), carry)[1], 0)
        self.cursor = last

    def run_in(self, index, each):
        def body(number, carry):
            @pl.when(number < self.length)
            def _():
                self.part(number)

            return carry

        lax.fori_loop(self.cursor + index * each, self.cursor + (index + 1) * each, body, 0)

    def skip(self, count):
        self.cursor = min(self.length, self.cursor + count)

    def run_until(self, group):
        self.run(self.PARTS * (self.offsets[group] + self.place.z_size + 2) - self.cursor)
        for piece in self.groups[group]:
            piece.arrive()

    def drain(self):
        self.run(self.length)
        for group in self.groups:
            for piece in group:
                piece.drain()


def halves(rows, zfirst, lead=None):
    return [Piece(lead, 0, rows // 2, zfirst, "x"), Piece(lead, rows // 2, rows // 2, zfirst, "y")]


def whole_shape(shard, sizes):
    y, x, z = chip_grid(sizes[0] * sizes[1])
    return shard.shape[:-2] + (y, x, z, 2) + shard.shape[-2:]


SMALL_LANES = 128


def plans():
    def feed(half):
        return [
            [Piece(pl.ds(half, 1), 0, 8, False, "x"), Piece(pl.ds(half, 1), 8, 8, False, "y")],
            [Piece(pl.ds(half, 1), 0, 32, True, "x"), Piece(pl.ds(half, 1), 32, 32, True, "y")],
        ]

    small = [Piece(None, 0, 16, False, "x")]
    square = [
        Piece(pl.ds(0, 4), 0, 8, False, "x"),
        Piece(pl.ds(0, 4), 8, 8, False, "y"),
        Piece(pl.ds(4, 2), 0, 8, True, "x"),
        Piece(pl.ds(4, 2), 8, 8, True, "y"),
    ]
    return [small] + feed(0), [square, halves(16, True)], feed(1)


def match_table(segments, valid):
    length = segments.shape[1]
    rows = lax.broadcasted_iota(jnp.int32, (128, length), 0)
    position = lax.broadcasted_iota(jnp.int32, (1, length), 1)
    table = jnp.where(rows == K, valid, jnp.where(rows == K + 1, segments, 0.0))
    for tap in range(K):
        moved = segments if tap == HALF else pltpu.roll(segments, (HALF - tap) % length, 1)
        inside = (position + tap - HALF >= 0) & (position + tap - HALF < length)
        table = jnp.where(rows == tap, jnp.where((moved == segments) & inside, 1.0, 0.0), table)
    return table.T


def forward_kernel(sizes, length, offsets, *refs):
    x_ref, seg_ref, valid_ref, pe_ref, small_ref, in_shard, out_shard, sq_shard, conv_shard = refs[:9]
    (a1_out, u1_out, qkv_out, rel_out, probs_out, ctx_out, a2_out, u_out, mixed_out, a3_out, s_out, match_out) = refs[9:21]
    in_full, out_full, sq_full, conv_full, small_full = refs[21:26]
    (a1, u1, qkv, rel, probs, ctx, a2, u, mixed, a3, s_ref, match, normed, padded, bias, small_own, small_whole, win, wout, square, conv) = refs[26:47]
    send, recv, local, loads, stores = refs[47:]
    frames = x_ref.shape[0]
    packs = frames // length

    place = Place(sizes)
    place.greet()
    small_own[...] = jnp.zeros_like(small_own)
    small_own[:, : small_ref.shape[1]] = small_ref[...]
    first, middle, last = plans()
    sources = [
        [(small_own, small_full), (in_shard, in_full), (out_shard, out_full)],
        [(sq_shard, sq_full), (conv_shard, conv_full)],
        [(in_shard, in_full), (out_shard, out_full)],
    ]
    groups, count = [], 0
    for plan, pairs in zip((first, middle, last), sources):
        group = []
        for pieces, (shard, full) in zip(plan, pairs):
            for piece in pieces:
                group.append(Gather(place, piece, shard, full, send.at[count], recv.at[count], local.at[count]))
                count += 1
        groups.append(group)
    program = GatherProgram(place, groups, offsets)
    program.begin()

    spilled = []

    def spill(source, target):
        copy = pltpu.make_async_copy(source, target, stores.at[len(spilled)])
        copy.start()
        spilled.append(copy)

    program.run(3)
    for pack in range(packs):
        rows = slice(pack * length, (pack + 1) * length)
        match[rows] = match_table(seg_ref[pack : pack + 1].astype(f32), valid_ref[pack : pack + 1].astype(f32))
    spill(match, match_out)
    query = lax.broadcasted_iota(jnp.int32, (length, length), 0)
    key = lax.broadcasted_iota(jnp.int32, (length, length), 1)
    for pack in range(packs):
        keyrow = jnp.where(valid_ref[pack : pack + 1] > 0, seg_ref[pack : pack + 1], -1).astype(f32)
        same = match[pack * length : (pack + 1) * length, K + 1 : K + 2] == keyrow
        bias[pack] = jnp.where(same | (query == key), 0.0, -1e30)

    program.run_until(0)
    load_small = pltpu.make_async_copy(small_full, small_whole, loads.at[0])
    load_in = pltpu.make_async_copy(in_full.at[0], win, loads.at[1])
    load_out = pltpu.make_async_copy(out_full.at[0], wout, loads.at[2])
    for load in (load_small, load_in, load_out):
        load.start()
    program.run(1)
    load_small.wait()
    s_ref[...] = small_whole[...].reshape(D, SMALL_LANES).T
    spill(s_ref, s_out)
    xhat, _ = normalize(x_ref[...])
    store_split(normed, xhat * s_ref[0:1] + s_ref[1:2])
    a1[...] = x_ref[...] + 0.5 * s_ref[17:18]
    load_in.wait()
    load_out.wait()
    width = FF // 8

    def chunk(index, carry):
        lanes = pl.ds(pl.multiple_of(index * width, width), width)
        bias_row = s_ref[pl.ds(23 + index // 2, 1), pl.ds(pl.multiple_of(lax.rem(index, 2) * width, width), width)]
        weight = win[:, :, :, :, :, lanes].reshape(D, width)
        value = dot3(load_split(normed), split(weight), NN) + bias_row
        u1[:, lanes] = value
        weight = wout[index // 4, lax.rem(index // 2, 2), pl.ds(lax.rem(index, 2) * 2, 2)].reshape(width, D)
        a1[...] += 0.5 * dot3(split(value * jax.nn.sigmoid(value)), split(weight), NN)
        program.run_in(index, 1)
        return carry

    lax.fori_loop(0, 8, chunk, 0)
    program.skip(8)
    spill(u1, u1_out)
    spill(a1, a1_out)
    xhat, _ = normalize(a1[...])
    store_split(normed, xhat * s_ref[2:3] + s_ref[3:4])

    program.run_until(1)
    load_square = pltpu.make_async_copy(sq_full, square, loads.at[3])
    load_conv = pltpu.make_async_copy(conv_full, conv, loads.at[4])
    load_square.start()
    load_conv.start()
    program.run(1)
    load_square.wait()
    load_conv.wait()

    def weight_split(index):
        return split(square[index].reshape(D, D))

    qkv[0] = dot3(load_split(normed), weight_split(0), NN) + s_ref[12:13]
    program.run(1)
    qkv[1] = dot3(load_split(normed), weight_split(1), NN)
    program.run(1)
    qkv[2] = dot3(load_split(normed), weight_split(2), NN) + s_ref[13:14]
    rel[...] = dot3(split(pe_ref[...]), weight_split(4), NN)
    program.run(1)
    spill(qkv, qkv_out)
    spill(rel, rel_out)
    attend(length, packs, qkv, rel, s_ref, bias, probs, ctx, lambda item: program.run_in(item, 1))
    program.skip(packs * (H // 2))
    spill(probs, probs_out)
    spill(ctx, ctx_out)
    a2[...] = a1[...] + dot3(split(ctx[...]), weight_split(3), NN) + s_ref[14:15]
    spill(a2, a2_out)
    program.run(1)

    xhat, _ = normalize(a2[...])
    store_split(normed, xhat * s_ref[4:5] + s_ref[5:6])
    for half in range(2):
        lanes = slice(half * D, (half + 1) * D)
        u[:, lanes] = dot3(load_split(normed), split(conv[:, :, :, :, :, lanes].reshape(D, D)), NN) + s_ref[19 + half : 20 + half]
        program.run(1)
    spill(u, u_out)
    mix(u, match, s_ref, padded, mixed)
    spill(mixed, mixed_out)
    program.run(1)
    inner, _ = normalize(mixed[...])
    inner = inner * s_ref[6:7] + s_ref[7:8]
    a3[...] = a2[...] + dot3(split(inner * jax.nn.sigmoid(inner)), weight_split(5), NN) + s_ref[22:23]
    spill(a3, a3_out)

    program.run_until(2)
    program.drain()
    for copy in spilled:
        copy.wait()


def head_lanes(pair, index, length):
    return pl.ds(pl.multiple_of((pair * 2 + index) * length, length), length)


def attend(length, packs, qkv_ref, rel_ref, s_ref, bias, probs_ref, ctx_ref, between):
    first, second = pair_masks()

    def heads(item, carry):
        pack, pair = item // (H // 2), lax.rem(item, H // 2)
        frames = pl.ds(pl.multiple_of(pack * length, length), length)
        lanes = pl.ds(pl.multiple_of(pair * 2 * DH, 2 * DH), 2 * DH)
        q = qkv_ref[0, frames, lanes]
        content = q + s_ref[15:16, lanes]
        position = q + s_ref[16:17, lanes]
        k = split(qkv_ref[1, frames, lanes])
        v = split(qkv_ref[2, frames, lanes])
        rel = split(rel_ref[:, lanes])
        total = jnp.zeros_like(q)
        for index, mask in enumerate((first, second)):
            scores = dot3(split(content * mask), k, NT) + shift_rows(dot3(split(position * mask), rel, NT))
            scores = scores * (1.0 / math.sqrt(DH)) + bias[pack]
            weights = jnp.exp(scores - jnp.max(scores, axis=-1, keepdims=True))
            weights = weights / jnp.sum(weights, axis=-1, keepdims=True)
            probs_ref[frames, head_lanes(pair, index, length)] = weights
            total = total + dot3(split(weights), v, NN) * mask
        ctx_ref[frames, lanes] = total
        between(item)
        return carry

    lax.fori_loop(0, packs * (H // 2), heads, 0)


def mix(u_ref, match_ref, s_ref, padded, mixed_ref):
    frames = mixed_ref.shape[0]
    padded[0:EDGE] = jnp.zeros((EDGE, D), f32)
    padded[EDGE + frames :] = jnp.zeros((EDGE, D), f32)
    padded[EDGE : EDGE + frames] = u_ref[:, :D] * jax.nn.sigmoid(u_ref[:, D:]) * match_ref[:, K : K + 1]
    for base in range(0, frames, STRIP):
        total = jnp.zeros((STRIP, D), f32) + s_ref[21:22]
        for tap in range(K):
            source = padded[base + EDGE + tap - HALF : base + EDGE + tap - HALF + STRIP]
            total = total + match_ref[base : base + STRIP, tap : tap + 1] * source * s_ref[TAP + tap : TAP + tap + 1]
        mixed_ref[base : base + STRIP] = total


def forward(sizes, x, segments, valid_mask, weights):
    feed_in, feed_out, square, proj, small = weights
    frames = x.shape[0]
    packs, length = segments.shape
    devices = sizes[0] * sizes[1]
    grid = chip_grid(devices) + (2,)
    z_size = grid[2]
    pe = jnp.asarray(sinusoid_table(length)[0])
    small_rows_here = small.shape[1]
    vmem = pl.BlockSpec(memory_space=pltpu.VMEM)
    kept = [
        (frames, D),
        (frames, FF),
        (3, frames, D),
        (length, D),
        (frames, H * length),
        (frames, D),
        (frames, D),
        (frames, 2 * D),
        (frames, D),
        (frames, D),
        (SMALL_LANES, D),
        (frames, 128),
    ]
    full = [
        (2,) + grid + feed_in.shape[1:],
        (2,) + grid + feed_out.shape[1:],
        (6,) + grid + square.shape[1:],
        grid + proj.shape,
        grid + (small_rows_here, SMALL_LANES),
    ]
    pieces = sum(len(p) for plan in plans() for p in plan)
    outs = pl.pallas_call(
        functools.partial(forward_kernel, sizes, length, GATHER_OFFSETS),
        in_specs=[vmem] * 9,
        out_specs=[pl.BlockSpec(memory_space=pl.ANY)] * (len(kept) + len(full)),
        out_shape=[jax.ShapeDtypeStruct(shape, f32) for shape in kept + full],
        scratch_shapes=[pltpu.VMEM(shape, f32) for shape in kept]
        + [
            pltpu.VMEM((2, frames, D), bf16),
            pltpu.VMEM((frames + 2 * EDGE, D), f32),
            pltpu.VMEM((packs, length, length), f32),
            pltpu.VMEM((small_rows_here, SMALL_LANES), f32),
            pltpu.VMEM(full[4], f32),
            pltpu.VMEM(full[0][1:], f32),
            pltpu.VMEM(full[1][1:], f32),
            pltpu.VMEM(full[2], f32),
            pltpu.VMEM(full[3], f32),
            pltpu.SemaphoreType.DMA((pieces, 5, z_size)),
            pltpu.SemaphoreType.DMA((pieces, 5, z_size)),
            pltpu.SemaphoreType.DMA((pieces,)),
            pltpu.SemaphoreType.DMA((5,)),
            pltpu.SemaphoreType.DMA((len(kept),)),
        ],
        compiler_params=pltpu.CompilerParams(collective_id=0, has_side_effects=True, vmem_limit_bytes=VMEM_LIMIT),
        name="forward",
    )(x, segments, valid_mask, pe, small.T, feed_in, feed_out, square, proj)
    return outs[: len(kept)], outs[len(kept) :]


GATHER_OFFSETS = (0, 3, 6)
S_CORE, S_FAR, S_NEAR, S_FROM_LEFT, S_FROM_RIGHT = range(5)


class Scatter:
    def __init__(self, place, piece, full, out, total, cores, fars, nears, lines, send, recv, local):
        self.place, self.piece, self.full, self.out = place, piece, full, out
        self.total, self.cores, self.fars, self.nears, self.lines = total, cores, fars, nears, lines
        self.send, self.recv, self.local = send, recv, local
        self.near, self.far = piece.here(place)

    def part(self, ref, near, far, z):
        y, x = (near, far) if self.piece.near == "y" else (far, near)
        index = (y, x, z)
        return ref.at[index] if self.piece.lead is None else ref.at[(EVERY,) + index]

    def staged(self, ref, *index):
        return ref.at[index] if self.piece.lead is None else ref.at[(EVERY,) + index]

    def add(self, target, source):
        target[...] = target[...] + source[...]

    def copy(self, kind, z, source, target, axis):
        return pltpu.make_async_remote_copy(
            src_ref=source,
            dst_ref=target,
            send_sem=self.send.at[kind, z],
            recv_sem=self.recv.at[kind, z],
            device_id=self.place.neighbour(axis),
            device_id_type=MESH_ID,
        )

    def core_copy(self, z):
        given = self.piece.blocks(self.full, self.place, EVERY, EVERY, z, 1 - self.place.core)
        return self.copy(S_CORE, z, given, self.part(self.cores, EVERY, EVERY, z), "core")

    def own_copy(self, z):
        kept = self.piece.blocks(self.full, self.place, EVERY, EVERY, z, self.place.core)
        return pltpu.make_async_copy(kept, self.part(self.total, EVERY, EVERY, z), self.local.at[z])

    def far_copy(self, z):
        return self.copy(S_FAR, z, self.part(self.total, EVERY, 1 - self.far, z), self.staged(self.fars, EVERY, z), self.piece.far)

    def near_copy(self, z):
        target = self.staged(self.nears, z if self.piece.zfirst else 0)
        return self.copy(S_NEAR, z, self.part(self.total, 1 - self.near, self.far, z), target, self.piece.near)

    def line_view(self, z):
        return self.part(self.total, self.near if self.piece.zfirst else EVERY, self.far, z)

    def line_staged(self, side, z):
        if self.piece.zfirst:
            return self.staged(self.lines, z + 1 - side)
        return self.staged(self.lines, z + 1 - side, EVERY)

    def line_copy(self, z, to_right):
        kind, side = (S_FROM_LEFT, 0) if to_right else (S_FROM_RIGHT, 1)
        return self.copy(kind, z, self.line_view(z), self.line_staged(side, z), "right" if to_right else "left")

    def begin(self):
        for distance in reversed(range(self.place.z_size)):
            for sign in (-1, 1) if distance else (1,):
                z = self.place.z + sign * distance

                @pl.when((z >= 0) & (z < self.place.z_size))
                def _():
                    self.core_copy(z).start()
                    self.own_copy(z).start()

    def core_step(self, z):
        self.core_copy(z).wait_recv()
        self.own_copy(z).wait()
        self.add(self.part(self.total, EVERY, EVERY, z), self.part(self.cores, EVERY, EVERY, z))

    def core_send(self, z):
        self.far_copy(z).start()

    def far_step(self, z):
        self.far_copy(z).wait_recv()
        self.add(self.part(self.total, EVERY, self.far, z), self.staged(self.fars, EVERY, z))

    def far_send(self, z):
        self.near_copy(z).start()

    def near_step(self, z):
        self.near_copy(z).wait_recv()
        self.add(self.part(self.total, self.near, self.far, z), self.staged(self.nears, z))

    def line_step(self, z):
        here = self.place.z

        @pl.when((z >= here) & (here > 0))
        def _():
            self.line_copy(z, True).wait_recv()
            self.add(self.line_view(z), self.line_staged(0, z))

        @pl.when((z <= here) & (here < self.place.z_size - 1))
        def _():
            self.line_copy(z, False).wait_recv()
            self.add(self.line_view(z), self.line_staged(1, z))

    def line_send(self, z):
        here = self.place.z

        @pl.when(z > here)
        def _():
            self.line_copy(z, True).start()

        @pl.when(z < here)
        def _():
            self.line_copy(z, False).start()

    def last_send(self):
        if not self.piece.zfirst:
            self.near_copy(self.place.z).start()

    def finish(self):
        z = self.place.z
        value = self.part(self.total, self.near, self.far, z)[...]
        if not self.piece.zfirst:
            self.near_copy(z).wait_recv()
            value = value + self.staged(self.nears, 0)[...]
        self.piece.own(self.out)[...] = value

    def drain(self):
        place = self.place
        for z in range(place.z_size):
            self.core_copy(z).wait_send()
            self.far_copy(z).wait_send()
            if self.piece.zfirst:
                self.near_copy(z).wait_send()

            @pl.when(z > place.z)
            def _():
                self.line_copy(z, True).wait_send()

            @pl.when(z < place.z)
            def _():
                self.line_copy(z, False).wait_send()

        if not self.piece.zfirst:
            self.near_copy(place.z).wait_send()


def scatter_stages(scatter):
    stages = [(scatter.core_step, scatter.core_send)]
    if scatter.piece.zfirst:
        return stages + [(scatter.far_step, scatter.far_send), (scatter.near_step, None), (scatter.line_step, scatter.line_send)]
    return stages + [(scatter.far_step, None), (scatter.line_step, scatter.line_send)]


class ScatterProgram:
    def __init__(self, place, scatters, lag):
        self.place, self.scatters = place, scatters
        self.staged = []
        for scatter in scatters:
            behind = 0
            for stage, (work, send) in enumerate(scatter_stages(scatter)):
                self.staged.append((behind, work, send))
                behind += 0 if send is None else lag[min(stage, 1)]
        self.length = max(stage[0] for stage in self.staged) + place.z_size
        self.cursor = 0

    def begin(self):
        for scatter in self.scatters:
            scatter.begin()

    def part(self, step):
        place = self.place
        for behind in sorted({stage[0] for stage in self.staged}, reverse=True):
            distance = place.z_size - 1 - (step - behind)

            def side(right, carry):
                z = jnp.where(right == 1, place.z + distance, place.z - distance)

                @pl.when((z >= 0) & (z < place.z_size))
                def _():
                    for action in (1, 2):
                        for stage in self.staged:
                            if stage[0] == behind and stage[action] is not None:
                                stage[action](z)

                return carry

            @pl.when((distance >= 0) & (distance < place.z_size))
            def _():
                lax.fori_loop(0, jnp.where(distance == 0, 1, 2), side, 0)

    def run(self, count):
        last = min(self.length, self.cursor + count)
        if last > self.cursor:
            lax.fori_loop(self.cursor, last, lambda number, carry: (self.part(number), carry)[1], 0)
        self.cursor = last

    def run_in(self, index, each=1):
        for extra in range(each):
            self.part(self.cursor + index * each + extra)

    def skip(self, count):
        self.cursor = min(self.length, self.cursor + count)

    def last_send(self):
        self.run(self.length)
        for scatter in self.scatters:
            scatter.last_send()

    def finish(self):
        for scatter in self.scatters:
            scatter.finish()
        for scatter in self.scatters:
            scatter.drain()


def scatter_scratch(piece, columns, place_sizes, lead):
    y, x, z = chip_grid(place_sizes[0] * place_sizes[1])
    rows = piece.rows.size
    head = () if piece.lead is None else (lead,)
    return [
        pltpu.VMEM(head + (y, x, z, rows, columns), f32),
        pltpu.VMEM(head + (y, x, z, rows, columns), f32),
        pltpu.VMEM(head + (2, z, rows, columns), f32),
        pltpu.VMEM(head + ((z,) if piece.zfirst else (1,)) + (rows, columns), f32),
        pltpu.VMEM(head + ((z + 1,) if piece.zfirst else (z + 1, 2)) + (rows, columns), f32),
    ]


def greet_all(place, sizes):
    devices = sizes[0] * sizes[1]
    barrier = pltpu.get_barrier_semaphore()

    def signal(offset, carry):
        other = lax.rem(place.index + offset, devices)
        pl.semaphore_signal(barrier, inc=1, device_id=(other // sizes[1], lax.rem(other, sizes[1])), device_id_type=MESH_ID)
        return carry

    lax.fori_loop(1, devices, signal, 0)
    pl.semaphore_wait(barrier, devices - 1)


def square_tile(values):
    squares = values * values
    tile = jnp.zeros((8, 128), f32)
    for r in range(0, values.shape[0], 8):
        for c in range(0, values.shape[1], 128):
            tile = tile + squares[r : r + 8, c : c + 128]
    return tile


def share_norm(place, sizes, outs, norms, own, send, recv):
    devices = sizes[0] * sizes[1]
    tile = jnp.zeros((8, 128), f32)
    for out in outs:
        for lead in range(out.shape[0]) if len(out.shape) == 3 else (None,):
            tile = tile + square_tile(out[...] if lead is None else out[lead])
    own[...] = tile
    norms[place.index] = tile

    def copy(offset, to):
        other = lax.rem(place.index + offset, devices)
        slot = place.index if to else other
        return pltpu.make_async_remote_copy(
            src_ref=own,
            dst_ref=norms.at[slot],
            send_sem=send.at[other],
            recv_sem=recv.at[slot],
            device_id=(other // sizes[1], lax.rem(other, sizes[1])),
            device_id_type=MESH_ID,
        )

    lax.fori_loop(1, devices, lambda offset, carry: (copy(offset, True).start(), carry)[1], 0)
    lax.fori_loop(1, devices, lambda offset, carry: (copy(offset, False).wait_recv(), carry)[1], 0)
    lax.fori_loop(1, devices, lambda offset, carry: (copy(offset, True).wait_send(), carry)[1], 0)


LAG = (1, 1)
WIDTH = FF // 8


def lanes_of(index, width=WIDTH):
    return pl.ds(pl.multiple_of(index * width, width), width)


def hidden_bias(s_ref, first_row, index):
    return s_ref.at[pl.ds(first_row + index // 2, 1), lanes_of(lax.rem(index, 2))]


def in_chunk(ref, index):
    return ref.at[:, :, :, :, :, lanes_of(index)]


def in_target(full, index):
    rows = full.shape[-2] // NC
    return full.at[:, :, :, :, pl.ds(pl.multiple_of(index // 2 * rows, rows), rows), lanes_of(lax.rem(index, 2))]


def out_chunk(ref, index):
    return ref.at[index // 4, lax.rem(index // 2, 2), pl.ds(lax.rem(index, 2) * 2, 2)]


class Copies:
    def __init__(self, semaphores):
        self.semaphores, self.started = semaphores, []

    def start(self, source, target):
        copy = pltpu.make_async_copy(source, target, self.semaphores.at[len(self.started)])
        copy.start()
        self.started.append(copy)
        return copy


class Outbox:
    def __init__(self, slots, semaphores):
        self.slots, self.semaphores = slots, semaphores

    def put(self, index, value, target, columns=None):
        slot = lax.rem(index, 2)
        source = self.slots.at[slot] if columns is None else self.slots.at[slot, :, :, :, :, :, :columns]
        copy = pltpu.make_async_copy(source, target, self.semaphores.at[slot])

        @pl.when(index >= 2)
        def _():
            copy.wait()

        source[...] = value
        copy.start()

    def close(self, count, target, columns=None):
        for index in range(max(0, count - 2), count):
            slot = index % 2
            source = self.slots.at[slot] if columns is None else self.slots.at[slot, :, :, :, :, :, :columns]
            pltpu.make_async_copy(source, target, self.semaphores.at[slot]).wait()


def make_scatters(place, pieces, full, out, scratch, sems, start, first_row=0):
    send, recv, local = sems
    made = []
    for index, piece in enumerate(pieces):
        count = start + index
        arrays = [array.at[(EVERY,) * (len(array.shape) - 2) + (pl.ds(first_row, piece.rows.size),)] for array in scratch[5 * index : 5 * index + 5]]
        made.append(Scatter(place, piece, full, out, *arrays, send.at[count], recv.at[count], local.at[count]))
    return made


class Hand:
    def __init__(self, place, semaphore):
        self.place, self.semaphore = place, semaphore

    def over(self):
        place = self.place

        def signal(axis):
            pl.semaphore_signal(self.semaphore, inc=1, device_id=place.neighbour(axis), device_id_type=MESH_ID)

        for axis in ("core", "x", "y"):
            signal(axis)
        pl.when(place.z > 0)(lambda: signal("left"))
        pl.when(place.z < place.z_size - 1)(lambda: signal("right"))

    def taken(self):
        pl.semaphore_wait(self.semaphore, self.place.peers())


def pieces_scratch(listed, sizes):
    scratch = []
    for pieces, columns in listed:
        for piece in pieces:
            scratch += scatter_scratch(piece, columns, sizes, None if piece.lead is None else piece.lead.size)
    return scratch


def feed_out_pass(index, hidden, df, box, out_full):
    u = hidden[:, lanes_of(index)]
    value = dot3(split(u * jax.nn.sigmoid(u)), load_split(df), TN)
    box.put(index, value.reshape(2, 2, 64, D), out_chunk(out_full, index))


def feed_in_pass(index, hidden, df, normed, win, wout, total, ds_ref, first_row, box, grid, in_full):
    u = hidden[:, lanes_of(index)]
    sig = jax.nn.sigmoid(u)
    weight = split(out_chunk(wout, index)[...].reshape(WIDTH, D))
    du = dot3(load_split(df), weight, NT) * (sig * (1.0 + u * (1.0 - sig)))
    hidden_bias(ds_ref, first_row, index)[...] = column_sum(du)
    du = split(du)
    weight = split(in_chunk(win, index)[...].reshape(D, WIDTH))
    total[...] += dot3(du, weight, NT)
    value = dot3(load_split(normed), du, TN)
    box.put(index, value.reshape(grid + (D // math.prod(grid), WIDTH)), in_target(in_full, index), WIDTH)


def attend_back_values(length, packs, dctx_turned, probs_ref, grads):
    def heads(item, carry):
        pack, pair = item // (H // 2), lax.rem(item, H // 2)
        frames = pl.ds(pl.multiple_of(pack * length, length), length)
        values = []
        for index in range(2):
            rows = pl.ds(pl.multiple_of(pair * 2 * DH + index * DH, DH), DH)
            weights = probs_ref[frames, head_lanes(pair, index, length)]
            values.append((rows, dot3(split(dctx_turned[rows, frames]), split(weights), NN)))
        for rows, value in values:
            grads[2, rows, frames] = value
        return carry

    lax.fori_loop(0, packs * (H // 2), heads, 0)


def attend_back(length, packs, turned, qkv_ref, dctx_ref, probs_ref, s_turned, flip, grads, drel_ref, sums_ref, between):
    q_ref, k_ref, rel_ref = turned
    lane = lax.broadcasted_iota(jnp.int32, (1, 128), 1)

    def heads(item, carry):
        between(item)
        pack, pair = item // (H // 2), lax.rem(item, H // 2)
        frames = pl.ds(pl.multiple_of(pack * length, length), length)
        lanes = pl.ds(pl.multiple_of(pair * 2 * DH, 2 * DH), 2 * DH)
        v = split(qkv_ref[2, frames, lanes])
        dc = dctx_ref[frames, lanes]
        both = []
        for index, mask in enumerate(pair_masks()):
            rows = pl.ds(pl.multiple_of(pair * 2 * DH + index * DH, DH), DH)
            weights = probs_ref[frames, head_lanes(pair, index, length)]
            q = q_ref[rows, frames]
            content, position = q + s_turned[rows, 15:16], q + s_turned[rows, 16:17]
            both.append((rows, weights, dc * mask, content, position, k_ref[rows, frames], rel_ref[rows]))
        dweights = [dot3(split(head[2]), v, NT) for head in both]
        dscores = [
            split(head[1] * (grad - jnp.sum(head[1] * grad, axis=-1, keepdims=True)) * (1.0 / math.sqrt(DH)))
            for head, grad in zip(both, dweights)
        ]
        flipped = [dot(grad[0], flip, NN) + dot(grad[1], flip, NN) for grad in dscores]
        dcontent = [dot3(split(head[5]), grad, NT) for head, grad in zip(both, dscores)]
        shifted = [split(shift_rows(grad)) for grad in flipped]
        dkey = [dot3(split(head[3]), grad, NN) for head, grad in zip(both, dscores)]
        dposition = [dot3(split(head[6]), grad, NT) for head, grad in zip(both, shifted)]
        drelation = [dot3(split(head[4]), grad, NN) for head, grad in zip(both, shifted)]
        for index, head in enumerate(both):
            rows = head[0]
            grads[1, rows, frames] = dkey[index]
            grads[0, rows, frames] = dcontent[index] + dposition[index]
            drel_ref[rows] += drelation[index]
            sum_u = jnp.sum(dcontent[index], axis=1, keepdims=True)
            sum_v = jnp.sum(dposition[index], axis=1, keepdims=True)
            sums_ref[rows] += jnp.where(lane == 0, sum_u, jnp.where(lane == 1, sum_v, 0.0))
        return carry

    lax.fori_loop(0, packs * (H // 2), heads, 0)


def group_pieces(rows, near, first_row=0):
    far = "y" if near == "x" else "x"
    return [Piece(None, first_row, rows // 2, True, near), Piece(None, first_row + rows // 2, rows // 2, False, far)]


def small_pieces():
    return [Piece(None, 0, 16, False, "x")]


def run_together(programs, count):
    starts = [program.cursor for program in programs]

    def body(step, carry):
        for program, start in zip(programs, starts):
            program.part(start + step)
        return carry

    lax.fori_loop(0, count, body, 0)
    for program in programs:
        program.skip(count)


def backward_kernel(sizes, length, *refs):
    (cot_in, x_in, a3_in, a2_in, a1_in, u1_in, qkv_in, rel_in, probs_in, ctx_in, u_in, mixed_in, s_in, match_in, pe_in) = refs[:15]
    in_all, out_all, sq_all, conv_all = refs[15:19]
    out_out, dx_out, in_full2, out_full2, conv_full, sq_full, in_full1, out_full1 = refs[19:27]
    g_in1, g_in2, g_out1, g_out2, g_sq, g_conv, g_small, norms = refs[27:35]
    (da3, a2, mixed, ctx, a1, u, conv, square, qkv, rel, hidden, s_ref, match, ds_ref, normed, df, box_in, box_out, small_full) = refs[35:54]
    scratch_one, scratch_two, scratch_three, scratch_small = refs[54:64], refs[64:74], refs[74:84], refs[84:89]
    send, recv, local, loads, stores, box_sems, free, norm_own, norm_send, norm_recv = refs[89:]
    frames = da3.shape[0]
    packs = frames // length
    grid = chip_grid(sizes[0] * sizes[1]) + (2,)
    place = Place(sizes)
    loading, storing = Copies(loads), Copies(stores)
    sems = (send, recv, local)

    def program(*parts):
        scatters = []
        for pieces, full, out, scratch, start, first_row in parts:
            scatters += make_scatters(place, pieces, full, out, scratch, sems, start, first_row)
        return ScatterProgram(place, scatters, LAG)

    def group(full, out, near, scratch, start):
        return group_pieces(out.shape[0], near), full, out, scratch, start, 0

    def half_group(half, full, out, near, scratch, start):
        rows = out.shape[0] // 2
        return group_pieces(rows, near, half * rows), full, out, scratch, start, half * rows // 2

    out_program2 = program(group(out_full2, g_out2, "x", scratch_one, 0))
    in_program2 = program(group(in_full2, g_in2, "y", scratch_two, 2))
    conv_program = program(group(conv_full, g_conv, "x", scratch_three, 4))
    sq_program = program(group(sq_full, g_sq, "y", scratch_one, 6))
    out_program1 = program(group(out_full1, g_out1, "x", scratch_two, 8))
    early_program1 = program(half_group(0, in_full1, g_in1, "y", scratch_three, 10))
    late_program1 = program(half_group(1, in_full1, g_in1, "x", scratch_three, 12), (small_pieces(), small_full, g_small, scratch_small, 14, 0))
    hand_one, hand_two, hand_three = (Hand(place, free.at[index]) for index in range(3))
    in_outbox = Outbox(box_in, box_sems.at[0])
    out_outbox = Outbox(box_out, box_sems.at[1])
    slots = in_outbox.slots
    cot, result, a3, da4 = ctx, a1, a2, qkv.at[0]
    side = max(frames, D)
    q_turned, k_turned = u.at[:D, :frames], u.at[:D, side : side + frames]
    u = u.at[:frames, : 2 * D]

    def put(slot, value, full, matrix):
        rows = slots.shape[-2]
        target = full.at[:, :, :, :, pl.ds(matrix * rows, rows)]
        slots[slot] = value.reshape(box_in.shape[1:])
        return storing.start(slots.at[slot], target)

    def second_module(win, wout):
        waits = [
            loading.start(source, target)
            for source, target in ((s_in, s_ref), (a3_in, a3), (in_all.at[1], win), (out_all.at[1], wout), (cot_in, cot))
        ]
        greet_all(place, sizes)
        waits[0].wait()
        waits[1].wait()
        later = [
            loading.start(source, target)
            for source, target in (
                (match_in, match),
                (mixed_in, mixed),
                (sq_all, square),
                (u_in, u),
                (conv_all, conv),
                (rel_in, rel),
            )
        ]
        ds_ref[...] = jnp.zeros_like(ds_ref)
        xhat, _ = normalize(a3[...])
        store_split(normed, xhat * s_ref[8:9] + s_ref[9:10])
        da4[...] = a3[...] + 0.5 * s_ref[18:19]
        waits[2].wait()
        waits[3].wait()

        def forward_chunk(index, carry):
            weight = in_chunk(win, index)[...].reshape(D, WIDTH)
            value = dot3(load_split(normed), split(weight), NN) + hidden_bias(s_ref, 23 + NC, index)[...]
            hidden[:, lanes_of(index)] = value
            weight = out_chunk(wout, index)[...].reshape(WIDTH, D)
            da4[...] += 0.5 * dot3(split(value * jax.nn.sigmoid(value)), split(weight), NN)
            return carry

        lax.fori_loop(0, 8, forward_chunk, 0)
        waits[4].wait()
        xhat, inverse = normalize(da4[...])
        result[...] = xhat * s_ref[10:11] + s_ref[11:12]
        store_result = storing.start(result, out_out)
        grad = cot[...]
        ds_ref[10:11] = column_sum(grad * xhat)
        ds_ref[11:12] = column_sum(grad)
        grad = normalize_back(grad * s_ref[10:11], xhat, inverse)
        da4[...] = grad
        half = 0.5 * grad
        store_split(df, half)
        ds_ref[18:19] = column_sum(half)
        da3[...] = jnp.zeros_like(da3)
        later.append(loading.start(ctx_in, ctx))

        def out_pass(index, carry):
            feed_out_pass(index, hidden, df, out_outbox, out_full2)
            return carry

        lax.fori_loop(0, 8, out_pass, 0)
        out_outbox.close(8, out_chunk(out_full2, 0))
        out_program2.begin()
        store_result.wait()
        later.append(loading.start(a1_in, a1))

        def in_pass(index, carry):
            feed_in_pass(index, hidden, df, normed, win, wout, da3, ds_ref, 23 + NC, in_outbox, grid, in_full2)

            @pl.when(lax.rem(index, 4) == 3)
            def _():
                out_program2.run_in(index // 4)

            return carry

        lax.fori_loop(0, 8, in_pass, 0)
        out_program2.skip(2)
        in_outbox.close(8, in_target(in_full2, 0), WIDTH)
        in_program2.begin()
        xhat, inverse = normalize(a3[...])
        dn = da3[...]
        ds_ref[8:9] = column_sum(dn * xhat)
        ds_ref[9:10] = column_sum(dn)
        da3[...] = da4[...] + normalize_back(dn * s_ref[8:9], xhat, inverse)
        for copy in later:
            copy.wait()

    piece = pltpu.VMEM((frames, D), f32)
    feed_weights = (pltpu.VMEM(grid + (D // math.prod(grid), FF), f32), pltpu.VMEM(grid + (FF // math.prod(grid), D), f32))
    pl.run_scoped(second_module, *feed_weights)
    load_a2 = loading.start(a2_in, a2)
    load_qkv = loading.start(qkv_in, qkv)
    probs = hidden.at[:, : probs_in.shape[1]]
    load_probs = loading.start(probs_in, probs)

    def convolution(padded, dpadded, dgated):
        da3_split = split(da3[...])
        ds_ref[22:23] = column_sum(da3[...])
        hat, inverse = normalize(mixed[...])
        inner = hat * s_ref[6:7] + s_ref[7:8]
        sig = jax.nn.sigmoid(inner)
        store_square = put(0, dot3(split(inner * sig), da3_split, TN), conv_full, 2)
        dinner = dot3(da3_split, split(square[5].reshape(D, D)), NT) * (sig * (1.0 + inner * (1.0 - sig)))
        ds_ref[6:7] = column_sum(dinner * hat)
        ds_ref[7:8] = column_sum(dinner)
        dmixed = normalize_back(dinner * s_ref[6:7], hat, inverse)
        ds_ref[21:22] = column_sum(dmixed)
        zeros = jnp.zeros((EDGE, D), f32)
        padded[0:EDGE] = zeros
        padded[EDGE + frames :] = zeros
        padded[EDGE : EDGE + frames] = u[:, :D] * jax.nn.sigmoid(u[:, D:]) * match[:, K : K + 1]
        dpadded[0:EDGE] = zeros
        dpadded[EDGE + frames :] = zeros
        dpadded[EDGE : EDGE + frames] = dmixed
        run_together((out_program2, in_program2), 1)
        for base in range(0, frames, STRIP):
            total = jnp.zeros((STRIP, D), f32)
            center = dpadded[base + EDGE : base + EDGE + STRIP]
            for tap in range(K):
                rows = slice(base + EDGE + tap - HALF, base + EDGE + tap - HALF + STRIP)
                same = match[base : base + STRIP, tap : tap + 1]
                total = total + same * dpadded[rows] * s_ref[TAP + K - 1 - tap : TAP + K - tap]
                ds_ref[TAP + tap : TAP + tap + 1] += column_sum(center * (same * padded[rows]))
            dgated[base : base + STRIP] = total * match[base : base + STRIP, K : K + 1]
        out_program2.run(1)
        gate = jax.nn.sigmoid(u[:, D:])
        dfirst = dgated[...] * gate
        dsecond = dfirst * u[:, :D] * (1.0 - gate)
        ds_ref[19:20] = column_sum(dfirst)
        ds_ref[20:21] = column_sum(dsecond)
        dfirst, dsecond = split(dfirst), split(dsecond)
        load_a2.wait()
        xhat, inverse = normalize(a2[...])
        store_split(normed, xhat * s_ref[4:5] + s_ref[5:6])
        store_square.wait()
        stored = [put(half, dot3(load_split(normed), grad, TN), conv_full, half) for half, grad in enumerate((dfirst, dsecond))]
        dn = dot3(dfirst, split(conv[:, :, :, :, :, :D].reshape(D, D)), NT) + dot3(dsecond, split(conv[:, :, :, :, :, D:].reshape(D, D)), NT)
        ds_ref[4:5] = column_sum(dn * xhat)
        ds_ref[5:6] = column_sum(dn)
        da3[...] = da3[...] + normalize_back(dn * s_ref[4:5], xhat, inverse)
        for copy in stored:
            copy.wait()
        run_together((out_program2, in_program2), 1)

    padded = pltpu.VMEM((frames + 2 * EDGE, D), f32)
    pl.run_scoped(convolution, padded, padded, piece)
    load_x = loading.start(x_in, a2)
    dn_ref = mixed

    def attention(dqkv, dctx_turned, dctx, relback, drel, row_sums, s_turned):
        da2_split = split(da3[...])
        ds_ref[14:15] = column_sum(da3[...])
        stored = [put(0, dot3(split(ctx[...]), da2_split, TN), conv_full, 3)]
        dctx[...] = dot3(da2_split, split(square[3].reshape(D, D)), NT)
        dctx_turned[...] = dctx[...].T
        xhat, _ = normalize(a1[...])
        store_split(normed, xhat * s_ref[2:3] + s_ref[3:4])
        load_probs.wait()
        attend_back_values(length, packs, dctx_turned, probs, dqkv)
        grad = dqkv[2].T
        ds_ref[13:14] = column_sum(grad)
        grad = split(grad)
        stored.append(put(1, dot3(load_split(normed), grad, TN), conv_full, 4))
        dn_ref[...] = dot3(grad, split(square[2].reshape(D, D)), NT)
        run_together((out_program2, in_program2), 1)
        out_program2.last_send()
        row_index = lax.broadcasted_iota(jnp.int32, (length, length), 0)
        lane_index = lax.broadcasted_iota(jnp.int32, (length, length), 1)
        flip = (row_index + lane_index == length - 1).astype(bf16)
        rel_split = split(rel[...])
        relback[...] = (dot(flip, rel_split[0], NN) + dot(flip, rel_split[1], NN)).T
        load_qkv.wait()
        q_turned[...] = qkv[0].T
        k_turned[...] = qkv[1].T
        s_turned[...] = s_ref[...].T
        drel[...] = jnp.zeros_like(drel)
        row_sums[...] = jnp.zeros_like(row_sums)
        load_pe = loading.start(pe_in, rel)
        for copy in stored:
            copy.wait()
        conv_program.begin()

        def between(item):
            @pl.when(lax.rem(item, 4) == 1)
            def _():
                in_program2.run_in(item // 4)

            @pl.when(lax.rem(item, 4) == 3)
            def _():
                conv_program.run_in(item // 4)

        attend_back(length, packs, (q_turned, k_turned, relback), qkv, dctx, probs, s_turned, flip, dqkv, drel, row_sums, between)
        conv_program.skip(2)
        in_program2.skip(2)
        in_program2.last_send()
        loading.start(u1_in, hidden.at[:, : u1_in.shape[1]])
        out_program2.finish()
        hand_one.over()
        ds_ref[15:17] = row_sums[...].T[0:2]
        stored = []
        for index in range(2):
            grad = dqkv[index].T
            if index == 0:
                ds_ref[12:13] = column_sum(grad)
            grad = split(grad)
            stored.append(put(index, dot3(load_split(normed), grad, TN), sq_full, index))
            dn_ref[...] += dot3(grad, split(square[index].reshape(D, D)), NT)
        conv_program.run(1)
        in_program2.finish()
        hand_two.over()
        load_pe.wait()
        stored[0].wait()
        stored.append(put(0, dot3(split(rel[...]), split(drel[...].T), TN), sq_full, 2))
        xhat, inverse = normalize(a1[...])
        dn = dn_ref[...]
        ds_ref[2:3] = column_sum(dn * xhat)
        ds_ref[3:4] = column_sum(dn)
        da3[...] = da3[...] + normalize_back(dn * s_ref[2:3], xhat, inverse)
        for copy in stored[1:]:
            copy.wait()

    features = pltpu.VMEM((D, frames), f32)
    positions = pltpu.VMEM((D, length), f32)
    pl.run_scoped(
        attention,
        pltpu.VMEM((3, D, frames), f32),
        features,
        piece,
        positions,
        positions,
        pltpu.VMEM((D, 128), f32),
        pltpu.VMEM((D, SMALL_LANES), f32),
    )

    x, dx = a2, mixed

    def first_module(win, wout):
        waits = [loading.start(in_all.at[0], win), loading.start(out_all.at[0], wout)]
        hand_one.taken()
        sq_program.begin()
        load_x.wait()
        xhat, _ = normalize(x[...])
        store_split(normed, xhat * s_ref[0:1] + s_ref[1:2])
        half = 0.5 * da3[...]
        store_split(df, half)
        ds_ref[17:18] = column_sum(half)
        dx[...] = jnp.zeros_like(dx)
        pltpu.make_async_copy(u1_in, hidden.at[:, : u1_in.shape[1]], loads.at[18]).wait()

        def out_pass(index, carry):
            feed_out_pass(index, hidden, df, out_outbox, out_full1)

            return carry

        lax.fori_loop(0, 8, out_pass, 0)
        out_outbox.close(8, out_chunk(out_full1, 0))
        hand_two.taken()
        out_program1.begin()
        run_together((conv_program, sq_program), 1)
        for copy in waits:
            copy.wait()

        def in_pass(index, carry):
            feed_in_pass(index, hidden, df, normed, win, wout, dx, ds_ref, 23, in_outbox, grid, in_full1)

            @pl.when(lax.rem(index, 2) == 0)
            def _():
                conv_program.run_in(index // 2)
                out_program1.run_in(index // 2)

            @pl.when(lax.rem(index, 2) == 1)
            def _():
                sq_program.run_in(index // 2)

            @pl.when(index == 5)
            def _():
                for scatter in conv_program.scatters:
                    scatter.last_send()
                conv_program.finish()
                hand_three.over()
                hand_three.taken()
                early_program1.begin()

            return carry

        lax.fori_loop(0, 8, in_pass, 0)
        for running in (sq_program, out_program1):
            running.skip(4)
        in_outbox.close(8, in_target(in_full1, 0), WIDTH)

    pl.run_scoped(first_module, *feed_weights)
    xhat, inverse = normalize(x[...])
    dn = dx[...]
    ds_ref[0:1] = column_sum(dn * xhat)
    ds_ref[1:2] = column_sum(dn)
    small_full[...] = ds_ref[...].T.reshape(small_full.shape)
    late_program1.begin()
    dx[...] = da3[...] + normalize_back(dn * s_ref[0:1], xhat, inverse)
    store_dx = storing.start(dx, dx_out)
    run_together((sq_program, out_program1, early_program1), 1)
    run_together((sq_program, out_program1, early_program1, late_program1), 1)
    sq_program.last_send()
    out_program1.last_send()
    run_together((early_program1, late_program1), 3)
    early_program1.last_send()
    late_program1.last_send()
    for ending in (sq_program, out_program1, early_program1, late_program1):
        ending.finish()
    share_norm(place, sizes, (g_in1, g_in2, g_out1, g_out2, g_sq, g_conv, g_small), norms, norm_own, norm_send, norm_recv)
    store_dx.wait()


def backward(sizes, length, cot, x, saved, full):
    a1, u1, qkv, rel, probs, ctx, a2, u, mixed, a3, s, match = saved
    in_all, out_all, sq_all, conv_all, _ = full
    frames = cot.shape[0]
    grid = chip_grid(sizes[0] * sizes[1]) + (2,)
    z_size = grid[2]
    devices = math.prod(grid)
    pe = jnp.asarray(sinusoid_table(length)[1])
    rows = D // devices
    hbm, vmem = pl.BlockSpec(memory_space=pl.ANY), pl.BlockSpec(memory_space=pltpu.VMEM)
    piece = (frames, D)
    shapes = [
        piece,
        piece,
        grid + (NC * rows, D),
        grid + (NC * rows, D),
        grid + (5 * rows, D),
        grid + (3 * rows, D),
        grid + (NC * rows, D),
        grid + (NC * rows, D),
        (NC * rows, D),
        (NC * rows, D),
        (NC * rows, D),
        (NC * rows, D),
        (3 * rows, D),
        (5 * rows, D),
        (rows, SMALL_LANES),
        (devices, 8, 128),
    ]
    listed = [(group_pieces(count * rows, "x"), D) for count in (NC, NC, 5)] + [(small_pieces(), SMALL_LANES)]
    return pl.pallas_call(
        functools.partial(backward_kernel, sizes, length),
        in_specs=[hbm] * 19,
        out_specs=[hbm] * 8 + [vmem] * 8,
        out_shape=[jax.ShapeDtypeStruct(shape, f32) for shape in shapes],
        scratch_shapes=[pltpu.VMEM(piece, f32)] * 5
        + [
            pltpu.VMEM((max(frames, D), 2 * max(frames, D)), f32),
            pltpu.VMEM(grid + (rows, 2 * D), f32),
            pltpu.VMEM((6,) + grid + (rows, D), f32),
            pltpu.VMEM((3, frames, D), f32),
            pltpu.VMEM((length, D), f32),
            pltpu.VMEM((frames, max(FF, H * length)), f32),
            pltpu.VMEM((SMALL_LANES, D), f32),
            pltpu.VMEM((frames, 128), f32),
            pltpu.VMEM((SMALL_LANES, D), f32),
            pltpu.VMEM((2, frames, D), bf16),
            pltpu.VMEM((2, frames, D), bf16),
            pltpu.VMEM((2,) + grid + (rows, D), f32),
            pltpu.VMEM((2, 2, 2, FF // devices, D), f32),
            pltpu.VMEM(grid + (rows, SMALL_LANES), f32),
        ]
        + pieces_scratch(listed, sizes)
        + [
            pltpu.SemaphoreType.DMA((15, 5, z_size)),
            pltpu.SemaphoreType.DMA((15, 5, z_size)),
            pltpu.SemaphoreType.DMA((15, z_size)),
            pltpu.SemaphoreType.DMA((24,)),
            pltpu.SemaphoreType.DMA((10,)),
            pltpu.SemaphoreType.DMA((2, 2)),
            pltpu.SemaphoreType.REGULAR((3,)),
            pltpu.VMEM((8, 128), f32),
            pltpu.SemaphoreType.DMA((devices,)),
            pltpu.SemaphoreType.DMA((devices,)),
        ],
        compiler_params=pltpu.CompilerParams(collective_id=1, has_side_effects=True, vmem_limit_bytes=VMEM_TOP),
        name="backward",
    )(cot, x, a3, a2, a1, u1, qkv, rel, probs, ctx, u, mixed, s, match, pe, in_all, out_all, sq_all, conv_all)


def adamw_kernel(step_ref, norms_ref, *refs):
    (g_in1, g_in2, g_out1, g_out2, g_sq, g_conv, g_small), refs = refs[:7], refs[7:]
    weights, firsts, seconds, outs = refs[0:5], refs[5:10], refs[10:15], refs[16:]
    norm = jnp.sqrt(jnp.sum(norms_ref[...], axis=(0, 1, 2), keepdims=True)[0])
    refs[15][...] = norm
    clip = jnp.minimum(1.0, CLIP_NORM / (norm + 1e-06))

    def geometric(_, carry):
        one, one_power, two, two_power = carry
        return one + one_power, one_power * BETA_ONE, two + two_power, two_power * BETA_TWO

    zero, unit = jnp.float32(0.0), jnp.float32(1.0)
    one, _, two, _ = lax.fori_loop(0, step_ref[0], geometric, (zero, unit, zero, unit))
    first_scale = jnp.full((1, 1), (1.0 - BETA_ONE) * one, f32)
    second_scale = jnp.full((1, 1), (1.0 - BETA_TWO) * two, f32)
    first_scale = 1.0 / first_scale
    second_scale = 1.0 / second_scale

    def update(number, index, gradient, rate, decay):
        weight, first, second = weights[number][index], firsts[number][index], seconds[number][index]
        clipped = clip * gradient
        first_next = BETA_ONE * first + (1.0 - BETA_ONE) * clipped
        second_next = BETA_TWO * second + (1.0 - BETA_TWO) * clipped * clipped
        step = (first_next * first_scale) / (jnp.sqrt(second_next * second_scale) + ADAM_EPS)
        if decay:
            step = step + decay * weight
        outs[3 * number][index] = first_next
        outs[3 * number + 1][index] = second_next
        outs[3 * number + 2][index] = weight - rate * step

    rows = weights[0].shape[1]

    def block(ref, index):
        return ref[index * rows : (index + 1) * rows]

    for half, (g_in, g_out) in enumerate(((g_in1, g_out1), (g_in2, g_out2))):
        for index in range(NC):
            update(0, (half, EVERY, slice(index * D, (index + 1) * D)), block(g_in, index), MATRIX_RATE, MATRIX_DECAY)
        update(1, half, g_out[...], MATRIX_RATE, MATRIX_DECAY)
    for index, (ref, place) in enumerate(((g_sq, 0), (g_sq, 1), (g_conv, 4), (g_conv, 3), (g_sq, 2), (g_conv, 2))):
        update(2, index, block(ref, place), MATRIX_RATE, MATRIX_DECAY)
    for half in range(2):
        update(3, (EVERY, slice(half * D, (half + 1) * D)), block(g_conv, half), MATRIX_RATE, MATRIX_DECAY)
    update(4, EVERY, g_small[:, : weights[4].shape[1]], VECTOR_RATE, 0.0)


def adamw(step, norms, grads, weights, firsts, seconds):
    vmem = pl.BlockSpec(memory_space=pltpu.VMEM)
    shapes = [jax.ShapeDtypeStruct((1, 1), f32)]
    for weight in weights:
        shapes += [jax.ShapeDtypeStruct(weight.shape, f32)] * 3
    return pl.pallas_call(
        adamw_kernel,
        in_specs=[pl.BlockSpec(memory_space=pltpu.SMEM)] + [vmem] * 23,
        out_specs=[vmem] * 16,
        out_shape=shapes,
        compiler_params=pltpu.CompilerParams(vmem_limit_bytes=VMEM_LIMIT),
        name="adamw",
    )(step, norms, *grads, *weights, *firsts, *seconds)


AXES = ("dp", "fsdp")


def gather_plain(feed_in, feed_out, square, proj, small):
    feed_in = lax.all_gather(feed_in, AXES, axis=1, tiled=True)
    feed_out = lax.all_gather(feed_out, AXES, axis=1, tiled=True)
    square = lax.all_gather(square, AXES, axis=1, tiled=True)
    proj = lax.all_gather(proj, AXES, axis=0, tiled=True)
    small = lax.all_gather(small, AXES, axis=1, tiled=True)
    return feed_in, feed_out, square, proj, small


def scatter_plain(grads):
    (in1, in2), (out1, out2), (dw, dw5), dproj, ds = grads

    def reduce(matrices):
        part = lax.psum_scatter(jnp.stack(matrices), AXES, scatter_dimension=1, tiled=True)
        return part.reshape(-1, D)

    def quarters(matrix):
        return [matrix[:, index * D : (index + 1) * D] for index in range(NC)]

    parts = [
        reduce(quarters(in1)),
        reduce(quarters(in2)),
        lax.psum_scatter(out1, AXES, scatter_dimension=0, tiled=True),
        lax.psum_scatter(out2, AXES, scatter_dimension=0, tiled=True),
        reduce([dw[0], dw[1], dw[4]]),
        reduce([dproj[:, :D], dproj[:, D:], dw5, dw[3], dw[2]]),
        lax.psum_scatter(ds.T, AXES, scatter_dimension=0, tiled=True),
    ]
    total = lax.psum(sum(jnp.sum(part * part) for part in parts), AXES)
    return tuple(parts), jnp.zeros((1, 8, 128), f32).at[0, 0, 0].set(total)


def overlapped_layer(sizes, inputs, cotangent, segments, valid_mask, weights):
    packs, length, _ = inputs.shape
    frames = packs * length
    x = inputs.reshape(frames, D)
    saved, full = forward(sizes, x, segments, valid_mask, weights)
    outs = backward(sizes, length, cotangent.reshape(frames, D), x, saved, full)
    out, dx, grads, norms = outs[0], outs[1], outs[8:15], outs[15]
    return out.reshape(inputs.shape), dx.reshape(inputs.shape), grads, norms


def local(sizes, inputs, cotangent, segments, valid_mask, step_count, *state):
    weights, moments = state[:5], state[5:]
    devices = sizes[0] * sizes[1]
    if D // devices % 16 == 0 and chip_grid(devices)[:2] == (2, 2):
        out, dx, grads, norms = overlapped_layer(sizes, inputs, cotangent, segments, valid_mask, weights)
    else:
        out, dx, grads = layer(inputs, cotangent, segments, valid_mask, gather_plain(*weights))
        grads, norms = scatter_plain(grads)

    def turned(values):
        return tuple(values[:-1]) + (values[-1].T,)

    norm, *updated = adamw(step_count, norms, grads, turned(weights), turned(moments[0::2]), turned(moments[1::2]))
    return (out, dx, norm.reshape(()), *updated[:-3], *(value.T for value in updated[-3:]))


def solution(mesh):
    sizes = (mesh.shape["dp"], mesh.shape["fsdp"])
    batch = P(AXES, None, None)
    rows = P(AXES, None)
    middle = P(None, AXES, None)
    columns = P(None, AXES)
    weights = (middle, middle, middle, rows, columns)
    moments = tuple(spec for spec in weights for _ in range(2))
    return jax.shard_map(
        functools.partial(local, sizes),
        mesh=mesh,
        in_specs=(batch, batch, rows, rows, P()) + weights + moments,
        out_specs=(batch, batch, P()) + tuple(spec for spec in weights for _ in range(3)),
        check_vma=False,
    )
```

```python
import functools
import math

import jax
import jax.numpy as jnp
import numpy as np
from jax import lax
from jax.experimental import pallas as pl
from jax.experimental.pallas import tpu as pltpu
from jax.sharding import PartitionSpec as P

D = 512
H = 8
DH = 64
FF = 2048
K = 9
NC = FF // D
TAP = 23 + 2 * NC
NORM_EPS = 1e-05
BETA_ONE = 0.9
BETA_TWO = 0.999
ADAM_EPS = 1e-08
CLIP_NORM = 1.0
MATRIX_RATE = 0.03
VECTOR_RATE = 0.4
MATRIX_DECAY = 0.01
VMEM_LIMIT = 60 * 2**20
VMEM_TOP = 67043328

f32 = jnp.float32
bf16 = jnp.bfloat16
NN = (((1,), (0,)), ((), ()))
NT = (((1,), (1,)), ((), ()))
TN = (((0,), (0,)), ((), ()))


def split(value):
    high = value.astype(bf16)
    return high, (value - high.astype(f32)).astype(bf16)


def dot(left, right, dims):
    return lax.dot_general(left, right, dims, preferred_element_type=f32)


def dot3(left, right, dims):
    return dot(left[0], right[0], dims) + (dot(left[0], right[1], dims) + dot(left[1], right[0], dims))


def normalize(values):
    centred = values - jnp.mean(values, axis=-1, keepdims=True)
    inverse = lax.rsqrt(jnp.mean(centred * centred, axis=-1, keepdims=True) + NORM_EPS)
    return centred * inverse, inverse


def normalize_back(scaled, xhat, inverse):
    return (scaled - jnp.mean(scaled, axis=-1, keepdims=True) - xhat * jnp.mean(scaled * xhat, axis=-1, keepdims=True)) * inverse


def column_sum(values):
    return jnp.sum(values, axis=0, keepdims=True)


def row(rows_ref, index):
    return rows_ref[pl.ds(index, 1), :]


def store_split(pair_ref, value):
    high, low = split(value)
    pair_ref[0] = high
    pair_ref[1] = low


def load_split(pair_ref, *index):
    if index:
        return pair_ref[(0,) + index], pair_ref[(1,) + index]
    return pair_ref[0], pair_ref[1]


def ffn_forward_chunk(normed, u_ref, win, wout, bias):
    u = dot3(normed, split(win), NN) + bias
    u_ref[...] = u
    return dot3(split(u * jax.nn.sigmoid(u)), split(wout), NN)


def ffn_backward_chunk(normed, u, df, win, wout):
    sig = jax.nn.sigmoid(u)
    dwout = dot3(split(u * sig), df, TN)
    du = dot3(df, split(wout), NT) * (sig * (1.0 + u * (1.0 - sig)))
    du_split = split(du)
    dwin = dot3(normed, du_split, TN)
    return dwin, dwout, column_sum(du), dot3(du_split, split(win), NT)


def ffn1_forward_kernel(x_ref, win_ref, wout_ref, s_ref, a1_ref, u_ref, normed):
    chunk = pl.program_id(0)

    @pl.when(chunk == 0)
    def _():
        xhat, _ = normalize(x_ref[...])
        store_split(normed, xhat * s_ref[0:1] + s_ref[1:2])
        a1_ref[...] = x_ref[...] + 0.5 * s_ref[17:18]

    out = ffn_forward_chunk(load_split(normed), u_ref, win_ref[...], wout_ref[...], row(s_ref, 23 + chunk))
    a1_ref[...] += 0.5 * out


def ffn1_forward(x, win, wout, s):
    frames = x.shape[0]
    whole = pl.BlockSpec((frames, D), lambda c: (0, 0))
    return pl.pallas_call(
        ffn1_forward_kernel,
        grid=(NC,),
        in_specs=[
            whole,
            pl.BlockSpec((D, D), lambda c: (0, c)),
            pl.BlockSpec((D, D), lambda c: (c, 0)),
            pl.BlockSpec(s.shape, lambda c: (0, 0)),
        ],
        out_specs=[whole, pl.BlockSpec((frames, D), lambda c: (0, c))],
        out_shape=[jax.ShapeDtypeStruct((frames, D), f32), jax.ShapeDtypeStruct((frames, FF), f32)],
        scratch_shapes=[pltpu.VMEM((2, frames, D), bf16)],
        compiler_params=pltpu.CompilerParams(vmem_limit_bytes=VMEM_LIMIT),
        name="ffn1_forward",
    )(x, win, wout, s)


def ffn1_backward_kernel(da_ref, x_ref, u_ref, win_ref, wout_ref, s_ref, dx_ref, dwin_ref, dwout_ref, ds_ref, normed, df):
    chunk = pl.program_id(0)

    @pl.when(chunk == 0)
    def _():
        xhat, _ = normalize(x_ref[...])
        store_split(normed, xhat * s_ref[0:1] + s_ref[1:2])
        half = 0.5 * da_ref[...]
        store_split(df, half)
        ds_ref[...] = jnp.zeros_like(ds_ref)
        ds_ref[2:3] = column_sum(half)
        dx_ref[...] = jnp.zeros_like(dx_ref)

    dwin, dwout, dbias, dnormed = ffn_backward_chunk(load_split(normed), u_ref[...], load_split(df), win_ref[...], wout_ref[...])
    dwin_ref[...] = dwin
    dwout_ref[...] = dwout
    ds_ref[pl.ds(4 + chunk, 1), :] = dbias
    dx_ref[...] += dnormed

    @pl.when(chunk == NC - 1)
    def _():
        xhat, inverse = normalize(x_ref[...])
        dn = dx_ref[...]
        ds_ref[0:1] = column_sum(dn * xhat)
        ds_ref[1:2] = column_sum(dn)
        dx_ref[...] = da_ref[...] + normalize_back(dn * s_ref[0:1], xhat, inverse)


def ffn1_backward(da, x, u, win, wout, s):
    frames = x.shape[0]
    whole = pl.BlockSpec((frames, D), lambda c: (0, 0))
    across = pl.BlockSpec((D, D), lambda c: (0, c))
    down = pl.BlockSpec((D, D), lambda c: (c, 0))
    return pl.pallas_call(
        ffn1_backward_kernel,
        grid=(NC,),
        in_specs=[whole, whole, pl.BlockSpec((frames, D), lambda c: (0, c)), across, down, pl.BlockSpec(s.shape, lambda c: (0, 0))],
        out_specs=[whole, across, down, pl.BlockSpec((8, D), lambda c: (0, 0))],
        out_shape=[
            jax.ShapeDtypeStruct((frames, D), f32),
            jax.ShapeDtypeStruct((D, FF), f32),
            jax.ShapeDtypeStruct((FF, D), f32),
            jax.ShapeDtypeStruct((8, D), f32),
        ],
        scratch_shapes=[pltpu.VMEM((2, frames, D), bf16), pltpu.VMEM((2, frames, D), bf16)],
        compiler_params=pltpu.CompilerParams(vmem_limit_bytes=VMEM_LIMIT),
        name="ffn1_backward",
    )(da, x, u, win, wout, s)


def ffn2_kernel(a3_ref, cot_ref, win_ref, wout_ref, s_ref, out_ref, da3_ref, dwin_ref, dwout_ref, ds_ref, normed, df, hidden, da4):
    step = pl.program_id(0)

    @pl.when(step == 0)
    def _():
        xhat, _ = normalize(a3_ref[...])
        store_split(normed, xhat * s_ref[8:9] + s_ref[9:10])
        da4[...] = a3_ref[...] + 0.5 * s_ref[18:19]

    @pl.when(step < NC)
    def _():
        out = ffn_forward_chunk(load_split(normed), hidden.at[step], win_ref[...], wout_ref[...], row(s_ref, 23 + NC + step))
        da4[...] += 0.5 * out

    @pl.when(step == NC - 1)
    def _():
        xhat, inverse = normalize(da4[...])
        out_ref[...] = xhat * s_ref[10:11] + s_ref[11:12]
        cot = cot_ref[...]
        ds_ref[...] = jnp.zeros_like(ds_ref)
        ds_ref[8:9] = column_sum(cot * xhat)
        ds_ref[9:10] = column_sum(cot)
        grad = normalize_back(cot * s_ref[10:11], xhat, inverse)
        da4[...] = grad
        half = 0.5 * grad
        store_split(df, half)
        ds_ref[2:3] = column_sum(half)
        da3_ref[...] = jnp.zeros_like(da3_ref)

    @pl.when(step >= NC)
    def _():
        dwin, dwout, dbias, dnormed = ffn_backward_chunk(load_split(normed), hidden[step - NC], load_split(df), win_ref[...], wout_ref[...])
        dwin_ref[...] = dwin
        dwout_ref[...] = dwout
        ds_ref[pl.ds(4 + step - NC, 1), :] = dbias
        da3_ref[...] += dnormed

    @pl.when(step == 2 * NC - 1)
    def _():
        xhat, inverse = normalize(a3_ref[...])
        dn = da3_ref[...]
        ds_ref[0:1] = column_sum(dn * xhat)
        ds_ref[1:2] = column_sum(dn)
        da3_ref[...] = da4[...] + normalize_back(dn * s_ref[8:9], xhat, inverse)


def ffn2(a3, cot, win, wout, s):
    frames = a3.shape[0]
    whole = pl.BlockSpec((frames, D), lambda c: (0, 0))
    return pl.pallas_call(
        ffn2_kernel,
        grid=(2 * NC,),
        in_specs=[
            whole,
            whole,
            pl.BlockSpec((D, D), lambda c: (0, lax.rem(c, NC))),
            pl.BlockSpec((D, D), lambda c: (lax.rem(c, NC), 0)),
            pl.BlockSpec(s.shape, lambda c: (0, 0)),
        ],
        out_specs=[
            whole,
            whole,
            pl.BlockSpec((D, D), lambda c: (0, jnp.maximum(c - NC, 0))),
            pl.BlockSpec((D, D), lambda c: (jnp.maximum(c - NC, 0), 0)),
            pl.BlockSpec((16, D), lambda c: (0, 0)),
        ],
        out_shape=[
            jax.ShapeDtypeStruct((frames, D), f32),
            jax.ShapeDtypeStruct((frames, D), f32),
            jax.ShapeDtypeStruct((D, FF), f32),
            jax.ShapeDtypeStruct((FF, D), f32),
            jax.ShapeDtypeStruct((16, D), f32),
        ],
        scratch_shapes=[
            pltpu.VMEM((2, frames, D), bf16),
            pltpu.VMEM((2, frames, D), bf16),
            pltpu.VMEM((NC, frames, D), f32),
            pltpu.VMEM((frames, D), f32),
        ],
        compiler_params=pltpu.CompilerParams(vmem_limit_bytes=VMEM_LIMIT),
        name="ffn2",
    )(a3, cot, win, wout, s)


def sinusoid_table(length):
    offsets = length // 2 - np.arange(length, dtype=np.float64)
    frequency = 10000.0 ** (-2.0 * np.arange(D // 2, dtype=np.float64) / D)
    angles = offsets[:, None] * frequency[None, :]
    table = np.concatenate([np.sin(angles), np.cos(angles)], axis=1).astype(np.float32)
    return np.stack([table, table[::-1]])


def shift_rows(scores):
    return pltpu.roll(scores, scores.shape[1] // 2, 1, stride=1, stride_axis=0)


def pair_masks():
    lane = lax.broadcasted_iota(jnp.int32, (1, 2 * DH), 1)
    first = (lane < DH).astype(f32)
    return first, 1.0 - first


def attention_forward_kernel(length, a1_ref, w_ref, pe_ref, s_ref, segcol_ref, keyrow_ref, a2_ref, qkv_ref, rel_ref, probs_ref, ctx_ref, bias):
    packs = a1_ref.shape[0] // length
    xhat, _ = normalize(a1_ref[...])
    normed = split(xhat * s_ref[2:3] + s_ref[3:4])
    qkv_ref[0] = dot3(normed, split(w_ref[0]), NN) + s_ref[12:13]
    qkv_ref[1] = dot3(normed, split(w_ref[1]), NN)
    qkv_ref[2] = dot3(normed, split(w_ref[2]), NN) + s_ref[13:14]
    rel_ref[...] = dot3(split(pe_ref[0]), split(w_ref[4]), NN)
    query = lax.broadcasted_iota(jnp.int32, (length, length), 0)
    key = lax.broadcasted_iota(jnp.int32, (length, length), 1)
    for pack in range(packs):
        same = segcol_ref[pl.ds(pack * length, length), 0:1] == keyrow_ref[pack : pack + 1, 0:length]
        bias[pack] = jnp.where(same | (query == key), 0.0, -1e30)
    first, second = pair_masks()

    def heads(item, carry):
        pack, pair = item // (H // 2), item % (H // 2)
        frames = pl.ds(pl.multiple_of(pack * length, length), length)
        lanes = pl.ds(pl.multiple_of(pair * 2 * DH, 2 * DH), 2 * DH)
        q = qkv_ref[0, frames, lanes]
        content = q + s_ref[15:16, lanes]
        position = q + s_ref[16:17, lanes]
        k = split(qkv_ref[1, frames, lanes])
        v = split(qkv_ref[2, frames, lanes])
        rel = split(rel_ref[:, lanes])
        total = jnp.zeros_like(q)
        for index, mask in enumerate((first, second)):
            scores = dot3(split(content * mask), k, NT) + shift_rows(dot3(split(position * mask), rel, NT))
            scores = scores * (1.0 / math.sqrt(DH)) + bias[pack]
            weights = jnp.exp(scores - jnp.max(scores, axis=-1, keepdims=True))
            weights = weights / jnp.sum(weights, axis=-1, keepdims=True)
            probs_ref[item * 2 + index] = weights
            total = total + dot3(split(weights), v, NN) * mask
        ctx_ref[frames, lanes] = total
        return carry

    lax.fori_loop(0, packs * (H // 2), heads, 0)
    a2_ref[...] = a1_ref[...] + dot3(split(ctx_ref[...]), split(w_ref[3]), NN) + s_ref[14:15]


def attention_forward(length, a1, square, pe, s, segcol, keyrow):
    frames = a1.shape[0]
    packs = frames // length
    vmem = pl.BlockSpec(memory_space=pltpu.VMEM)
    return pl.pallas_call(
        functools.partial(attention_forward_kernel, length),
        in_specs=[vmem] * 6,
        out_specs=[vmem] * 5,
        out_shape=[
            jax.ShapeDtypeStruct((frames, D), f32),
            jax.ShapeDtypeStruct((3, frames, D), f32),
            jax.ShapeDtypeStruct((length, D), f32),
            jax.ShapeDtypeStruct((packs * H, length, length), f32),
            jax.ShapeDtypeStruct((frames, D), f32),
        ],
        scratch_shapes=[pltpu.VMEM((packs, length, length), f32)],
        compiler_params=pltpu.CompilerParams(vmem_limit_bytes=VMEM_LIMIT),
        name="attention_forward",
    )(a1, square, pe, s, segcol, keyrow)


def attention_backward_kernel(
    length, da2_ref, a1_ref, qkv_ref, rel_ref, probs_ref, ctx_ref, w_ref, pe_ref, s_ref, da1_ref, dw_ref, ds_ref, dctx, dqkv, drel, relback, du, dv
):
    packs = a1_ref.shape[0] // length
    row_index = lax.broadcasted_iota(jnp.int32, (length, length), 0)
    lane_index = lax.broadcasted_iota(jnp.int32, (length, length), 1)
    flip = (row_index + lane_index == length - 1).astype(bf16)
    da2 = da2_ref[...]
    da2_split = split(da2)
    ds_ref[...] = jnp.zeros_like(ds_ref)
    ds_ref[2:3] = column_sum(da2)
    dw_ref[3] = dot3(split(ctx_ref[...]), da2_split, TN)
    dctx[...] = dot3(da2_split, split(w_ref[3]), NT)
    rel_split = split(rel_ref[...])
    relback[...] = dot(flip, rel_split[0], NN) + dot(flip, rel_split[1], NN)
    drel[...] = jnp.zeros_like(drel)
    du[...] = jnp.zeros_like(du)
    dv[...] = jnp.zeros_like(dv)
    first, second = pair_masks()

    def heads(item, carry):
        pack, pair = item // (H // 2), item % (H // 2)
        frames = pl.ds(pl.multiple_of(pack * length, length), length)
        lanes = pl.ds(pl.multiple_of(pair * 2 * DH, 2 * DH), 2 * DH)
        q = qkv_ref[0, frames, lanes]
        content = q + s_ref[15:16, lanes]
        position = q + s_ref[16:17, lanes]
        k = qkv_ref[1, frames, lanes]
        v = split(qkv_ref[2, frames, lanes])
        rel = relback[:, lanes]
        dc = dctx[frames, lanes]
        dcontent = jnp.zeros_like(q)
        dposition = jnp.zeros_like(q)
        dkey = jnp.zeros_like(q)
        dvalue = jnp.zeros_like(q)
        drelation = jnp.zeros_like(rel)
        for index, mask in enumerate((first, second)):
            weights = probs_ref[item * 2 + index]
            dc_split = split(dc * mask)
            dvalue = dvalue + dot3(split(weights), dc_split, TN)
            dweights = dot3(dc_split, v, NT)
            dscores = weights * (dweights - jnp.sum(weights * dweights, axis=-1, keepdims=True)) * (1.0 / math.sqrt(DH))
            ds_split = split(dscores)
            dcontent = dcontent + dot3(ds_split, split(k * mask), NN)
            dkey = dkey + dot3(ds_split, split(content * mask), TN)
            shifted = split(shift_rows(dot(ds_split[0], flip, NN) + dot(ds_split[1], flip, NN)))
            dposition = dposition + dot3(shifted, split(rel * mask), NN)
            drelation = drelation + dot3(shifted, split(position * mask), TN)
        dqkv[0, frames, lanes] = dcontent + dposition
        dqkv[1, frames, lanes] = dkey
        dqkv[2, frames, lanes] = dvalue
        drel[:, lanes] += drelation
        du[0:1, lanes] += column_sum(dcontent)
        dv[0:1, lanes] += column_sum(dposition)
        return carry

    lax.fori_loop(0, packs * (H // 2), heads, 0)
    ds_ref[3:4] = du[0:1]
    ds_ref[4:5] = dv[0:1]
    ds_ref[5:6] = column_sum(dqkv[0])
    ds_ref[6:7] = column_sum(dqkv[2])
    xhat, inverse = normalize(a1_ref[...])
    normed = split(xhat * s_ref[2:3] + s_ref[3:4])
    dnormed = jnp.zeros_like(xhat)
    for index in range(3):
        grad = split(dqkv[index])
        dw_ref[index] = dot3(normed, grad, TN)
        dnormed = dnormed + dot3(grad, split(w_ref[index]), NT)
    dw_ref[4] = dot3(split(pe_ref[1]), split(drel[...]), TN)
    ds_ref[0:1] = column_sum(dnormed * xhat)
    ds_ref[1:2] = column_sum(dnormed)
    da1_ref[...] = da2_ref[...] + normalize_back(dnormed * s_ref[2:3], xhat, inverse)


def attention_backward(length, da2, a1, qkv, rel, probs, ctx, square, pe, s):
    frames = a1.shape[0]
    vmem = pl.BlockSpec(memory_space=pltpu.VMEM)
    return pl.pallas_call(
        functools.partial(attention_backward_kernel, length),
        in_specs=[vmem] * 9,
        out_specs=[vmem] * 3,
        out_shape=[
            jax.ShapeDtypeStruct((frames, D), f32),
            jax.ShapeDtypeStruct((5, D, D), f32),
            jax.ShapeDtypeStruct((8, D), f32),
        ],
        scratch_shapes=[
            pltpu.VMEM((frames, D), f32),
            pltpu.VMEM((3, frames, D), f32),
            pltpu.VMEM((length, D), f32),
            pltpu.VMEM((length, D), f32),
            pltpu.VMEM((8, D), f32),
            pltpu.VMEM((8, D), f32),
        ],
        compiler_params=pltpu.CompilerParams(vmem_limit_bytes=VMEM_LIMIT),
        name="attention_backward",
    )(da2, a1, qkv, rel, probs, ctx, square, pe, s)


EDGE = 8
HALF = (K - 1) // 2
STRIP = 64


def convolution_forward_kernel(a2_ref, proj_ref, w_ref, s_ref, match_ref, a3_ref, u_ref, mixed_ref, padded):
    frames = a2_ref.shape[0]
    xhat, _ = normalize(a2_ref[...])
    normed = split(xhat * s_ref[4:5] + s_ref[5:6])
    u_ref[:, :D] = dot3(normed, split(proj_ref[:, :D]), NN) + s_ref[19:20]
    u_ref[:, D:] = dot3(normed, split(proj_ref[:, D:]), NN) + s_ref[20:21]
    padded[0:EDGE] = jnp.zeros((EDGE, D), f32)
    padded[EDGE + frames :] = jnp.zeros((EDGE, D), f32)
    padded[EDGE : EDGE + frames] = u_ref[:, :D] * jax.nn.sigmoid(u_ref[:, D:]) * match_ref[:, K : K + 1]
    for base in range(0, frames, STRIP):
        total = jnp.zeros((STRIP, D), f32) + s_ref[21:22]
        for tap in range(K):
            source = padded[base + EDGE + tap - HALF : base + EDGE + tap - HALF + STRIP]
            total = total + match_ref[base : base + STRIP, tap : tap + 1] * source * s_ref[TAP + tap : TAP + tap + 1]
        mixed_ref[base : base + STRIP] = total
    inner, _ = normalize(mixed_ref[...])
    inner = inner * s_ref[6:7] + s_ref[7:8]
    a3_ref[...] = a2_ref[...] + dot3(split(inner * jax.nn.sigmoid(inner)), split(w_ref[...]), NN) + s_ref[22:23]


def convolution_forward(a2, proj, weight, s, match):
    frames = a2.shape[0]
    vmem = pl.BlockSpec(memory_space=pltpu.VMEM)
    return pl.pallas_call(
        convolution_forward_kernel,
        in_specs=[vmem] * 5,
        out_specs=[vmem] * 3,
        out_shape=[
            jax.ShapeDtypeStruct((frames, D), f32),
            jax.ShapeDtypeStruct((frames, 2 * D), f32),
            jax.ShapeDtypeStruct((frames, D), f32),
        ],
        scratch_shapes=[pltpu.VMEM((frames + 2 * EDGE, D), f32)],
        compiler_params=pltpu.CompilerParams(vmem_limit_bytes=VMEM_LIMIT),
        name="convolution_forward",
    )(a2, proj, weight, s, match)


def convolution_backward_kernel(
    da3_ref, a2_ref, u_ref, mixed_ref, proj_ref, w_ref, s_ref, match_ref, da2_ref, dproj_ref, dw_ref, ds_ref, padded, dpadded, dgated
):
    frames = a2_ref.shape[0]
    da3 = da3_ref[...]
    da3_split = split(da3)
    ds_ref[...] = jnp.zeros_like(ds_ref)
    ds_ref[2:3] = column_sum(da3)
    hat, inverse = normalize(mixed_ref[...])
    inner = hat * s_ref[6:7] + s_ref[7:8]
    sig = jax.nn.sigmoid(inner)
    dw_ref[...] = dot3(split(inner * sig), da3_split, TN)
    dinner = dot3(da3_split, split(w_ref[...]), NT) * (sig * (1.0 + inner * (1.0 - sig)))
    ds_ref[3:4] = column_sum(dinner * hat)
    ds_ref[4:5] = column_sum(dinner)
    dmixed = normalize_back(dinner * s_ref[6:7], hat, inverse)
    ds_ref[5:6] = column_sum(dmixed)
    zeros = jnp.zeros((EDGE, D), f32)
    padded[0:EDGE] = zeros
    padded[EDGE + frames :] = zeros
    padded[EDGE : EDGE + frames] = u_ref[:, :D] * jax.nn.sigmoid(u_ref[:, D:]) * match_ref[:, K : K + 1]
    dpadded[0:EDGE] = zeros
    dpadded[EDGE + frames :] = zeros
    dpadded[EDGE : EDGE + frames] = dmixed
    for base in range(0, frames, STRIP):
        total = jnp.zeros((STRIP, D), f32)
        center = dpadded[base + EDGE : base + EDGE + STRIP]
        for tap in range(K):
            rows = slice(base + EDGE + tap - HALF, base + EDGE + tap - HALF + STRIP)
            match = match_ref[base : base + STRIP, tap : tap + 1]
            total = total + match * dpadded[rows] * s_ref[TAP + K - 1 - tap : TAP + K - tap]
            ds_ref[8 + tap : 9 + tap] += column_sum(center * (match * padded[rows]))
        dgated[base : base + STRIP] = total * match_ref[base : base + STRIP, K : K + 1]
    gate = jax.nn.sigmoid(u_ref[:, D:])
    dfirst = dgated[...] * gate
    dsecond = dfirst * u_ref[:, :D] * (1.0 - gate)
    ds_ref[6:7] = column_sum(dfirst)
    ds_ref[7:8] = column_sum(dsecond)
    xhat, inverse = normalize(a2_ref[...])
    normed = split(xhat * s_ref[4:5] + s_ref[5:6])
    dfirst = split(dfirst)
    dsecond = split(dsecond)
    dproj_ref[:, :D] = dot3(normed, dfirst, TN)
    dproj_ref[:, D:] = dot3(normed, dsecond, TN)
    dnormed = dot3(dfirst, split(proj_ref[:, :D]), NT) + dot3(dsecond, split(proj_ref[:, D:]), NT)
    ds_ref[0:1] = column_sum(dnormed * xhat)
    ds_ref[1:2] = column_sum(dnormed)
    da2_ref[...] = da3_ref[...] + normalize_back(dnormed * s_ref[4:5], xhat, inverse)


def convolution_backward(da3, a2, u, mixed, proj, weight, s, match):
    frames = a2.shape[0]
    vmem = pl.BlockSpec(memory_space=pltpu.VMEM)
    return pl.pallas_call(
        convolution_backward_kernel,
        in_specs=[vmem] * 8,
        out_specs=[vmem] * 4,
        out_shape=[
            jax.ShapeDtypeStruct((frames, D), f32),
            jax.ShapeDtypeStruct((D, 2 * D), f32),
            jax.ShapeDtypeStruct((D, D), f32),
            jax.ShapeDtypeStruct((24, D), f32),
        ],
        scratch_shapes=[
            pltpu.VMEM((frames + 2 * EDGE, D), f32),
            pltpu.VMEM((frames + 2 * EDGE, D), f32),
            pltpu.VMEM((frames, D), f32),
        ],
        compiler_params=pltpu.CompilerParams(vmem_limit_bytes=VMEM_LIMIT),
        name="convolution_backward",
    )(da3, a2, u, mixed, proj, weight, s, match)


def frame_tables(segments, valid_mask):
    packs, length = segments.shape
    position = jnp.arange(length, dtype=jnp.int32)
    columns = []
    for tap in range(K):
        moved = jnp.roll(segments, HALF - tap, axis=1)
        inside = (position + tap - HALF >= 0) & (position + tap - HALF < length)
        columns.append(((moved == segments) & inside[None, :]).astype(f32))
    columns.append(valid_mask.astype(f32))
    match = jnp.stack(columns, axis=-1).reshape(packs * length, K + 1)
    match = jnp.pad(match, ((0, 0), (0, 128 - K - 1)))
    segcol = jnp.broadcast_to(segments.reshape(packs * length, 1), (packs * length, 128))
    keyrow = jnp.pad(jnp.where(valid_mask > 0, segments, -1), ((0, -packs % 8), (0, 0)))
    return match, segcol, keyrow


def small_rows(parts):
    first, attend, conv, second = parts
    return jnp.concatenate(
        [
            first[0:2],
            attend[0:2],
            conv[0:2],
            conv[3:5],
            second[0:2],
            second[8:10],
            attend[5:7],
            attend[2:5],
            first[2:3],
            second[2:3],
            conv[6:8],
            conv[5:6],
            conv[2:3],
            first[4:8],
            second[4:8],
            conv[8 : 8 + K],
        ],
        axis=0,
    )


def layer(inputs, cotangent, segments, valid_mask, weights):
    feed_in, feed_out, square, proj, s = weights
    packs, length, _ = inputs.shape
    frames = packs * length
    x = inputs.reshape(frames, D)
    cot = cotangent.reshape(frames, D)
    match, segcol, keyrow = frame_tables(segments, valid_mask)
    pe = jnp.asarray(sinusoid_table(length))
    a1, u1 = ffn1_forward(x, feed_in[0], feed_out[0], s)
    a2, qkv, rel, probs, ctx = attention_forward(length, a1, square, pe, s, segcol, keyrow)
    a3, u, mixed = convolution_forward(a2, proj, square[5], s, match)
    out, da3, dwin2, dwout2, ds2 = ffn2(a3, cot, feed_in[1], feed_out[1], s)
    da2, dproj, dw5, dsc = convolution_backward(da3, a2, u, mixed, proj, square[5], s, match)
    da1, dw, dsa = attention_backward(length, da2, a1, qkv, rel, probs, ctx, square, pe, s)
    dx, dwin1, dwout1, ds1 = ffn1_backward(da1, x, u1, feed_in[0], feed_out[0], s)
    grads = (dwin1, dwin2), (dwout1, dwout2), (dw, dw5), dproj, small_rows((ds1, dsa, dsc, ds2))
    return out.reshape(inputs.shape), dx.reshape(inputs.shape), grads

MESH_ID = pl.DeviceIdType.MESH


def chip_grid(devices):
    side = 1
    while side * side * 2 * side * 2 < devices:
        side *= 2
    return side, side, 2 * side


class Place:
    def __init__(self, sizes):
        self.fsdp = sizes[1]
        self.y_size, self.x_size, self.z_size = chip_grid(sizes[0] * sizes[1])
        index = lax.axis_index("dp") * sizes[1] + lax.axis_index("fsdp")
        self.index = index
        self.core = lax.rem(index, 2)
        self.z = lax.rem(index // 2, self.z_size)
        self.x = lax.rem(index // (2 * self.z_size), 2)
        self.y = index // (4 * self.z_size)

    def device(self, y=None, x=None, z=None, core=None):
        y = self.y if y is None else y
        x = self.x if x is None else x
        z = self.z if z is None else z
        core = self.core if core is None else core
        index = ((y * 2 + x) * self.z_size + z) * 2 + core
        return index // self.fsdp, lax.rem(index, self.fsdp)

    def neighbour(self, axis):
        if axis == "core":
            return self.device(core=1 - self.core)
        if axis == "x":
            return self.device(x=1 - self.x)
        if axis == "y":
            return self.device(y=1 - self.y)
        return self.device(z=self.z + (1 if axis == "right" else -1))

    def greet(self):
        barrier = pltpu.get_barrier_semaphore()
        for axis in ("core", "x", "y"):
            pl.semaphore_signal(barrier, inc=1, device_id=self.neighbour(axis), device_id_type=MESH_ID)

        @pl.when(self.z > 0)
        def _():
            pl.semaphore_signal(barrier, inc=1, device_id=self.neighbour("left"), device_id_type=MESH_ID)

        @pl.when(self.z < self.z_size - 1)
        def _():
            pl.semaphore_signal(barrier, inc=1, device_id=self.neighbour("right"), device_id_type=MESH_ID)

        pl.semaphore_wait(barrier, self.peers())

    def peers(self):
        return 3 + (self.z > 0).astype(jnp.int32) + (self.z < self.z_size - 1).astype(jnp.int32)


EVERY = slice(None)


class Piece:
    def __init__(self, lead, first_row, rows, zfirst, near):
        self.lead, self.rows, self.zfirst, self.near = lead, pl.ds(first_row, rows), zfirst, near
        self.far = "y" if near == "x" else "x"

    def own(self, shard):
        return shard.at[self.rows] if self.lead is None else shard.at[self.lead, self.rows]

    def blocks(self, full, place, near, far, z, core):
        y, x = (near, far) if self.near == "y" else (far, near)
        index = (y, x, z, core, self.rows)
        return full.at[index] if self.lead is None else full.at[(self.lead,) + index]

    def here(self, place):
        return (place.x, place.y) if self.near == "x" else (place.y, place.x)


G_RIGHT, G_LEFT, G_NEAR, G_FAR, G_CORE = range(5)


class Gather:
    def __init__(self, place, piece, shard, full, send, recv, local):
        self.place, self.piece, self.shard, self.full = place, piece, shard, full
        self.send, self.recv, self.local = send, recv, local

    def view(self, near, far, z, core=None):
        return self.piece.blocks(self.full, self.place, near, far, z, self.place.core if core is None else core)

    def copy(self, kind, z, ref, axis, source=None):
        return pltpu.make_async_remote_copy(
            src_ref=ref if source is None else source,
            dst_ref=ref,
            send_sem=self.send.at[kind, z],
            recv_sem=self.recv.at[G_RIGHT if kind == G_LEFT else kind, z],
            device_id=self.place.neighbour(axis),
            device_id_type=MESH_ID,
        )

    def z_view(self, z):
        near, far = self.piece.here(self.place)
        return self.view(near if self.piece.zfirst else EVERY, far, z)

    def near_view(self, near, z):
        return self.view(near, self.piece.here(self.place)[1], z)

    def far_view(self, far, z):
        return self.view(EVERY, far, z)

    def core_view(self, core, z):
        return self.view(EVERY, EVERY, z, core)

    def own_copy(self):
        near, far = self.piece.here(self.place)
        return pltpu.make_async_copy(self.piece.own(self.shard), self.view(near, far, self.place.z), self.local)

    def begin(self):
        self.own_copy().start()
        if not self.piece.zfirst:
            near, _ = self.piece.here(self.place)
            self.copy(G_NEAR, self.place.z, self.near_view(near, self.place.z), self.piece.near, self.piece.own(self.shard)).start()

    def z_step(self, z, own, from_left):
        place = self.place
        near, far = self.piece.here(place)

        @pl.when(own)
        def _():
            self.own_copy().wait()
            if not self.piece.zfirst:
                self.copy(G_NEAR, z, self.near_view(1 - near, z), self.piece.near).wait_recv()

        @pl.when(jnp.logical_not(own))
        def _():
            self.copy(G_RIGHT, z, self.z_view(z), "left").wait_recv()

        @pl.when((own | from_left) & (place.z < place.z_size - 1))
        def _():
            self.copy(G_RIGHT, z, self.z_view(z), "right").start()

        @pl.when((own | jnp.logical_not(from_left)) & (place.z > 0))
        def _():
            self.copy(G_LEFT, z, self.z_view(z), "left").start()

        if self.piece.zfirst:
            self.copy(G_NEAR, z, self.near_view(near, z), self.piece.near).start()
        else:
            self.copy(G_FAR, z, self.far_view(far, z), self.piece.far).start()

    def near_step(self, z, own, from_left):
        near, far = self.piece.here(self.place)
        self.copy(G_NEAR, z, self.near_view(1 - near, z), self.piece.near).wait_recv()
        self.copy(G_FAR, z, self.far_view(far, z), self.piece.far).start()

    def far_step(self, z, own, from_left):
        _, far = self.piece.here(self.place)
        self.copy(G_FAR, z, self.far_view(1 - far, z), self.piece.far).wait_recv()
        self.copy(G_CORE, z, self.core_view(self.place.core, z), "core").start()

    def stages(self):
        if self.piece.zfirst:
            return [(0, self.z_step), (1, self.near_step), (2, self.far_step)]
        return [(1, self.z_step), (2, self.far_step)]

    def arrive(self):
        for z in range(self.place.z_size):
            self.copy(G_CORE, z, self.core_view(1 - self.place.core, z), "core").wait_recv()

    def drain(self):
        place = self.place
        near, far = self.piece.here(place)
        for z in range(place.z_size):
            self.copy(G_CORE, z, self.core_view(place.core, z), "core").wait_send()
            self.copy(G_FAR, z, self.far_view(far, z), self.piece.far).wait_send()
            if self.piece.zfirst:
                self.copy(G_NEAR, z, self.near_view(near, z), self.piece.near).wait_send()

            @pl.when((place.z < place.z_size - 1) & (z <= place.z))
            def _():
                self.copy(G_RIGHT, z, self.z_view(z), "right").wait_send()

            @pl.when((place.z > 0) & (z >= place.z))
            def _():
                self.copy(G_LEFT, z, self.z_view(z), "left").wait_send()

        if not self.piece.zfirst:
            self.copy(G_NEAR, place.z, self.near_view(near, place.z), self.piece.near).wait_send()


class GatherProgram:
    PARTS = 3

    def __init__(self, place, groups, offsets):
        self.place, self.groups, self.offsets = place, groups, offsets
        self.cursor = 0
        self.length = self.PARTS * (max(offsets) + place.z_size + 2)

    def begin(self):
        for group in self.groups:
            for piece in group:
                piece.begin()

    def part(self, number):
        step, part = number // self.PARTS, lax.rem(number, self.PARTS)
        place = self.place
        for group, offset in zip(self.groups, self.offsets):
            stages = {}
            for piece in group:
                for index, (behind, work) in enumerate(piece.stages()):
                    stages.setdefault((index if piece.piece.zfirst else 2 * index, behind), []).append(work)
            for (index, behind), works in stages.items():
                distance = step - offset - behind
                for from_left in (True, False):
                    z = place.z - distance if from_left else place.z + distance
                    least = 0 if from_left else 1

                    @pl.when((part == index) & (distance >= least) & (distance < place.z_size) & (z >= 0) & (z < place.z_size))
                    def _():
                        for work in works:
                            work(z, distance == 0, jnp.bool_(from_left))

    def run(self, count):
        last = min(self.length, self.cursor + count)
        if last > self.cursor:
            lax.fori_loop(self.cursor, last, lambda number, carry: (self.part(number), carry)[1], 0)
        self.cursor = max(self.cursor, last)

    def run_in(self, index, each):
        def body(number, carry):
            @pl.when(number < self.length)
            def _():
                self.part(number)

            return carry

        lax.fori_loop(self.cursor + index * each, self.cursor + (index + 1) * each, body, 0)

    def skip(self, count):
        self.cursor = min(self.length, self.cursor + count)

    def run_until(self, group):
        self.run(self.PARTS * (self.offsets[group] + self.place.z_size + 2) - self.cursor)
        for piece in self.groups[group]:
            piece.arrive()

    def drain(self):
        self.run(self.length)
        for group in self.groups:
            for piece in group:
                piece.drain()


def halves(rows, zfirst, lead=None):
    return [Piece(lead, 0, rows // 2, zfirst, "x"), Piece(lead, rows // 2, rows // 2, zfirst, "y")]


def whole_shape(shard, sizes):
    y, x, z = chip_grid(sizes[0] * sizes[1])
    return shard.shape[:-2] + (y, x, z, 2) + shard.shape[-2:]


S_CORE, S_FAR, S_NEAR, S_FROM_LEFT, S_FROM_RIGHT = range(5)


class Scatter:
    def __init__(self, place, piece, full, out, total, cores, fars, nears, lines, send, recv, local):
        self.place, self.piece, self.full, self.out = place, piece, full, out
        self.total, self.cores, self.fars, self.nears, self.lines = total, cores, fars, nears, lines
        self.send, self.recv, self.local = send, recv, local
        self.near, self.far = piece.here(place)

    def part(self, ref, near, far, z):
        y, x = (near, far) if self.piece.near == "y" else (far, near)
        index = (y, x, z)
        return ref.at[index] if self.piece.lead is None else ref.at[(EVERY,) + index]

    def staged(self, ref, *index):
        return ref.at[index] if self.piece.lead is None else ref.at[(EVERY,) + index]

    def add(self, target, source):
        target[...] = target[...] + source[...]

    def copy(self, kind, z, source, target, axis):
        return pltpu.make_async_remote_copy(
            src_ref=source,
            dst_ref=target,
            send_sem=self.send.at[kind, z],
            recv_sem=self.recv.at[kind, z],
            device_id=self.place.neighbour(axis),
            device_id_type=MESH_ID,
        )

    def core_copy(self, z):
        given = self.piece.blocks(self.full, self.place, EVERY, EVERY, z, 1 - self.place.core)
        return self.copy(S_CORE, z, given, self.part(self.cores, EVERY, EVERY, z), "core")

    def own_copy(self, z):
        kept = self.piece.blocks(self.full, self.place, EVERY, EVERY, z, self.place.core)
        return pltpu.make_async_copy(kept, self.part(self.total, EVERY, EVERY, z), self.local.at[z])

    def far_copy(self, z):
        return self.copy(S_FAR, z, self.part(self.total, EVERY, 1 - self.far, z), self.staged(self.fars, EVERY, z), self.piece.far)

    def near_copy(self, z):
        target = self.staged(self.nears, z if self.piece.zfirst else 0)
        return self.copy(S_NEAR, z, self.part(self.total, 1 - self.near, self.far, z), target, self.piece.near)

    def line_view(self, z):
        return self.part(self.total, self.near if self.piece.zfirst else EVERY, self.far, z)

    def line_staged(self, side, z):
        if self.piece.zfirst:
            return self.staged(self.lines, z + 1 - side)
        return self.staged(self.lines, z + 1 - side, EVERY)

    def line_copy(self, z, to_right):
        kind, side = (S_FROM_LEFT, 0) if to_right else (S_FROM_RIGHT, 1)
        return self.copy(kind, z, self.line_view(z), self.line_staged(side, z), "right" if to_right else "left")

    def begin(self):
        for distance in reversed(range(self.place.z_size)):
            for sign in (-1, 1) if distance else (1,):
                z = self.place.z + sign * distance

                @pl.when((z >= 0) & (z < self.place.z_size))
                def _():
                    self.core_copy(z).start()
                    self.own_copy(z).start()

    def core_step(self, z):
        self.core_copy(z).wait_recv()
        self.own_copy(z).wait()
        self.add(self.part(self.total, EVERY, EVERY, z), self.part(self.cores, EVERY, EVERY, z))

    def core_send(self, z):
        self.far_copy(z).start()

    def far_step(self, z):
        self.far_copy(z).wait_recv()
        self.add(self.part(self.total, EVERY, self.far, z), self.staged(self.fars, EVERY, z))

    def far_send(self, z):
        self.near_copy(z).start()

    def near_step(self, z):
        self.near_copy(z).wait_recv()
        self.add(self.part(self.total, self.near, self.far, z), self.staged(self.nears, z))

    def line_step(self, z):
        here = self.place.z

        @pl.when((z >= here) & (here > 0))
        def _():
            self.line_copy(z, True).wait_recv()
            self.add(self.line_view(z), self.line_staged(0, z))

        @pl.when((z <= here) & (here < self.place.z_size - 1))
        def _():
            self.line_copy(z, False).wait_recv()
            self.add(self.line_view(z), self.line_staged(1, z))

    def line_send(self, z):
        here = self.place.z

        @pl.when(z > here)
        def _():
            self.line_copy(z, True).start()

        @pl.when(z < here)
        def _():
            self.line_copy(z, False).start()

    def last_send(self):
        if not self.piece.zfirst:
            self.near_copy(self.place.z).start()

    def finish(self):
        z = self.place.z
        value = self.part(self.total, self.near, self.far, z)[...]
        if not self.piece.zfirst:
            self.near_copy(z).wait_recv()
            value = value + self.staged(self.nears, 0)[...]
        self.piece.own(self.out)[...] = value

    def drain(self):
        place = self.place
        for z in range(place.z_size):
            self.core_copy(z).wait_send()
            self.far_copy(z).wait_send()
            if self.piece.zfirst:
                self.near_copy(z).wait_send()

            @pl.when(z > place.z)
            def _():
                self.line_copy(z, True).wait_send()

            @pl.when(z < place.z)
            def _():
                self.line_copy(z, False).wait_send()

        if not self.piece.zfirst:
            self.near_copy(place.z).wait_send()


def scatter_stages(scatter):
    stages = [(scatter.core_step, scatter.core_send)]
    if scatter.piece.zfirst:
        return stages + [(scatter.far_step, scatter.far_send), (scatter.near_step, None), (scatter.line_step, scatter.line_send)]
    return stages + [(scatter.far_step, None), (scatter.line_step, scatter.line_send)]


class ScatterProgram:
    def __init__(self, place, scatters, lag):
        self.place, self.scatters = place, scatters
        self.staged = []
        for scatter in scatters:
            behind = 0
            for stage, (work, send) in enumerate(scatter_stages(scatter)):
                self.staged.append((behind, work, send))
                behind += 0 if send is None else lag[min(stage, 1)]
        self.length = max(stage[0] for stage in self.staged) + place.z_size
        self.cursor = 0

    def begin(self):
        for scatter in self.scatters:
            scatter.begin()

    def part(self, step):
        place = self.place
        for behind in sorted({stage[0] for stage in self.staged}, reverse=True):
            distance = place.z_size - 1 - (step - behind)

            def side(right, carry):
                z = jnp.where(right == 1, place.z + distance, place.z - distance)

                @pl.when((z >= 0) & (z < place.z_size))
                def _():
                    for action in (1, 2):
                        for stage in self.staged:
                            if stage[0] == behind and stage[action] is not None:
                                stage[action](z)

                return carry

            @pl.when((distance >= 0) & (distance < place.z_size))
            def _():
                lax.fori_loop(0, jnp.where(distance == 0, 1, 2), side, 0)

    def run(self, count):
        last = min(self.length, self.cursor + count)
        if last > self.cursor:
            lax.fori_loop(self.cursor, last, lambda number, carry: (self.part(number), carry)[1], 0)
        self.cursor = max(self.cursor, last)

    def run_in(self, index, each=1):
        for extra in range(each):
            self.part(self.cursor + index * each + extra)

    def skip(self, count):
        self.cursor = min(self.length, self.cursor + count)

    def last_send(self):
        self.run(self.length)
        for scatter in self.scatters:
            scatter.last_send()

    def finish(self):
        for scatter in self.scatters:
            scatter.finish()
        for scatter in self.scatters:
            scatter.drain()


def scatter_scratch(piece, columns, place_sizes, lead):
    y, x, z = chip_grid(place_sizes[0] * place_sizes[1])
    rows = piece.rows.size
    head = () if piece.lead is None else (lead,)
    return [
        pltpu.VMEM(head + (y, x, z, rows, columns), f32),
        pltpu.VMEM(head + (y, x, z, rows, columns), f32),
        pltpu.VMEM(head + (2, z, rows, columns), f32),
        pltpu.VMEM(head + ((z,) if piece.zfirst else (1,)) + (rows, columns), f32),
        pltpu.VMEM(head + ((z + 1,) if piece.zfirst else (z + 1, 2)) + (rows, columns), f32),
    ]


def greet_all(place, sizes):
    devices = sizes[0] * sizes[1]
    barrier = pltpu.get_barrier_semaphore()

    def signal(offset, carry):
        other = lax.rem(place.index + offset, devices)
        pl.semaphore_signal(barrier, inc=1, device_id=(other // sizes[1], lax.rem(other, sizes[1])), device_id_type=MESH_ID)
        return carry

    lax.fori_loop(1, devices, signal, 0)
    pl.semaphore_wait(barrier, devices - 1)


def square_tile(values):
    squares = values * values
    tile = jnp.zeros((8, 128), f32)
    for r in range(0, values.shape[0], 8):
        for c in range(0, values.shape[1], 128):
            tile = tile + squares[r : r + 8, c : c + 128]
    return tile


def share_norm(place, sizes, outs, norms, own, send, recv):
    devices = sizes[0] * sizes[1]
    tile = jnp.zeros((8, 128), f32)
    for out in outs:
        for lead in range(out.shape[0]) if len(out.shape) == 3 else (None,):
            tile = tile + square_tile(out[...] if lead is None else out[lead])
    own[...] = tile
    norms[place.index] = tile

    def copy(offset, to):
        other = lax.rem(place.index + offset, devices)
        slot = place.index if to else other
        return pltpu.make_async_remote_copy(
            src_ref=own,
            dst_ref=norms.at[slot],
            send_sem=send.at[other],
            recv_sem=recv.at[slot],
            device_id=(other // sizes[1], lax.rem(other, sizes[1])),
            device_id_type=MESH_ID,
        )

    lax.fori_loop(1, devices, lambda offset, carry: (copy(offset, True).start(), carry)[1], 0)
    lax.fori_loop(1, devices, lambda offset, carry: (copy(offset, False).wait_recv(), carry)[1], 0)
    lax.fori_loop(1, devices, lambda offset, carry: (copy(offset, True).wait_send(), carry)[1], 0)


LAG = (1, 1)
WIDTH = FF // 8


def lanes_of(index, width=WIDTH):
    return pl.ds(pl.multiple_of(index * width, width), width)


def hidden_bias(s_ref, first_row, index):
    return s_ref.at[pl.ds(first_row + index // 2, 1), lanes_of(lax.rem(index, 2))]


def in_chunk(ref, index):
    return ref.at[:, :, :, :, :, lanes_of(index)]


def in_target(full, index):
    rows = full.shape[-2] // NC
    return full.at[:, :, :, :, pl.ds(pl.multiple_of(index // 2 * rows, rows), rows), lanes_of(lax.rem(index, 2))]


def out_chunk(ref, index):
    return ref.at[index // 4, lax.rem(index // 2, 2), pl.ds(lax.rem(index, 2) * 2, 2)]


class Copies:
    def __init__(self, semaphores):
        self.semaphores, self.started = semaphores, []

    def start(self, source, target):
        copy = pltpu.make_async_copy(source, target, self.semaphores.at[len(self.started)])
        copy.start()
        self.started.append(copy)
        return copy


class Outbox:
    def __init__(self, slots, semaphores):
        self.slots, self.semaphores = slots, semaphores

    def put(self, index, value, target, columns=None):
        slot = lax.rem(index, 2)
        source = self.slots.at[slot] if columns is None else self.slots.at[slot, :, :, :, :, :, :columns]
        copy = pltpu.make_async_copy(source, target, self.semaphores.at[slot])

        @pl.when(index >= 2)
        def _():
            copy.wait()

        source[...] = value
        copy.start()

    def close(self, count, target, columns=None):
        for index in range(max(0, count - 2), count):
            slot = index % 2
            source = self.slots.at[slot] if columns is None else self.slots.at[slot, :, :, :, :, :, :columns]
            pltpu.make_async_copy(source, target, self.semaphores.at[slot]).wait()


def make_scatters(place, pieces, full, out, scratch, sems, start, first_row=0):
    send, recv, local = sems
    made = []
    for index, piece in enumerate(pieces):
        count = start + index
        arrays = [array.at[(EVERY,) * (len(array.shape) - 2) + (pl.ds(first_row, piece.rows.size),)] for array in scratch[5 * index : 5 * index + 5]]
        made.append(Scatter(place, piece, full, out, *arrays, send.at[count], recv.at[count], local.at[count]))
    return made


class Hand:
    def __init__(self, place, semaphore):
        self.place, self.semaphore = place, semaphore

    def over(self):
        place = self.place

        def signal(axis):
            pl.semaphore_signal(self.semaphore, inc=1, device_id=place.neighbour(axis), device_id_type=MESH_ID)

        for axis in ("core", "x", "y"):
            signal(axis)
        pl.when(place.z > 0)(lambda: signal("left"))
        pl.when(place.z < place.z_size - 1)(lambda: signal("right"))

    def taken(self):
        pl.semaphore_wait(self.semaphore, self.place.peers())


def pieces_scratch(listed, sizes):
    scratch = []
    for pieces, columns in listed:
        for piece in pieces:
            scratch += scatter_scratch(piece, columns, sizes, None if piece.lead is None else piece.lead.size)
    return scratch


def feed_out_pass(index, hidden, df, box, out_full):
    u = hidden[:, lanes_of(index)]
    value = dot3(split(u * jax.nn.sigmoid(u)), load_split(df), TN)
    box.put(index, value.reshape(2, 2, 64, D), out_chunk(out_full, index))


def feed_in_pass(index, hidden, df, normed, win, wout, total, ds_ref, first_row, box, grid, in_full):
    u = hidden[:, lanes_of(index)]
    sig = jax.nn.sigmoid(u)
    weight = split(out_chunk(wout, index)[...].reshape(WIDTH, D))
    du = dot3(load_split(df), weight, NT) * (sig * (1.0 + u * (1.0 - sig)))
    hidden_bias(ds_ref, first_row, index)[...] = column_sum(du)
    du = split(du)
    weight = split(in_chunk(win, index)[...].reshape(D, WIDTH))
    total[...] += dot3(du, weight, NT)
    value = dot3(load_split(normed), du, TN)
    box.put(index, value.reshape(grid + (D // math.prod(grid), WIDTH)), in_target(in_full, index), WIDTH)


def attend_back_values(length, packs, dctx_turned, probs_ref, grads):
    def heads(item, carry):
        pack, pair = item // (H // 2), lax.rem(item, H // 2)
        frames = pl.ds(pl.multiple_of(pack * length, length), length)
        values = []
        for index in range(2):
            rows = pl.ds(pl.multiple_of(pair * 2 * DH + index * DH, DH), DH)
            weights = probs_ref[frames, head_lanes(pair, index, length)]
            values.append((rows, dot3(split(dctx_turned[rows, frames]), split(weights), NN)))
        for rows, value in values:
            grads[2, rows, frames] = value
        return carry

    lax.fori_loop(0, packs * (H // 2), heads, 0)


def attend_back(length, packs, turned, qkv_ref, dctx_ref, probs_ref, s_turned, flip, grads, drel_ref, sums_ref, between):
    q_ref, k_ref, rel_ref = turned
    lane = lax.broadcasted_iota(jnp.int32, (1, 128), 1)

    def heads(item, carry):
        between(item)
        pack, pair = item // (H // 2), lax.rem(item, H // 2)
        frames = pl.ds(pl.multiple_of(pack * length, length), length)
        lanes = pl.ds(pl.multiple_of(pair * 2 * DH, 2 * DH), 2 * DH)
        v = split(qkv_ref[2, frames, lanes])
        dc = dctx_ref[frames, lanes]
        both = []
        for index, mask in enumerate(pair_masks()):
            rows = pl.ds(pl.multiple_of(pair * 2 * DH + index * DH, DH), DH)
            weights = probs_ref[frames, head_lanes(pair, index, length)]
            q = q_ref[rows, frames]
            content, position = q + s_turned[rows, 15:16], q + s_turned[rows, 16:17]
            both.append((rows, weights, dc * mask, content, position, k_ref[rows, frames], rel_ref[rows]))
        dweights = [dot3(split(head[2]), v, NT) for head in both]
        dscores = [
            split(head[1] * (grad - jnp.sum(head[1] * grad, axis=-1, keepdims=True)) * (1.0 / math.sqrt(DH)))
            for head, grad in zip(both, dweights)
        ]
        flipped = [dot(grad[0], flip, NN) + dot(grad[1], flip, NN) for grad in dscores]
        dcontent = [dot3(split(head[5]), grad, NT) for head, grad in zip(both, dscores)]
        shifted = [split(shift_rows(grad)) for grad in flipped]
        dkey = [dot3(split(head[3]), grad, NN) for head, grad in zip(both, dscores)]
        dposition = [dot3(split(head[6]), grad, NT) for head, grad in zip(both, shifted)]
        drelation = [dot3(split(head[4]), grad, NN) for head, grad in zip(both, shifted)]
        for index, head in enumerate(both):
            rows = head[0]
            grads[1, rows, frames] = dkey[index]
            grads[0, rows, frames] = dcontent[index] + dposition[index]
            drel_ref[rows] += drelation[index]
            sum_u = jnp.sum(dcontent[index], axis=1, keepdims=True)
            sum_v = jnp.sum(dposition[index], axis=1, keepdims=True)
            sums_ref[rows] += jnp.where(lane == 0, sum_u, jnp.where(lane == 1, sum_v, 0.0))
        return carry

    lax.fori_loop(0, packs * (H // 2), heads, 0)


def group_pieces(rows, near, first_row=0):
    far = "y" if near == "x" else "x"
    return [Piece(None, first_row, rows // 2, True, near), Piece(None, first_row + rows // 2, rows // 2, False, far)]


def small_pieces():
    return [Piece(None, 0, 16, False, "x")]


def run_together(programs, count):
    starts = [program.cursor for program in programs]

    def body(step, carry):
        for program, start in zip(programs, starts):
            program.part(start + step)
        return carry

    lax.fori_loop(0, count, body, 0)
    for program in programs:
        program.skip(count)


def backward_kernel(sizes, length, *refs):
    (cot_in, x_in, a3_in, a2_in, a1_in, u1_in, qkv_in, rel_in, probs_in, ctx_in, u_in, mixed_in, s_in, match_in, pe_in) = refs[:15]
    in_all, out_all, sq_all, conv_all = refs[15:19]
    out_out, dx_out, in_full2, out_full2, conv_full, sq_full, in_full1, out_full1 = refs[19:27]
    g_in1, g_in2, g_out1, g_out2, g_sq, g_conv, g_small, norms = refs[27:35]
    (da3, a2, mixed, ctx, a1, u, conv, square, qkv, rel, hidden, s_ref, match, ds_ref, normed, df, box_in, box_out, small_full) = refs[35:54]
    scratch_one, scratch_two, scratch_three, scratch_small = refs[54:64], refs[64:74], refs[74:84], refs[84:89]
    send, recv, local, loads, stores, box_sems, free, norm_own, norm_send, norm_recv = refs[89:]
    frames = da3.shape[0]
    packs = frames // length
    grid = chip_grid(sizes[0] * sizes[1]) + (2,)
    place = Place(sizes)
    loading, storing = Copies(loads), Copies(stores)
    sems = (send, recv, local)

    def program(*parts):
        scatters = []
        for pieces, full, out, scratch, start, first_row in parts:
            scatters += make_scatters(place, pieces, full, out, scratch, sems, start, first_row)
        return ScatterProgram(place, scatters, LAG)

    def group(full, out, near, scratch, start):
        return group_pieces(out.shape[0], near), full, out, scratch, start, 0

    def half_group(half, full, out, near, scratch, start):
        rows = out.shape[0] // 2
        return group_pieces(rows, near, half * rows), full, out, scratch, start, half * rows // 2

    out_program2 = program(group(out_full2, g_out2, "x", scratch_one, 0))
    in_program2 = program(group(in_full2, g_in2, "y", scratch_two, 2))
    conv_program = program(group(conv_full, g_conv, "x", scratch_three, 4))
    sq_program = program(group(sq_full, g_sq, "y", scratch_one, 6))
    out_program1 = program(group(out_full1, g_out1, "x", scratch_two, 8))
    early_program1 = program(half_group(0, in_full1, g_in1, "y", scratch_three, 10))
    late_program1 = program(half_group(1, in_full1, g_in1, "x", scratch_three, 12), (small_pieces(), small_full, g_small, scratch_small, 14, 0))
    hand_one, hand_two, hand_three = (Hand(place, free.at[index]) for index in range(3))
    in_outbox = Outbox(box_in, box_sems.at[0])
    out_outbox = Outbox(box_out, box_sems.at[1])
    slots = in_outbox.slots
    cot, result, a3, da4 = ctx, a1, a2, qkv.at[0]
    side = max(frames, D)
    q_turned, k_turned = u.at[:D, :frames], u.at[:D, side : side + frames]
    u = u.at[:frames, : 2 * D]

    def put(slot, value, full, matrix):
        rows = slots.shape[-2]
        target = full.at[:, :, :, :, pl.ds(matrix * rows, rows)]
        slots[slot] = value.reshape(box_in.shape[1:])
        return storing.start(slots.at[slot], target)

    def second_module(win, wout):
        waits = [
            loading.start(source, target)
            for source, target in ((s_in, s_ref), (a3_in, a3), (in_all.at[1], win), (out_all.at[1], wout), (cot_in, cot))
        ]
        greet_all(place, sizes)
        waits[0].wait()
        waits[1].wait()
        later = [
            loading.start(source, target)
            for source, target in (
                (match_in, match),
                (mixed_in, mixed),
                (sq_all, square),
                (u_in, u),
                (conv_all, conv),
                (rel_in, rel),
            )
        ]
        ds_ref[...] = jnp.zeros_like(ds_ref)
        xhat, _ = normalize(a3[...])
        store_split(normed, xhat * s_ref[8:9] + s_ref[9:10])
        da4[...] = a3[...] + 0.5 * s_ref[18:19]
        waits[2].wait()
        waits[3].wait()

        def forward_chunk(index, carry):
            weight = in_chunk(win, index)[...].reshape(D, WIDTH)
            value = dot3(load_split(normed), split(weight), NN) + hidden_bias(s_ref, 23 + NC, index)[...]
            hidden[:, lanes_of(index)] = value
            weight = out_chunk(wout, index)[...].reshape(WIDTH, D)
            da4[...] += 0.5 * dot3(split(value * jax.nn.sigmoid(value)), split(weight), NN)
            return carry

        lax.fori_loop(0, 8, forward_chunk, 0)
        waits[4].wait()
        xhat, inverse = normalize(da4[...])
        result[...] = xhat * s_ref[10:11] + s_ref[11:12]
        store_result = storing.start(result, out_out)
        grad = cot[...]
        ds_ref[10:11] = column_sum(grad * xhat)
        ds_ref[11:12] = column_sum(grad)
        grad = normalize_back(grad * s_ref[10:11], xhat, inverse)
        da4[...] = grad
        half = 0.5 * grad
        store_split(df, half)
        ds_ref[18:19] = column_sum(half)
        da3[...] = jnp.zeros_like(da3)
        later.append(loading.start(ctx_in, ctx))

        def out_pass(index, carry):
            feed_out_pass(index, hidden, df, out_outbox, out_full2)
            return carry

        lax.fori_loop(0, 8, out_pass, 0)
        out_outbox.close(8, out_chunk(out_full2, 0))
        out_program2.begin()
        store_result.wait()
        later.append(loading.start(a1_in, a1))

        def in_pass(index, carry):
            feed_in_pass(index, hidden, df, normed, win, wout, da3, ds_ref, 23 + NC, in_outbox, grid, in_full2)

            @pl.when(lax.rem(index, 4) == 3)
            def _():
                out_program2.run_in(index // 4)

            return carry

        lax.fori_loop(0, 8, in_pass, 0)
        out_program2.skip(2)
        in_outbox.close(8, in_target(in_full2, 0), WIDTH)
        in_program2.begin()
        xhat, inverse = normalize(a3[...])
        dn = da3[...]
        ds_ref[8:9] = column_sum(dn * xhat)
        ds_ref[9:10] = column_sum(dn)
        da3[...] = da4[...] + normalize_back(dn * s_ref[8:9], xhat, inverse)
        for copy in later:
            copy.wait()

    piece = pltpu.VMEM((frames, D), f32)
    feed_weights = (pltpu.VMEM(grid + (D // math.prod(grid), FF), f32), pltpu.VMEM(grid + (FF // math.prod(grid), D), f32))
    pl.run_scoped(second_module, *feed_weights)
    load_a2 = loading.start(a2_in, a2)
    load_qkv = loading.start(qkv_in, qkv)
    probs = hidden.at[:, : probs_in.shape[1]]
    load_probs = loading.start(probs_in, probs)

    def convolution(padded, dpadded, dgated):
        da3_split = split(da3[...])
        ds_ref[22:23] = column_sum(da3[...])
        hat, inverse = normalize(mixed[...])
        inner = hat * s_ref[6:7] + s_ref[7:8]
        sig = jax.nn.sigmoid(inner)
        store_square = put(0, dot3(split(inner * sig), da3_split, TN), conv_full, 2)
        dinner = dot3(da3_split, split(square[5].reshape(D, D)), NT) * (sig * (1.0 + inner * (1.0 - sig)))
        ds_ref[6:7] = column_sum(dinner * hat)
        ds_ref[7:8] = column_sum(dinner)
        dmixed = normalize_back(dinner * s_ref[6:7], hat, inverse)
        ds_ref[21:22] = column_sum(dmixed)
        zeros = jnp.zeros((EDGE, D), f32)
        padded[0:EDGE] = zeros
        padded[EDGE + frames :] = zeros
        padded[EDGE : EDGE + frames] = u[:, :D] * jax.nn.sigmoid(u[:, D:]) * match[:, K : K + 1]
        dpadded[0:EDGE] = zeros
        dpadded[EDGE + frames :] = zeros
        dpadded[EDGE : EDGE + frames] = dmixed
        run_together((out_program2, in_program2), 1)
        for base in range(0, frames, STRIP):
            total = jnp.zeros((STRIP, D), f32)
            center = dpadded[base + EDGE : base + EDGE + STRIP]
            for tap in range(K):
                rows = slice(base + EDGE + tap - HALF, base + EDGE + tap - HALF + STRIP)
                same = match[base : base + STRIP, tap : tap + 1]
                total = total + same * dpadded[rows] * s_ref[TAP + K - 1 - tap : TAP + K - tap]
                ds_ref[TAP + tap : TAP + tap + 1] += column_sum(center * (same * padded[rows]))
            dgated[base : base + STRIP] = total * match[base : base + STRIP, K : K + 1]
        out_program2.run(1)
        gate = jax.nn.sigmoid(u[:, D:])
        dfirst = dgated[...] * gate
        dsecond = dfirst * u[:, :D] * (1.0 - gate)
        ds_ref[19:20] = column_sum(dfirst)
        ds_ref[20:21] = column_sum(dsecond)
        dfirst, dsecond = split(dfirst), split(dsecond)
        load_a2.wait()
        xhat, inverse = normalize(a2[...])
        store_split(normed, xhat * s_ref[4:5] + s_ref[5:6])
        store_square.wait()
        stored = [put(half, dot3(load_split(normed), grad, TN), conv_full, half) for half, grad in enumerate((dfirst, dsecond))]
        dn = dot3(dfirst, split(conv[:, :, :, :, :, :D].reshape(D, D)), NT) + dot3(dsecond, split(conv[:, :, :, :, :, D:].reshape(D, D)), NT)
        ds_ref[4:5] = column_sum(dn * xhat)
        ds_ref[5:6] = column_sum(dn)
        da3[...] = da3[...] + normalize_back(dn * s_ref[4:5], xhat, inverse)
        for copy in stored:
            copy.wait()
        run_together((out_program2, in_program2), 1)

    padded = pltpu.VMEM((frames + 2 * EDGE, D), f32)
    pl.run_scoped(convolution, padded, padded, piece)
    load_x = loading.start(x_in, a2)
    dn_ref = mixed

    def attention(dqkv, dctx_turned, dctx, relback, drel, row_sums, s_turned):
        da2_split = split(da3[...])
        ds_ref[14:15] = column_sum(da3[...])
        stored = [put(0, dot3(split(ctx[...]), da2_split, TN), conv_full, 3)]
        dctx[...] = dot3(da2_split, split(square[3].reshape(D, D)), NT)
        dctx_turned[...] = dctx[...].T
        xhat, _ = normalize(a1[...])
        store_split(normed, xhat * s_ref[2:3] + s_ref[3:4])
        load_probs.wait()
        attend_back_values(length, packs, dctx_turned, probs, dqkv)
        grad = dqkv[2].T
        ds_ref[13:14] = column_sum(grad)
        grad = split(grad)
        stored.append(put(1, dot3(load_split(normed), grad, TN), conv_full, 4))
        dn_ref[...] = dot3(grad, split(square[2].reshape(D, D)), NT)
        run_together((out_program2, in_program2), 1)
        out_program2.last_send()
        row_index = lax.broadcasted_iota(jnp.int32, (length, length), 0)
        lane_index = lax.broadcasted_iota(jnp.int32, (length, length), 1)
        flip = (row_index + lane_index == length - 1).astype(bf16)
        rel_split = split(rel[...])
        relback[...] = (dot(flip, rel_split[0], NN) + dot(flip, rel_split[1], NN)).T
        load_qkv.wait()
        q_turned[...] = qkv[0].T
        k_turned[...] = qkv[1].T
        s_turned[...] = s_ref[...].T
        drel[...] = jnp.zeros_like(drel)
        row_sums[...] = jnp.zeros_like(row_sums)
        load_pe = loading.start(pe_in, rel)
        for copy in stored:
            copy.wait()
        conv_program.begin()

        def between(item):
            @pl.when(lax.rem(item, 4) == 1)
            def _():
                in_program2.run_in(item // 4)

            @pl.when(lax.rem(item, 4) == 3)
            def _():
                conv_program.run_in(item // 4)

        attend_back(length, packs, (q_turned, k_turned, relback), qkv, dctx, probs, s_turned, flip, dqkv, drel, row_sums, between)
        conv_program.skip(2)
        in_program2.skip(2)
        in_program2.last_send()
        loading.start(u1_in, hidden.at[:, : u1_in.shape[1]])
        out_program2.finish()
        hand_one.over()
        ds_ref[15:17] = row_sums[...].T[0:2]

        def weight_gradient(index, carry):
            grad = dqkv[index].T
            ds_ref[12:13] = jnp.where(index == 0, column_sum(grad), ds_ref[12:13])
            grad = split(grad)
            rows = slots.shape[-2]
            slots[index] = dot3(load_split(normed), grad, TN).reshape(box_in.shape[1:])
            target = sq_full.at[:, :, :, :, pl.ds(pl.multiple_of(index * rows, rows), rows)]
            pltpu.make_async_copy(slots.at[index], target, box_sems.at[0, index]).start()
            dn_ref[...] += dot3(grad, split(square[index].reshape(D, D)), NT)
            return carry

        lax.fori_loop(0, 2, weight_gradient, 0)
        conv_program.run(1)
        in_program2.finish()
        hand_two.over()
        load_pe.wait()
        rows = slots.shape[-2]
        for index in range(2):
            pltpu.make_async_copy(slots.at[index], sq_full.at[:, :, :, :, pl.ds(index * rows, rows)], box_sems.at[0, index]).wait()
        stored = [put(0, dot3(split(rel[...]), split(drel[...].T), TN), sq_full, 2)]
        xhat, inverse = normalize(a1[...])
        dn = dn_ref[...]
        ds_ref[2:3] = column_sum(dn * xhat)
        ds_ref[3:4] = column_sum(dn)
        da3[...] = da3[...] + normalize_back(dn * s_ref[2:3], xhat, inverse)
        for copy in stored:
            copy.wait()

    features = pltpu.VMEM((D, frames), f32)
    positions = pltpu.VMEM((D, length), f32)
    pl.run_scoped(
        attention,
        pltpu.VMEM((3, D, frames), f32),
        features,
        piece,
        positions,
        positions,
        pltpu.VMEM((D, 128), f32),
        pltpu.VMEM((D, SMALL_LANES), f32),
    )

    x, dx = a2, mixed

    def first_module(win, wout):
        waits = [loading.start(in_all.at[0], win), loading.start(out_all.at[0], wout)]
        hand_one.taken()
        sq_program.begin()
        load_x.wait()
        xhat, _ = normalize(x[...])
        store_split(normed, xhat * s_ref[0:1] + s_ref[1:2])
        half = 0.5 * da3[...]
        store_split(df, half)
        ds_ref[17:18] = column_sum(half)
        dx[...] = jnp.zeros_like(dx)
        pltpu.make_async_copy(u1_in, hidden.at[:, : u1_in.shape[1]], loads.at[18]).wait()

        def out_pass(index, carry):
            feed_out_pass(index, hidden, df, out_outbox, out_full1)

            return carry

        lax.fori_loop(0, 8, out_pass, 0)
        out_outbox.close(8, out_chunk(out_full1, 0))
        hand_two.taken()
        out_program1.begin()
        run_together((conv_program, sq_program), 1)
        for copy in waits:
            copy.wait()

        def in_pass(index, carry):
            feed_in_pass(index, hidden, df, normed, win, wout, dx, ds_ref, 23, in_outbox, grid, in_full1)

            @pl.when(lax.rem(index, 2) == 0)
            def _():
                conv_program.run_in(index // 2)
                out_program1.run_in(index // 2)

            @pl.when(lax.rem(index, 2) == 1)
            def _():
                sq_program.run_in(index // 2)

            @pl.when(index == 5)
            def _():
                for scatter in conv_program.scatters:
                    scatter.last_send()
                conv_program.finish()
                hand_three.over()
                hand_three.taken()
                early_program1.begin()

            return carry

        lax.fori_loop(0, 8, in_pass, 0)
        for running in (sq_program, out_program1):
            running.skip(4)
        in_outbox.close(8, in_target(in_full1, 0), WIDTH)

    pl.run_scoped(first_module, *feed_weights)
    xhat, inverse = normalize(x[...])
    dn = dx[...]
    ds_ref[0:1] = column_sum(dn * xhat)
    ds_ref[1:2] = column_sum(dn)
    small_full[...] = ds_ref[...].T.reshape(small_full.shape)
    late_program1.begin()
    dx[...] = da3[...] + normalize_back(dn * s_ref[0:1], xhat, inverse)
    store_dx = storing.start(dx, dx_out)
    run_together((sq_program, out_program1, early_program1), 1)
    run_together((sq_program, out_program1, early_program1, late_program1), 1)
    sq_program.last_send()
    out_program1.last_send()
    run_together((early_program1, late_program1), 3)
    early_program1.last_send()
    late_program1.last_send()
    for ending in (sq_program, out_program1, early_program1, late_program1):
        ending.finish()
    share_norm(place, sizes, (g_in1, g_in2, g_out1, g_out2, g_sq, g_conv, g_small), norms, norm_own, norm_send, norm_recv)
    store_dx.wait()


def backward(sizes, length, cot, x, saved, full):
    a1, u1, qkv, rel, probs, ctx, a2, u, mixed, a3, s, match = saved
    in_all, out_all, sq_all, conv_all, _ = full
    frames = cot.shape[0]
    grid = chip_grid(sizes[0] * sizes[1]) + (2,)
    z_size = grid[2]
    devices = math.prod(grid)
    pe = jnp.asarray(sinusoid_table(length)[1])
    rows = D // devices
    hbm, vmem = pl.BlockSpec(memory_space=pl.ANY), pl.BlockSpec(memory_space=pltpu.VMEM)
    piece = (frames, D)
    shapes = [
        piece,
        piece,
        grid + (NC * rows, D),
        grid + (NC * rows, D),
        grid + (5 * rows, D),
        grid + (3 * rows, D),
        grid + (NC * rows, D),
        grid + (NC * rows, D),
        (NC * rows, D),
        (NC * rows, D),
        (NC * rows, D),
        (NC * rows, D),
        (3 * rows, D),
        (5 * rows, D),
        (rows, SMALL_LANES),
        (devices, 8, 128),
    ]
    listed = [(group_pieces(count * rows, "x"), D) for count in (NC, NC, 5)] + [(small_pieces(), SMALL_LANES)]
    return pl.pallas_call(
        functools.partial(backward_kernel, sizes, length),
        in_specs=[hbm] * 19,
        out_specs=[hbm] * 8 + [vmem] * 8,
        out_shape=[jax.ShapeDtypeStruct(shape, f32) for shape in shapes],
        scratch_shapes=[pltpu.VMEM(piece, f32)] * 5
        + [
            pltpu.VMEM((max(frames, D), 2 * max(frames, D)), f32),
            pltpu.VMEM(grid + (rows, 2 * D), f32),
            pltpu.VMEM((6,) + grid + (rows, D), f32),
            pltpu.VMEM((3, frames, D), f32),
            pltpu.VMEM((length, D), f32),
            pltpu.VMEM((frames, max(FF, H * length)), f32),
            pltpu.VMEM((SMALL_LANES, D), f32),
            pltpu.VMEM((frames, 128), f32),
            pltpu.VMEM((SMALL_LANES, D), f32),
            pltpu.VMEM((2, frames, D), bf16),
            pltpu.VMEM((2, frames, D), bf16),
            pltpu.VMEM((2,) + grid + (rows, D), f32),
            pltpu.VMEM((2, 2, 2, FF // devices, D), f32),
            pltpu.VMEM(grid + (rows, SMALL_LANES), f32),
        ]
        + pieces_scratch(listed, sizes)
        + [
            pltpu.SemaphoreType.DMA((15, 5, z_size)),
            pltpu.SemaphoreType.DMA((15, 5, z_size)),
            pltpu.SemaphoreType.DMA((15, z_size)),
            pltpu.SemaphoreType.DMA((24,)),
            pltpu.SemaphoreType.DMA((10,)),
            pltpu.SemaphoreType.DMA((2, 2)),
            pltpu.SemaphoreType.REGULAR((3,)),
            pltpu.VMEM((8, 128), f32),
            pltpu.SemaphoreType.DMA((devices,)),
            pltpu.SemaphoreType.DMA((devices,)),
        ],
        compiler_params=pltpu.CompilerParams(collective_id=1, has_side_effects=True, vmem_limit_bytes=VMEM_TOP),
        name="backward",
    )(cot, x, a3, a2, a1, u1, qkv, rel, probs, ctx, u, mixed, s, match, pe, in_all, out_all, sq_all, conv_all)

SMALL_LANES = 128


def plans():
    def feed(half):
        return [
            [Piece(pl.ds(half, 1), 0, 8, False, "x"), Piece(pl.ds(half, 1), 8, 8, False, "y")],
            [Piece(pl.ds(half, 1), 0, 32, True, "x"), Piece(pl.ds(half, 1), 32, 32, True, "y")],
        ]

    small = [Piece(None, 0, 16, False, "x")]
    square = [
        Piece(pl.ds(0, 4), 0, 8, False, "x"),
        Piece(pl.ds(0, 4), 8, 8, False, "y"),
        Piece(pl.ds(4, 2), 0, 8, True, "x"),
        Piece(pl.ds(4, 2), 8, 8, True, "y"),
    ]
    return [small] + feed(0), [square, halves(16, True)], feed(1)


def match_table(segments, valid):
    length = segments.shape[1]
    rows = lax.broadcasted_iota(jnp.int32, (128, length), 0)
    position = lax.broadcasted_iota(jnp.int32, (1, length), 1)
    table = jnp.where(rows == K, valid, jnp.where(rows == K + 1, segments, 0.0))
    for tap in range(K):
        moved = segments if tap == HALF else pltpu.roll(segments, (HALF - tap) % length, 1)
        inside = (position + tap - HALF >= 0) & (position + tap - HALF < length)
        table = jnp.where(rows == tap, jnp.where((moved == segments) & inside, 1.0, 0.0), table)
    return table.T


def forward_kernel(sizes, length, offsets, *refs):
    x_ref, seg_ref, valid_ref, pe_ref, small_ref, in_shard, out_shard, sq_shard, conv_shard = refs[:9]
    (a1_out, u1_out, qkv_out, rel_out, probs_out, ctx_out, a2_out, u_out, mixed_out, a3_out, s_out, match_out) = refs[9:21]
    in_full, out_full, sq_full, conv_full, small_full = refs[21:26]
    (a1, u1, qkv, rel, probs, ctx, a2, u, mixed, a3, s_ref, match, normed, padded, bias, small_own, small_whole, win, wout, square, conv) = refs[26:47]
    send, recv, local, loads, stores = refs[47:]
    frames = x_ref.shape[0]
    packs = frames // length

    place = Place(sizes)
    place.greet()
    small_own[...] = jnp.zeros_like(small_own)
    small_own[:, : small_ref.shape[1]] = small_ref[...]
    first, middle, last = plans()
    sources = [
        [(small_own, small_full), (in_shard, in_full), (out_shard, out_full)],
        [(sq_shard, sq_full), (conv_shard, conv_full)],
        [(in_shard, in_full), (out_shard, out_full)],
    ]
    groups, count = [], 0
    for plan, pairs in zip((first, middle, last), sources):
        group = []
        for pieces, (shard, full) in zip(plan, pairs):
            for piece in pieces:
                group.append(Gather(place, piece, shard, full, send.at[count], recv.at[count], local.at[count]))
                count += 1
        groups.append(group)
    program = GatherProgram(place, groups, offsets)
    program.begin()

    spilled = []

    def spill(source, target):
        copy = pltpu.make_async_copy(source, target, stores.at[len(spilled)])
        copy.start()
        spilled.append(copy)

    program.run(3)
    for pack in range(packs):
        rows = slice(pack * length, (pack + 1) * length)
        match[rows] = match_table(seg_ref[pack : pack + 1].astype(f32), valid_ref[pack : pack + 1].astype(f32))
    spill(match, match_out)
    query = lax.broadcasted_iota(jnp.int32, (length, length), 0)
    key = lax.broadcasted_iota(jnp.int32, (length, length), 1)
    for pack in range(packs):
        keyrow = jnp.where(valid_ref[pack : pack + 1] > 0, seg_ref[pack : pack + 1], -1).astype(f32)
        same = match[pack * length : (pack + 1) * length, K + 1 : K + 2] == keyrow
        bias[pack] = jnp.where(same | (query == key), 0.0, -1e30)

    program.run_until(0)
    load_small = pltpu.make_async_copy(small_full, small_whole, loads.at[0])
    load_in = pltpu.make_async_copy(in_full.at[0], win, loads.at[1])
    load_out = pltpu.make_async_copy(out_full.at[0], wout, loads.at[2])
    for load in (load_small, load_in, load_out):
        load.start()
    program.run(1)
    load_small.wait()
    s_ref[...] = small_whole[...].reshape(D, SMALL_LANES).T
    spill(s_ref, s_out)
    xhat, _ = normalize(x_ref[...])
    store_split(normed, xhat * s_ref[0:1] + s_ref[1:2])
    a1[...] = x_ref[...] + 0.5 * s_ref[17:18]
    load_in.wait()
    load_out.wait()
    width = FF // 8

    def chunk(index, carry):
        lanes = pl.ds(pl.multiple_of(index * width, width), width)
        bias_row = s_ref[pl.ds(23 + index // 2, 1), pl.ds(pl.multiple_of(lax.rem(index, 2) * width, width), width)]
        weight = win[:, :, :, :, :, lanes].reshape(D, width)
        value = dot3(load_split(normed), split(weight), NN) + bias_row
        u1[:, lanes] = value
        weight = wout[index // 4, lax.rem(index // 2, 2), pl.ds(lax.rem(index, 2) * 2, 2)].reshape(width, D)
        a1[...] += 0.5 * dot3(split(value * jax.nn.sigmoid(value)), split(weight), NN)
        program.run_in(index, 1)
        return carry

    lax.fori_loop(0, 8, chunk, 0)
    program.skip(8)
    spill(u1, u1_out)
    spill(a1, a1_out)
    xhat, _ = normalize(a1[...])
    store_split(normed, xhat * s_ref[2:3] + s_ref[3:4])

    program.run_until(1)
    load_square = pltpu.make_async_copy(sq_full, square, loads.at[3])
    load_conv = pltpu.make_async_copy(conv_full, conv, loads.at[4])
    load_square.start()
    load_conv.start()
    program.run(1)
    load_square.wait()
    load_conv.wait()

    def weight_split(index):
        return split(square[index].reshape(D, D))

    qkv[0] = dot3(load_split(normed), weight_split(0), NN) + s_ref[12:13]
    program.run(1)
    qkv[1] = dot3(load_split(normed), weight_split(1), NN)
    program.run(1)
    qkv[2] = dot3(load_split(normed), weight_split(2), NN) + s_ref[13:14]
    rel[...] = dot3(split(pe_ref[...]), weight_split(4), NN)
    program.run(1)
    spill(qkv, qkv_out)
    spill(rel, rel_out)
    attend(length, packs, qkv, rel, s_ref, bias, probs, ctx, lambda item: program.run_in(item, 1))
    program.skip(packs * (H // 2))
    spill(probs, probs_out)
    spill(ctx, ctx_out)
    a2[...] = a1[...] + dot3(split(ctx[...]), weight_split(3), NN) + s_ref[14:15]
    spill(a2, a2_out)
    program.run(1)

    xhat, _ = normalize(a2[...])
    store_split(normed, xhat * s_ref[4:5] + s_ref[5:6])
    for half in range(2):
        lanes = slice(half * D, (half + 1) * D)
        u[:, lanes] = dot3(load_split(normed), split(conv[:, :, :, :, :, lanes].reshape(D, D)), NN) + s_ref[19 + half : 20 + half]
        program.run(1)
    spill(u, u_out)
    mix(u, match, s_ref, padded, mixed)
    spill(mixed, mixed_out)
    program.run(1)
    inner, _ = normalize(mixed[...])
    inner = inner * s_ref[6:7] + s_ref[7:8]
    a3[...] = a2[...] + dot3(split(inner * jax.nn.sigmoid(inner)), weight_split(5), NN) + s_ref[22:23]
    spill(a3, a3_out)

    program.run_until(2)
    program.drain()
    for copy in spilled:
        copy.wait()


def head_lanes(pair, index, length):
    return pl.ds(pl.multiple_of((pair * 2 + index) * length, length), length)


def attend(length, packs, qkv_ref, rel_ref, s_ref, bias, probs_ref, ctx_ref, between):
    first, second = pair_masks()

    def heads(item, carry):
        pack, pair = item // (H // 2), lax.rem(item, H // 2)
        frames = pl.ds(pl.multiple_of(pack * length, length), length)
        lanes = pl.ds(pl.multiple_of(pair * 2 * DH, 2 * DH), 2 * DH)
        q = qkv_ref[0, frames, lanes]
        content = q + s_ref[15:16, lanes]
        position = q + s_ref[16:17, lanes]
        k = split(qkv_ref[1, frames, lanes])
        v = split(qkv_ref[2, frames, lanes])
        rel = split(rel_ref[:, lanes])
        total = jnp.zeros_like(q)
        for index, mask in enumerate((first, second)):
            scores = dot3(split(content * mask), k, NT) + shift_rows(dot3(split(position * mask), rel, NT))
            scores = scores * (1.0 / math.sqrt(DH)) + bias[pack]
            weights = jnp.exp(scores - jnp.max(scores, axis=-1, keepdims=True))
            weights = weights / jnp.sum(weights, axis=-1, keepdims=True)
            probs_ref[frames, head_lanes(pair, index, length)] = weights
            total = total + dot3(split(weights), v, NN) * mask
        ctx_ref[frames, lanes] = total
        between(item)
        return carry

    lax.fori_loop(0, packs * (H // 2), heads, 0)


def mix(u_ref, match_ref, s_ref, padded, mixed_ref):
    frames = mixed_ref.shape[0]
    padded[0:EDGE] = jnp.zeros((EDGE, D), f32)
    padded[EDGE + frames :] = jnp.zeros((EDGE, D), f32)
    padded[EDGE : EDGE + frames] = u_ref[:, :D] * jax.nn.sigmoid(u_ref[:, D:]) * match_ref[:, K : K + 1]
    for base in range(0, frames, STRIP):
        total = jnp.zeros((STRIP, D), f32) + s_ref[21:22]
        for tap in range(K):
            source = padded[base + EDGE + tap - HALF : base + EDGE + tap - HALF + STRIP]
            total = total + match_ref[base : base + STRIP, tap : tap + 1] * source * s_ref[TAP + tap : TAP + tap + 1]
        mixed_ref[base : base + STRIP] = total


def forward(sizes, x, segments, valid_mask, weights):
    feed_in, feed_out, square, proj, small = weights
    frames = x.shape[0]
    packs, length = segments.shape
    devices = sizes[0] * sizes[1]
    grid = chip_grid(devices) + (2,)
    z_size = grid[2]
    pe = jnp.asarray(sinusoid_table(length)[0])
    small_rows_here = small.shape[1]
    vmem = pl.BlockSpec(memory_space=pltpu.VMEM)
    kept = [
        (frames, D),
        (frames, FF),
        (3, frames, D),
        (length, D),
        (frames, H * length),
        (frames, D),
        (frames, D),
        (frames, 2 * D),
        (frames, D),
        (frames, D),
        (SMALL_LANES, D),
        (frames, 128),
    ]
    full = [
        (2,) + grid + feed_in.shape[1:],
        (2,) + grid + feed_out.shape[1:],
        (6,) + grid + square.shape[1:],
        grid + proj.shape,
        grid + (small_rows_here, SMALL_LANES),
    ]
    pieces = sum(len(p) for plan in plans() for p in plan)
    outs = pl.pallas_call(
        functools.partial(forward_kernel, sizes, length, GATHER_OFFSETS),
        in_specs=[vmem] * 9,
        out_specs=[pl.BlockSpec(memory_space=pl.ANY)] * (len(kept) + len(full)),
        out_shape=[jax.ShapeDtypeStruct(shape, f32) for shape in kept + full],
        scratch_shapes=[pltpu.VMEM(shape, f32) for shape in kept]
        + [
            pltpu.VMEM((2, frames, D), bf16),
            pltpu.VMEM((frames + 2 * EDGE, D), f32),
            pltpu.VMEM((packs, length, length), f32),
            pltpu.VMEM((small_rows_here, SMALL_LANES), f32),
            pltpu.VMEM(full[4], f32),
            pltpu.VMEM(full[0][1:], f32),
            pltpu.VMEM(full[1][1:], f32),
            pltpu.VMEM(full[2], f32),
            pltpu.VMEM(full[3], f32),
            pltpu.SemaphoreType.DMA((pieces, 5, z_size)),
            pltpu.SemaphoreType.DMA((pieces, 5, z_size)),
            pltpu.SemaphoreType.DMA((pieces,)),
            pltpu.SemaphoreType.DMA((5,)),
            pltpu.SemaphoreType.DMA((len(kept),)),
        ],
        compiler_params=pltpu.CompilerParams(collective_id=0, has_side_effects=True, vmem_limit_bytes=VMEM_LIMIT),
        name="forward",
    )(x, segments, valid_mask, pe, small.T, feed_in, feed_out, square, proj)
    return outs[: len(kept)], outs[len(kept) :]


GATHER_OFFSETS = (0, 3, 6)


def adamw_kernel(step_ref, norms_ref, out_ref, dx_ref, *refs):
    (g_in1, g_in2, g_out1, g_out2, g_sq, g_conv, g_small), refs = refs[:7], refs[7:]
    weights, firsts, seconds, outs = refs[0:5], refs[5:10], refs[10:15], refs[16:]
    outs[15][...] = out_ref[...]
    outs[16][...] = dx_ref[...]
    norm = jnp.sqrt(jnp.sum(norms_ref[...], axis=(0, 1, 2), keepdims=True)[0])
    refs[15][...] = norm
    clip = jnp.minimum(1.0, CLIP_NORM / (norm + 1e-06))

    def geometric(_, carry):
        one, one_power, two, two_power = carry
        return one + one_power, one_power * BETA_ONE, two + two_power, two_power * BETA_TWO

    zero, unit = jnp.float32(0.0), jnp.float32(1.0)
    one, _, two, _ = lax.fori_loop(0, step_ref[0], geometric, (zero, unit, zero, unit))
    first_scale = jnp.full((1, 1), (1.0 - BETA_ONE) * one, f32)
    second_scale = jnp.full((1, 1), (1.0 - BETA_TWO) * two, f32)
    first_scale = 1.0 / first_scale
    second_scale = 1.0 / second_scale

    def update(number, index, gradient, rate, decay):
        weight, first, second = weights[number][index], firsts[number][index], seconds[number][index]
        clipped = clip * gradient
        first_next = BETA_ONE * first + (1.0 - BETA_ONE) * clipped
        second_next = BETA_TWO * second + (1.0 - BETA_TWO) * clipped * clipped
        step = (first_next * first_scale) / (jnp.sqrt(second_next * second_scale) + ADAM_EPS)
        if decay:
            step = step + decay * weight
        outs[3 * number][index] = first_next
        outs[3 * number + 1][index] = second_next
        outs[3 * number + 2][index] = weight - rate * step

    rows = weights[0].shape[1]

    def block(ref, index):
        return ref[index * rows : (index + 1) * rows]

    for half, (g_in, g_out) in enumerate(((g_in1, g_out1), (g_in2, g_out2))):
        for index in range(NC):
            update(0, (half, EVERY, slice(index * D, (index + 1) * D)), block(g_in, index), MATRIX_RATE, MATRIX_DECAY)
        update(1, half, g_out[...], MATRIX_RATE, MATRIX_DECAY)
    for index, (ref, place) in enumerate(((g_sq, 0), (g_sq, 1), (g_conv, 4), (g_conv, 3), (g_sq, 2), (g_conv, 2))):
        update(2, index, block(ref, place), MATRIX_RATE, MATRIX_DECAY)
    for half in range(2):
        update(3, (EVERY, slice(half * D, (half + 1) * D)), block(g_conv, half), MATRIX_RATE, MATRIX_DECAY)
    update(4, EVERY, g_small[:, : weights[4].shape[1]], VECTOR_RATE, 0.0)


def adamw(step, norms, out, dx, grads, weights, firsts, seconds):
    vmem = pl.BlockSpec(memory_space=pltpu.VMEM)
    shapes = [jax.ShapeDtypeStruct((1, 1), f32)]
    for weight in weights:
        shapes += [jax.ShapeDtypeStruct(weight.shape, f32)] * 3
    shapes += [jax.ShapeDtypeStruct(out.shape, f32), jax.ShapeDtypeStruct(dx.shape, f32)]
    return pl.pallas_call(
        adamw_kernel,
        in_specs=[pl.BlockSpec(memory_space=pltpu.SMEM)] + [vmem] * 25,
        out_specs=[vmem] * 18,
        out_shape=shapes,
        compiler_params=pltpu.CompilerParams(vmem_limit_bytes=VMEM_LIMIT),
        name="adamw",
    )(step, norms, out, dx, *grads, *weights, *firsts, *seconds)


AXES = ("dp", "fsdp")


def gather_plain(feed_in, feed_out, square, proj, small):
    feed_in = lax.all_gather(feed_in, AXES, axis=1, tiled=True)
    feed_out = lax.all_gather(feed_out, AXES, axis=1, tiled=True)
    square = lax.all_gather(square, AXES, axis=1, tiled=True)
    proj = lax.all_gather(proj, AXES, axis=0, tiled=True)
    small = lax.all_gather(small, AXES, axis=1, tiled=True)
    return feed_in, feed_out, square, proj, small


def scatter_plain(grads):
    (in1, in2), (out1, out2), (dw, dw5), dproj, ds = grads

    def reduce(matrices):
        part = lax.psum_scatter(jnp.stack(matrices), AXES, scatter_dimension=1, tiled=True)
        return part.reshape(-1, D)

    def quarters(matrix):
        return [matrix[:, index * D : (index + 1) * D] for index in range(NC)]

    parts = [
        reduce(quarters(in1)),
        reduce(quarters(in2)),
        lax.psum_scatter(out1, AXES, scatter_dimension=0, tiled=True),
        lax.psum_scatter(out2, AXES, scatter_dimension=0, tiled=True),
        reduce([dw[0], dw[1], dw[4]]),
        reduce([dproj[:, :D], dproj[:, D:], dw5, dw[3], dw[2]]),
        lax.psum_scatter(ds.T, AXES, scatter_dimension=0, tiled=True),
    ]
    total = lax.psum(sum(jnp.sum(part * part) for part in parts), AXES)
    return tuple(parts), jnp.zeros((1, 8, 128), f32).at[0, 0, 0].set(total)


def overlapped_layer(sizes, inputs, cotangent, segments, valid_mask, weights):
    packs, length, _ = inputs.shape
    frames = packs * length
    x = inputs.reshape(frames, D)
    saved, full = forward(sizes, x, segments, valid_mask, weights)
    outs = backward(sizes, length, cotangent.reshape(frames, D), x, saved, full)
    out, dx, grads, norms = outs[0], outs[1], outs[8:15], outs[15]
    return out.reshape(inputs.shape), dx.reshape(inputs.shape), grads, norms


def local(sizes, inputs, cotangent, segments, valid_mask, step_count, *state):
    weights, moments = state[:5], state[5:]
    devices = sizes[0] * sizes[1]
    if D // devices % 16 == 0 and chip_grid(devices)[:2] == (2, 2):
        out, dx, grads, norms = overlapped_layer(sizes, inputs, cotangent, segments, valid_mask, weights)
    else:
        out, dx, grads = layer(inputs, cotangent, segments, valid_mask, gather_plain(*weights))
        grads, norms = scatter_plain(grads)

    def turned(values):
        return tuple(values[:-1]) + (values[-1].T,)

    norm, *updated = adamw(step_count, norms, out, dx, grads, turned(weights), turned(moments[0::2]), turned(moments[1::2]))
    updated, (out, dx) = updated[:-2], updated[-2:]
    return (out, dx, norm.reshape(()), *updated[:-3], *(value.T for value in updated[-3:]))


def solution(mesh):
    sizes = (mesh.shape["dp"], mesh.shape["fsdp"])
    batch = P(AXES, None, None)
    rows = P(AXES, None)
    middle = P(None, AXES, None)
    columns = P(None, AXES)
    weights = (middle, middle, middle, rows, columns)
    moments = tuple(spec for spec in weights for _ in range(2))
    return jax.shard_map(
        functools.partial(local, sizes),
        mesh=mesh,
        in_specs=(batch, batch, rows, rows, P()) + weights + moments,
        out_specs=(batch, batch, P()) + tuple(spec for spec in weights for _ in range(3)),
        check_vma=False,
    )
```
